32 devices in a mesh: seq: 8 (over y, x, core), fsdp: 4 (over z).
Axes of the slice: x: 2, y: 2, z: 4, core: 2. Of those that a mesh axis runs over, the one named last changes fastest.
Arguments:
- tokens: bfloat16 [8192, 768], P(('seq', 'fsdp')), may hold values from -6 to 6
- query_small: bfloat16 [768, 512], P(('seq', 'fsdp')), may hold values from -0.21875 to 0.21875
- key_small: bfloat16 [768, 512], P(('seq', 'fsdp')), may hold values from -0.21875 to 0.21875
- value_small: bfloat16 [768, 512], P(('seq', 'fsdp')), may hold values from -0.21875 to 0.21875
- out_small: bfloat16 [512, 768], P(None, ('seq', 'fsdp')), may hold values from -1.5 to 1.5
- query_large: bfloat16 [768, 768], P(('seq', 'fsdp')), may hold values from -0.21875 to 0.21875
- key_large: bfloat16 [768, 768], P(('seq', 'fsdp')), may hold values from -0.21875 to 0.21875
- value_large: bfloat16 [768, 768], P(('seq', 'fsdp')), may hold values from -0.21875 to 0.21875
- out_large: bfloat16 [768, 768], P(None, ('seq', 'fsdp')), may hold values from -1.25 to 1.25
- attend_gain: bfloat16 [768], P(('seq', 'fsdp')), may hold values from 0.5 to 1.5
- attend_router: bfloat16 [768], P(('seq', 'fsdp')), may hold values from -0.15625 to 0.15625
- gate_small: bfloat16 [768, 1024], P(('seq', 'fsdp')), may hold values from -0.21875 to 0.21875
- up_small: bfloat16 [768, 1024], P(('seq', 'fsdp')), may hold values from -0.21875 to 0.21875
- down_small: bfloat16 [1024, 768], P(None, ('seq', 'fsdp')), may hold values from -0.1875 to 0.1875
- gate_large: bfloat16 [768, 4096], P(('seq', 'fsdp')), may hold values from -0.21875 to 0.21875
- up_large: bfloat16 [768, 4096], P(('seq', 'fsdp')), may hold values from -0.21875 to 0.21875
- down_large: bfloat16 [4096, 768], P(None, ('seq', 'fsdp')), may hold values from -0.09375 to 0.09375
- feed_gain: bfloat16 [768], P(('seq', 'fsdp')), may hold values from 0.5 to 1.5
- feed_router: bfloat16 [768], P(('seq', 'fsdp')), may hold values from -0.15625 to 0.15625
- lengths: int32 [2], replicated, may hold values from 256 to 7936, as said below
- query_route: int32 [32, 32], replicated, may hold values from 0 to 256, as said below
- key_route: int32 [32, 32], replicated, may hold values from 0 to 256, as said below
- feed_route: int32 [32, 32], P(('seq', 'fsdp')), may hold values from 0 to 256, as said below
- cotangent: bfloat16 [8192, 768], P(('seq', 'fsdp')), may hold values from -6 to 6
Outputs:
- result: bfloat16 [8192, 768], P(('seq', 'fsdp'))
- tokens_grad: float32 [8192, 768], P(('seq', 'fsdp'))
- query_small_grad: float32 [768, 512], P(('seq', 'fsdp'))
- key_small_grad: float32 [768, 512], P(('seq', 'fsdp'))
- value_small_grad: float32 [768, 512], P(('seq', 'fsdp'))
- out_small_grad: float32 [512, 768], P(None, ('seq', 'fsdp'))
- query_large_grad: float32 [768, 768], P(('seq', 'fsdp'))
- key_large_grad: float32 [768, 768], P(('seq', 'fsdp'))
- value_large_grad: float32 [768, 768], P(('seq', 'fsdp'))
- out_large_grad: float32 [768, 768], P(None, ('seq', 'fsdp'))
- attend_gain_grad: float32 [768], P(('seq', 'fsdp'))
- attend_router_grad: float32 [768], P(('seq', 'fsdp'))
- gate_small_grad: float32 [768, 1024], P(('seq', 'fsdp'))
- up_small_grad: float32 [768, 1024], P(('seq', 'fsdp'))
- down_small_grad: float32 [1024, 768], P(None, ('seq', 'fsdp'))
- gate_large_grad: float32 [768, 4096], P(('seq', 'fsdp'))
- up_large_grad: float32 [768, 4096], P(('seq', 'fsdp'))
- down_large_grad: float32 [4096, 768], P(None, ('seq', 'fsdp'))
- feed_gain_grad: float32 [768], P(('seq', 'fsdp'))
- feed_router_grad: float32 [768], P(('seq', 'fsdp'))
The draws below stay inside these ranges and needn't reach their ends.
Inputs may be any that keep to these rules, and one draw needn't show every extreme that they name: `lengths`: entry 1 (the short document) lies between 256 and 512; both entries together leave at most 128 padding tokens at the end of the pack. `query_route`: row b lists distinct live positions inside aligned block b of 256 tokens, filled slots first and 256 in empty ones; every block with a live token has at least one; in every draw some block fills all 32. `key_route`: row b lists distinct live positions inside aligned block b of 256 tokens, filled slots first and 256 in empty ones; every block with a live token has at least one; in every draw some block fills all 32. `feed_route`: row b lists distinct live positions inside aligned block b of 256 tokens, filled slots first and 256 in empty ones; every block with a live token has at least one; in every draw some block fills all 32.
All inputs are finite; a program needn't handle non-finite values.
Results may differ from the reference program's by a relative error of at most 0.014.
Values may be sent and summed in bfloat16 or wider, within the bound.
No kernel may reach another device: no remote copies, remote signals or barrier semaphores. Data moves between devices by JAX's collectives and lax.ppermute only.
A program may use at most 256 MiB of HBM per device.

```python
import math
import jax
import jax.numpy as jnp
from jax import lax

D = 768
HL = 8
HDL = 64
FFL = 1024
HH = 12
HDH = 64
FFH = 4096
RADIUS = 128
TOK_DEV = 256
TOKENS = 8192
BLOCKS = 32
CAPQ = 32
CAPK = 32
CAPF = 32


def make_lengths(key):
    shorter = jax.random.randint(jax.random.fold_in(key, 11), (), TOKENS // 32, TOKENS // 16 + 1)
    padding = jax.random.randint(jax.random.fold_in(key, 12), (), 0, TOK_DEV // 2 + 1)
    longer = TOKENS - padding - shorter
    return jnp.stack([longer, shorter]).astype(jnp.int32)


def make_routes(key, salt, capacity):
    lengths = make_lengths(key)
    live_end = lengths[0] + lengths[1]
    branch = jax.random.fold_in(key, salt)
    starts = jnp.arange(BLOCKS, dtype=jnp.int32) * TOK_DEV
    live = jnp.clip(live_end - starts, 0, TOK_DEV)
    counts = jax.random.randint(jax.random.fold_in(branch, 1), (BLOCKS,), 1, capacity + 1)
    forced = jax.random.randint(jax.random.fold_in(branch, 2), (), 0, BLOCKS // 2)
    counts = jnp.where(jnp.arange(BLOCKS, dtype=jnp.int32) == forced, capacity, counts)
    counts = jnp.minimum(counts, live)
    column = jnp.arange(TOK_DEV, dtype=jnp.int32)
    scores = jax.random.randint(jax.random.fold_in(branch, 3), (BLOCKS, TOK_DEV), 0, 1 << 18) * TOK_DEV + column[None, :]
    scores = jnp.where(column[None, :] < live[:, None], scores, -1 - column[None, :])
    unused, picked = lax.top_k(scores, capacity)
    slot_index = jnp.arange(capacity, dtype=jnp.int32)
    return jnp.where(slot_index[None, :] < counts[:, None], picked, TOK_DEV).astype(jnp.int32)


def draw_lengths(key, part):
    return make_lengths(key)


def draw_query_route(key, part):
    return make_routes(key, 21, CAPQ)


def draw_key_route(key, part):
    return make_routes(key, 22, CAPK)


def draw_feed_route(key, part):
    return make_routes(key, 23, CAPF)


def shard_levels(stream_key, shape, cuts, low, high):
    def one(axis_at, parts):
        heights = jax.random.uniform(jax.random.fold_in(jax.random.fold_in(stream_key, 6), axis_at), (parts,), jnp.float32, low / len(cuts), high / len(cuts))
        return jnp.repeat(jnp.exp(heights), shape[axis_at] // parts).reshape((-1,) + (1,) * (len(shape) - axis_at - 1))

    loudness = one(*cuts[0])
    for cut in cuts[1:]:
        loudness = loudness * one(*cut)
    return loudness


def gaussian(own_key, dims, width, reach, shards=(), held_as=jnp.bfloat16):
    array = jax.random.normal(own_key, dims, jnp.float32) * width
    if len(shards) > 0:
        array = shard_levels(own_key, dims, shards, -0.22, 0.18) * array
    return jnp.clip(array, min=-reach, max=reach).astype(held_as)


def setup_inputs(seed: int = 0) -> dict:
    arg_keys = jax.random.split(jax.random.key(seed), 25)
    return {
        "tokens": gaussian(arg_keys[0], (TOKENS, D), 1.0, 6.0, ((0, 32),)),
        "query_small": gaussian(arg_keys[1], (D, HL * HDL), D ** -0.5, 0.21875, ((0, 32),)),
        "key_small": gaussian(arg_keys[2], (D, HL * HDL), D ** -0.5, 0.21875, ((0, 32),)),
        "value_small": gaussian(arg_keys[3], (D, HL * HDL), D ** -0.5, 0.21875, ((0, 32),)),
        "out_small": gaussian(arg_keys[4], (HL * HDL, D), (max(HL * HDL // 32, 1)) ** -0.5, 1.5, ((1, 32),)),
        "query_large": gaussian(arg_keys[5], (D, HH * HDH), D ** -0.5, 0.21875, ((0, 32),)),
        "key_large": gaussian(arg_keys[6], (D, HH * HDH), D ** -0.5, 0.21875, ((0, 32),)),
        "value_large": gaussian(arg_keys[7], (D, HH * HDH), D ** -0.5, 0.21875, ((0, 32),)),
        "out_large": gaussian(arg_keys[8], (HH * HDH, D), (max(HH * HDH // 32, 1)) ** -0.5, 1.25, ((1, 32),)),
        "attend_gain": jnp.clip(1.0 + 0.1 * jax.random.normal(arg_keys[9], (D,), jnp.float32), 0.5, 1.5).astype(jnp.bfloat16),
        "attend_router": gaussian(arg_keys[10], (D,), (2 * D) ** -0.5, 0.15625, ((0, 32),)),
        "gate_small": gaussian(arg_keys[11], (D, FFL), D ** -0.5, 0.21875, ((0, 32),)),
        "up_small": gaussian(arg_keys[12], (D, FFL), D ** -0.5, 0.21875, ((0, 32),)),
        "down_small": gaussian(arg_keys[13], (FFL, D), FFL ** -0.5, 0.1875, ((1, 32),)),
        "gate_large": gaussian(arg_keys[14], (D, FFH), D ** -0.5, 0.21875, ((0, 32),)),
        "up_large": gaussian(arg_keys[15], (D, FFH), D ** -0.5, 0.21875, ((0, 32),)),
        "down_large": gaussian(arg_keys[16], (FFH, D), FFH ** -0.5, 0.09375, ((1, 32),)),
        "feed_gain": jnp.clip(1.0 + 0.1 * jax.random.normal(arg_keys[17], (D,), jnp.float32), 0.5, 1.5).astype(jnp.bfloat16),
        "feed_router": gaussian(arg_keys[18], (D,), (2 * D) ** -0.5, 0.15625, ((0, 32),)),
        "lengths": draw_lengths(jax.random.fold_in(arg_keys[24], 71), 0),
        "query_route": draw_query_route(jax.random.fold_in(arg_keys[24], 71), 0),
        "key_route": draw_key_route(jax.random.fold_in(arg_keys[24], 71), 0),
        "feed_route": draw_feed_route(jax.random.fold_in(arg_keys[24], 71), 0),
        "cotangent": gaussian(arg_keys[23], (TOKENS, D), 1.0, 6.0, ((0, 32),)),
    }


@jax.custom_vjp
def low(v):
    return lax.optimization_barrier(v.astype(jnp.bfloat16)).astype(jnp.float32)

@jax.custom_vjp
def low_back(v):
    return v

def low_keep(v):
    return (low(v), None)

def low_pass(kept, grad):
    return (grad,)

def back_keep(v):
    return (v, None)

def back_low(kept, grad):
    return (low(grad),)
low.defvjp(low_keep, low_pass)
low_back.defvjp(back_keep, back_low)
NEG = -1e+30
EPS = 1e-06
HIGH = lax.Precision.HIGHEST

def matmul(left, right):
    return jnp.dot(left, right, precision=HIGH, preferred_element_type=jnp.float32)

def normed(values, gain):
    return values * lax.rsqrt(lax.optimization_barrier(jnp.mean(values * values, -1, keepdims=True)) + EPS) * gain

def geglu(gate, upper):
    return jax.nn.gelu(gate, approximate=True) * upper

def document_of(places, lengths):
    return (places >= lengths[0]).astype(jnp.int32)

def local_mask(query_pos, key_pos, lengths, total):
    inside = (key_pos >= 0) & (key_pos < total)
    live_end = lengths[0] + lengths[1]
    live_query = query_pos < live_end
    live_key = inside & (key_pos < live_end)
    same = document_of(query_pos, lengths)[:, None] == document_of(key_pos, lengths)[None, :]
    near = jnp.abs(query_pos[:, None] - key_pos[None, :]) <= RADIUS
    both = live_query[:, None] & live_key[None, :] | (query_pos[:, None] == key_pos[None, :])
    return near & inside[None, :] & same & both

def routed_positions(route):
    starts = jnp.arange(route.shape[0], dtype=jnp.int32)[:, None] * TOK_DEV
    return ((starts + route).reshape(-1).astype(jnp.int32), (route < TOK_DEV).reshape(-1))

def select_rows(values, places, valid):
    picked = jnp.take(values, jnp.clip(places, 0, values.shape[0] - 1), axis=0)
    return picked * valid[:, None].astype(jnp.float32)

def spread_rows(values, places, valid, rows):
    base = jnp.zeros((rows, values.shape[1]), jnp.float32)
    return base.at[jnp.clip(places, 0, rows - 1)].add(values * valid[:, None].astype(jnp.float32))

def light_attention(query, keys, values, lengths):
    rows = query.shape[0]
    span = min(512, rows)
    key_pad = jnp.pad(keys, ((RADIUS, RADIUS), (0, 0)))
    value_pad = jnp.pad(values, ((RADIUS, RADIUS), (0, 0)))
    scale = 1.0 / math.sqrt(HDL)

    def one_block(index):
        begin = index * span
        query_block = lax.dynamic_slice_in_dim(query, begin, span, 0).reshape(span, HL, HDL)
        key_block = lax.dynamic_slice_in_dim(key_pad, begin, span + 2 * RADIUS, 0).reshape(-1, HL, HDL)
        value_block = lax.dynamic_slice_in_dim(value_pad, begin, span + 2 * RADIUS, 0).reshape(-1, HL, HDL)
        scores = low_back(jnp.einsum('qhd,khd->hqk', query_block, key_block, precision=HIGH) * scale)
        query_pos = begin + jnp.arange(span, dtype=jnp.int32)
        key_pos = begin - RADIUS + jnp.arange(span + 2 * RADIUS, dtype=jnp.int32)
        mask = local_mask(query_pos, key_pos, lengths, rows)
        probs = jax.nn.softmax(jnp.where(mask[None], scores, NEG), axis=-1)
        mixed = jnp.einsum('hqk,khd->qhd', low(probs), value_block, precision=HIGH)
        return mixed.reshape(span, HL * HDL)
    pieces = lax.map(jax.checkpoint(one_block), jnp.arange(rows // span, dtype=jnp.int32))
    return pieces.reshape(rows, HL * HDL)

def heavy_attention(query, keys, values, query_doc, key_doc, key_valid):
    rows = query.shape[0]
    span = min(512, rows)
    scale = 1.0 / math.sqrt(HDH)
    key_heads = keys.reshape(-1, HH, HDH)
    value_heads = values.reshape(-1, HH, HDH)

    def one_block(index):
        begin = index * span
        query_block = lax.dynamic_slice_in_dim(query, begin, span, 0).reshape(span, HH, HDH)
        doc_block = lax.dynamic_slice_in_dim(query_doc, begin, span, 0)
        scores = low_back(jnp.einsum('qhd,khd->hqk', query_block, key_heads, precision=HIGH) * scale)
        mask = (doc_block[:, None] == key_doc[None, :]) & key_valid[None, :]
        probs = jax.nn.softmax(jnp.where(mask[None], scores, NEG), axis=-1)
        mixed = jnp.einsum('hqk,khd->qhd', low(probs), value_heads, precision=HIGH)
        return mixed.reshape(span, HH * HDH)
    pieces = lax.map(jax.checkpoint(one_block), jnp.arange(rows // span, dtype=jnp.int32))
    return pieces.reshape(rows, HH * HDH)

def reference(tokens, query_small, key_small, value_small, out_small, query_large, key_large, value_large, out_large, attend_gain, attend_router, gate_small, up_small, down_small, gate_large, up_large, down_large, feed_gain, feed_router, lengths, query_route, key_route, feed_route, cotangent):
    floats = tuple((item.astype(jnp.float32) for item in (tokens, query_small, key_small, value_small, out_small, query_large, key_large, value_large, out_large, attend_gain, attend_router, gate_small, up_small, down_small, gate_large, up_large, down_large, feed_gain, feed_router)))
    rows = tokens.shape[0]
    query_places, query_valid = routed_positions(query_route)
    key_places, key_valid = routed_positions(key_route)
    feed_places, feed_valid = routed_positions(feed_route)
    query_doc = document_of(query_places, lengths)
    key_doc = document_of(key_places, lengths)

    def forward(inputs, w_query_small, w_key_small, w_value_small, w_out_small, w_query_large, w_key_large, w_value_large, w_out_large, gain_one, router_one, w_gate_small, w_up_small, w_down_small, w_gate_large, w_up_large, w_down_large, gain_two, router_two):
        normed_one = low(normed(inputs, gain_one))
        query_rows = low_back(low(matmul(normed_one, w_query_small)))
        key_rows = low_back(low(matmul(normed_one, w_key_small)))
        value_rows = low_back(low(matmul(normed_one, w_value_small)))
        light_mixed = low_back(low(light_attention(query_rows, key_rows, value_rows, lengths)))
        light_branch = low_back(matmul(light_mixed, w_out_small))
        routed_rows = select_rows(normed_one, query_places, query_valid)
        keyed_rows = select_rows(normed_one, key_places, key_valid)
        attend_score = jax.nn.sigmoid(matmul(routed_rows, router_one))
        routed_query = low_back(low(matmul(routed_rows, w_query_large)))
        routed_key = low_back(low(matmul(keyed_rows, w_key_large)))
        routed_value = low_back(low(matmul(keyed_rows, w_value_large)))
        heavy_mixed = low_back(low(heavy_attention(routed_query, routed_key, routed_value, query_doc, key_doc, key_valid)))
        heavy_branch = low_back(matmul(heavy_mixed, w_out_large))
        middle = inputs + light_branch + spread_rows(attend_score[:, None] * heavy_branch, query_places, query_valid, rows)
        normed_two = low(normed(middle, gain_two))
        gate_light = low_back(matmul(normed_two, w_gate_small))
        upper_light = low_back(matmul(normed_two, w_up_small))
        feed_light = low_back(matmul(low(geglu(gate_light, upper_light)), w_down_small))
        feed_rows = select_rows(normed_two, feed_places, feed_valid)
        feed_score = jax.nn.sigmoid(matmul(feed_rows, router_two))
        gate_heavy = low_back(matmul(feed_rows, w_gate_large))
        upper_heavy = low_back(matmul(feed_rows, w_up_large))
        feed_heavy = low_back(matmul(low(geglu(gate_heavy, upper_heavy)), w_down_large))
        return middle + feed_light + spread_rows(feed_score[:, None] * feed_heavy, feed_places, feed_valid, rows)
    output, pull = jax.vjp(forward, *floats)
    grads = pull(cotangent.astype(jnp.float32))
    return (output.astype(jnp.bfloat16), grads[0], grads[1], grads[2], grads[3], grads[4], grads[5], grads[6], grads[7], grads[8], grads[9], grads[10], grads[11], grads[12], grads[13], grads[14], grads[15], grads[16], grads[17], grads[18])
```

```python
import math

import jax
import jax.numpy as jnp
from jax import lax
from jax.sharding import PartitionSpec as P

HL = 8
HDL = 64
HH = 12
HDH = 64
RADIUS = 128

NEG = -1e30
EPS = 1e-06
HIGH = lax.Precision.HIGHEST
AXES = ("seq", "fsdp")
F32 = jnp.float32
BF16 = jnp.bfloat16


def dot(left, right, dims):
    return lax.dot_general(left, right, (dims, ((), ())), preferred_element_type=F32)


def nn(left, right):
    return dot(left, right, ((1,), (0,)))


def nt(left, right):
    return dot(left, right, ((1,), (1,)))


def tn(left, right):
    return dot(left, right, ((0,), (0,)))


def reverse_bits(value, count):
    out = value * 0
    for j in range(count):
        out = out | (((value >> j) & 1) << (count - 1 - j))
    return out


class Net:
    def __init__(self):
        self.seq = lax.axis_size("seq")
        self.depth = lax.axis_size("fsdp")
        self.levels = (self.seq // 2).bit_length() - 1
        self.count = self.seq * self.depth
        s = lax.axis_index("seq")
        self.core, self.pair = s & 1, s >> 1
        self.z = lax.axis_index("fsdp")
        self.device = s * self.depth + self.z

    def pairs(self, move):
        out = []
        for s in range(self.seq):
            for z in range(self.depth):
                pair, core, to_z = move(s >> 1, s & 1, z)
                out.append((s * self.depth + z, (pair * 2 + core) * self.depth + to_z))
        return out

    def by_core(self, array):
        return lax.ppermute(array, AXES, self.pairs(lambda p, c, z: (p, 1 - c, z)))

    def by_bit(self, array, j):
        top = self.levels - 1 - j
        return lax.ppermute(
            array, AXES, self.pairs(lambda p, c, z: (p ^ (1 << (j if c else top)), c, z))
        )

    def by_z(self, array, k):
        return lax.ppermute(array, AXES, self.pairs(lambda p, c, z: (p, c, z ^ k)))

    def target(self, relative):
        zr = relative % self.depth
        bits = (relative // self.depth) % (self.seq // 2)
        core = self.core ^ (relative // (self.count // 2))
        pair = self.pair ^ jnp.where(core == 1, bits, reverse_bits(bits, self.levels))
        return (pair * 2 + core) * self.depth + (self.z ^ zr)

    def gather_z(self, shard):
        return jnp.concatenate([shard] + [self.by_z(shard, k) for k in range(1, self.depth)], axis=0)

    def gather_seq(self, shard):
        for j in range(self.levels):
            shard = jnp.concatenate([shard, self.by_bit(shard, j)], axis=0)
        return shard, self.by_core(shard)

    def gather(self, shard):
        return self.gather_seq(self.gather_z(shard))

    def reduce_seq(self, keep, send):
        total = keep + self.by_core(send.astype(BF16)).astype(F32)
        for j in reversed(range(self.levels)):
            half = total.shape[0] // 2
            moved = self.by_bit(total[half:].astype(BF16), j)
            total = total[:half] + moved.astype(F32)
        return total

    def reduce_z(self, total):
        width = total.shape[0] // self.depth
        out = total[:width]
        for k in range(1, self.depth):
            part = total[k * width : (k + 1) * width].astype(BF16)
            out = out + self.by_z(part, k).astype(F32)
        return out

    def reduce(self, keep, send):
        return self.reduce_z(self.reduce_seq(keep, send))


def unit_rms(values):
    scale = lax.rsqrt(jnp.mean(values * values, -1, keepdims=True) + EPS)
    return values * scale, scale


def norm_back(grad, gain, unit, scale):
    scaled = grad * gain
    return scale * (scaled - unit * jnp.mean(scaled * unit, -1, keepdims=True))


def geglu(gate, upper):
    return jax.nn.gelu(gate, approximate=True) * upper


def document_of(places, lengths):
    return (places >= lengths[0]).astype(jnp.int32)


def local_mask(query_pos, key_pos, lengths, total):
    inside = (key_pos >= 0) & (key_pos < total)
    live_end = lengths[0] + lengths[1]
    live_query = query_pos < live_end
    live_key = inside & (key_pos < live_end)
    same = document_of(query_pos, lengths)[:, None] == document_of(key_pos, lengths)[None, :]
    near = jnp.abs(query_pos[:, None] - key_pos[None, :]) <= RADIUS
    both = live_query[:, None] & live_key[None, :] | (query_pos[:, None] == key_pos[None, :])
    return near & inside[None, :] & same & both


def one_hot(route_row, rows):
    return (route_row[:, None] == jnp.arange(rows, dtype=jnp.int32)[None, :]).astype(BF16)


def spread(select, values):
    return lax.dot_general(
        select.astype(F32),
        values,
        (((0,), (0,)), ((), ())),
        precision=HIGH,
        preferred_element_type=F32,
    )


def pick_wide(select, values):
    return jnp.dot(select.astype(F32), values, precision=HIGH, preferred_element_type=F32)


def soft(scores):
    top = jnp.max(scores, -1, keepdims=True)
    expo = jnp.exp(scores - top)
    return expo / jnp.sum(expo, -1, keepdims=True)


def reorder_wide(values, order):
    high = values.astype(BF16)
    low = (values - high.astype(F32)).astype(BF16)
    return nn(high, order) + nn(low, order)


def per_device(
    tokens,
    query_small,
    key_small,
    value_small,
    out_small,
    query_large,
    key_large,
    value_large,
    out_large,
    attend_gain,
    attend_router,
    gate_small,
    up_small,
    down_small,
    gate_large,
    up_large,
    down_large,
    feed_gain,
    feed_router,
    lengths,
    query_route,
    key_route,
    feed_route,
    cotangent,
):
    net = Net()
    rows, width = tokens.shape
    blocks = net.count
    part = width // blocks
    half = width // 2
    total = rows * blocks
    first = net.device * rows
    light = HL * HDL
    heavy = HH * HDH
    narrow = down_small.shape[0]
    wide = down_large.shape[0]
    light_scale = 1.0 / math.sqrt(HDL)
    heavy_scale = 1.0 / math.sqrt(HDH)

    step = [(i, i + 1) for i in range(blocks - 1)]
    back = [(i + 1, i) for i in range(blocks - 1)]
    above = lax.ppermute(tokens[rows - RADIUS :], AXES, step)
    below = lax.ppermute(tokens[:RADIUS], AXES, back)
    own_keys = lax.dynamic_slice_in_dim(key_route, net.device, 1, 0)[0]
    own_queries = lax.dynamic_slice_in_dim(query_route, net.device, 1, 0)[0]
    key_select = one_hot(own_keys, rows)
    query_select = one_hot(own_queries, rows)
    feed_select = one_hot(feed_route[0], rows)
    keyed_raw = nn(key_select, tokens).astype(BF16)
    keyed_raw = lax.all_gather(keyed_raw, AXES, axis=0, tiled=True)

    vectors = jnp.stack([attend_gain, attend_router, feed_gain, feed_router], axis=1)
    vectors = jnp.pad(vectors, ((0, 0), (0, 124)))
    first_set = net.gather(
        jnp.concatenate([query_small, key_small, value_small, vectors], axis=1)
    )
    second_set = net.gather(
        jnp.concatenate(
            [query_large, key_large, value_large, out_large.T, out_small.T], axis=1
        )
    )
    third_set = net.gather(jnp.concatenate([gate_small, up_small, down_small.T], axis=1))

    share = wide // net.seq
    stacked = jnp.stack([gate_large, up_large, down_large.T], axis=0)
    stacked = stacked.reshape(3, part, net.seq, share).transpose(2, 1, 0, 3)
    stacked = stacked.reshape(net.seq, part, 3 * share)
    stacked = lax.all_to_all(stacked, "seq", 0, 0, tiled=True)
    expert = net.gather_z(stacked.reshape(net.seq * part, 3 * share))
    gate_slice = expert[:, :share]
    up_slice = expert[:, share : 2 * share]
    down_slice = expert[:, 2 * share :]

    column = jnp.arange(width, dtype=jnp.int32)
    own_order = net.target(column // part) * part + column % part
    group = column // part
    group_order = (group % net.seq) * net.depth + (net.z ^ (group // net.seq))
    group_order = group_order * part + column % part
    to_own = (column[:, None] == own_order[None, :]).astype(BF16)
    own_to_group = (own_order[:, None] == group_order[None, :]).astype(BF16)

    ext = jnp.concatenate([above, tokens, below], axis=0)
    ext_raw = nn(ext, to_own)
    keyed_mine = nn(keyed_raw, to_own)
    cot = nn(cotangent, to_own).astype(BF16)

    def halves(pack, lo, hi):
        return pack[0][:, lo:hi], pack[1][:, lo:hi]

    def into(values, pack):
        return nn(values[:, :half], pack[0]) + nn(values[:, half:], pack[1])

    def onto(values, pack):
        return jnp.concatenate([nt(values, pack[0]), nt(values, pack[1])], axis=1)

    vector_rows = jnp.concatenate(halves(first_set, 3 * light, 3 * light + 8), axis=0)
    vector_rows = vector_rows.T.astype(F32)
    gain_one, router_one, gain_two, router_two = (vector_rows[i : i + 1] for i in range(4))

    unit_ext, scale_ext = unit_rms(ext_raw)
    normed_ext = (unit_ext * gain_one).astype(BF16)
    unit_one, scale_one = unit_ext[RADIUS : RADIUS + rows], scale_ext[RADIUS : RADIUS + rows]
    normed_one = normed_ext[RADIUS : RADIUS + rows]
    inputs = ext_raw[RADIUS : RADIUS + rows]
    unit_key, unused_scale = unit_rms(keyed_mine)
    keyed_rows = (unit_key * gain_one).astype(BF16)

    w_query = halves(first_set, 0, light)
    w_pair = halves(first_set, light, 3 * light)
    w_query_large = halves(second_set, 0, heavy)
    w_pair_large = halves(second_set, heavy, 3 * heavy)
    w_out_large = halves(second_set, 3 * heavy, 4 * heavy)
    w_out = halves(second_set, 4 * heavy, 4 * heavy + light)
    w_gate_up = halves(third_set, 0, 2 * narrow)
    w_down = halves(third_set, 2 * narrow, 3 * narrow)

    query_rows = into(normed_one, w_query).astype(BF16)
    pair_rows = into(normed_ext, w_pair).astype(BF16)
    positions = first + jnp.arange(rows, dtype=jnp.int32)
    key_positions = first - RADIUS + jnp.arange(rows + 2 * RADIUS, dtype=jnp.int32)
    light_mask = local_mask(positions, key_positions, lengths, total)
    query_heads = query_rows.reshape(rows, HL, HDL)
    key_heads = pair_rows[:, :light].reshape(-1, HL, HDL)
    value_heads = pair_rows[:, light:].reshape(-1, HL, HDL)

    def per_head(pattern, left, right):
        return jnp.einsum(pattern, left, right, preferred_element_type=F32)

    light_scores = per_head("qhd,khd->hqk", query_heads, key_heads) * light_scale
    light_probs = soft(jnp.where(light_mask[None], light_scores, NEG))
    light_low = light_probs.astype(BF16)
    light_mixed = per_head("hqk,khd->qhd", light_low, value_heads)
    light_mixed = light_mixed.reshape(rows, light).astype(BF16)
    light_branch = onto(light_mixed, w_out)

    routed_rows = nn(query_select, normed_one).astype(BF16)
    attend_score = jax.nn.sigmoid(jnp.sum(routed_rows.astype(F32) * router_one, -1, keepdims=True))
    routed_query = into(routed_rows, w_query_large).astype(BF16)
    heavy_pair = into(keyed_rows, w_pair_large).astype(BF16)
    key_slots = (jnp.arange(blocks, dtype=jnp.int32)[:, None] * rows + key_route).reshape(-1)
    key_valid = (key_route < rows).reshape(-1)
    key_docs = document_of(key_slots, lengths)
    query_docs = document_of(first + own_queries, lengths)
    heavy_mask = (query_docs[:, None] == key_docs[None, :]) & key_valid[None, :]
    routed_heads = routed_query.reshape(-1, HH, HDH)
    heavy_keys = heavy_pair[:, :heavy].reshape(-1, HH, HDH)
    heavy_values = heavy_pair[:, heavy:].reshape(-1, HH, HDH)
    heavy_scores = per_head("qhd,khd->hqk", routed_heads, heavy_keys) * heavy_scale
    heavy_probs = soft(jnp.where(heavy_mask[None], heavy_scores, NEG))
    heavy_low = heavy_probs.astype(BF16)
    heavy_mixed = per_head("hqk,khd->qhd", heavy_low, heavy_values)
    heavy_mixed = heavy_mixed.reshape(-1, heavy).astype(BF16)
    heavy_branch = onto(heavy_mixed, w_out_large)
    middle = inputs + light_branch + spread(query_select, attend_score * heavy_branch)

    unit_two, scale_two = unit_rms(middle)
    normed_two = (unit_two * gain_two).astype(BF16)
    feed_rows = nn(feed_select, normed_two).astype(BF16)
    feed_grad_rows = nn(feed_select, cot)
    feed_score = jax.nn.sigmoid(jnp.sum(feed_rows.astype(F32) * router_two, -1, keepdims=True))
    grad_feed_heavy = (feed_score * feed_grad_rows).astype(BF16)
    slots = feed_rows.shape[0]
    sent = nn(jnp.concatenate([feed_rows, grad_feed_heavy], axis=0), own_to_group).astype(BF16)
    sent = jnp.concatenate([sent[:slots], sent[slots:]], axis=1)
    got = jnp.concatenate(net.gather_seq(sent), axis=0)
    all_rows, all_grads = got[:, :width], got[:, width:]

    gate_up = into(normed_two, w_gate_up)
    gate_light, upper_light = gate_up[:, :narrow], gate_up[:, narrow:]
    hidden_f, light_pull = jax.vjp(geglu, gate_light, upper_light)
    hidden_light = hidden_f.astype(BF16)
    feed_light = onto(hidden_light, w_down)

    gate_heavy, upper_heavy = nn(all_rows, gate_slice), nn(all_rows, up_slice)
    hidden_hf, heavy_pull = jax.vjp(geglu, gate_heavy, upper_heavy)
    hidden_heavy = hidden_hf.astype(BF16)
    grad_gate_hf, grad_upper_hf = heavy_pull(nn(all_grads, down_slice))
    grad_gate_heavy = grad_gate_hf.astype(BF16)
    grad_upper_heavy = grad_upper_hf.astype(BF16)
    partial = jnp.concatenate(
        [
            nt(hidden_heavy, down_slice),
            nt(grad_gate_heavy, gate_slice) + nt(grad_upper_heavy, up_slice),
        ],
        axis=1,
    )
    kept = partial.shape[0] // 2
    summed = net.reduce_seq(partial[:kept], partial[kept:])
    expert_grad = jnp.concatenate(
        [
            tn(all_rows, grad_gate_heavy),
            tn(all_rows, grad_upper_heavy),
            tn(all_grads, hidden_heavy),
        ],
        axis=1,
    )
    expert_grad = net.reduce_z(expert_grad).astype(BF16)
    expert_grad = expert_grad.reshape(net.seq, part, 3 * share)
    expert_grad = lax.all_to_all(expert_grad, "seq", 0, 0, tiled=True)
    expert_grad = expert_grad.reshape(net.seq, part, 3, share).transpose(2, 1, 0, 3)
    expert_grad = expert_grad.reshape(3, part, wide).astype(F32)

    group_to_own = (group_order[:, None] == own_order[None, :]).astype(BF16)
    summed = reorder_wide(
        jnp.concatenate([summed[:, :width], summed[:, width:]], axis=0), group_to_own
    )
    feed_heavy, grad_feed_rows = summed[:slots], summed[slots:]
    result = middle + feed_light + spread(feed_select, feed_score * feed_heavy)
    result = nt(result.astype(BF16), to_own).astype(BF16)

    grad_result = cot.astype(F32)
    grad_gate_f, grad_upper_f = light_pull(into(cot, w_down))
    grad_gate_up = jnp.concatenate([grad_gate_f.astype(BF16), grad_upper_f.astype(BF16)], axis=1)

    def weight_grad(left, right):
        return tn(left[:, :half], right), tn(left[:, half:], right).astype(BF16)

    def beside(*parts):
        return tuple(jnp.concatenate(side, axis=1) for side in zip(*parts))

    third_grad = net.reduce(
        *beside(weight_grad(normed_two, grad_gate_up), weight_grad(cot, hidden_light))
    )
    feed_logit_grad = jnp.sum(feed_grad_rows * feed_heavy, -1, keepdims=True)
    feed_logit_grad = feed_logit_grad * feed_score * (1.0 - feed_score)
    grad_feed_rows = grad_feed_rows + feed_logit_grad * router_two
    grad_router_two = jnp.sum(feed_rows.astype(F32) * feed_logit_grad, 0)
    grad_normed_two = onto(grad_gate_up, w_gate_up) + spread(feed_select, grad_feed_rows)
    grad_gain_two = jnp.sum(grad_normed_two * unit_two, 0)
    grad_middle = grad_result + norm_back(grad_normed_two, gain_two, unit_two, scale_two)

    grad_middle_low = grad_middle.astype(BF16)
    attend_grad_rows = pick_wide(query_select, grad_middle)
    grad_heavy_branch = (attend_score * attend_grad_rows).astype(BF16)
    attend_logit_grad = jnp.sum(attend_grad_rows * heavy_branch, -1, keepdims=True)
    attend_logit_grad = attend_logit_grad * attend_score * (1.0 - attend_score)
    grad_heavy_mixed = into(grad_heavy_branch, w_out_large).astype(BF16)
    grad_heavy_heads = grad_heavy_mixed.reshape(-1, HH, HDH)
    grad_heavy_probs = per_head("qhd,khd->hqk", grad_heavy_heads, heavy_values)
    heavy_delta = jnp.sum(heavy_probs * grad_heavy_probs, -1, keepdims=True)
    grad_heavy_scores = (heavy_probs * (grad_heavy_probs - heavy_delta)).astype(BF16)
    grad_routed_query = per_head("hqk,khd->qhd", grad_heavy_scores, heavy_keys) * heavy_scale
    grad_routed_query = grad_routed_query.reshape(-1, heavy).astype(BF16)
    grad_keys = per_head("hqk,qhd->khd", grad_heavy_scores, routed_heads) * heavy_scale
    grad_values = per_head("hqk,qhd->khd", heavy_low, grad_heavy_heads)
    grad_heavy_pair = jnp.concatenate(
        [grad_keys.reshape(-1, heavy).astype(BF16), grad_values.reshape(-1, heavy).astype(BF16)],
        axis=1,
    )
    grad_routed = onto(grad_routed_query, w_query_large) + attend_logit_grad * router_one
    grad_router_one = jnp.sum(routed_rows.astype(F32) * attend_logit_grad, 0)
    grad_keyed = onto(grad_heavy_pair, w_pair_large)
    key_gain_grad = jnp.sum(grad_keyed * unit_key, 0)
    grad_keyed_low = nt(grad_keyed.astype(BF16), to_own)
    relative = net.target(jnp.arange(blocks, dtype=jnp.int32))
    per_block = grad_keyed_low.astype(BF16).reshape(blocks, -1, width)
    per_block = jnp.take(per_block, relative, axis=0)
    capacity = per_block.shape[1]
    per_block = per_block.reshape(blocks * capacity, width)
    cut = blocks * capacity // 2
    grad_keyed_own = net.reduce(per_block[:cut].astype(F32), per_block[cut:])

    grad_light_mixed = into(grad_middle_low, w_out).astype(BF16)
    second_grad = net.reduce(
        *beside(
            weight_grad(routed_rows, grad_routed_query),
            weight_grad(keyed_rows, grad_heavy_pair),
            weight_grad(grad_heavy_branch, heavy_mixed),
            weight_grad(grad_middle_low, light_mixed),
        )
    )
    grad_light_heads = grad_light_mixed.reshape(rows, HL, HDL)
    grad_light_probs = per_head("qhd,khd->hqk", grad_light_heads, value_heads)
    light_delta = jnp.sum(light_probs * grad_light_probs, -1, keepdims=True)
    grad_light_scores = (light_probs * (grad_light_probs - light_delta)).astype(BF16)
    grad_query_rows = per_head("hqk,khd->qhd", grad_light_scores, key_heads) * light_scale
    grad_query_rows = grad_query_rows.reshape(rows, light).astype(BF16)
    grad_key_ext = per_head("hqk,qhd->khd", grad_light_scores, query_heads) * light_scale
    grad_value_ext = per_head("hqk,qhd->khd", light_low, grad_light_heads)
    grad_pair = jnp.concatenate(
        [
            grad_key_ext.reshape(-1, light).astype(BF16),
            grad_value_ext.reshape(-1, light).astype(BF16),
        ],
        axis=1,
    )
    grad_ext = onto(grad_pair, w_pair)
    outer = jnp.concatenate([grad_ext[:RADIUS], grad_ext[RADIUS + rows :]], axis=0)
    outer = nt(outer.astype(BF16), to_own).astype(BF16)
    from_next = lax.ppermute(outer[:RADIUS], AXES, back)
    from_prev = lax.ppermute(outer[RADIUS:], AXES, step)
    grad_mine = (
        grad_ext[RADIUS : RADIUS + rows]
        + onto(grad_query_rows, w_query)
        + spread(query_select, grad_routed)
    )
    grad_gain_one = (
        jnp.sum(grad_mine * unit_one, 0)
        + jnp.sum(grad_ext[:RADIUS] * unit_ext[:RADIUS], 0)
        + jnp.sum(grad_ext[RADIUS + rows :] * unit_ext[RADIUS + rows :], 0)
        + key_gain_grad
    )
    vector_grads = jnp.stack([grad_gain_one, grad_router_one, grad_gain_two, grad_router_two], 1)
    vector_grads = jnp.pad(vector_grads, ((0, 0), (0, 124)))
    first_grad = net.reduce(
        *beside(
            weight_grad(normed_one, grad_query_rows),
            weight_grad(normed_ext, grad_pair),
            (vector_grads[:half], vector_grads[half:].astype(BF16)),
        )
    )

    arrived = jnp.concatenate([from_prev, from_next, grad_keyed_own.astype(BF16)], axis=0)
    arrived = nn(arrived, to_own)
    grad_normed_one = (
        grad_mine
        + jnp.pad(arrived[:RADIUS], ((0, rows - RADIUS), (0, 0)))
        + jnp.pad(arrived[RADIUS : 2 * RADIUS], ((rows - RADIUS, 0), (0, 0)))
        + spread(key_select, arrived[2 * RADIUS :])
    )
    grad_inputs = grad_middle + norm_back(grad_normed_one, gain_one, unit_one, scale_one)
    back_order = (own_order[:, None] == column[None, :]).astype(BF16)
    tokens_grad = reorder_wide(grad_inputs, back_order)

    vector_out = first_grad[:, 3 * light : 3 * light + 4].T
    return (
        result,
        tokens_grad,
        first_grad[:, :light],
        first_grad[:, light : 2 * light],
        first_grad[:, 2 * light : 3 * light],
        second_grad[:, 4 * heavy :].T,
        second_grad[:, :heavy],
        second_grad[:, heavy : 2 * heavy],
        second_grad[:, 2 * heavy : 3 * heavy],
        second_grad[:, 3 * heavy : 4 * heavy].T,
        vector_out[0],
        vector_out[1],
        third_grad[:, :narrow],
        third_grad[:, narrow : 2 * narrow],
        third_grad[:, 2 * narrow :].T,
        expert_grad[0],
        expert_grad[1],
        expert_grad[2].T,
        vector_out[2],
        vector_out[3],
    )


def solution(mesh):
    by_rows = P(AXES, None)
    by_columns = P(None, AXES)
    vector = P(AXES)
    return jax.shard_map(
        per_device,
        mesh=mesh,
        in_specs=(
            by_rows,
            by_rows,
            by_rows,
            by_rows,
            by_columns,
            by_rows,
            by_rows,
            by_rows,
            by_columns,
            vector,
            vector,
            by_rows,
            by_rows,
            by_columns,
            by_rows,
            by_rows,
            by_columns,
            vector,
            vector,
            P(),
            P(),
            P(),
            by_rows,
            by_rows,
        ),
        out_specs=(
            by_rows,
            by_rows,
            by_rows,
            by_rows,
            by_rows,
            by_columns,
            by_rows,
            by_rows,
            by_rows,
            by_columns,
            vector,
            vector,
            by_rows,
            by_rows,
            by_columns,
            by_rows,
            by_rows,
            by_columns,
            vector,
            vector,
        ),
        check_vma=False,
    )
```

```python
import functools
import math

import jax
import jax.numpy as jnp
from jax import lax
from jax.experimental import pallas as pl
from jax.experimental.pallas import tpu as pltpu
from jax.sharding import PartitionSpec as P

HL = 8
HDL = 64
HH = 12
HDH = 64
RADIUS = 128

NEG = -1e30
EPS = 1e-06
HIGH = lax.Precision.HIGHEST
AXES = ("seq", "fsdp")
F32 = jnp.float32
BF16 = jnp.bfloat16
ROOM = 12 << 20
PACE = 1e9
TIMES = {
    "pack": 2.5,
    "select": 3.2,
    "prepare": 0.8,
    "light_rows": 1.8,
    "light_forward": 4.2,
    "heavy_rows": 8.7,
    "heavy_forward": 2.7,
    "join": 2.1,
    "feed": 4.4,
    "feed_weight": 1.4,
    "expert": 6.0,
    "turn": 2.9,
    "heavy_scores": 4.0,
    "heavy_weights": 10.0,
    "light_scores": 5.6,
    "light_weights": 3.4,
    "finish": 2.9,
}


def dot(left, right, dims):
    return lax.dot_general(left, right, (dims, ((), ())), preferred_element_type=F32)


def nn(left, right):
    return dot(left, right, ((1,), (0,)))


def nt(left, right):
    return dot(left, right, ((1,), (1,)))


def tn(left, right):
    return dot(left, right, ((0,), (0,)))


def reverse_bits(value, count):
    out = value * 0
    for j in range(count):
        out = out | (((value >> j) & 1) << (count - 1 - j))
    return out


class Net:
    def __init__(self):
        self.seq = lax.axis_size("seq")
        self.depth = lax.axis_size("fsdp")
        self.levels = (self.seq // 2).bit_length() - 1
        self.count = self.seq * self.depth
        s = lax.axis_index("seq")
        self.core, self.pair = s & 1, s >> 1
        self.z = lax.axis_index("fsdp")
        self.device = s * self.depth + self.z

    def pairs(self, move):
        out = []
        for s in range(self.seq):
            for z in range(self.depth):
                pair, core, to_z = move(s >> 1, s & 1, z)
                out.append((s * self.depth + z, (pair * 2 + core) * self.depth + to_z))
        return out

    def by_core(self, array):
        return lax.ppermute(array, AXES, self.pairs(lambda p, c, z: (p, 1 - c, z)))

    def by_bit(self, array, j):
        top = self.levels - 1 - j
        return lax.ppermute(
            array, AXES, self.pairs(lambda p, c, z: (p ^ (1 << (j if c else top)), c, z))
        )

    def by_z(self, array, k):
        return lax.ppermute(array, AXES, self.pairs(lambda p, c, z: (p, c, z ^ k)))

    def target(self, relative):
        zr = relative % self.depth
        bits = (relative // self.depth) % (self.seq // 2)
        core = self.core ^ (relative // (self.count // 2))
        pair = self.pair ^ jnp.where(core == 1, bits, reverse_bits(bits, self.levels))
        return (pair * 2 + core) * self.depth + (self.z ^ zr)

    def from_z(self, shard):
        return [shard] + [self.by_z(shard, k) for k in range(1, self.depth)]

    def exchange_z(self, pieces):
        return [pieces[0]] + [self.by_z(pieces[k], k) for k in range(1, self.depth)]

    def gather(self, shard):
        shard = jnp.concatenate(self.from_z(shard), axis=0)
        for j in range(self.levels):
            shard = jnp.concatenate([shard, self.by_bit(shard, j)], axis=0)
        return shard, self.by_core(shard)

    def reduce(self, keep, send):
        keep, send = fold(keep, self.by_core(send), 2)
        for j in reversed(range(self.levels)):
            pieces = 2 if j else self.depth
            out = fold(keep, self.by_bit(send, j), pieces)
            keep, send = out[0], out[1]
        return self.exchange_z(out)

    def members(self):
        relative = jnp.arange(2 * self.depth, dtype=jnp.int32)
        core = self.core ^ (relative // self.depth)
        return core * self.depth + (self.z ^ (relative % self.depth))


class Order:
    def __init__(self):
        self.last = ()

    def hold(self, array):
        return after(array, *self.last)

    def note(self, array):
        self.last = (array,)
        return array


def stack_rows(arrays):
    height = sum(a.shape[0] for a in arrays)
    if len(arrays) < 3 or any(a.shape[0] % 8 for a in arrays):
        return jnp.concatenate(arrays, axis=0)

    def body(*refs):
        at = 0
        for ref in refs[:-1]:
            refs[-1][at : at + ref.shape[0]] = ref[...]
            at += ref.shape[0]

    return run(body, "stack", [((height, arrays[0].shape[1]), arrays[0].dtype)], arrays)[0]


def after(array, *earlier):
    return lax.optimization_barrier((array, *earlier))[0]


def unit_rms(values):
    scale = lax.rsqrt(jnp.mean(values * values, -1, keepdims=True) + EPS)
    return values * scale, scale


def norm_back(grad, gain, unit, scale):
    scaled = grad * gain
    return scale * (scaled - unit * jnp.mean(scaled * unit, -1, keepdims=True))


def document_of(places, lengths):
    return (places >= lengths[0]).astype(jnp.int32)


def sigmoid(values):
    return 1.0 / (1.0 + jnp.exp(-values))


def soft(scores):
    top = jnp.max(scores, -1, keepdims=True)
    expo = jnp.exp(scores - top)
    return expo / jnp.sum(expo, -1, keepdims=True)


def two_parts(values):
    high = values.astype(BF16)
    return high, (values - high.astype(F32)).astype(BF16)


def place_rows(select, values):
    high, low = two_parts(values)
    return tn(select, high) + tn(select, low)


def take_rows(select, values):
    high, low = two_parts(values)
    return nn(select, high) + nn(select, low)


def reorder(values, order):
    high, low = two_parts(values)
    return nn(high, order) + nn(low, order)


def reorder_back(values, order):
    high, low = two_parts(values)
    return nt(high, order) + nt(low, order)


def into(values, first, second):
    half = first.shape[0]
    return nn(values[:, :half], first) + nn(values[:, half:], second)


def onto(values, first, second):
    return jnp.concatenate([nt(values, first), nt(values, second)], axis=1)


def lanes(rows, width=128):
    return lax.broadcasted_iota(jnp.int32, (rows, width), 1)


def both_heads(pair):
    first = lanes(pair.shape[0]) < HDL
    zero = jnp.zeros_like(pair)
    return jnp.concatenate([jnp.where(first, pair, zero), jnp.where(first, zero, pair)], axis=0)


def one_pair(stacked):
    rows = stacked.shape[0] // 2
    return jnp.where(lanes(rows) < HDL, stacked[:rows], stacked[rows:])


def run(body, name, outs, args, smem=0, scratch=(), columns=None, room=ROOM):
    vmem = pl.BlockSpec(memory_space=pltpu.VMEM)
    specs = [pl.BlockSpec(memory_space=pltpu.SMEM)] * smem + [vmem] * (len(args) - smem)
    for i, count in (columns or {}).items():
        specs[i] = pl.BlockSpec(
            (args[i].shape[0], count), lambda i: (0, 0), pipeline_mode=pl.Buffered(1)
        )
    held = sum(math.prod(piece.shape) * jnp.dtype(piece.dtype).itemsize for piece in scratch)
    return pl.pallas_call(
        body,
        name=name,
        compiler_params=pltpu.CompilerParams(vmem_limit_bytes=held + room),
        out_shape=[jax.ShapeDtypeStruct(shape, kind) for shape, kind in outs],
        grid=(1,) if columns else (),
        in_specs=specs,
        out_specs=[vmem] * len(outs),
        scratch_shapes=list(scratch),
        cost_estimate=pl.CostEstimate(flops=int(TIMES.get(name, 1.0) * PACE) + 1, bytes_accessed=1, transcendentals=0),
    )(*args)


def fold(keep, moved, pieces, kind=BF16):
    height, width = keep.shape
    piece = height // pieces
    parts = 2 if piece % 32 == 0 else 1
    step = piece // parts

    def body(*refs):
        for k in range(pieces):
            total = refs[k][...].astype(F32) + refs[pieces + k][...].astype(F32)
            refs[2 * pieces + k][...] = total.astype(kind)

    def spec(k):
        return pl.BlockSpec((step, width), lambda i, k=k: (k * parts + i, 0))

    if piece % 8:
        total = keep.astype(F32) + moved.astype(F32)
        return [total[k * piece : (k + 1) * piece].astype(kind) for k in range(pieces)]
    return pl.pallas_call(
        body,
        name="fold",
        compiler_params=pltpu.CompilerParams(vmem_limit_bytes=ROOM),
        grid=(parts,),
        out_shape=[jax.ShapeDtypeStruct((piece, width), kind)] * pieces,
        in_specs=[spec(k) for k in range(pieces)] * 2,
        out_specs=[spec(0)] * pieces,
        cost_estimate=pl.CostEstimate(flops=int(0.6 * PACE) + 1, bytes_accessed=1, transcendentals=0),
    )(*([keep] * pieces + [moved] * pieces))


def settle(pieces, widths, name):
    def body(*refs):
        parts, outs = refs[: len(pieces)], refs[len(pieces) :]
        at = 0
        for out, width in zip(outs, widths):
            total = parts[0][:, at : at + width].astype(F32)
            for part in parts[1:]:
                total = total + part[:, at : at + width].astype(F32)
            out[...] = total
            at += width

    rows = pieces[0].shape[0]
    return run(body, name, [((rows, width), F32) for width in widths], pieces)


def hot(column, rows):
    return jnp.where(column == lanes(column.shape[0], rows), 1.0, 0.0).astype(BF16)


def as_column(row):
    count = row.shape[1]
    eye = lax.broadcasted_iota(jnp.int32, (count, count), 0) == lanes(count, count)
    spread = jnp.where(eye, row.astype(F32), 0.0)
    return jnp.sum(spread, -1, keepdims=True).astype(jnp.int32)


def order_matrix(order):
    width = order.shape[1]
    rows = lax.broadcasted_iota(jnp.int32, (width, width), 0)
    return jnp.where(rows == order, 1.0, 0.0).astype(BF16)


def select_body(
    place, orders, query_route, key_route, feed_route, cotangent, to_own, to_slice, cot, query_select, key_select, feed_select, query_doc
):
    rows = cotangent.shape[0]
    to_own[...] = order_matrix(orders[0:1])
    to_slice[...] = order_matrix(orders[1:2])
    cot[...] = nn(cotangent[...], to_own[...]).astype(BF16)
    queries = as_column(query_route[pl.ds(place[4], 1)])
    query_select[...] = hot(queries, rows)
    key_select[...] = hot(as_column(key_route[pl.ds(place[4], 1)]), rows)
    feed_select[...] = hot(as_column(feed_route[...]), rows)
    query_doc[...] = jnp.where(place[0] + queries >= place[1], 1, 0)


def pack_body(
    place, key_spots, tokens, key_route, q_l, k_l, v_l, o_l, o_s, gate_s, up_s, down_s, gate_l, up_l, down_l,
    second, third, expert_keep, expert_send, key_docs
):
    part, width = q_l.shape
    at = 0
    for ref in (o_l, o_s, q_l, k_l, v_l):
        second[:, at : at + ref.shape[1]] = ref[...]
        at += ref.shape[1]
    keyed = nn(hot(as_column(key_route[pl.ds(place[4], 1)]), tokens.shape[0]), tokens[...])
    second[:, at : at + width] = keyed[:part].astype(BF16)
    rest = keyed[part:]
    chunk = width * rest.shape[0] // part
    pieces = [rest[:, i * chunk : (i + 1) * chunk] for i in range(width // chunk)]
    second[:, at + width :] = jnp.concatenate(pieces, axis=0).astype(BF16)
    narrow = gate_s.shape[1]
    for i, ref in enumerate((gate_s, up_s, down_s)):
        third[:, i * narrow : (i + 1) * narrow] = ref[...]
    share = expert_keep.shape[1] // 3
    depth = expert_keep.shape[0] // part
    for c, expert in enumerate((expert_keep, expert_send)):
        for k in range(depth):
            at = ((place[5] ^ c) * depth + (place[6] ^ k)) * share
            at = pl.ds(pl.multiple_of(at, share), share)
            for i, ref in enumerate((gate_l, up_l, down_l)):
                expert[k * part : (k + 1) * part, i * share : (i + 1) * share] = ref[:, at]
    blocks, slots = key_route.shape
    keys = key_spots.shape[1]
    block = lax.broadcasted_iota(jnp.int32, (blocks, keys), 0) == key_spots[0:1]
    table = key_route[...].astype(F32).T.astype(BF16)
    found = nn(table, jnp.where(block, 1.0, 0.0).astype(BF16))
    slot = lax.broadcasted_iota(jnp.int32, (slots, keys), 0) == key_spots[1:2]
    position = jnp.sum(jnp.where(slot, found, 0.0), 0, keepdims=True).astype(jnp.int32)
    rows = tokens.shape[0]
    document = jnp.where(key_spots[0:1] * rows + position >= place[1], 1, 0)
    key_docs[...] = jnp.where(position < rows, document, -1)


def prepare_body(to_own, above, tokens, below, raw):
    order = to_own[...]
    at = 0
    for ref in (above, tokens, below):
        raw[at : at + ref.shape[0]] = nn(ref[...], order).astype(BF16)
        at += ref.shape[0]


def unpack_body(place, keep, got, gate, up, down):
    part = gate.shape[0]
    depth = keep.shape[0] // part
    share = keep.shape[1] // 3
    for c, source in enumerate((keep, got)):
        for k in range(depth):
            at = ((place[5] ^ c) * depth + (place[6] ^ k)) * share
            at = pl.ds(pl.multiple_of(at, share), share)
            for i, out in enumerate((gate, up, down)):
                piece = source[k * part : (k + 1) * part, i * share : (i + 1) * share]
                out[:, at] = piece.astype(F32)


def pair_up(first, second, part):
    count = first.shape[0] // part
    width = first.shape[1]
    if part % 8:
        cuts = [slice(k * part, (k + 1) * part) for k in range(count)]
        return [jnp.concatenate([first[c], second[c]], axis=0) for c in cuts]

    def body(*refs):
        for k in range(count):
            for i in range(2):
                refs[2 + k][i * part : (i + 1) * part] = refs[i][k * part : (k + 1) * part]

    return run(body, "pair_up", [((2 * part, width), BF16)] * count, (first, second))


def take_apart(pieces, part):
    width = pieces[0].shape[1]
    count = len(pieces)
    if part % 8:
        return [jnp.concatenate([p[i * part : (i + 1) * part] for p in pieces], axis=0) for i in range(2)]

    def body(*refs):
        for k in range(count):
            for i in range(2):
                refs[count + i][k * part : (k + 1) * part] = refs[k][i * part : (i + 1) * part]

    return run(body, "take_apart", [((count * part, width), BF16)] * 2, pieces)


def local_mask(place, tile, reach, stacked, span):
    shape = (stacked, span)
    row = lax.broadcasted_iota(jnp.int32, shape, 0) & (reach - 1)
    query = place[0] + tile * reach + row
    key = place[0] + (tile - 1) * reach + lax.broadcasted_iota(jnp.int32, shape, 1)
    split, live, total = place[1], place[1] + place[2], place[3]
    inside = (key >= 0) & (key < total)
    same = jnp.where(query >= split, 1, 0) == jnp.where(key >= split, 1, 0)
    near = jnp.abs(query - key) <= reach
    both = ((query < live) & (key < live)) | (query == key)
    return near & inside & same & both


def light_rows_body(raw, w0, w1, normed, queries, pairs, vectors):
    light = HL * HDL
    reach = RADIUS
    rows = queries.shape[0]
    columns = [w[:, 3 * light :].astype(F32).T[:8] for w in (w0, w1)]
    vectors[...] = jnp.concatenate(columns, axis=1)
    unit, unused = unit_rms(raw[...].astype(F32))
    normed[...] = (unit * vectors[0:1]).astype(BF16)
    own = normed[reach : reach + rows]
    queries[...] = into(own, w0[:, :light], w1[:, :light]).astype(BF16)
    pairs[...] = into(normed[...], w0[:, light : 3 * light], w1[:, light : 3 * light]).astype(BF16)


def light_forward_body(place, queries, pairs, mixed, sums):
    light = HL * HDL
    reach = RADIUS
    rows = queries.shape[0]
    scale = 1.0 / math.sqrt(HDL)
    lane = lanes(reach)
    for tile in range(rows // reach):
        mine = slice(tile * reach, (tile + 1) * reach)
        seen = slice(tile * reach, (tile + 3) * reach)
        mask = local_mask(place, tile, reach, 2 * reach, 3 * reach)
        logs = jnp.zeros((reach, 128), F32)
        for p in range(HL // 2):
            at = slice(p * 128, (p + 1) * 128)
            query = both_heads(queries[mine, at])
            scores = jnp.where(mask, nt(query, pairs[seen, at]) * scale, NEG)
            top = jnp.max(scores, -1, keepdims=True)
            expo = jnp.exp(scores - top)
            total = jnp.sum(expo, -1, keepdims=True)
            probs = (expo * (1.0 / total)).astype(BF16)
            value = pairs[seen, light + p * 128 : light + (p + 1) * 128]
            mixed[mine, at] = one_pair(nn(probs, value)).astype(BF16)
            log = top + jnp.log(total)
            logs = jnp.where(lane == 2 * p, log[:reach], logs)
            logs = jnp.where(lane == 2 * p + 1, log[reach:], logs)
        sums[mine] = logs


def piece_select(block_rows, rest, part, piece):
    shape = (block_rows // part * rest, block_rows)
    k = lax.broadcasted_iota(jnp.int32, shape, 0)
    row = lax.broadcasted_iota(jnp.int32, shape, 1)
    shift = rest.bit_length() - 1
    want = (k >> shift) * part + piece * rest + (k & (rest - 1))
    return jnp.where(row == want, 1.0, 0.0).astype(BF16)


def heavy_rows_body(select, normed, vectors, to_own, s0, s1, keyed, pairs, routed, queries, held):
    width = normed.shape[1]
    heavy = HH * HDH
    half = s0.shape[0]
    slots = routed.shape[0]
    at = width + HL * HDL + 3 * heavy
    q_at = slice(width + HL * HDL, width + HL * HDL + heavy)
    kv_at = slice(width + HL * HDL + heavy, at)
    part = half // (keyed.shape[0] // slots // 2)
    rest = slots - part
    chunk = width * rest // part
    for i, ref in enumerate((s0, s1)):
        held[i * half : (i + 1) * half] = ref[:, at : at + width]
        low = 2 * half + i * (half // part * rest)
        for piece in range(part // rest):
            picked = nn(piece_select(half, rest, part, piece), ref[:, at + width :])
            held[low : low + half // part * rest, piece * chunk : (piece + 1) * chunk] = picked.astype(BF16)
    step = 256

    def project(t, carry):
        rows = pl.ds(pl.multiple_of(t * step, step), step)
        unit, unused = unit_rms(nn(held[rows], to_own[...]))
        keyed[rows] = (unit * vectors[0:1]).astype(BF16)
        pairs[rows] = into(keyed[rows], s0[:, kv_at], s1[:, kv_at]).astype(BF16)
        return carry

    lax.fori_loop(0, keyed.shape[0] // step, project, 0)
    own = normed[RADIUS : normed.shape[0] - RADIUS]
    routed[...] = nn(select[...], own).astype(BF16)
    queries[...] = into(routed[...], s0[:, q_at], s1[:, q_at]).astype(BF16)


def heavy_forward_body(query_doc, key_doc, queries, pairs, mixed, sums):
    heavy = HH * HDH
    slots = queries.shape[0]
    scale = 1.0 / math.sqrt(HDH)
    mask = jnp.concatenate([query_doc[...], query_doc[...]], axis=0) == key_doc[...]
    logs = jnp.zeros((2 * slots, 128), F32)
    for p in range(HH // 2):
        at = slice(p * 128, (p + 1) * 128)
        scores = jnp.where(mask, nt(both_heads(queries[:, at]), pairs[:, at]) * scale, NEG)
        top = jnp.max(scores, -1, keepdims=True)
        expo = jnp.exp(scores - top)
        total = jnp.sum(expo, -1, keepdims=True)
        probs = (expo * (1.0 / total)).astype(BF16)
        mixed[:, at] = one_pair(nn(probs, pairs[:, heavy + p * 128 : heavy + (p + 1) * 128])).astype(BF16)
        logs = jnp.where(lanes(2 * slots) == p, top + jnp.log(total), logs)
    sums[...] = logs


def join_body(
    raw, light_mixed, heavy_mixed, routed, query_select, feed_select, vectors, cot, to_own, s0, s1,
    middle, normed, heavy_branch, feed_rows, feed_grads, sent
):
    heavy = HH * HDH
    width = raw.shape[1]
    rows = middle.shape[0]
    at = slice(heavy, heavy + HL * HDL)
    light_branch = onto(light_mixed[...], s0[:, at], s1[:, at])
    at = slice(0, heavy)
    heavy_branch[...] = onto(heavy_mixed[...], s0[:, at], s1[:, at])
    score = sigmoid(jnp.sum(routed[...].astype(F32) * vectors[1:2], -1, keepdims=True))
    inputs = raw[RADIUS : RADIUS + rows].astype(F32)
    middle[...] = inputs + light_branch + place_rows(query_select[...], score * heavy_branch[...])
    unit, unused = unit_rms(middle[...])
    normed[...] = (unit * vectors[2:3]).astype(BF16)
    feed_rows[...] = nn(feed_select[...], normed[...]).astype(BF16)
    feed_grads[...] = nn(feed_select[...], cot[...])
    score = sigmoid(jnp.sum(feed_rows[...].astype(F32) * vectors[3:4], -1, keepdims=True))
    sent[:, :width] = nt(feed_rows[...], to_own[...]).astype(BF16)
    sent[:, width:] = nt((score * feed_grads[...]).astype(BF16), to_own[...]).astype(BF16)


def geglu_rows(gate, upper, grad_hidden):
    c0, c1 = 0.7978845608028654, 0.044715
    square = gate * gate
    bent = jnp.tanh(c0 * gate * (1.0 + c1 * square))
    bell = 0.5 * (1.0 + bent)
    gelu = gate * bell
    slope = bell + 0.5 * gate * (1.0 - bent * bent) * (c0 * (1.0 + 3.0 * c1 * square))
    return gelu * upper, grad_hidden * upper * slope, grad_hidden * gelu


def geglu_loop(wide, grad_hidden, hidden, grads):
    count = hidden.shape[1]
    step = 32

    def rows_at(t, carry):
        rows = pl.ds(pl.multiple_of(t * step, step), step)
        out, grad_gate, grad_upper = geglu_rows(
            wide[rows, :count], wide[rows, count:], grad_hidden[rows]
        )
        hidden[rows] = out.astype(BF16)
        grads[rows, :count] = grad_gate.astype(BF16)
        grads[rows, count:] = grad_upper.astype(BF16)
        return carry

    lax.fori_loop(0, hidden.shape[0] // step, rows_at, 0)


def feed_body(normed, cot, t0, t1, feed, grad_normed, hidden, grads, wide, grad_hidden):
    narrow = hidden.shape[1]
    wide[...] = into(normed[...], t0[:, : 2 * narrow], t1[:, : 2 * narrow])
    grad_hidden[...] = into(cot[...], t0[:, 2 * narrow :], t1[:, 2 * narrow :])
    geglu_loop(wide, grad_hidden, hidden, grads)
    feed[...] = onto(hidden[...], t0[:, 2 * narrow :], t1[:, 2 * narrow :])
    grad_normed[...] = onto(grads[...], t0[:, : 2 * narrow], t1[:, : 2 * narrow])


def feed_weight_body(normed, cot, hidden, grads, keep, send):
    narrow = hidden.shape[1]
    half = keep.shape[0]
    for out, at in ((send, slice(half, None)), (keep, slice(0, half))):
        out[:, : 2 * narrow] = tn(normed[:, at], grads[...]).astype(out.dtype)
        out[:, 2 * narrow :] = tn(cot[:, at], hidden[...]).astype(out.dtype)


def expert_body(got0, got1, to_slice, weights, keep, send, grad_keep, grad_send, rows, row_grads, wide, grad_hidden, hidden, grads):
    width = to_slice.shape[0]
    share = hidden.shape[1]
    count = got0.shape[0]
    for i, got in enumerate((got0, got1)):
        at = slice(i * count, (i + 1) * count)
        rows[at] = nn(got[:, :width], to_slice[...]).astype(BF16)
        row_grads[at] = nn(got[:, width:], to_slice[...]).astype(BF16)
    wide[...] = nn(rows[...], weights[:, : 2 * share])
    grad_hidden[...] = nn(row_grads[...], weights[:, 2 * share :])
    geglu_loop(wide, grad_hidden, hidden, grads)
    for out, at in ((send, slice(count, None)), (keep, slice(0, count))):
        feed = nt(hidden[at], weights[:, 2 * share :]).astype(BF16)
        back = nt(grads[at], weights[:, : 2 * share]).astype(BF16)
        out[:, :width] = nt(feed, to_slice[...]).astype(out.dtype)
        out[:, width:] = nt(back, to_slice[...]).astype(out.dtype)
    half = grad_keep.shape[0]
    for out, at in ((grad_send, slice(half, None)), (grad_keep, slice(0, half))):
        out[:, : 2 * share] = tn(rows[:, at], grads[...]).astype(out.dtype)
        out[:, 2 * share :] = tn(row_grads[:, at], hidden[...]).astype(out.dtype)


def turn_body(*refs):
    pieces = refs[:-12]
    (
        middle, feed, grad_normed, feed_rows, feed_grads, feed_select, vectors, cot, to_own,
        result, grad_middle, vector_grads,
    ) = refs[-12:]
    width = middle.shape[1]
    summed = pieces[0][...].astype(F32)
    for piece in pieces[1:]:
        summed = summed + piece[...].astype(F32)
    feed_heavy = reorder(summed[:, :width], to_own[...])
    grad_rows = reorder(summed[:, width:], to_own[...])
    rows = feed_rows[...].astype(F32)
    score = sigmoid(jnp.sum(rows * vectors[3:4], -1, keepdims=True))
    logit = jnp.sum(feed_grads[...] * feed_heavy, -1, keepdims=True) * score * (1.0 - score)
    grad_rows = grad_rows + logit * vectors[3:4]
    grads = grad_normed[...] + place_rows(feed_select[...], grad_rows)
    unit, scale = unit_rms(middle[...])
    grad_middle[...] = cot[...].astype(F32) + norm_back(grads, vectors[2:3], unit, scale)
    vector_grads[...] = jnp.concatenate(
        [
            jnp.zeros((2, width), F32),
            jnp.sum(grads * unit, 0, keepdims=True),
            jnp.sum(rows * logit, 0, keepdims=True),
            jnp.zeros((4, width), F32),
        ],
        axis=0,
    )
    out = middle[...] + feed[...] + place_rows(feed_select[...], score * feed_heavy)
    result[...] = nt(out.astype(BF16), to_own[...]).astype(BF16)


def heavy_scores_body(
    query_doc, key_doc, grad_middle, query_select, routed, pairs, queries, heavy_branch, sums, vectors, s0, s1,
    grad_branch, grad_queries, grad_pairs, logits
):
    heavy = HH * HDH
    score = sigmoid(jnp.sum(routed[...].astype(F32) * vectors[1:2], -1, keepdims=True))
    grad_rows = take_rows(query_select[...], grad_middle[...])
    grad_branch[...] = (score * grad_rows).astype(BF16)
    logit = jnp.sum(grad_rows * heavy_branch[...], -1, keepdims=True) * score * (1.0 - score)
    logits[...] = jnp.broadcast_to(logit, logits.shape)
    at = slice(0, heavy)
    grad_mixed = into(grad_branch[...], s0[:, at], s1[:, at]).astype(BF16)
    scale = 1.0 / math.sqrt(HDH)
    mask = jnp.concatenate([query_doc[...], query_doc[...]], axis=0) == key_doc[...]
    for p in range(HH // 2):
        at = slice(p * 128, (p + 1) * 128)
        beyond = slice(heavy + p * 128, heavy + (p + 1) * 128)
        query = both_heads(queries[:, at])
        grad_out = both_heads(grad_mixed[:, at])
        scores = jnp.where(mask, nt(query, pairs[:, at]) * scale, NEG)
        probs = jnp.exp(scores - sums[:, p : p + 1])
        grad_probs = nt(grad_out, pairs[:, beyond])
        delta = jnp.sum(probs * grad_probs, -1, keepdims=True)
        grad_scores = (probs * (grad_probs - delta)).astype(BF16)
        grad_queries[:, at] = one_pair(nn(grad_scores, pairs[:, at]) * scale).astype(BF16)
        grad_pairs[:, at] = (tn(grad_scores, query) * scale).astype(BF16)
        grad_pairs[:, beyond] = tn(probs.astype(BF16), grad_out).astype(BF16)


def heavy_weights_body(
    grad_middle, routed, keyed, light_mixed, heavy_mixed, grad_branch, grad_queries, grad_pairs, logits, vectors, to_own, s0, s1,
    keep, send, grad_routed, vector_grads, moved
):
    width = grad_middle.shape[1]
    heavy = HH * HDH
    light = HL * HDL
    half = s0.shape[0]
    slots = routed.shape[0]
    q_at = slice(width + light, width + light + heavy)
    kv_at = slice(width + light + heavy, width + light + 3 * heavy)
    logit = logits[:, 0:1]
    grad_routed[...] = onto(grad_queries[...], s0[:, q_at], s1[:, q_at]) + logit * vectors[1:2]
    step = 256

    def back(t, gain):
        rows = pl.ds(pl.multiple_of(t * step, step), step)
        grads = onto(grad_pairs[rows], s0[:, kv_at], s1[:, kv_at])
        moved[rows] = nt(grads.astype(BF16), to_own[...]).astype(BF16)
        return gain + jnp.sum(grads * keyed[rows].astype(F32), 0, keepdims=True)

    gain = lax.fori_loop(0, keyed.shape[0] // step, back, jnp.zeros((1, width), F32))
    vector_grads[...] = jnp.concatenate(
        [
            gain / vectors[0:1],
            jnp.sum(routed[...].astype(F32) * logit, 0, keepdims=True),
            jnp.zeros((6, width), F32),
        ],
        axis=0,
    )
    low = grad_middle[...].astype(BF16)
    part = half // (keyed.shape[0] // slots // 2)
    rest = slots - part
    chunk = width * rest // part
    for i, out in ((1, send), (0, keep)):
        at = slice(i * half, (i + 1) * half)
        out[:, :width] = tn(grad_branch[:, at], heavy_mixed[...]).astype(BF16)
        out[:, width : width + light] = tn(low[:, at], light_mixed[...]).astype(BF16)
        out[:, q_at] = tn(routed[:, at], grad_queries[...]).astype(BF16)
        out[:, kv_at] = tn(keyed[:, at], grad_pairs[...]).astype(BF16)
        to = width + light + 3 * heavy
        out[:, to : to + width] = moved[at]
        at = 2 * half + i * (half // part * rest)
        total = 0.0
        for piece in range(part // rest):
            block = moved[at : at + half // part * rest, piece * chunk : (piece + 1) * chunk]
            total = total + tn(piece_select(half, rest, part, piece), block)
        out[:, to + width :] = total.astype(BF16)


def light_scores_body(place, grad_middle, queries, pairs, sums, s0, s1, grad_queries, grad_pairs, held):
    light = HL * HDL
    heavy = HH * HDH
    reach = RADIUS
    rows = queries.shape[0]
    at = slice(heavy, heavy + light)
    grad_mixed = into(grad_middle[...].astype(BF16), s0[:, at], s1[:, at]).astype(BF16)
    held[...] = jnp.zeros_like(held)
    scale = 1.0 / math.sqrt(HDL)
    for tile in range(rows // reach):
        mine = slice(tile * reach, (tile + 1) * reach)
        seen = slice(tile * reach, (tile + 3) * reach)
        mask = local_mask(place, tile, reach, 2 * reach, 3 * reach)
        for p in range(HL // 2):
            at = slice(p * 128, (p + 1) * 128)
            beyond = slice(light + p * 128, light + (p + 1) * 128)
            query = both_heads(queries[mine, at])
            grad_out = both_heads(grad_mixed[mine, at])
            key = pairs[seen, at]
            log = jnp.concatenate([sums[mine, 2 * p : 2 * p + 1], sums[mine, 2 * p + 1 : 2 * p + 2]], axis=0)
            probs = jnp.exp(jnp.where(mask, nt(query, key) * scale, NEG) - log)
            grad_probs = nt(grad_out, pairs[seen, beyond])
            delta = jnp.sum(probs * grad_probs, -1, keepdims=True)
            grad_scores = (probs * (grad_probs - delta)).astype(BF16)
            grad_queries[mine, at] = one_pair(nn(grad_scores, key) * scale).astype(BF16)
            held[seen, at] = held[seen, at] + tn(grad_scores, query) * scale
            held[seen, beyond] = held[seen, beyond] + tn(probs.astype(BF16), grad_out)
    grad_pairs[...] = held[...].astype(BF16)


def light_weights_body(
    raw, normed, grad_queries, grad_pairs, grad_routed, query_select, feed_vectors, heavy_vectors, to_own, f0, f1,
    keep, send, outer, grad_mine
):
    light = HL * HDL
    reach = RADIUS
    rows = grad_queries.shape[0]
    half = f0.shape[0]
    grads = onto(grad_pairs[...], f0[:, light : 3 * light], f1[:, light : 3 * light])
    for i, at in enumerate((slice(0, reach), slice(reach + rows, None))):
        outer[i * reach : (i + 1) * reach] = nt(grads[at].astype(BF16), to_own[...]).astype(BF16)
    own = onto(grad_queries[...], f0[:, :light], f1[:, :light])
    own = own + grads[reach : reach + rows] + place_rows(query_select[...], grad_routed[...])
    grad_mine[...] = own
    unit, unused = unit_rms(raw[...].astype(F32))
    gain = jnp.sum(own * unit[reach : reach + rows], 0, keepdims=True)
    for at in (slice(0, reach), slice(reach + rows, None)):
        gain = gain + jnp.sum(grads[at] * unit[at], 0, keepdims=True)
    vector_rows = feed_vectors[...] + heavy_vectors[...]
    first = lax.broadcasted_iota(jnp.int32, vector_rows.shape, 0) == 0
    vector_rows = vector_rows + jnp.where(first, gain, 0.0)
    filler = jnp.zeros((120, raw.shape[1]), F32)
    columns = jnp.concatenate([vector_rows, filler], axis=0)
    for i, out in ((1, send), (0, keep)):
        at = slice(i * half, (i + 1) * half)
        out[:, :light] = tn(normed[reach : reach + rows, at], grad_queries[...]).astype(BF16)
        out[:, light : 3 * light] = tn(normed[:, at], grad_pairs[...]).astype(BF16)
        out[:, 3 * light :] = columns[:, at].T.astype(BF16)


def finish_body(from_prev, from_next, keyed_grads, key_select, grad_mine, grad_middle, raw, vectors, to_own, out):
    reach = RADIUS
    rows, width = grad_mine.shape
    order = to_own[...]
    grads = [grad_mine[:reach] + nn(from_prev[...], order)]
    if rows > 2 * reach:
        grads.append(grad_mine[reach : rows - reach])
    grads.append(grad_mine[rows - reach :] + nn(from_next[...], order))
    keyed = keyed_grads[...]
    if keyed.shape[0] < key_select.shape[0]:
        rest = key_select.shape[0] - keyed.shape[0]
        tail = [keyed[i * rest : (i + 1) * rest, width:] for i in range(keyed.shape[0] // rest)]
        keyed = jnp.concatenate([keyed[:, :width], jnp.concatenate(tail, axis=1)], axis=0)
    keyed = nn(keyed.astype(BF16), order).astype(BF16)
    total = jnp.concatenate(grads, axis=0) + tn(key_select[...], keyed)
    unit, scale = unit_rms(raw[reach : reach + rows].astype(F32))
    total = grad_middle[...] + norm_back(total, vectors[0:1], unit, scale)
    out[...] = reorder_back(total, order)


def heavy_forward_wide(query_doc, key_doc, select, normed, vectors, to_own, s0, s1, keyed_raw):
    heavy = HH * HDH
    at = vectors.shape[1] + HL * HDL
    q_at, kv_at = slice(at, at + heavy), slice(at + heavy, at + 3 * heavy)
    unit, unused = unit_rms(nn(keyed_raw, to_own))
    keyed = (unit * vectors[0:1]).astype(BF16)
    pairs = into(keyed, s0[:, kv_at], s1[:, kv_at]).astype(BF16)
    routed = nn(select, normed[RADIUS : normed.shape[0] - RADIUS]).astype(BF16)
    queries = into(routed, s0[:, q_at], s1[:, q_at]).astype(BF16)

    def heads(array):
        return array.reshape(-1, HH, HDH)

    scores = jnp.einsum(
        "qhd,khd->hqk", heads(queries), heads(pairs[:, :heavy]), preferred_element_type=F32
    ) / math.sqrt(HDH)
    probs = soft(jnp.where((query_doc == key_doc)[None], scores, NEG))
    mixed = jnp.einsum(
        "hqk,khd->qhd", probs.astype(BF16), heads(pairs[:, heavy:]), preferred_element_type=F32
    )
    return keyed, pairs, routed, queries, mixed.reshape(-1, heavy).astype(BF16), probs


def heavy_backward_wide(
    grad_middle, query_select, routed, keyed, pairs, queries, light_mixed, heavy_mixed, heavy_branch, probs,
    vectors, to_own, s0, s1
):
    heavy = HH * HDH
    scale = 1.0 / math.sqrt(HDH)
    half = s0.shape[0]
    at = vectors.shape[1] + HL * HDL
    q_at, kv_at = slice(at, at + heavy), slice(at + heavy, at + 3 * heavy)
    score = sigmoid(jnp.sum(routed.astype(F32) * vectors[1:2], -1, keepdims=True))
    grad_rows = take_rows(query_select, grad_middle)
    grad_branch = (score * grad_rows).astype(BF16)
    logit = jnp.sum(grad_rows * heavy_branch, -1, keepdims=True) * score * (1.0 - score)
    at = slice(0, heavy)
    grad_mixed = into(grad_branch, s0[:, at], s1[:, at]).astype(BF16)

    def heads(array):
        return array.reshape(-1, HH, HDH)

    def mix(pattern, left, right):
        return jnp.einsum(pattern, left, right, preferred_element_type=F32)

    grad_probs = mix("qhd,khd->hqk", heads(grad_mixed), heads(pairs[:, heavy:]))
    delta = jnp.sum(probs * grad_probs, -1, keepdims=True)
    grad_scores = (probs * (grad_probs - delta)).astype(BF16)
    grad_queries = mix("hqk,khd->qhd", grad_scores, heads(pairs[:, :heavy])) * scale
    grad_queries = grad_queries.reshape(-1, heavy).astype(BF16)
    grad_keys = mix("hqk,qhd->khd", grad_scores, heads(queries)) * scale
    grad_values = mix("hqk,qhd->khd", probs.astype(BF16), heads(grad_mixed))
    grad_pairs = jnp.concatenate(
        [grad_keys.reshape(-1, heavy).astype(BF16), grad_values.reshape(-1, heavy).astype(BF16)], axis=1
    )
    grad_routed = onto(grad_queries, s0[:, q_at], s1[:, q_at]) + logit * vectors[1:2]
    grads = onto(grad_pairs, s0[:, kv_at], s1[:, kv_at])
    vector_grads = jnp.concatenate(
        [
            jnp.sum(grads * keyed.astype(F32), 0, keepdims=True) / vectors[0:1],
            jnp.sum(routed.astype(F32) * logit, 0, keepdims=True),
            jnp.zeros((6, grads.shape[1]), F32),
        ],
        axis=0,
    )
    moved = nt(grads.astype(BF16), to_own).astype(BF16)
    low = grad_middle.astype(BF16)
    sides = []
    for at in (slice(0, half), slice(half, None)):
        columns = (
            tn(grad_branch[:, at], heavy_mixed),
            tn(low[:, at], light_mixed),
            tn(routed[:, at], grad_queries),
            tn(keyed[:, at], grad_pairs),
        )
        sides.append(jnp.concatenate(columns, axis=1).astype(BF16))
    return sides[0], sides[1], grad_routed, vector_grads, moved


def per_device(
    tokens,
    query_small,
    key_small,
    value_small,
    out_small,
    query_large,
    key_large,
    value_large,
    out_large,
    attend_gain,
    attend_router,
    gate_small,
    up_small,
    down_small,
    gate_large,
    up_large,
    down_large,
    feed_gain,
    feed_router,
    lengths,
    query_route,
    key_route,
    feed_route,
    cotangent,
):
    net = Net()
    rows, width = tokens.shape
    blocks = net.count
    part = width // blocks
    half = width // 2
    first = net.device * rows
    light = HL * HDL
    heavy = HH * HDH
    narrow = down_small.shape[0]
    wide = down_large.shape[0]
    slots = query_route.shape[1]
    members = 2 * net.depth
    share = wide // members
    pooled = members * slots
    keys = blocks * slots
    rest = slots - part
    packed = part % 8 == 0 and rest > 0 and rest % 8 == 0 and part % rest == 0 and keys <= 2048

    step = [(i, i + 1) for i in range(blocks - 1)]
    back = [(i + 1, i) for i in range(blocks - 1)]
    vector_pack = jnp.stack([attend_gain, attend_router, feed_gain, feed_router], axis=1)
    vector_pack = jnp.pad(vector_pack, ((0, 0), (0, 124)))
    first_parts = net.from_z(
        jnp.concatenate([query_small, key_small, value_small, vector_pack], axis=1)
    )
    above = lax.ppermute(tokens[rows - RADIUS :], AXES, step)
    below = lax.ppermute(tokens[:RADIUS], AXES, back)
    column = jnp.arange(width, dtype=jnp.int32)
    own_order = net.target(column // part) * part + column % part
    bits = column // part // members
    bits = jnp.where(net.core == 1, bits, reverse_bits(bits, net.levels))
    member = column // part % members
    member = (net.core ^ (member % 2)) * net.depth + (net.z ^ (member // 2))
    slice_order = ((net.pair ^ bits) * members + member) * part + column % part
    orders = jnp.stack([own_order, slice_order])
    place = jnp.stack([first, lengths[0], lengths[1], jnp.int32(rows * blocks), net.device, net.core, net.z])
    square = ((width, width), BF16)
    chosen = ((slots, rows), BF16)

    if packed:
        tall = blocks * part
        spot = jnp.arange(keys, dtype=jnp.int32)
        spot_block = jnp.where(spot < tall, spot // part, (spot - tall) // rest)
        spot_slot = jnp.where(spot < tall, spot % part, part + (spot - tall) % rest)
        second_set, third_set, slices_keep, slices_send, key_docs = run(
            pack_body,
            "pack",
            [
                ((part, 5 * width + light + width * rest // part), BF16),
                ((part, 3 * narrow), BF16),
                ((net.depth * part, 3 * share), BF16),
                ((net.depth * part, 3 * share), BF16),
                ((1, keys), jnp.int32),
            ],
            (
                place, jnp.stack([net.target(spot_block), spot_slot]), tokens, key_route,
                query_large, key_large, value_large, out_large.T, out_small.T,
                gate_small, up_small, down_small.T, gate_large, up_large, down_large.T,
            ),
            smem=1,
            room=56 << 20,
        )
    else:
        second_set = jnp.concatenate(
            [out_large.T, out_small.T, query_large, key_large, value_large], axis=1
        )
        third_set = jnp.concatenate([gate_small, up_small, down_small.T], axis=1)
        stacked = jnp.stack([gate_large, up_large, down_large.T], axis=0)
        stacked = stacked.reshape(3, part, members, share).transpose(2, 1, 0, 3)
        stacked = jnp.take(stacked.reshape(members, part, 3 * share), net.members(), axis=0)
        slices_keep, slices_send = stacked.reshape(2, net.depth * part, 3 * share)
    order = Order()
    top_bit = net.levels - 1

    def take_z(pieces):
        return order.note(stack_rows([order.hold(pieces[0])] + pieces[1:]))

    def take(whole, moved):
        return order.note(jnp.concatenate([whole, order.hold(moved)], axis=0))

    def first_moved(whole):
        return net.by_bit(whole, 0)

    def rest_moved(whole, moved):
        for j in range(1, net.levels):
            whole = take(whole, moved)
            moved = net.by_bit(whole, j)
        return whole, moved

    order.note(second_set)
    first_set = take_z(first_parts)
    first_moving = first_moved(first_set)
    second_parts = net.from_z(after(second_set, first_set))
    to_own, to_slice, cot, query_select, key_select, feed_select, query_docs = run(
        select_body,
        "select",
        [square, square, ((rows, width), BF16), chosen, chosen, chosen, ((slots, 1), jnp.int32)],
        (place, orders, query_route, key_route, feed_route, order.hold(cotangent)),
        smem=1,
        room=56 << 20,
    )
    order.note(cot)
    first_set, first_moving = rest_moved(first_set, first_moving)
    second_set = take_z(second_parts)
    (raw,) = run(
        prepare_body,
        "prepare",
        [((rows + 2 * RADIUS, width), BF16)],
        (order.hold(to_own), above, tokens, below),
    )
    order.note(raw)
    f0 = take(first_set, first_moving)
    f1 = net.by_core(f0)
    second_moving = first_moved(after(second_set, f0))
    third_parts = net.from_z(after(third_set, second_set))

    normed_ext, query_rows, pair_rows, vectors = run(
        light_rows_body,
        "light_rows",
        [
            ((rows + 2 * RADIUS, width), BF16),
            ((rows, light), BF16),
            ((rows + 2 * RADIUS, 2 * light), BF16),
            ((8, width), F32),
        ],
        (order.hold(raw), f0, f1),
    )
    order.note(query_rows)
    second_set, second_moving = rest_moved(second_set, second_moving)
    slices_got = net.by_core(after(slices_send, query_rows))
    light_mixed, light_sums = run(
        light_forward_body,
        "light_forward",
        [((rows, light), BF16), ((rows, 128), F32)],
        (place, order.hold(query_rows), pair_rows),
        smem=1,
    )
    order.note(light_mixed)
    third_set = take_z(third_parts)
    slices = net.exchange_z(pair_up(after(slices_keep, third_set), slices_got, part))
    s0 = take(second_set, second_moving)
    s1 = net.by_core(s0)
    third_moving = first_moved(after(third_set, s0))
    expert = take_z(slices)

    if packed:
        keyed, heavy_pairs, routed, routed_query = run(
            heavy_rows_body,
            "heavy_rows",
            [
                ((keys, width), BF16),
                ((keys, 2 * heavy), BF16),
                ((slots, width), BF16),
                ((slots, heavy), BF16),
            ],
            (order.hold(query_select), normed_ext, vectors, to_own, s0, s1),
            scratch=[pltpu.VMEM((keys, width), BF16)],
        )
        order.note(routed_query)
        third_set, third_moving = rest_moved(third_set, third_moving)
        heavy_mixed, heavy_sums = run(
            heavy_forward_body,
            "heavy_forward",
            [((slots, heavy), BF16), ((2 * slots, 128), F32)],
            (query_docs, key_docs, order.hold(routed_query), heavy_pairs),
        )
    else:
        relative = net.target(jnp.arange(blocks, dtype=jnp.int32))
        near_routes = jnp.take(key_route, relative, axis=0)
        key_docs = document_of(relative[:, None] * rows + near_routes, lengths)
        key_docs = jnp.where(near_routes < rows, key_docs, -1).reshape(1, -1)
        keyed_raw = net.gather(nn(key_select, tokens).astype(BF16))
        keyed, heavy_pairs, routed, routed_query, heavy_mixed, heavy_sums = heavy_forward_wide(
            query_docs, key_docs, query_select, normed_ext, vectors, to_own, s0, s1,
            jnp.concatenate(keyed_raw, axis=0),
        )
        third_set, third_moving = rest_moved(third_set, third_moving)
    order.note(heavy_mixed)

    middle, normed_two, heavy_branch, feed_rows, feed_grads, sent = run(
        join_body,
        "join",
        [
            ((rows, width), F32),
            ((rows, width), BF16),
            ((slots, width), F32),
            ((slots, width), BF16),
            ((slots, width), F32),
            ((slots, 2 * width), BF16),
        ],
        (
            raw, light_mixed, order.hold(heavy_mixed), routed, query_select, feed_select, vectors, cot, to_own, s0, s1,
        ),
        columns={9: heavy + light, 10: heavy + light},
    )
    order.note(sent)

    got_parts = net.from_z(sent)
    t0 = take(third_set, third_moving)
    t1 = net.by_core(t0)
    expert_moving = first_moved(after(expert, t0))
    got0 = take_z(got_parts)
    got1 = net.by_core(got0)
    feed_light, grad_normed, hidden, hidden_grads = run(
        feed_body,
        "feed",
        [
            ((rows, width), F32),
            ((rows, width), F32),
            ((rows, narrow), BF16),
            ((rows, 2 * narrow), BF16),
        ],
        (order.hold(normed_two), cot, t0, t1),
        scratch=[pltpu.VMEM((rows, 2 * narrow), F32), pltpu.VMEM((rows, narrow), F32)],
    )
    order.note(hidden)
    expert, expert_moving = rest_moved(expert, expert_moving)
    third_keep, third_send = run(
        feed_weight_body,
        "feed_weight",
        [((half, 3 * narrow), BF16), ((half, 3 * narrow), BF16)],
        (normed_two, cot, order.hold(hidden), hidden_grads),
    )
    order.note(third_send)
    third_moving = net.by_core(third_send)
    expert = take(expert, expert_moving)
    keep, send, expert_keep, expert_send = run(
        expert_body,
        "expert",
        [
            ((pooled // 2, 2 * width), BF16),
            ((pooled // 2, 2 * width), BF16),
            ((half, 3 * share), BF16),
            ((half, 3 * share), BF16),
        ],
        (order.hold(got0), got1, to_slice, expert),
        scratch=[
            pltpu.VMEM((pooled, width), BF16),
            pltpu.VMEM((pooled, width), BF16),
            pltpu.VMEM((pooled, 2 * share), F32),
            pltpu.VMEM((pooled, share), F32),
            pltpu.VMEM((pooled, share), BF16),
            pltpu.VMEM((pooled, 2 * share), BF16),
        ],
    )
    order.note(send)
    moving = net.by_core(send)
    expert_moving = net.by_bit(expert_send, top_bit)

    def give(keep, moved, pieces):
        out = fold(keep, order.hold(moved), pieces)
        order.note(out[0])
        return out

    def descend(keep, moved):
        for j in reversed(range(net.levels - 1)):
            keep, send = give(keep, moved, 2)
            moved = net.by_bit(send, j)
        return keep, moved

    third_keep, third_send = give(third_keep, third_moving, 2)
    summed = net.exchange_z(give(keep, moving, net.depth))
    third_moving = net.by_bit(third_send, top_bit)

    result, grad_middle, feed_vectors = run(
        turn_body,
        "turn",
        [((rows, width), BF16), ((rows, width), F32), ((8, width), F32)],
        (
            order.hold(summed[0]), *summed[1:], middle, feed_light, grad_normed, feed_rows, feed_grads, feed_select,
            vectors, cot, to_own,
        ),
    )
    order.note(grad_middle)
    expert_keep, expert_moving = descend(expert_keep, expert_moving)
    if packed:
        grad_branch, grad_queries, grad_heavy_pairs, logits = run(
            heavy_scores_body,
            "heavy_scores",
            [
                ((slots, width), BF16),
                ((slots, heavy), BF16),
                ((keys, 2 * heavy), BF16),
                ((slots, 128), F32),
            ],
            (
                query_docs, key_docs, order.hold(grad_middle), query_select, routed, heavy_pairs, routed_query,
                heavy_branch, heavy_sums, vectors, s0, s1,
            ),
            columns={10: heavy + light, 11: heavy + light},
        )
        order.note(grad_branch)
    expert_parts = net.exchange_z(give(expert_keep, expert_moving, net.depth))
    third_keep, third_moving = descend(third_keep, third_moving)
    if packed:
        second_keep, second_send, grad_routed, heavy_vectors = run(
            heavy_weights_body,
            "heavy_weights",
            [
                ((half, 5 * width + light + width * rest // part), BF16),
                ((half, 5 * width + light + width * rest // part), BF16),
                ((slots, width), F32),
                ((8, width), F32),
            ],
            (
                grad_middle, routed, keyed, light_mixed, heavy_mixed, order.hold(grad_branch), grad_queries,
                grad_heavy_pairs, logits, vectors, to_own, s0, s1,
            ),
            scratch=[pltpu.VMEM((keys, width), BF16)],
            columns={11: 4 * heavy + light, 12: 4 * heavy + light},
        )
    else:
        second_keep, second_send, grad_routed, heavy_vectors, keyed_grads = heavy_backward_wide(
            grad_middle, query_select, routed, keyed, heavy_pairs, routed_query, light_mixed, heavy_mixed,
            heavy_branch, heavy_sums, vectors, to_own, s0, s1,
        )
    order.note(second_send)
    second_moving = net.by_core(second_send)
    expert_keep, expert_send = take_apart([order.hold(expert_parts[0])] + expert_parts[1:], part)
    order.note(expert_send)
    expert_got = net.by_core(expert_send)
    third_parts = net.exchange_z(give(third_keep, third_moving, net.depth))
    grad_queries, grad_pairs = run(
        light_scores_body,
        "light_scores",
        [((rows, light), BF16), ((rows + 2 * RADIUS, 2 * light), BF16)],
        (place, order.hold(grad_middle), query_rows, pair_rows, light_sums, s0, s1),
        smem=1,
        scratch=[pltpu.VMEM((rows + 2 * RADIUS, 2 * light), F32)],
        columns={5: heavy + light, 6: heavy + light},
    )
    order.note(grad_queries)
    second_keep, second_send = give(second_keep, second_moving, 2)
    second_moving = net.by_bit(second_send, top_bit)
    first_keep, first_send, outer, grad_mine = run(
        light_weights_body,
        "light_weights",
        [
            ((half, 3 * light + 128), BF16),
            ((half, 3 * light + 128), BF16),
            ((2 * RADIUS, width), BF16),
            ((rows, width), F32),
        ],
        (
            raw, normed_ext, order.hold(grad_queries), grad_pairs, grad_routed, query_select, feed_vectors, heavy_vectors,
            to_own, f0, f1,
        ),
    )
    order.note(first_send)
    first_moving = net.by_core(first_send)
    from_next = lax.ppermute(outer[:RADIUS], AXES, back)
    from_prev = lax.ppermute(outer[RADIUS:], AXES, step)

    if packed:
        gate_grad, up_grad, down_grad = run(
            unpack_body,
            "unpack",
            [((part, wide), F32)] * 3,
            (place, order.hold(expert_keep), expert_got),
            smem=1,
        )
    else:
        expert_grad = jnp.concatenate([order.hold(expert_keep), expert_got], axis=0)
        expert_grad = jnp.take(expert_grad.reshape(members, part, 3 * share), net.members(), axis=0)
        expert_grad = expert_grad.reshape(members, part, 3, share).transpose(2, 1, 0, 3)
        gate_grad, up_grad, down_grad = expert_grad.reshape(3, part, wide).astype(F32)
    order.note(gate_grad)
    first_keep, first_send = give(first_keep, first_moving, 2)
    first_moving = net.by_bit(first_send, top_bit)
    third_grad = settle([order.hold(third_parts[0])] + third_parts[1:], [narrow] * 3, "settle_third")
    order.note(third_grad[0])
    second_keep, second_moving = descend(second_keep, second_moving)
    first_keep, first_moving = descend(first_keep, first_moving)
    second_parts = net.exchange_z(give(second_keep, second_moving, net.depth))
    first_parts = net.exchange_z(give(first_keep, first_moving, net.depth))
    widths = [width, light, heavy, heavy, heavy]
    if packed:
        widths.append(width + width * rest // part)
    second_grad = settle([order.hold(second_parts[0])] + second_parts[1:], widths, "settle_second")
    order.note(second_grad[0])
    if packed:
        keyed_own = second_grad[5]
    else:
        cut = keys // 2
        keyed_own = settle(net.reduce(keyed_grads[:cut], keyed_grads[cut:]), [width], "settle_keyed")[0]
    first_grad = settle(
        [order.hold(first_parts[0])] + first_parts[1:], [light, light, light, 128], "settle_first"
    )
    order.note(first_grad[0])
    (tokens_grad,) = run(
        finish_body,
        "finish",
        [((rows, width), F32)],
        (
            from_prev, from_next, keyed_own, key_select, grad_mine, grad_middle, raw, vectors, to_own,
        ),
    )
    vector_out = first_grad[3][:, :4].T
    return (
        result,
        tokens_grad,
        first_grad[0],
        first_grad[1],
        first_grad[2],
        second_grad[1].T,
        second_grad[2],
        second_grad[3],
        second_grad[4],
        second_grad[0].T,
        vector_out[0],
        vector_out[1],
        third_grad[0],
        third_grad[1],
        third_grad[2].T,
        gate_grad,
        up_grad,
        down_grad.T,
        vector_out[2],
        vector_out[3],
    )


def solution(mesh):
    by_rows = P(AXES, None)
    by_columns = P(None, AXES)
    vector = P(AXES)
    return jax.shard_map(
        per_device,
        mesh=mesh,
        in_specs=(
            by_rows,
            by_rows,
            by_rows,
            by_rows,
            by_columns,
            by_rows,
            by_rows,
            by_rows,
            by_columns,
            vector,
            vector,
            by_rows,
            by_rows,
            by_columns,
            by_rows,
            by_rows,
            by_columns,
            vector,
            vector,
            P(),
            P(),
            P(),
            by_rows,
            by_rows,
        ),
        out_specs=(
            by_rows,
            by_rows,
            by_rows,
            by_rows,
            by_rows,
            by_columns,
            by_rows,
            by_rows,
            by_rows,
            by_columns,
            vector,
            vector,
            by_rows,
            by_rows,
            by_columns,
            by_rows,
            by_rows,
            by_columns,
            vector,
            vector,
        ),
        check_vma=False,
    )
```

```python
import functools
import math

import jax
import jax.numpy as jnp
from jax import lax
from jax.experimental import pallas as pl
from jax.experimental.pallas import tpu as pltpu
from jax.sharding import PartitionSpec as P

HL = 8
HDL = 64
HH = 12
HDH = 64
RADIUS = 128

NEG = -1e30
EPS = 1e-06
HIGH = lax.Precision.HIGHEST
AXES = ("seq", "fsdp")
F32 = jnp.float32
BF16 = jnp.bfloat16
ROOM = 12 << 20
LENGTHS = {
    "select": 60,
    "prepare": 2,
    "light_forward": 60,
    "heavy_pairs": 60,
    "join": 20,
    "feed": 60,
    "feed_weight": 20,
    "expert": 60,
    "turn": 60,
    "heavy_scores": 60,
    "heavy_weights": 20,
    "take_apart": 60,
    "pair_up": 20,
}


def declared(name):
    flops = int(LENGTHS.get(name, 0.05) * 1e9)
    return pl.CostEstimate(flops=flops, bytes_accessed=10**10, transcendentals=0)


class Columns:
    def __init__(self, array, start, stop):
        self.array, self.start, self.stop = array, start, stop


def dot(left, right, dims):
    return lax.dot_general(left, right, (dims, ((), ())), preferred_element_type=F32)


def nn(left, right):
    return dot(left, right, ((1,), (0,)))


def nt(left, right):
    return dot(left, right, ((1,), (1,)))


def tn(left, right):
    return dot(left, right, ((0,), (0,)))


def reverse_bits(value, count):
    out = value * 0
    for j in range(count):
        out = out | (((value >> j) & 1) << (count - 1 - j))
    return out


class Net:
    def __init__(self):
        self.seq = lax.axis_size("seq")
        self.depth = lax.axis_size("fsdp")
        self.levels = (self.seq // 2).bit_length() - 1
        self.count = self.seq * self.depth
        s = lax.axis_index("seq")
        self.core, self.pair = s & 1, s >> 1
        self.z = lax.axis_index("fsdp")
        self.device = s * self.depth + self.z

    def pairs(self, move):
        out = []
        for s in range(self.seq):
            for z in range(self.depth):
                pair, core, to_z = move(s >> 1, s & 1, z)
                out.append((s * self.depth + z, (pair * 2 + core) * self.depth + to_z))
        return out

    def by_core(self, array):
        return lax.ppermute(array, AXES, self.pairs(lambda p, c, z: (p, 1 - c, z)))

    def by_bit(self, array, j):
        top = self.levels - 1 - j
        return lax.ppermute(
            array, AXES, self.pairs(lambda p, c, z: (p ^ (1 << (j if c else top)), c, z))
        )

    def by_z(self, array, k):
        return lax.ppermute(array, AXES, self.pairs(lambda p, c, z: (p, c, z ^ k)))

    def target(self, relative):
        zr = relative % self.depth
        bits = (relative // self.depth) % (self.seq // 2)
        core = self.core ^ (relative // (self.count // 2))
        pair = self.pair ^ jnp.where(core == 1, bits, reverse_bits(bits, self.levels))
        return (pair * 2 + core) * self.depth + (self.z ^ zr)

    def from_z(self, shard):
        return [shard] + [self.by_z(shard, k) for k in range(1, self.depth)]

    def exchange_z(self, pieces):
        return [pieces[0]] + [self.by_z(pieces[k], k) for k in range(1, self.depth)]

    def gather(self, shard):
        shard = jnp.concatenate(self.from_z(shard), axis=0)
        for j in range(self.levels):
            shard = jnp.concatenate([shard, self.by_bit(shard, j)], axis=0)
        return shard, self.by_core(shard)

    def reduce(self, keep, send):
        keep, send = fold(keep, self.by_core(send), 2)
        for j in reversed(range(self.levels)):
            pieces = 2 if j else self.depth
            out = fold(keep, self.by_bit(send, j), pieces)
            keep, send = out[0], out[1]
        return self.exchange_z(out)

    def members(self):
        relative = jnp.arange(2 * self.depth, dtype=jnp.int32)
        core = self.core ^ (relative // self.depth)
        return core * self.depth + (self.z ^ (relative % self.depth))


class Order:
    def __init__(self):
        self.last = ()

    def hold(self, array):
        return after(array, *self.last)

    def note(self, array):
        self.last = (array,)
        return array


def stack_rows(arrays):
    height = sum(a.shape[0] for a in arrays)
    if any(a.shape[0] % 8 for a in arrays):
        return jnp.concatenate(arrays, axis=0)

    def body(*refs):
        at = 0
        for ref in refs[:-1]:
            refs[-1][at : at + ref.shape[0]] = ref[...]
            at += ref.shape[0]

    return run(body, "stack", [((height, arrays[0].shape[1]), arrays[0].dtype)], arrays)[0]


def after(array, *earlier):
    return lax.optimization_barrier((array, *earlier))[0]


def unit_rms(values):
    scale = lax.rsqrt(jnp.mean(values * values, -1, keepdims=True) + EPS)
    return values * scale, scale


def norm_back(grad, gain, unit, scale):
    scaled = grad * gain
    return scale * (scaled - unit * jnp.mean(scaled * unit, -1, keepdims=True))


def document_of(places, lengths):
    return (places >= lengths[0]).astype(jnp.int32)


def sigmoid(values):
    return 1.0 / (1.0 + jnp.exp(-values))


def soft(scores):
    top = jnp.max(scores, -1, keepdims=True)
    expo = jnp.exp(scores - top)
    return expo / jnp.sum(expo, -1, keepdims=True)


def two_parts(values):
    high = values.astype(BF16)
    return high, (values - high.astype(F32)).astype(BF16)


def place_rows(select, values):
    high, low = two_parts(values)
    return tn(select, high) + tn(select, low)


def take_rows(select, values):
    high, low = two_parts(values)
    return nn(select, high) + nn(select, low)


def reorder(values, order):
    high, low = two_parts(values)
    return nn(high, order) + nn(low, order)


def reorder_back(values, order):
    high, low = two_parts(values)
    return nt(high, order) + nt(low, order)


def into(values, first, second):
    half = first.shape[0]
    return nn(values[:, :half], first) + nn(values[:, half:], second)


def onto(values, first, second):
    return jnp.concatenate([nt(values, first), nt(values, second)], axis=1)


def lanes(rows, width=128):
    return lax.broadcasted_iota(jnp.int32, (rows, width), 1)


def both_heads(pair):
    first = lanes(pair.shape[0]) < HDL
    zero = jnp.zeros_like(pair)
    return jnp.concatenate([jnp.where(first, pair, zero), jnp.where(first, zero, pair)], axis=0)


def one_pair(stacked):
    rows = stacked.shape[0] // 2
    return jnp.where(lanes(rows) < HDL, stacked[:rows], stacked[rows:])


def run(body, name, outs, args, smem=0, scratch=(), room=ROOM):
    vmem = pl.BlockSpec(memory_space=pltpu.VMEM)
    held = sum(math.prod(piece.shape) * jnp.dtype(piece.dtype).itemsize for piece in scratch)
    cuts = {i: a for i, a in enumerate(args) if isinstance(a, Columns)}

    def kernel(*refs):
        refs = list(refs)
        for i, cut in cuts.items():
            refs[i] = refs[i].at[:, cut.start : cut.stop]
        body(*refs)

    return pl.pallas_call(
        kernel,
        name=name,
        compiler_params=pltpu.CompilerParams(vmem_limit_bytes=held + room),
        out_shape=[jax.ShapeDtypeStruct(shape, kind) for shape, kind in outs],
        in_specs=[pl.BlockSpec(memory_space=pltpu.SMEM)] * smem + [vmem] * (len(args) - smem),
        out_specs=[vmem] * len(outs),
        scratch_shapes=list(scratch),
        cost_estimate=declared(name),
    )(*[a.array if isinstance(a, Columns) else a for a in args])


def fold(keep, moved, pieces, kind=BF16):
    height, width = keep.shape
    piece = height // pieces
    parts = 2 if piece % 32 == 0 else 1
    step = piece // parts

    def body(*refs):
        for k in range(pieces):
            total = refs[k][...].astype(F32) + refs[pieces + k][...].astype(F32)
            refs[2 * pieces + k][...] = total.astype(kind)

    def spec(k):
        return pl.BlockSpec((step, width), lambda i, k=k: (k * parts + i, 0))

    if piece % 8:
        total = keep.astype(F32) + moved.astype(F32)
        return [total[k * piece : (k + 1) * piece].astype(kind) for k in range(pieces)]
    return pl.pallas_call(
        body,
        name="fold",
        compiler_params=pltpu.CompilerParams(vmem_limit_bytes=ROOM),
        grid=(parts,),
        out_shape=[jax.ShapeDtypeStruct((piece, width), kind)] * pieces,
        in_specs=[spec(k) for k in range(pieces)] * 2,
        out_specs=[spec(0)] * pieces,
        cost_estimate=declared("fold"),
    )(*([keep] * pieces + [moved] * pieces))


def settle(pieces, widths, name):
    def body(*refs):
        parts, outs = refs[: len(pieces)], refs[len(pieces) :]
        at = 0
        for out, width in zip(outs, widths):
            total = parts[0][:, at : at + width].astype(F32)
            for part in parts[1:]:
                total = total + part[:, at : at + width].astype(F32)
            out[...] = total
            at += width

    rows = pieces[0].shape[0]
    return run(body, name, [((rows, width), F32) for width in widths], pieces)


def hot(column, rows):
    return jnp.where(column == lanes(column.shape[0], rows), 1.0, 0.0).astype(BF16)


def as_column(row):
    count = row.shape[1]
    eye = lax.broadcasted_iota(jnp.int32, (count, count), 0) == lanes(count, count)
    spread = jnp.where(eye, row.astype(F32), 0.0)
    return jnp.sum(spread, -1, keepdims=True).astype(jnp.int32)


def order_matrix(order):
    width = order.shape[1]
    rows = lax.broadcasted_iota(jnp.int32, (width, width), 0)
    return jnp.where(rows == order, 1.0, 0.0).astype(BF16)


def orders_body(orders, to_own, to_slice):
    to_own[...] = order_matrix(orders[0:1])
    to_slice[...] = order_matrix(orders[1:2])


def select_body(
    place, to_own, query_route, key_route, feed_route, cotangent, cot, query_select, key_select, feed_select, query_doc
):
    rows = cotangent.shape[0]
    cot[...] = nn(cotangent[...], to_own[...]).astype(BF16)
    queries = as_column(query_route[pl.ds(place[4], 1)])
    query_select[...] = hot(queries, rows)
    key_select[...] = hot(as_column(key_route[pl.ds(place[4], 1)]), rows)
    feed_select[...] = hot(as_column(feed_route[...]), rows)
    query_doc[...] = jnp.where(place[0] + queries >= place[1], 1, 0)


def pack_body(
    place, key_spots, tokens, key_route, q_l, k_l, v_l, o_l, o_s,
    gate_s, up_s, down_s, gate_l, up_l, down_l, second, third, expert_keep, expert_send, key_docs
):
    part, width = q_l.shape
    at = 0
    for ref in (o_l, o_s, q_l, k_l, v_l):
        second[:, at : at + ref.shape[1]] = ref[...]
        at += ref.shape[1]
    keyed = nn(hot(as_column(key_route[pl.ds(place[4], 1)]), tokens.shape[0]), tokens[...])
    second[:, at : at + width] = keyed[:part].astype(BF16)
    rest = keyed[part:]
    chunk = width * rest.shape[0] // part
    pieces = [rest[:, i * chunk : (i + 1) * chunk] for i in range(width // chunk)]
    second[:, at + width :] = jnp.concatenate(pieces, axis=0).astype(BF16)
    narrow = gate_s.shape[1]
    for i, ref in enumerate((gate_s, up_s, down_s)):
        third[:, i * narrow : (i + 1) * narrow] = ref[...]
    share = expert_keep.shape[1] // 3
    depth = expert_keep.shape[0] // part
    for c, expert in enumerate((expert_keep, expert_send)):
        for k in range(depth):
            at = ((place[5] ^ c) * depth + (place[6] ^ k)) * share
            at = pl.ds(pl.multiple_of(at, share), share)
            for i, ref in enumerate((gate_l, up_l, down_l)):
                expert[k * part : (k + 1) * part, i * share : (i + 1) * share] = ref[:, at]
    blocks, slots = key_route.shape
    keys = key_spots.shape[1]
    block = lax.broadcasted_iota(jnp.int32, (blocks, keys), 0) == key_spots[0:1]
    table = key_route[...].astype(F32).T.astype(BF16)
    found = nn(table, jnp.where(block, 1.0, 0.0).astype(BF16))
    slot = lax.broadcasted_iota(jnp.int32, (slots, keys), 0) == key_spots[1:2]
    position = jnp.sum(jnp.where(slot, found, 0.0), 0, keepdims=True).astype(jnp.int32)
    rows = tokens.shape[0]
    document = jnp.where(key_spots[0:1] * rows + position >= place[1], 1, 0)
    key_docs[...] = jnp.where(position < rows, document, -1)


def prepare_body(to_own, above, tokens, below, raw):
    order = to_own[...]
    at = 0
    for ref in (above, tokens, below):
        raw[at : at + ref.shape[0]] = nn(ref[...], order).astype(BF16)
        at += ref.shape[0]


def unpack_body(place, keep, got, gate, up, down):
    part = gate.shape[0]
    depth = keep.shape[0] // part
    share = keep.shape[1] // 3
    for c, source in enumerate((keep, got)):
        for k in range(depth):
            at = ((place[5] ^ c) * depth + (place[6] ^ k)) * share
            at = pl.ds(pl.multiple_of(at, share), share)
            for i, out in enumerate((gate, up, down)):
                piece = source[k * part : (k + 1) * part, i * share : (i + 1) * share]
                out[:, at] = piece.astype(F32)


def pair_up(first, second, part):
    count = first.shape[0] // part
    width = first.shape[1]
    if part % 8:
        cuts = [slice(k * part, (k + 1) * part) for k in range(count)]
        return [jnp.concatenate([first[c], second[c]], axis=0) for c in cuts]

    def body(*refs):
        for k in range(count):
            for i in range(2):
                refs[2 + k][i * part : (i + 1) * part] = refs[i][k * part : (k + 1) * part]

    return run(body, "pair_up", [((2 * part, width), BF16)] * count, (first, second))


def take_apart(pieces, part):
    width = pieces[0].shape[1]
    count = len(pieces)
    if part % 8:
        return [jnp.concatenate([p[i * part : (i + 1) * part] for p in pieces], axis=0) for i in range(2)]

    def body(*refs):
        for k in range(count):
            for i in range(2):
                refs[count + i][k * part : (k + 1) * part] = refs[k][i * part : (i + 1) * part]

    return run(body, "take_apart", [((count * part, width), BF16)] * 2, pieces)


def local_mask(place, tile, reach, stacked, span):
    shape = (stacked, span)
    row = lax.broadcasted_iota(jnp.int32, shape, 0) & (reach - 1)
    query = place[0] + tile * reach + row
    key = place[0] + (tile - 1) * reach + lax.broadcasted_iota(jnp.int32, shape, 1)
    split, live, total = place[1], place[1] + place[2], place[3]
    inside = (key >= 0) & (key < total)
    same = jnp.where(query >= split, 1, 0) == jnp.where(key >= split, 1, 0)
    near = jnp.abs(query - key) <= reach
    both = ((query < live) & (key < live)) | (query == key)
    return near & inside & same & both


def light_rows_body(raw, w0, w1, normed, queries, pairs, vectors):
    light = HL * HDL
    reach = RADIUS
    rows = queries.shape[0]
    columns = [w[:, 3 * light :].astype(F32).T[:8] for w in (w0, w1)]
    vectors[...] = jnp.concatenate(columns, axis=1)
    unit, unused = unit_rms(raw[...].astype(F32))
    normed[...] = (unit * vectors[0:1]).astype(BF16)
    own = normed[reach : reach + rows]
    queries[...] = into(own, w0[:, :light], w1[:, :light]).astype(BF16)
    pairs[...] = into(normed[...], w0[:, light : 3 * light], w1[:, light : 3 * light]).astype(BF16)


def light_forward_body(place, queries, pairs, mixed, sums):
    light = HL * HDL
    reach = RADIUS
    rows = queries.shape[0]
    scale = 1.0 / math.sqrt(HDL)
    lane = lanes(reach)
    for tile in range(rows // reach):
        mine = slice(tile * reach, (tile + 1) * reach)
        seen = slice(tile * reach, (tile + 3) * reach)
        mask = local_mask(place, tile, reach, 2 * reach, 3 * reach)
        logs = jnp.zeros((reach, 128), F32)
        for p in range(HL // 2):
            at = slice(p * 128, (p + 1) * 128)
            query = both_heads(queries[mine, at])
            scores = jnp.where(mask, nt(query, pairs[seen, at]) * scale, NEG)
            top = jnp.max(scores, -1, keepdims=True)
            expo = jnp.exp(scores - top)
            total = jnp.sum(expo, -1, keepdims=True)
            probs = (expo * (1.0 / total)).astype(BF16)
            value = pairs[seen, light + p * 128 : light + (p + 1) * 128]
            mixed[mine, at] = one_pair(nn(probs, value)).astype(BF16)
            log = top + jnp.log(total)
            logs = jnp.where(lane == 2 * p, log[:reach], logs)
            logs = jnp.where(lane == 2 * p + 1, log[reach:], logs)
        sums[mine] = logs


def piece_select(block_rows, rest, part, piece):
    shape = (block_rows // part * rest, block_rows)
    k = lax.broadcasted_iota(jnp.int32, shape, 0)
    row = lax.broadcasted_iota(jnp.int32, shape, 1)
    shift = rest.bit_length() - 1
    want = (k >> shift) * part + piece * rest + (k & (rest - 1))
    return jnp.where(row == want, 1.0, 0.0).astype(BF16)


def heavy_rows_body(slots, vectors, to_own, s0, s1, keyed, held):
    width = to_own.shape[0]
    half = s0.shape[0]
    at = width + HL * HDL + 3 * HH * HDH
    part = half // (keyed.shape[0] // slots // 2)
    rest = slots - part
    chunk = width * rest // part
    for i, ref in enumerate((s0, s1)):
        held[i * half : (i + 1) * half] = ref[:, at : at + width]
        low = 2 * half + i * (half // part * rest)
        for piece in range(part // rest):
            picked = nn(piece_select(half, rest, part, piece), ref[:, at + width :])
            held[low : low + half // part * rest, piece * chunk : (piece + 1) * chunk] = picked.astype(BF16)
    step = 256

    def project(t, carry):
        rows = pl.ds(pl.multiple_of(t * step, step), step)
        unit, unused = unit_rms(nn(held[rows], to_own[...]))
        keyed[rows] = (unit * vectors[0:1]).astype(BF16)
        return carry

    lax.fori_loop(0, keyed.shape[0] // step, project, 0)


def heavy_pairs_body(select, normed, keyed, s0, s1, pairs, routed, queries):
    width = normed.shape[1]
    heavy = HH * HDH
    q_at = slice(width + HL * HDL, width + HL * HDL + heavy)
    kv_at = slice(width + HL * HDL + heavy, width + HL * HDL + 3 * heavy)
    step = 256

    def project(t, carry):
        rows = pl.ds(pl.multiple_of(t * step, step), step)
        pairs[rows] = into(keyed[rows], s0[:, kv_at], s1[:, kv_at]).astype(BF16)
        return carry

    lax.fori_loop(0, keyed.shape[0] // step, project, 0)
    own = normed[RADIUS : normed.shape[0] - RADIUS]
    routed[...] = nn(select[...], own).astype(BF16)
    queries[...] = into(routed[...], s0[:, q_at], s1[:, q_at]).astype(BF16)


def heavy_forward_body(query_doc, key_doc, queries, pairs, mixed, sums):
    heavy = HH * HDH
    slots = queries.shape[0]
    scale = 1.0 / math.sqrt(HDH)
    mask = jnp.concatenate([query_doc[...], query_doc[...]], axis=0) == key_doc[...]
    logs = jnp.zeros((2 * slots, 128), F32)
    for p in range(HH // 2):
        at = slice(p * 128, (p + 1) * 128)
        scores = jnp.where(mask, nt(both_heads(queries[:, at]), pairs[:, at]) * scale, NEG)
        top = jnp.max(scores, -1, keepdims=True)
        expo = jnp.exp(scores - top)
        total = jnp.sum(expo, -1, keepdims=True)
        probs = (expo * (1.0 / total)).astype(BF16)
        mixed[:, at] = one_pair(nn(probs, pairs[:, heavy + p * 128 : heavy + (p + 1) * 128])).astype(BF16)
        logs = jnp.where(lanes(2 * slots) == p, top + jnp.log(total), logs)
    sums[...] = logs


def join_body(
    raw, light_mixed, heavy_mixed, routed, query_select, feed_select, vectors, cot, to_own, s0, s1,
    middle, normed, heavy_branch, feed_rows, feed_grads, sent
):
    heavy = HH * HDH
    width = raw.shape[1]
    rows = middle.shape[0]
    at = slice(heavy, heavy + HL * HDL)
    light_branch = onto(light_mixed[...], s0[:, at], s1[:, at])
    at = slice(0, heavy)
    heavy_branch[...] = onto(heavy_mixed[...], s0[:, at], s1[:, at])
    score = sigmoid(jnp.sum(routed[...].astype(F32) * vectors[1:2], -1, keepdims=True))
    inputs = raw[RADIUS : RADIUS + rows].astype(F32)
    middle[...] = inputs + light_branch + place_rows(query_select[...], score * heavy_branch[...])
    unit, unused = unit_rms(middle[...])
    normed[...] = (unit * vectors[2:3]).astype(BF16)
    feed_rows[...] = nn(feed_select[...], normed[...]).astype(BF16)
    feed_grads[...] = nn(feed_select[...], cot[...])
    score = sigmoid(jnp.sum(feed_rows[...].astype(F32) * vectors[3:4], -1, keepdims=True))
    sent[:, :width] = nt(feed_rows[...], to_own[...]).astype(BF16)
    sent[:, width:] = nt((score * feed_grads[...]).astype(BF16), to_own[...]).astype(BF16)


def geglu_rows(gate, upper, grad_hidden):
    c0, c1 = 0.7978845608028654, 0.044715
    square = gate * gate
    bent = jnp.tanh(c0 * gate * (1.0 + c1 * square))
    bell = 0.5 * (1.0 + bent)
    gelu = gate * bell
    slope = bell + 0.5 * gate * (1.0 - bent * bent) * (c0 * (1.0 + 3.0 * c1 * square))
    return gelu * upper, grad_hidden * upper * slope, grad_hidden * gelu


def geglu_loop(wide, grad_hidden, hidden, grads):
    count = hidden.shape[1]
    step = 32

    def rows_at(t, carry):
        rows = pl.ds(pl.multiple_of(t * step, step), step)
        out, grad_gate, grad_upper = geglu_rows(
            wide[rows, :count], wide[rows, count:], grad_hidden[rows]
        )
        hidden[rows] = out.astype(BF16)
        grads[rows, :count] = grad_gate.astype(BF16)
        grads[rows, count:] = grad_upper.astype(BF16)
        return carry

    lax.fori_loop(0, hidden.shape[0] // step, rows_at, 0)


def feed_body(normed, cot, t0, t1, feed, grad_normed, hidden, grads, wide, grad_hidden):
    narrow = hidden.shape[1]
    wide[...] = into(normed[...], t0[:, : 2 * narrow], t1[:, : 2 * narrow])
    grad_hidden[...] = into(cot[...], t0[:, 2 * narrow :], t1[:, 2 * narrow :])
    geglu_loop(wide, grad_hidden, hidden, grads)
    feed[...] = onto(hidden[...], t0[:, 2 * narrow :], t1[:, 2 * narrow :])
    grad_normed[...] = onto(grads[...], t0[:, : 2 * narrow], t1[:, : 2 * narrow])


def feed_weight_body(normed, cot, hidden, grads, keep, send):
    narrow = hidden.shape[1]
    half = keep.shape[0]
    for out, at in ((send, slice(half, None)), (keep, slice(0, half))):
        out[:, : 2 * narrow] = tn(normed[:, at], grads[...]).astype(out.dtype)
        out[:, 2 * narrow :] = tn(cot[:, at], hidden[...]).astype(out.dtype)


def expert_body(got0, got1, to_slice, weights, keep, send, grad_keep, grad_send, rows, row_grads, wide, grad_hidden, hidden, grads):
    width = to_slice.shape[0]
    share = hidden.shape[1]
    count = got0.shape[0]
    for i, got in enumerate((got0, got1)):
        at = slice(i * count, (i + 1) * count)
        rows[at] = nn(got[:, :width], to_slice[...]).astype(BF16)
        row_grads[at] = nn(got[:, width:], to_slice[...]).astype(BF16)
    wide[...] = nn(rows[...], weights[:, : 2 * share])
    grad_hidden[...] = nn(row_grads[...], weights[:, 2 * share :])
    geglu_loop(wide, grad_hidden, hidden, grads)
    for out, at in ((send, slice(count, None)), (keep, slice(0, count))):
        feed = nt(hidden[at], weights[:, 2 * share :]).astype(BF16)
        back = nt(grads[at], weights[:, : 2 * share]).astype(BF16)
        out[:, :width] = nt(feed, to_slice[...]).astype(out.dtype)
        out[:, width:] = nt(back, to_slice[...]).astype(out.dtype)
    half = grad_keep.shape[0]
    for out, at in ((grad_send, slice(half, None)), (grad_keep, slice(0, half))):
        out[:, : 2 * share] = tn(rows[:, at], grads[...]).astype(out.dtype)
        out[:, 2 * share :] = tn(row_grads[:, at], hidden[...]).astype(out.dtype)


def turn_body(*refs):
    pieces = refs[:-12]
    (
        middle, feed, grad_normed, feed_rows, feed_grads, feed_select, vectors, cot, to_own,
        result, grad_middle, vector_grads,
    ) = refs[-12:]
    width = middle.shape[1]
    summed = pieces[0][...].astype(F32)
    for piece in pieces[1:]:
        summed = summed + piece[...].astype(F32)
    feed_heavy = reorder(summed[:, :width], to_own[...])
    grad_rows = reorder(summed[:, width:], to_own[...])
    rows = feed_rows[...].astype(F32)
    score = sigmoid(jnp.sum(rows * vectors[3:4], -1, keepdims=True))
    logit = jnp.sum(feed_grads[...] * feed_heavy, -1, keepdims=True) * score * (1.0 - score)
    grad_rows = grad_rows + logit * vectors[3:4]
    grads = grad_normed[...] + place_rows(feed_select[...], grad_rows)
    unit, scale = unit_rms(middle[...])
    grad_middle[...] = cot[...].astype(F32) + norm_back(grads, vectors[2:3], unit, scale)
    vector_grads[...] = jnp.concatenate(
        [
            jnp.zeros((2, width), F32),
            jnp.sum(grads * unit, 0, keepdims=True),
            jnp.sum(rows * logit, 0, keepdims=True),
            jnp.zeros((4, width), F32),
        ],
        axis=0,
    )
    out = middle[...] + feed[...] + place_rows(feed_select[...], score * feed_heavy)
    result[...] = nt(out.astype(BF16), to_own[...]).astype(BF16)


def heavy_scores_body(
    query_doc, key_doc, grad_middle, query_select, routed, pairs, queries, heavy_branch, sums, vectors, s0, s1,
    grad_branch, grad_queries, grad_pairs, logits
):
    heavy = HH * HDH
    score = sigmoid(jnp.sum(routed[...].astype(F32) * vectors[1:2], -1, keepdims=True))
    grad_rows = take_rows(query_select[...], grad_middle[...])
    grad_branch[...] = (score * grad_rows).astype(BF16)
    logit = jnp.sum(grad_rows * heavy_branch[...], -1, keepdims=True) * score * (1.0 - score)
    logits[...] = jnp.broadcast_to(logit, logits.shape)
    at = slice(0, heavy)
    grad_mixed = into(grad_branch[...], s0[:, at], s1[:, at]).astype(BF16)
    scale = 1.0 / math.sqrt(HDH)
    mask = jnp.concatenate([query_doc[...], query_doc[...]], axis=0) == key_doc[...]
    for p in range(HH // 2):
        at = slice(p * 128, (p + 1) * 128)
        beyond = slice(heavy + p * 128, heavy + (p + 1) * 128)
        query = both_heads(queries[:, at])
        grad_out = both_heads(grad_mixed[:, at])
        scores = jnp.where(mask, nt(query, pairs[:, at]) * scale, NEG)
        probs = jnp.exp(scores - sums[:, p : p + 1])
        grad_probs = nt(grad_out, pairs[:, beyond])
        delta = jnp.sum(probs * grad_probs, -1, keepdims=True)
        grad_scores = (probs * (grad_probs - delta)).astype(BF16)
        grad_queries[:, at] = one_pair(nn(grad_scores, pairs[:, at]) * scale).astype(BF16)
        grad_pairs[:, at] = (tn(grad_scores, query) * scale).astype(BF16)
        grad_pairs[:, beyond] = tn(probs.astype(BF16), grad_out).astype(BF16)


def heavy_weights_body(
    grad_middle, routed, keyed, light_mixed, heavy_mixed, grad_branch, grad_queries, grad_pairs, logits, vectors, to_own, s0, s1,
    keep, send, grad_routed, vector_grads, moved
):
    width = grad_middle.shape[1]
    heavy = HH * HDH
    light = HL * HDL
    half = s0.shape[0]
    slots = routed.shape[0]
    q_at = slice(width + light, width + light + heavy)
    kv_at = slice(width + light + heavy, width + light + 3 * heavy)
    logit = logits[:, 0:1]
    grad_routed[...] = onto(grad_queries[...], s0[:, q_at], s1[:, q_at]) + logit * vectors[1:2]
    step = 256

    def back(t, gain):
        rows = pl.ds(pl.multiple_of(t * step, step), step)
        grads = onto(grad_pairs[rows], s0[:, kv_at], s1[:, kv_at])
        moved[rows] = nt(grads.astype(BF16), to_own[...]).astype(BF16)
        return gain + jnp.sum(grads * keyed[rows].astype(F32), 0, keepdims=True)

    gain = lax.fori_loop(0, keyed.shape[0] // step, back, jnp.zeros((1, width), F32))
    vector_grads[...] = jnp.concatenate(
        [
            gain / vectors[0:1],
            jnp.sum(routed[...].astype(F32) * logit, 0, keepdims=True),
            jnp.zeros((6, width), F32),
        ],
        axis=0,
    )
    low = grad_middle[...].astype(BF16)
    part = half // (keyed.shape[0] // slots // 2)
    rest = slots - part
    chunk = width * rest // part
    for i, out in ((1, send), (0, keep)):
        at = slice(i * half, (i + 1) * half)
        out[:, :width] = tn(grad_branch[:, at], heavy_mixed[...]).astype(BF16)
        out[:, width : width + light] = tn(low[:, at], light_mixed[...]).astype(BF16)
        out[:, q_at] = tn(routed[:, at], grad_queries[...]).astype(BF16)
        out[:, kv_at] = tn(keyed[:, at], grad_pairs[...]).astype(BF16)
        to = width + light + 3 * heavy
        out[:, to : to + width] = moved[at]
        at = 2 * half + i * (half // part * rest)
        total = 0.0
        for piece in range(part // rest):
            block = moved[at : at + half // part * rest, piece * chunk : (piece + 1) * chunk]
            total = total + tn(piece_select(half, rest, part, piece), block)
        out[:, to + width :] = total.astype(BF16)


def light_scores_body(place, grad_middle, queries, pairs, sums, s0, s1, grad_queries, grad_pairs, held):
    light = HL * HDL
    heavy = HH * HDH
    reach = RADIUS
    rows = queries.shape[0]
    at = slice(heavy, heavy + light)
    grad_mixed = into(grad_middle[...].astype(BF16), s0[:, at], s1[:, at]).astype(BF16)
    held[...] = jnp.zeros_like(held)
    scale = 1.0 / math.sqrt(HDL)
    for tile in range(rows // reach):
        mine = slice(tile * reach, (tile + 1) * reach)
        seen = slice(tile * reach, (tile + 3) * reach)
        mask = local_mask(place, tile, reach, 2 * reach, 3 * reach)
        for p in range(HL // 2):
            at = slice(p * 128, (p + 1) * 128)
            beyond = slice(light + p * 128, light + (p + 1) * 128)
            query = both_heads(queries[mine, at])
            grad_out = both_heads(grad_mixed[mine, at])
            key = pairs[seen, at]
            log = jnp.concatenate([sums[mine, 2 * p : 2 * p + 1], sums[mine, 2 * p + 1 : 2 * p + 2]], axis=0)
            probs = jnp.exp(jnp.where(mask, nt(query, key) * scale, NEG) - log)
            grad_probs = nt(grad_out, pairs[seen, beyond])
            delta = jnp.sum(probs * grad_probs, -1, keepdims=True)
            grad_scores = (probs * (grad_probs - delta)).astype(BF16)
            grad_queries[mine, at] = one_pair(nn(grad_scores, key) * scale).astype(BF16)
            held[seen, at] = held[seen, at] + tn(grad_scores, query) * scale
            held[seen, beyond] = held[seen, beyond] + tn(probs.astype(BF16), grad_out)
    grad_pairs[...] = held[...].astype(BF16)


def light_weights_body(
    raw, normed, grad_queries, grad_pairs, grad_routed, query_select, feed_vectors, heavy_vectors, to_own, f0, f1,
    keep, send, outer, grad_mine
):
    light = HL * HDL
    reach = RADIUS
    rows = grad_queries.shape[0]
    half = f0.shape[0]
    grads = onto(grad_pairs[...], f0[:, light : 3 * light], f1[:, light : 3 * light])
    for i, at in enumerate((slice(0, reach), slice(reach + rows, None))):
        outer[i * reach : (i + 1) * reach] = nt(grads[at].astype(BF16), to_own[...]).astype(BF16)
    own = onto(grad_queries[...], f0[:, :light], f1[:, :light])
    own = own + grads[reach : reach + rows] + place_rows(query_select[...], grad_routed[...])
    grad_mine[...] = own
    unit, unused = unit_rms(raw[...].astype(F32))
    gain = jnp.sum(own * unit[reach : reach + rows], 0, keepdims=True)
    for at in (slice(0, reach), slice(reach + rows, None)):
        gain = gain + jnp.sum(grads[at] * unit[at], 0, keepdims=True)
    vector_rows = feed_vectors[...] + heavy_vectors[...]
    first = lax.broadcasted_iota(jnp.int32, vector_rows.shape, 0) == 0
    vector_rows = vector_rows + jnp.where(first, gain, 0.0)
    filler = jnp.zeros((120, raw.shape[1]), F32)
    columns = jnp.concatenate([vector_rows, filler], axis=0)
    for i, out in ((1, send), (0, keep)):
        at = slice(i * half, (i + 1) * half)
        out[:, :light] = tn(normed[reach : reach + rows, at], grad_queries[...]).astype(BF16)
        out[:, light : 3 * light] = tn(normed[:, at], grad_pairs[...]).astype(BF16)
        out[:, 3 * light :] = columns[:, at].T.astype(BF16)


def halo_body(from_prev, from_next, grad_mine, to_own, out):
    reach = RADIUS
    rows = grad_mine.shape[0]
    order = to_own[...]
    out[...] = grad_mine[...]
    out[:reach] = out[:reach] + nn(from_prev[...], order)
    out[rows - reach :] = out[rows - reach :] + nn(from_next[...], order)


def finish_body(keyed_grads, key_select, grads, grad_middle, raw, vectors, to_own, out):
    reach = RADIUS
    rows, width = grads.shape
    order = to_own[...]
    keyed = keyed_grads[...]
    if keyed.shape[0] < key_select.shape[0]:
        rest = key_select.shape[0] - keyed.shape[0]
        tail = [keyed[i * rest : (i + 1) * rest, width:] for i in range(keyed.shape[0] // rest)]
        keyed = jnp.concatenate([keyed[:, :width], jnp.concatenate(tail, axis=1)], axis=0)
    keyed = nn(keyed.astype(BF16), order).astype(BF16)
    total = grads[...] + tn(key_select[...], keyed)
    unit, scale = unit_rms(raw[reach : reach + rows].astype(F32))
    total = grad_middle[...] + norm_back(total, vectors[0:1], unit, scale)
    out[...] = reorder_back(total, order)


def heavy_forward_wide(query_doc, key_doc, select, normed, vectors, to_own, s0, s1, keyed_raw):
    heavy = HH * HDH
    at = vectors.shape[1] + HL * HDL
    q_at, kv_at = slice(at, at + heavy), slice(at + heavy, at + 3 * heavy)
    unit, unused = unit_rms(nn(keyed_raw, to_own))
    keyed = (unit * vectors[0:1]).astype(BF16)
    pairs = into(keyed, s0[:, kv_at], s1[:, kv_at]).astype(BF16)
    routed = nn(select, normed[RADIUS : normed.shape[0] - RADIUS]).astype(BF16)
    queries = into(routed, s0[:, q_at], s1[:, q_at]).astype(BF16)

    def heads(array):
        return array.reshape(-1, HH, HDH)

    scores = jnp.einsum(
        "qhd,khd->hqk", heads(queries), heads(pairs[:, :heavy]), preferred_element_type=F32
    ) / math.sqrt(HDH)
    probs = soft(jnp.where((query_doc == key_doc)[None], scores, NEG))
    mixed = jnp.einsum(
        "hqk,khd->qhd", probs.astype(BF16), heads(pairs[:, heavy:]), preferred_element_type=F32
    )
    return keyed, pairs, routed, queries, mixed.reshape(-1, heavy).astype(BF16), probs


def heavy_backward_wide(
    grad_middle, query_select, routed, keyed, pairs, queries, light_mixed, heavy_mixed, heavy_branch, probs,
    vectors, to_own, s0, s1
):
    heavy = HH * HDH
    scale = 1.0 / math.sqrt(HDH)
    half = s0.shape[0]
    at = vectors.shape[1] + HL * HDL
    q_at, kv_at = slice(at, at + heavy), slice(at + heavy, at + 3 * heavy)
    score = sigmoid(jnp.sum(routed.astype(F32) * vectors[1:2], -1, keepdims=True))
    grad_rows = take_rows(query_select, grad_middle)
    grad_branch = (score * grad_rows).astype(BF16)
    logit = jnp.sum(grad_rows * heavy_branch, -1, keepdims=True) * score * (1.0 - score)
    at = slice(0, heavy)
    grad_mixed = into(grad_branch, s0[:, at], s1[:, at]).astype(BF16)

    def heads(array):
        return array.reshape(-1, HH, HDH)

    def mix(pattern, left, right):
        return jnp.einsum(pattern, left, right, preferred_element_type=F32)

    grad_probs = mix("qhd,khd->hqk", heads(grad_mixed), heads(pairs[:, heavy:]))
    delta = jnp.sum(probs * grad_probs, -1, keepdims=True)
    grad_scores = (probs * (grad_probs - delta)).astype(BF16)
    grad_queries = mix("hqk,khd->qhd", grad_scores, heads(pairs[:, :heavy])) * scale
    grad_queries = grad_queries.reshape(-1, heavy).astype(BF16)
    grad_keys = mix("hqk,qhd->khd", grad_scores, heads(queries)) * scale
    grad_values = mix("hqk,qhd->khd", probs.astype(BF16), heads(grad_mixed))
    grad_pairs = jnp.concatenate(
        [grad_keys.reshape(-1, heavy).astype(BF16), grad_values.reshape(-1, heavy).astype(BF16)], axis=1
    )
    grad_routed = onto(grad_queries, s0[:, q_at], s1[:, q_at]) + logit * vectors[1:2]
    grads = onto(grad_pairs, s0[:, kv_at], s1[:, kv_at])
    vector_grads = jnp.concatenate(
        [
            jnp.sum(grads * keyed.astype(F32), 0, keepdims=True) / vectors[0:1],
            jnp.sum(routed.astype(F32) * logit, 0, keepdims=True),
            jnp.zeros((6, grads.shape[1]), F32),
        ],
        axis=0,
    )
    moved = nt(grads.astype(BF16), to_own).astype(BF16)
    low = grad_middle.astype(BF16)
    sides = []
    for at in (slice(0, half), slice(half, None)):
        columns = (
            tn(grad_branch[:, at], heavy_mixed),
            tn(low[:, at], light_mixed),
            tn(routed[:, at], grad_queries),
            tn(keyed[:, at], grad_pairs),
        )
        sides.append(jnp.concatenate(columns, axis=1).astype(BF16))
    return sides[0], sides[1], grad_routed, vector_grads, moved


def per_device(
    tokens,
    query_small,
    key_small,
    value_small,
    out_small,
    query_large,
    key_large,
    value_large,
    out_large,
    attend_gain,
    attend_router,
    gate_small,
    up_small,
    down_small,
    gate_large,
    up_large,
    down_large,
    feed_gain,
    feed_router,
    lengths,
    query_route,
    key_route,
    feed_route,
    cotangent,
):
    net = Net()
    rows, width = tokens.shape
    blocks = net.count
    part = width // blocks
    half = width // 2
    first = net.device * rows
    light = HL * HDL
    heavy = HH * HDH
    narrow = down_small.shape[0]
    wide = down_large.shape[0]
    slots = query_route.shape[1]
    members = 2 * net.depth
    share = wide // members
    pooled = members * slots
    keys = blocks * slots
    rest = slots - part
    packed = part % 8 == 0 and rest > 0 and rest % 8 == 0 and part % rest == 0 and keys <= 2048

    step = [(i, i + 1) for i in range(blocks - 1)]
    back = [(i + 1, i) for i in range(blocks - 1)]
    vector_pack = jnp.stack([attend_gain, attend_router, feed_gain, feed_router], axis=1)
    vector_pack = jnp.pad(vector_pack, ((0, 0), (0, 124)))
    first_parts = net.from_z(
        jnp.concatenate([query_small, key_small, value_small, vector_pack], axis=1)
    )
    column = jnp.arange(width, dtype=jnp.int32)
    own_order = net.target(column // part) * part + column % part
    bits = column // part // members
    bits = jnp.where(net.core == 1, bits, reverse_bits(bits, net.levels))
    member = column // part % members
    member = (net.core ^ (member % 2)) * net.depth + (net.z ^ (member // 2))
    slice_order = ((net.pair ^ bits) * members + member) * part + column % part
    orders = jnp.stack([own_order, slice_order])
    place = jnp.stack([first, lengths[0], lengths[1], jnp.int32(rows * blocks), net.device, net.core, net.z])
    square = ((width, width), BF16)
    chosen = ((slots, rows), BF16)

    if packed:
        tall = blocks * part
        spot = jnp.arange(keys, dtype=jnp.int32)
        spot_block = jnp.where(spot < tall, spot // part, (spot - tall) // rest)
        spot_slot = jnp.where(spot < tall, spot % part, part + (spot - tall) % rest)
        second_set, third_set, slices_keep, slices_send, key_docs = run(
            pack_body,
            "pack",
            [
                ((part, 5 * width + light + width * rest // part), BF16),
                ((part, 3 * narrow), BF16),
                ((net.depth * part, 3 * share), BF16),
                ((net.depth * part, 3 * share), BF16),
                ((1, keys), jnp.int32),
            ],
            (
                place, jnp.stack([net.target(spot_block), spot_slot]), tokens, key_route,
                query_large, key_large, value_large, out_large.T, out_small.T,
                gate_small, up_small, down_small.T, gate_large, up_large, down_large.T,
            ),
            smem=1,
            room=56 << 20,
        )
    else:
        second_set = jnp.concatenate(
            [out_large.T, out_small.T, query_large, key_large, value_large], axis=1
        )
        third_set = jnp.concatenate([gate_small, up_small, down_small.T], axis=1)
        stacked = jnp.stack([gate_large, up_large, down_large.T], axis=0)
        stacked = stacked.reshape(3, part, members, share).transpose(2, 1, 0, 3)
        stacked = jnp.take(stacked.reshape(members, part, 3 * share), net.members(), axis=0)
        slices_keep, slices_send = stacked.reshape(2, net.depth * part, 3 * share)
    order = Order()
    top_bit = net.levels - 1

    def take_z(pieces):
        return order.note(stack_rows([order.hold(pieces[0])] + pieces[1:]))

    def take(whole, moved):
        return order.note(stack_rows([whole, order.hold(moved)]))

    def first_moved(whole):
        return net.by_bit(whole, 0)

    def rest_moved(whole, moved):
        for j in range(1, net.levels):
            whole = take(whole, moved)
            moved = net.by_bit(whole, j)
        return whole, moved

    order.note(second_set)
    first_set = take_z(first_parts)
    first_moving = first_moved(first_set)
    second_parts = net.from_z(after(second_set, first_set))
    to_own, to_slice = run(orders_body, "orders", [square, square], (order.hold(orders),))
    order.note(to_own)
    first_set, first_moving = rest_moved(first_set, first_moving)
    second_set = take_z(second_parts)
    third_parts = net.from_z(after(third_set, second_set))
    cot, query_select, key_select, feed_select, query_docs = run(
        select_body,
        "select",
        [((rows, width), BF16), chosen, chosen, chosen, ((slots, 1), jnp.int32)],
        (place, to_own, query_route, key_route, feed_route, order.hold(cotangent)),
        smem=1,
    )
    order.note(cot)
    f0 = take(first_set, first_moving)
    f1 = net.by_core(f0)
    second_moving = first_moved(after(second_set, f0))
    slices_got = net.by_core(after(slices_send, f0))
    second_set, second_moving = rest_moved(second_set, second_moving)
    third_set = take_z(third_parts)
    near_tokens = after(tokens, third_set)
    above = lax.ppermute(near_tokens[rows - RADIUS :], AXES, step)
    below = lax.ppermute(near_tokens[:RADIUS], AXES, back)
    slices = pair_up(order.hold(slices_keep), slices_got, part)
    order.note(slices[0])
    expert_parts = net.exchange_z(slices)
    s0 = take(second_set, second_moving)
    s1 = net.by_core(s0)
    third_moving = first_moved(after(third_set, s0))
    (raw,) = run(
        prepare_body,
        "prepare",
        [((rows + 2 * RADIUS, width), BF16)],
        (order.hold(to_own), above, tokens, below),
    )
    order.note(raw)


    normed_ext, query_rows, pair_rows, vectors = run(
        light_rows_body,
        "light_rows",
        [
            ((rows + 2 * RADIUS, width), BF16),
            ((rows, light), BF16),
            ((rows + 2 * RADIUS, 2 * light), BF16),
            ((8, width), F32),
        ],
        (order.hold(raw), f0, f1),
    )
    order.note(query_rows)
    light_mixed, light_sums = run(
        light_forward_body,
        "light_forward",
        [((rows, light), BF16), ((rows, 128), F32)],
        (place, order.hold(query_rows), pair_rows),
        smem=1,
    )
    order.note(light_mixed)
    third_set, third_moving = rest_moved(third_set, third_moving)
    if packed:
        (keyed,) = run(
            functools.partial(heavy_rows_body, slots),
            "heavy_rows",
            [((keys, width), BF16)],
            (order.hold(vectors), to_own, s0, s1),
            scratch=[pltpu.VMEM((keys, width), BF16)],
        )
        order.note(keyed)
        heavy_pairs, routed, routed_query = run(
            heavy_pairs_body,
            "heavy_pairs",
            [((keys, 2 * heavy), BF16), ((slots, width), BF16), ((slots, heavy), BF16)],
            (order.hold(query_select), normed_ext, keyed, s0, s1),
        )
        order.note(routed_query)
        expert = take_z(expert_parts)
        heavy_mixed, heavy_sums = run(
            heavy_forward_body,
            "heavy_forward",
            [((slots, heavy), BF16), ((2 * slots, 128), F32)],
            (query_docs, key_docs, order.hold(routed_query), heavy_pairs),
        )
    else:
        expert = take_z(expert_parts)
        relative = net.target(jnp.arange(blocks, dtype=jnp.int32))
        near_routes = jnp.take(key_route, relative, axis=0)
        key_docs = document_of(relative[:, None] * rows + near_routes, lengths)
        key_docs = jnp.where(near_routes < rows, key_docs, -1).reshape(1, -1)
        keyed_raw = net.gather(nn(key_select, tokens).astype(BF16))
        keyed, heavy_pairs, routed, routed_query, heavy_mixed, heavy_sums = heavy_forward_wide(
            query_docs, key_docs, query_select, normed_ext, vectors, to_own,
            s0, s1, jnp.concatenate(keyed_raw, axis=0),
        )
    order.note(heavy_mixed)

    middle, normed_two, heavy_branch, feed_rows, feed_grads, sent = run(
        join_body,
        "join",
        [
            ((rows, width), F32),
            ((rows, width), BF16),
            ((slots, width), F32),
            ((slots, width), BF16),
            ((slots, width), F32),
            ((slots, 2 * width), BF16),
        ],
        (
            raw, light_mixed, order.hold(heavy_mixed), routed, query_select, feed_select, vectors, cot, to_own, s0, s1,
        ),
    )
    order.note(sent)

    got_parts = net.from_z(sent)
    t0 = take(third_set, third_moving)
    t1 = net.by_core(t0)
    expert_moving = first_moved(after(expert, t0))
    expert, expert_moving = rest_moved(expert, expert_moving)
    got0 = take_z(got_parts)
    got1 = net.by_core(got0)
    feed_light, grad_normed, hidden, hidden_grads = run(
        feed_body,
        "feed",
        [
            ((rows, width), F32),
            ((rows, width), F32),
            ((rows, narrow), BF16),
            ((rows, 2 * narrow), BF16),
        ],
        (order.hold(normed_two), cot, t0, t1),
        scratch=[pltpu.VMEM((rows, 2 * narrow), F32), pltpu.VMEM((rows, narrow), F32)],
    )
    order.note(hidden)
    third_keep, third_send = run(
        feed_weight_body,
        "feed_weight",
        [((half, 3 * narrow), BF16), ((half, 3 * narrow), BF16)],
        (normed_two, cot, order.hold(hidden), hidden_grads),
    )
    order.note(third_send)
    third_moving = net.by_core(third_send)
    expert = take(expert, expert_moving)
    keep, send, expert_keep, expert_send = run(
        expert_body,
        "expert",
        [
            ((pooled // 2, 2 * width), BF16),
            ((pooled // 2, 2 * width), BF16),
            ((half, 3 * share), BF16),
            ((half, 3 * share), BF16),
        ],
        (order.hold(got0), got1, to_slice, expert),
        scratch=[
            pltpu.VMEM((pooled, width), BF16),
            pltpu.VMEM((pooled, width), BF16),
            pltpu.VMEM((pooled, 2 * share), F32),
            pltpu.VMEM((pooled, share), F32),
            pltpu.VMEM((pooled, share), BF16),
            pltpu.VMEM((pooled, 2 * share), BF16),
        ],
    )
    order.note(send)
    moving = net.by_core(send)
    expert_moving = net.by_bit(expert_send, top_bit)

    def give(keep, moved, pieces):
        out = fold(keep, order.hold(moved), pieces)
        order.note(out[0])
        return out

    def descend(keep, moved):
        for j in reversed(range(net.levels - 1)):
            keep, send = give(keep, moved, 2)
            moved = net.by_bit(send, j)
        return keep, moved

    third_keep, third_send = give(third_keep, third_moving, 2)
    summed = net.exchange_z(give(keep, moving, net.depth))
    third_moving = net.by_bit(third_send, top_bit)

    expert_keep, expert_moving = descend(expert_keep, expert_moving)

    result, grad_middle, feed_vectors = run(
        turn_body,
        "turn",
        [((rows, width), BF16), ((rows, width), F32), ((8, width), F32)],
        (
            order.hold(summed[0]), *summed[1:], middle, feed_light, grad_normed, feed_rows, feed_grads, feed_select,
            vectors, cot, to_own,
        ),
    )
    order.note(grad_middle)
    if packed:
        grad_branch, grad_queries, grad_heavy_pairs, logits = run(
            heavy_scores_body,
            "heavy_scores",
            [
                ((slots, width), BF16),
                ((slots, heavy), BF16),
                ((keys, 2 * heavy), BF16),
                ((slots, 128), F32),
            ],
            (
                query_docs, key_docs, order.hold(grad_middle), query_select, routed, heavy_pairs, routed_query,
                heavy_branch, heavy_sums, vectors, s0, s1,
            ),
        )
        order.note(grad_branch)
    expert_parts = net.exchange_z(give(expert_keep, expert_moving, net.depth))
    third_keep, third_moving = descend(third_keep, third_moving)
    if packed:
        second_keep, second_send, grad_routed, heavy_vectors = run(
            heavy_weights_body,
            "heavy_weights",
            [
                ((half, 5 * width + light + width * rest // part), BF16),
                ((half, 5 * width + light + width * rest // part), BF16),
                ((slots, width), F32),
                ((8, width), F32),
            ],
            (
                grad_middle, routed, keyed, light_mixed, heavy_mixed, order.hold(grad_branch), grad_queries,
                grad_heavy_pairs, logits, vectors, to_own, s0, s1,
            ),
            scratch=[pltpu.VMEM((keys, width), BF16)],
        )
    else:
        second_keep, second_send, grad_routed, heavy_vectors, keyed_grads = heavy_backward_wide(
            grad_middle, query_select, routed, keyed, heavy_pairs, routed_query, light_mixed, heavy_mixed,
            heavy_branch, heavy_sums, vectors, to_own, s0, s1,
        )
    order.note(second_send)
    second_moving = net.by_core(second_send)
    third_parts = net.exchange_z(give(third_keep, third_moving, net.depth))
    expert_keep, expert_send = take_apart([order.hold(expert_parts[0])] + expert_parts[1:], part)
    order.note(expert_send)
    expert_got = net.by_core(expert_send)
    second_keep, second_send = give(second_keep, second_moving, 2)
    second_moving = net.by_bit(second_send, top_bit)
    grad_queries, grad_pairs = run(
        light_scores_body,
        "light_scores",
        [((rows, light), BF16), ((rows + 2 * RADIUS, 2 * light), BF16)],
        (place, order.hold(grad_middle), query_rows, pair_rows, light_sums, s0, s1),
        smem=1,
        scratch=[pltpu.VMEM((rows + 2 * RADIUS, 2 * light), F32)],
    )
    order.note(grad_queries)
    third_grad = settle([order.hold(third_parts[0])] + third_parts[1:], [narrow] * 3, "settle_third")
    order.note(third_grad[0])
    first_keep, first_send, outer, grad_mine = run(
        light_weights_body,
        "light_weights",
        [
            ((half, 3 * light + 128), BF16),
            ((half, 3 * light + 128), BF16),
            ((2 * RADIUS, width), BF16),
            ((rows, width), F32),
        ],
        (
            raw, normed_ext, order.hold(grad_queries), grad_pairs, grad_routed, query_select, feed_vectors, heavy_vectors,
            to_own, f0, f1,
        ),
    )
    order.note(first_send)
    first_moving = net.by_core(first_send)
    from_next = lax.ppermute(outer[:RADIUS], AXES, back)
    from_prev = lax.ppermute(outer[RADIUS:], AXES, step)

    if packed:
        gate_grad, up_grad, down_grad = run(
            unpack_body,
            "unpack",
            [((part, wide), F32)] * 3,
            (place, order.hold(expert_keep), expert_got),
            smem=1,
        )
    else:
        expert_grad = jnp.concatenate([order.hold(expert_keep), expert_got], axis=0)
        expert_grad = jnp.take(expert_grad.reshape(members, part, 3 * share), net.members(), axis=0)
        expert_grad = expert_grad.reshape(members, part, 3, share).transpose(2, 1, 0, 3)
        gate_grad, up_grad, down_grad = expert_grad.reshape(3, part, wide).astype(F32)
    order.note(gate_grad)
    second_keep, second_moving = descend(second_keep, second_moving)
    first_keep, first_send = give(first_keep, first_moving, 2)
    first_moving = net.by_bit(first_send, top_bit)
    (grad_near,) = run(
        halo_body, "halo", [((rows, width), F32)], (from_prev, from_next, order.hold(grad_mine), to_own)
    )
    order.note(grad_near)
    second_parts = net.exchange_z(give(second_keep, second_moving, net.depth))
    first_keep, first_moving = descend(first_keep, first_moving)
    first_parts = net.exchange_z(give(first_keep, first_moving, net.depth))
    widths = [width, light, heavy, heavy, heavy]
    if packed:
        widths.append(width + width * rest // part)
    second_grad = settle([order.hold(second_parts[0])] + second_parts[1:], widths, "settle_second")
    order.note(second_grad[0])
    if packed:
        keyed_own = second_grad[5]
    else:
        cut = keys // 2
        keyed_own = settle(net.reduce(keyed_grads[:cut], keyed_grads[cut:]), [width], "settle_keyed")[0]
    (tokens_grad,) = run(
        finish_body,
        "finish",
        [((rows, width), F32)],
        (order.hold(keyed_own), key_select, grad_near, grad_middle, raw, vectors, to_own),
    )
    order.note(tokens_grad)
    first_grad = settle(
        [order.hold(first_parts[0])] + first_parts[1:], [light, light, light, 128], "settle_first"
    )
    vector_out = first_grad[3][:, :4].T
    return (
        result,
        tokens_grad,
        first_grad[0],
        first_grad[1],
        first_grad[2],
        second_grad[1].T,
        second_grad[2],
        second_grad[3],
        second_grad[4],
        second_grad[0].T,
        vector_out[0],
        vector_out[1],
        third_grad[0],
        third_grad[1],
        third_grad[2].T,
        gate_grad,
        up_grad,
        down_grad.T,
        vector_out[2],
        vector_out[3],
    )


def solution(mesh):
    by_rows = P(AXES, None)
    by_columns = P(None, AXES)
    vector = P(AXES)
    return jax.shard_map(
        per_device,
        mesh=mesh,
        in_specs=(
            by_rows,
            by_rows,
            by_rows,
            by_rows,
            by_columns,
            by_rows,
            by_rows,
            by_rows,
            by_columns,
            vector,
            vector,
            by_rows,
            by_rows,
            by_columns,
            by_rows,
            by_rows,
            by_columns,
            vector,
            vector,
            P(),
            P(),
            P(),
            by_rows,
            by_rows,
        ),
        out_specs=(
            by_rows,
            by_rows,
            by_rows,
            by_rows,
            by_rows,
            by_columns,
            by_rows,
            by_rows,
            by_rows,
            by_columns,
            vector,
            vector,
            by_rows,
            by_rows,
            by_columns,
            by_rows,
            by_rows,
            by_columns,
            vector,
            vector,
        ),
        check_vma=False,
    )
```

```python
import functools
import math

import jax
import jax.numpy as jnp
from jax import lax
from jax.experimental import pallas as pl
from jax.experimental.pallas import tpu as pltpu
from jax.sharding import PartitionSpec as P

HL = 8
HDL = 64
HH = 12
HDH = 64
RADIUS = 128

NEG = -1e30
EPS = 1e-06
HIGH = lax.Precision.HIGHEST
AXES = ("seq", "fsdp")
F32 = jnp.float32
BF16 = jnp.bfloat16
ROOM = 12 << 20
LENGTHS = {
    "select": 60,
    "weave": 20,
    "light_forward": 60,
    "heavy_pairs": 60,
    "expert": 60,
    "feed": 60,
    "feed_weight": 20,
    "turn": 5.6,
    "routed": 60,
    "settle_third": 12,
}


def declared(name):
    flops = int(LENGTHS.get(name, 0.05) * 1e9)
    return pl.CostEstimate(flops=flops, bytes_accessed=10**10, transcendentals=0)


class Columns:
    def __init__(self, array, start, stop):
        self.array, self.start, self.stop = array, start, stop


def dot(left, right, dims):
    return lax.dot_general(left, right, (dims, ((), ())), preferred_element_type=F32)


def nn(left, right):
    return dot(left, right, ((1,), (0,)))


def nt(left, right):
    return dot(left, right, ((1,), (1,)))


def tn(left, right):
    return dot(left, right, ((0,), (0,)))


def reverse_bits(value, count):
    out = value * 0
    for j in range(count):
        out = out | (((value >> j) & 1) << (count - 1 - j))
    return out


class Net:
    def __init__(self):
        self.seq = lax.axis_size("seq")
        self.depth = lax.axis_size("fsdp")
        self.levels = (self.seq // 2).bit_length() - 1
        self.count = self.seq * self.depth
        s = lax.axis_index("seq")
        self.core, self.pair = s & 1, s >> 1
        self.z = lax.axis_index("fsdp")
        self.device = s * self.depth + self.z

    def pairs(self, move):
        out = []
        for s in range(self.seq):
            for z in range(self.depth):
                pair, core, to_z = move(s >> 1, s & 1, z)
                out.append((s * self.depth + z, (pair * 2 + core) * self.depth + to_z))
        return out

    def by_core(self, array):
        return lax.ppermute(array, AXES, self.pairs(lambda p, c, z: (p, 1 - c, z)))

    def by_bit(self, array, j):
        top = self.levels - 1 - j
        return lax.ppermute(
            array, AXES, self.pairs(lambda p, c, z: (p ^ (1 << (j if c else top)), c, z))
        )

    def by_z(self, array, k):
        return lax.ppermute(array, AXES, self.pairs(lambda p, c, z: (p, c, z ^ k)))

    def target(self, relative):
        zr = relative % self.depth
        bits = (relative // self.depth) % (self.seq // 2)
        core = self.core ^ (relative // (self.count // 2))
        pair = self.pair ^ jnp.where(core == 1, bits, reverse_bits(bits, self.levels))
        return (pair * 2 + core) * self.depth + (self.z ^ zr)

    def from_z(self, shard):
        return [shard] + [self.by_z(shard, k) for k in range(1, self.depth)]

    def exchange_z(self, pieces):
        return [pieces[0]] + [self.by_z(pieces[k], k) for k in range(1, self.depth)]

    def gather(self, shard):
        shard = jnp.concatenate(self.from_z(shard), axis=0)
        for j in range(self.levels):
            shard = jnp.concatenate([shard, self.by_bit(shard, j)], axis=0)
        return shard, self.by_core(shard)

    def reduce(self, keep, send):
        keep, send = fold(keep, self.by_core(send), 2)
        for j in reversed(range(self.levels)):
            pieces = 2 if j else self.depth
            out = fold(keep, self.by_bit(send, j), pieces)
            keep, send = out[0], out[1]
        return self.exchange_z(out)

    def members(self):
        relative = jnp.arange(2 * self.depth, dtype=jnp.int32)
        core = self.core ^ (relative // self.depth)
        return core * self.depth + (self.z ^ (relative % self.depth))


class Order:
    def __init__(self):
        self.last = ()

    def hold(self, array):
        return after(array, *self.last)

    def note(self, array):
        self.last = (array,)
        return array


def stack_rows(arrays):
    height = sum(a.shape[0] for a in arrays)
    if any(a.shape[0] % 8 for a in arrays):
        return jnp.concatenate(arrays, axis=0)

    def body(*refs):
        at = 0
        for ref in refs[:-1]:
            refs[-1][at : at + ref.shape[0]] = ref[...]
            at += ref.shape[0]

    return run(body, "stack", [((height, arrays[0].shape[1]), arrays[0].dtype)], arrays)[0]


def after(array, *earlier):
    return lax.optimization_barrier((array, *earlier))[0]


def unit_rms(values):
    scale = lax.rsqrt(jnp.mean(values * values, -1, keepdims=True) + EPS)
    return values * scale, scale


def norm_back(grad, gain, unit, scale):
    scaled = grad * gain
    return scale * (scaled - unit * jnp.mean(scaled * unit, -1, keepdims=True))


def document_of(places, lengths):
    return (places >= lengths[0]).astype(jnp.int32)


def sigmoid(values):
    return 1.0 / (1.0 + jnp.exp(-values))


def soft(scores):
    top = jnp.max(scores, -1, keepdims=True)
    expo = jnp.exp(scores - top)
    return expo / jnp.sum(expo, -1, keepdims=True)


def two_parts(values):
    high = values.astype(BF16)
    return high, (values - high.astype(F32)).astype(BF16)


def place_rows(select, values):
    high, low = two_parts(values)
    return tn(select, high) + tn(select, low)


def take_rows(select, values):
    high, low = two_parts(values)
    return nn(select, high) + nn(select, low)


def reorder(values, order):
    high, low = two_parts(values)
    return nn(high, order) + nn(low, order)


def reorder_back(values, order):
    high, low = two_parts(values)
    return nt(high, order) + nt(low, order)


def into(values, first, second):
    half = first.shape[0]
    return nn(values[:, :half], first) + nn(values[:, half:], second)


def onto(values, first, second):
    return jnp.concatenate([nt(values, first), nt(values, second)], axis=1)


def lanes(rows, width=128):
    return lax.broadcasted_iota(jnp.int32, (rows, width), 1)


def both_heads(pair):
    first = lanes(pair.shape[0]) < HDL
    zero = jnp.zeros_like(pair)
    return jnp.concatenate([jnp.where(first, pair, zero), jnp.where(first, zero, pair)], axis=0)


def one_pair(stacked):
    rows = stacked.shape[0] // 2
    return jnp.where(lanes(rows) < HDL, stacked[:rows], stacked[rows:])


def run(body, name, outs, args, smem=0, scratch=(), room=ROOM):
    vmem = pl.BlockSpec(memory_space=pltpu.VMEM)
    held = sum(math.prod(piece.shape) * jnp.dtype(piece.dtype).itemsize for piece in scratch)
    cuts = {i: a for i, a in enumerate(args) if isinstance(a, Columns)}

    def kernel(*refs):
        refs = list(refs)
        for i, cut in cuts.items():
            refs[i] = refs[i].at[:, cut.start : cut.stop]
        body(*refs)

    return pl.pallas_call(
        kernel,
        name=name,
        compiler_params=pltpu.CompilerParams(vmem_limit_bytes=held + room),
        out_shape=[jax.ShapeDtypeStruct(shape, kind) for shape, kind in outs],
        in_specs=[pl.BlockSpec(memory_space=pltpu.SMEM)] * smem + [vmem] * (len(args) - smem),
        out_specs=[vmem] * len(outs),
        scratch_shapes=list(scratch),
        cost_estimate=declared(name),
    )(*[a.array if isinstance(a, Columns) else a for a in args])


def rearrange(name, sources, outs, room=ROOM):
    bounds = [b for unused, moves in outs for m in moves for b in (*m[1], m[3])]
    if any(b % 8 for b in bounds):
        made = []
        for shape, moves in outs:
            out = jnp.zeros(shape, BF16)
            for i, (r0, r1), (c0, c1), row, column in moves:
                out = lax.dynamic_update_slice(out, sources[i][r0:r1, c0:c1], (row, column))
            made.append(out)
        return made

    def body(*refs):
        for out, (unused, moves) in zip(refs[len(sources) :], outs):
            for i, (r0, r1), (c0, c1), row, column in moves:
                out[row : row + r1 - r0, column : column + c1 - c0] = refs[i][r0:r1, c0:c1]

    return run(body, name, [(shape, BF16) for shape, unused in outs], sources, room=room)


def fold(keep, moved, pieces, kind=BF16):
    height, width = keep.shape
    piece = height // pieces
    parts = 2 if piece % 32 == 0 else 1
    step = piece // parts

    def body(*refs):
        for k in range(pieces):
            total = refs[k][...].astype(F32) + refs[pieces + k][...].astype(F32)
            refs[2 * pieces + k][...] = total.astype(kind)

    def spec(k):
        return pl.BlockSpec((step, width), lambda i, k=k: (k * parts + i, 0))

    if piece % 8:
        total = keep.astype(F32) + moved.astype(F32)
        return [total[k * piece : (k + 1) * piece].astype(kind) for k in range(pieces)]
    return pl.pallas_call(
        body,
        name="fold",
        compiler_params=pltpu.CompilerParams(vmem_limit_bytes=ROOM),
        grid=(parts,),
        out_shape=[jax.ShapeDtypeStruct((piece, width), kind)] * pieces,
        in_specs=[spec(k) for k in range(pieces)] * 2,
        out_specs=[spec(0)] * pieces,
        cost_estimate=declared("fold"),
    )(*([keep] * pieces + [moved] * pieces))


def settle(pieces, widths, name, rows=None):
    rows = rows or pieces[0].shape[0]

    def body(*refs):
        parts, outs = refs[: len(pieces)], refs[len(pieces) :]
        at = 0
        for out, width in zip(outs, widths):
            total = parts[0][:rows, at : at + width].astype(F32)
            for part in parts[1:]:
                total = total + part[:rows, at : at + width].astype(F32)
            out[...] = total
            at += width

    return run(body, name, [((rows, width), F32) for width in widths], pieces)


def hot(column, rows):
    return jnp.where(column == lanes(column.shape[0], rows), 1.0, 0.0).astype(BF16)


def as_column(row):
    count = row.shape[1]
    eye = lax.broadcasted_iota(jnp.int32, (count, count), 0) == lanes(count, count)
    spread = jnp.where(eye, row.astype(F32), 0.0)
    return jnp.sum(spread, -1, keepdims=True).astype(jnp.int32)


def order_matrix(order):
    width = order.shape[1]
    rows = lax.broadcasted_iota(jnp.int32, (width, width), 0)
    return jnp.where(rows == order, 1.0, 0.0).astype(BF16)


def orders_body(orders, to_own, to_slice):
    to_own[...] = order_matrix(orders[0:1])
    to_slice[...] = order_matrix(orders[1:2])


def select_body(
    place, to_own, query_route, key_route, feed_route, cotangent, cot, query_select, key_select, feed_select, query_doc
):
    rows = cotangent.shape[0]
    cot[...] = nn(cotangent[...], to_own[...]).astype(BF16)
    queries = as_column(query_route[pl.ds(place[4], 1)])
    query_select[...] = hot(queries, rows)
    key_select[...] = hot(as_column(key_route[pl.ds(place[4], 1)]), rows)
    feed_select[...] = hot(as_column(feed_route[...]), rows)
    query_doc[...] = jnp.where(place[0] + queries >= place[1], 1, 0)


def pack_body(
    place, key_spots, tokens, key_route, q_l, k_l, v_l,
    gate_s, up_s, down_s, gate_l, up_l, down_l, second, third, expert_keep, expert_send, key_docs
):
    part, width = q_l.shape
    at = 0
    for ref in (q_l, k_l, v_l):
        second[:, at : at + ref.shape[1]] = ref[...]
        at += ref.shape[1]
    keyed = nn(hot(as_column(key_route[pl.ds(place[4], 1)]), tokens.shape[0]), tokens[...])
    second[:, at : at + width] = keyed[:part].astype(BF16)
    rest = keyed[part:]
    chunk = width * rest.shape[0] // part
    pieces = [rest[:, i * chunk : (i + 1) * chunk] for i in range(width // chunk)]
    second[:, at + width :] = jnp.concatenate(pieces, axis=0).astype(BF16)
    narrow = gate_s.shape[1]
    for i, ref in enumerate((gate_s, up_s, down_s)):
        third[:, i * narrow : (i + 1) * narrow] = ref[...]
    share = expert_keep.shape[1] // 3
    depth = expert_keep.shape[0] // part
    for c, expert in enumerate((expert_keep, expert_send)):
        for k in range(depth):
            at = ((place[5] ^ c) * depth + (place[6] ^ k)) * share
            at = pl.ds(pl.multiple_of(at, share), share)
            for i, ref in enumerate((gate_l, up_l, down_l)):
                expert[k * part : (k + 1) * part, i * share : (i + 1) * share] = ref[:, at]
    blocks, slots = key_route.shape
    keys = key_spots.shape[1]
    block = lax.broadcasted_iota(jnp.int32, (blocks, keys), 0) == key_spots[0:1]
    table = key_route[...].astype(F32).T.astype(BF16)
    found = nn(table, jnp.where(block, 1.0, 0.0).astype(BF16))
    slot = lax.broadcasted_iota(jnp.int32, (slots, keys), 0) == key_spots[1:2]
    position = jnp.sum(jnp.where(slot, found, 0.0), 0, keepdims=True).astype(jnp.int32)
    rows = tokens.shape[0]
    document = jnp.where(key_spots[0:1] * rows + position >= place[1], 1, 0)
    key_docs[...] = jnp.where(position < rows, document, -1)


def prepare_body(to_own, above, tokens, below, raw):
    order = to_own[...]
    at = 0
    for ref in (above, tokens, below):
        raw[at : at + ref.shape[0]] = nn(ref[...], order).astype(BF16)
        at += ref.shape[0]


def unpack_body(place, keep, got, gate, up, down):
    part = gate.shape[0]
    depth = keep.shape[0] // part
    share = keep.shape[1] // 3
    for c, source in enumerate((keep, got)):
        for k in range(depth):
            at = ((place[5] ^ c) * depth + (place[6] ^ k)) * share
            at = pl.ds(pl.multiple_of(at, share), share)
            for i, out in enumerate((gate, up, down)):
                piece = source[k * part : (k + 1) * part, i * share : (i + 1) * share]
                out[:, at] = piece.astype(F32)


def pair_up(shard, first, second, part):
    count = first.shape[0] // part
    width = first.shape[1]
    whole, own = (0, part), (0, width)
    outs = []
    for k in range(count):
        at = (k * part, (k + 1) * part)
        moves = [(0, whole, (0, 2 * width), 0, 0), (1, at, own, part, 0), (2, at, own, part, width)]
        outs.append(((2 * part, 2 * width), moves))
    return rearrange("pair_up", (shard, first, second), outs)


def stack_both(pieces, name="stack_both"):
    height = sum(p.shape[0] for p in pieces)
    width = pieces[0].shape[1]
    moves, row = [], 0
    for i, piece in enumerate(pieces):
        n = piece.shape[0] // 2
        moves.append((i, (0, n), (0, width), row, 0))
        moves.append((i, (n, 2 * n), (0, width), height // 2 + row, 0))
        row += n
    return rearrange(name, pieces, [((height, width), moves)])[0]


def part_both(pieces, name):
    height = sum(p.shape[0] for p in pieces) // 2
    width = pieces[0].shape[1]
    first, second, row = [], [], 0
    for i, piece in enumerate(pieces):
        n = piece.shape[0] // 2
        first.append((i, (0, n), (0, width), row, 0))
        second.append((i, (n, 2 * n), (0, width), row, 0))
        row += n
    return rearrange(name, pieces, [((height, width), first), ((height, width), second)])


def take_apart(pieces, part):
    width = pieces[0].shape[1] // 2
    outs = []
    for side in range(2):
        columns = (side * width, (side + 1) * width)
        moves = [(k, (0, part), columns, k * part, 0) for k in range(len(pieces))]
        outs.append(((len(pieces) * part, width), moves))
    return rearrange("take_apart", pieces, outs)


def local_mask(place, tile, reach, stacked, span):
    shape = (stacked, span)
    row = lax.broadcasted_iota(jnp.int32, shape, 0) & (reach - 1)
    query = place[0] + tile * reach + row
    key = place[0] + (tile - 1) * reach + lax.broadcasted_iota(jnp.int32, shape, 1)
    split, live, total = place[1], place[1] + place[2], place[3]
    inside = (key >= 0) & (key < total)
    same = jnp.where(query >= split, 1, 0) == jnp.where(key >= split, 1, 0)
    near = jnp.abs(query - key) <= reach
    both = ((query < live) & (key < live)) | (query == key)
    return near & inside & same & both


def light_rows_body(raw, w0, w1, normed, queries, pairs, vectors):
    light = HL * HDL
    reach = RADIUS
    rows = queries.shape[0]
    columns = [w[:, 3 * light :].astype(F32).T[:8] for w in (w0, w1)]
    vectors[...] = jnp.concatenate(columns, axis=1)
    unit, unused = unit_rms(raw[...].astype(F32))
    normed[...] = (unit * vectors[0:1]).astype(BF16)
    own = normed[reach : reach + rows]
    queries[...] = into(own, w0[:, :light], w1[:, :light]).astype(BF16)
    pairs[...] = into(normed[...], w0[:, light : 3 * light], w1[:, light : 3 * light]).astype(BF16)


def light_forward_body(place, queries, pairs, mixed, sums):
    light = HL * HDL
    reach = RADIUS
    rows = queries.shape[0]
    scale = 1.0 / math.sqrt(HDL)
    lane = lanes(reach)
    for tile in range(rows // reach):
        mine = slice(tile * reach, (tile + 1) * reach)
        seen = slice(tile * reach, (tile + 3) * reach)
        mask = local_mask(place, tile, reach, 2 * reach, 3 * reach)
        logs = jnp.zeros((reach, 128), F32)
        for p in range(HL // 2):
            at = slice(p * 128, (p + 1) * 128)
            query = both_heads(queries[mine, at])
            scores = jnp.where(mask, nt(query, pairs[seen, at]) * scale, NEG)
            top = jnp.max(scores, -1, keepdims=True)
            expo = jnp.exp(scores - top)
            total = jnp.sum(expo, -1, keepdims=True)
            probs = (expo * (1.0 / total)).astype(BF16)
            value = pairs[seen, light + p * 128 : light + (p + 1) * 128]
            mixed[mine, at] = one_pair(nn(probs, value)).astype(BF16)
            log = top + jnp.log(total)
            logs = jnp.where(lane == 2 * p, log[:reach], logs)
            logs = jnp.where(lane == 2 * p + 1, log[reach:], logs)
        sums[mine] = logs


def piece_select(block_rows, rest, part, piece):
    shape = (block_rows // part * rest, block_rows)
    k = lax.broadcasted_iota(jnp.int32, shape, 0)
    row = lax.broadcasted_iota(jnp.int32, shape, 1)
    shift = rest.bit_length() - 1
    want = (k >> shift) * part + piece * rest + (k & (rest - 1))
    return jnp.where(row == want, 1.0, 0.0).astype(BF16)


def heavy_rows_body(slots, vectors, to_own, s0, s1, keyed, held):
    width = to_own.shape[0]
    half = s0.shape[0]
    at = 3 * HH * HDH
    part = half // (keyed.shape[0] // slots // 2)
    rest = slots - part
    chunk = width * rest // part
    for i, ref in enumerate((s0, s1)):
        held[i * half : (i + 1) * half] = ref[:, at : at + width]
        low = 2 * half + i * (half // part * rest)
        for piece in range(part // rest):
            picked = nn(piece_select(half, rest, part, piece), ref[:, at + width :])
            held[low : low + half // part * rest, piece * chunk : (piece + 1) * chunk] = picked.astype(BF16)
    step = 256

    def project(t, carry):
        rows = pl.ds(pl.multiple_of(t * step, step), step)
        unit, unused = unit_rms(nn(held[rows], to_own[...]))
        keyed[rows] = (unit * vectors[0:1]).astype(BF16)
        return carry

    lax.fori_loop(0, keyed.shape[0] // step, project, 0)


def heavy_pairs_body(select, normed, keyed, s0, s1, pairs, routed, queries):
    heavy = HH * HDH
    q_at = slice(0, heavy)
    kv_at = slice(heavy, 3 * heavy)
    step = 256

    def project(t, carry):
        rows = pl.ds(pl.multiple_of(t * step, step), step)
        pairs[rows] = into(keyed[rows], s0[:, kv_at], s1[:, kv_at]).astype(BF16)
        return carry

    lax.fori_loop(0, keyed.shape[0] // step, project, 0)
    own = normed[RADIUS : normed.shape[0] - RADIUS]
    routed[...] = nn(select[...], own).astype(BF16)
    queries[...] = into(routed[...], s0[:, q_at], s1[:, q_at]).astype(BF16)


def heavy_forward_body(query_doc, key_doc, queries, pairs, mixed, sums):
    heavy = HH * HDH
    slots = queries.shape[0]
    scale = 1.0 / math.sqrt(HDH)
    mask = jnp.concatenate([query_doc[...], query_doc[...]], axis=0) == key_doc[...]
    logs = jnp.zeros((2 * slots, 128), F32)
    for p in range(HH // 2):
        at = slice(p * 128, (p + 1) * 128)
        scores = jnp.where(mask, nt(both_heads(queries[:, at]), pairs[:, at]) * scale, NEG)
        top = jnp.max(scores, -1, keepdims=True)
        expo = jnp.exp(scores - top)
        total = jnp.sum(expo, -1, keepdims=True)
        probs = (expo * (1.0 / total)).astype(BF16)
        mixed[:, at] = one_pair(nn(probs, pairs[:, heavy + p * 128 : heavy + (p + 1) * 128])).astype(BF16)
        logs = jnp.where(lanes(2 * slots) == p, top + jnp.log(total), logs)
    sums[...] = logs


def join_body(
    raw, light_mixed, heavy_mixed, routed, query_select, feed_select, vectors, cot, to_own, s0, s1,
    middle, normed, heavy_branch, feed_rows, feed_grads, sent
):
    heavy = HH * HDH
    width = raw.shape[1]
    rows = middle.shape[0]
    at = slice(heavy, heavy + HL * HDL)
    light_branch = onto(light_mixed[...], s0[:, at], s1[:, at])
    at = slice(0, heavy)
    heavy_branch[...] = onto(heavy_mixed[...], s0[:, at], s1[:, at])
    score = sigmoid(jnp.sum(routed[...].astype(F32) * vectors[1:2], -1, keepdims=True))
    inputs = raw[RADIUS : RADIUS + rows].astype(F32)
    middle[...] = inputs + light_branch + place_rows(query_select[...], score * heavy_branch[...])
    unit, unused = unit_rms(middle[...])
    normed[...] = (unit * vectors[2:3]).astype(BF16)
    feed_rows[...] = nn(feed_select[...], normed[...]).astype(BF16)
    feed_grads[...] = nn(feed_select[...], cot[...])
    score = sigmoid(jnp.sum(feed_rows[...].astype(F32) * vectors[3:4], -1, keepdims=True))
    sent[:, :width] = nt(feed_rows[...], to_own[...]).astype(BF16)
    sent[:, width:] = nt((score * feed_grads[...]).astype(BF16), to_own[...]).astype(BF16)


def geglu_rows(gate, upper, grad_hidden):
    c0, c1 = 0.7978845608028654, 0.044715
    square = gate * gate
    bent = jnp.tanh(c0 * gate * (1.0 + c1 * square))
    bell = 0.5 * (1.0 + bent)
    gelu = gate * bell
    slope = bell + 0.5 * gate * (1.0 - bent * bent) * (c0 * (1.0 + 3.0 * c1 * square))
    return gelu * upper, grad_hidden * upper * slope, grad_hidden * gelu


def geglu_loop(wide, grad_hidden, hidden, grads):
    count = hidden.shape[1]
    step = 32

    def rows_at(t, carry):
        rows = pl.ds(pl.multiple_of(t * step, step), step)
        out, grad_gate, grad_upper = geglu_rows(
            wide[rows, :count], wide[rows, count:], grad_hidden[rows]
        )
        hidden[rows] = out.astype(BF16)
        grads[rows, :count] = grad_gate.astype(BF16)
        grads[rows, count:] = grad_upper.astype(BF16)
        return carry

    lax.fori_loop(0, hidden.shape[0] // step, rows_at, 0)


def feed_body(normed, cot, t0, t1, feed, grad_normed, hidden, grads, wide, grad_hidden):
    narrow = hidden.shape[1]
    wide[...] = into(normed[...], t0[:, : 2 * narrow], t1[:, : 2 * narrow])
    grad_hidden[...] = into(cot[...], t0[:, 2 * narrow :], t1[:, 2 * narrow :])
    geglu_loop(wide, grad_hidden, hidden, grads)
    feed[...] = onto(hidden[...], t0[:, 2 * narrow :], t1[:, 2 * narrow :])
    grad_normed[...] = onto(grads[...], t0[:, : 2 * narrow], t1[:, : 2 * narrow])


def feed_weight_body(normed, cot, hidden, grads, keep, send):
    narrow = hidden.shape[1]
    half = keep.shape[0]
    for out, at in ((send, slice(half, None)), (keep, slice(0, half))):
        out[:, : 2 * narrow] = tn(normed[:, at], grads[...]).astype(out.dtype)
        out[:, 2 * narrow :] = tn(cot[:, at], hidden[...]).astype(out.dtype)


def expert_body(got0, got1, to_slice, weights, keep, send, grad_keep, grad_send, rows, row_grads, wide, grad_hidden, hidden, grads):
    width = to_slice.shape[0]
    share = hidden.shape[1]
    count = got0.shape[0]
    for i, got in enumerate((got0, got1)):
        at = slice(i * count, (i + 1) * count)
        rows[at] = nn(got[:, :width], to_slice[...]).astype(BF16)
        row_grads[at] = nn(got[:, width:], to_slice[...]).astype(BF16)
    first, second = weights[:, : 2 * share], weights[:, 3 * share : 5 * share]
    first_down, second_down = weights[:, 2 * share : 3 * share], weights[:, 5 * share :]
    wide[...] = into(rows[...], first, second)
    grad_hidden[...] = into(row_grads[...], first_down, second_down)
    geglu_loop(wide, grad_hidden, hidden, grads)
    for out, at in ((send, slice(count, None)), (keep, slice(0, count))):
        feed = onto(hidden[at], first_down, second_down).astype(BF16)
        back = onto(grads[at], first, second).astype(BF16)
        out[:, :width] = nt(feed, to_slice[...]).astype(out.dtype)
        out[:, width:] = nt(back, to_slice[...]).astype(out.dtype)
    half = weights.shape[0]
    low = grad_keep.shape[0]
    for i in range(2):
        at = slice(i * half, (i + 1) * half)
        to = 3 * share * i
        for left, right, columns in (
            (rows, grads, slice(to, to + 2 * share)), (row_grads, hidden, slice(to + 2 * share, to + 3 * share))
        ):
            product = tn(left[:, at], right[...]).astype(BF16)
            grad_keep[:, columns] = product[:low]
            grad_send[:, columns] = product[low:]


def turn_body(*refs):
    pieces = refs[:-12]
    (
        middle, feed, grad_normed, feed_rows, feed_grads, feed_select, vectors, cot, to_own,
        result, grad_middle, vector_grads,
    ) = refs[-12:]
    width = middle.shape[1]
    summed = pieces[0][...].astype(F32)
    for piece in pieces[1:]:
        summed = summed + piece[...].astype(F32)
    feed_heavy = reorder(summed[:, :width], to_own[...])
    grad_rows = reorder(summed[:, width:], to_own[...])
    rows = feed_rows[...].astype(F32)
    score = sigmoid(jnp.sum(rows * vectors[3:4], -1, keepdims=True))
    logit = jnp.sum(feed_grads[...] * feed_heavy, -1, keepdims=True) * score * (1.0 - score)
    grad_rows = grad_rows + logit * vectors[3:4]
    grads = grad_normed[...] + place_rows(feed_select[...], grad_rows)
    unit, scale = unit_rms(middle[...])
    grad_middle[...] = cot[...].astype(F32) + norm_back(grads, vectors[2:3], unit, scale)
    vector_grads[...] = jnp.concatenate(
        [
            jnp.zeros((2, width), F32),
            jnp.sum(grads * unit, 0, keepdims=True),
            jnp.sum(rows * logit, 0, keepdims=True),
            jnp.zeros((4, width), F32),
        ],
        axis=0,
    )
    out = middle[...] + feed[...] + place_rows(feed_select[...], score * feed_heavy)
    result[...] = nt(out.astype(BF16), to_own[...]).astype(BF16)


def heavy_scores_body(
    query_doc, key_doc, grad_middle, query_select, routed, pairs, queries, heavy_branch, sums, vectors, s0, s1,
    grad_branch, grad_queries, grad_pairs, logits
):
    heavy = HH * HDH
    score = sigmoid(jnp.sum(routed[...].astype(F32) * vectors[1:2], -1, keepdims=True))
    grad_rows = take_rows(query_select[...], grad_middle[...])
    grad_branch[...] = (score * grad_rows).astype(BF16)
    logit = jnp.sum(grad_rows * heavy_branch[...], -1, keepdims=True) * score * (1.0 - score)
    logits[...] = jnp.broadcast_to(logit, logits.shape)
    at = slice(0, heavy)
    grad_mixed = into(grad_branch[...], s0[:, at], s1[:, at]).astype(BF16)
    scale = 1.0 / math.sqrt(HDH)
    mask = jnp.concatenate([query_doc[...], query_doc[...]], axis=0) == key_doc[...]
    for p in range(HH // 2):
        at = slice(p * 128, (p + 1) * 128)
        beyond = slice(heavy + p * 128, heavy + (p + 1) * 128)
        query = both_heads(queries[:, at])
        grad_out = both_heads(grad_mixed[:, at])
        scores = jnp.where(mask, nt(query, pairs[:, at]) * scale, NEG)
        probs = jnp.exp(scores - sums[:, p : p + 1])
        grad_probs = nt(grad_out, pairs[:, beyond])
        delta = jnp.sum(probs * grad_probs, -1, keepdims=True)
        grad_scores = (probs * (grad_probs - delta)).astype(BF16)
        grad_queries[:, at] = one_pair(nn(grad_scores, pairs[:, at]) * scale).astype(BF16)
        grad_pairs[:, at] = (tn(grad_scores, query) * scale).astype(BF16)
        grad_pairs[:, beyond] = tn(probs.astype(BF16), grad_out).astype(BF16)


def heavy_weights_body(
    grad_middle, routed, keyed, light_mixed, heavy_mixed, grad_branch, grad_queries, grad_pairs, logits, vectors, to_own, s0, s1,
    keep, send, vector_grads, moved
):
    width = grad_middle.shape[1]
    heavy = HH * HDH
    light = HL * HDL
    half = s0.shape[0]
    slots = routed.shape[0]
    q_at = slice(width + light, width + light + heavy)
    kv_at = slice(width + light + heavy, width + light + 3 * heavy)
    logit = logits[:, 0:1]
    step = 256

    def back(t, gain):
        rows = pl.ds(pl.multiple_of(t * step, step), step)
        grads = onto(grad_pairs[rows], s0[:, heavy : 3 * heavy], s1[:, heavy : 3 * heavy])
        moved[rows] = nt(grads.astype(BF16), to_own[...]).astype(BF16)
        return gain + jnp.sum(grads * keyed[rows].astype(F32), 0, keepdims=True)

    gain = lax.fori_loop(0, keyed.shape[0] // step, back, jnp.zeros((1, width), F32))
    vector_grads[...] = jnp.concatenate(
        [
            gain / vectors[0:1],
            jnp.sum(routed[...].astype(F32) * logit, 0, keepdims=True),
            jnp.zeros((6, width), F32),
        ],
        axis=0,
    )
    low = grad_middle[...].astype(BF16)
    part = half // (keyed.shape[0] // slots // 2)
    rest = slots - part
    chunk = width * rest // part
    for i, out in ((1, send), (0, keep)):
        at = slice(i * half, (i + 1) * half)
        out[:, :width] = tn(grad_branch[:, at], heavy_mixed[...]).astype(BF16)
        out[:, width : width + light] = tn(low[:, at], light_mixed[...]).astype(BF16)
        out[:, q_at] = tn(routed[:, at], grad_queries[...]).astype(BF16)
        out[:, kv_at] = tn(keyed[:, at], grad_pairs[...]).astype(BF16)
        to = width + light + 3 * heavy
        out[:, to : to + width] = moved[at]
        at = 2 * half + i * (half // part * rest)
        total = 0.0
        for piece in range(part // rest):
            block = moved[at : at + half // part * rest, piece * chunk : (piece + 1) * chunk]
            total = total + tn(piece_select(half, rest, part, piece), block)
        out[:, to + width :] = total.astype(BF16)


def routed_body(grad_queries, logits, vectors, s0, s1, grad_routed):
    at = slice(0, HH * HDH)
    grad_routed[...] = onto(grad_queries[...], s0[:, at], s1[:, at]) + logits[:, 0:1] * vectors[1:2]


def light_scores_body(place, grad_middle, queries, pairs, sums, s0, s1, grad_queries, grad_pairs, held):
    light = HL * HDL
    heavy = HH * HDH
    reach = RADIUS
    rows = queries.shape[0]
    at = slice(heavy, heavy + light)
    grad_mixed = into(grad_middle[...].astype(BF16), s0[:, at], s1[:, at]).astype(BF16)
    held[...] = jnp.zeros_like(held)
    scale = 1.0 / math.sqrt(HDL)
    for tile in range(rows // reach):
        mine = slice(tile * reach, (tile + 1) * reach)
        seen = slice(tile * reach, (tile + 3) * reach)
        mask = local_mask(place, tile, reach, 2 * reach, 3 * reach)
        for p in range(HL // 2):
            at = slice(p * 128, (p + 1) * 128)
            beyond = slice(light + p * 128, light + (p + 1) * 128)
            query = both_heads(queries[mine, at])
            grad_out = both_heads(grad_mixed[mine, at])
            key = pairs[seen, at]
            log = jnp.concatenate([sums[mine, 2 * p : 2 * p + 1], sums[mine, 2 * p + 1 : 2 * p + 2]], axis=0)
            probs = jnp.exp(jnp.where(mask, nt(query, key) * scale, NEG) - log)
            grad_probs = nt(grad_out, pairs[seen, beyond])
            delta = jnp.sum(probs * grad_probs, -1, keepdims=True)
            grad_scores = (probs * (grad_probs - delta)).astype(BF16)
            grad_queries[mine, at] = one_pair(nn(grad_scores, key) * scale).astype(BF16)
            held[seen, at] = held[seen, at] + tn(grad_scores, query) * scale
            held[seen, beyond] = held[seen, beyond] + tn(probs.astype(BF16), grad_out)
    grad_pairs[...] = held[...].astype(BF16)


def light_weights_body(
    raw, normed, grad_queries, grad_pairs, grad_routed, query_select, feed_vectors, heavy_vectors, to_own, f0, f1,
    keep, send, outer, grad_mine
):
    light = HL * HDL
    reach = RADIUS
    rows = grad_queries.shape[0]
    half = f0.shape[0]
    grads = onto(grad_pairs[...], f0[:, light : 3 * light], f1[:, light : 3 * light])
    for i, at in enumerate((slice(0, reach), slice(reach + rows, None))):
        outer[i * reach : (i + 1) * reach] = nt(grads[at].astype(BF16), to_own[...]).astype(BF16)
    own = onto(grad_queries[...], f0[:, :light], f1[:, :light])
    own = own + grads[reach : reach + rows] + place_rows(query_select[...], grad_routed[...])
    grad_mine[...] = own
    unit, unused = unit_rms(raw[...].astype(F32))
    gain = jnp.sum(own * unit[reach : reach + rows], 0, keepdims=True)
    for at in (slice(0, reach), slice(reach + rows, None)):
        gain = gain + jnp.sum(grads[at] * unit[at], 0, keepdims=True)
    vector_rows = feed_vectors[...] + heavy_vectors[...]
    first = lax.broadcasted_iota(jnp.int32, vector_rows.shape, 0) == 0
    vector_rows = vector_rows + jnp.where(first, gain, 0.0)
    filler = jnp.zeros((120, raw.shape[1]), F32)
    columns = jnp.concatenate([vector_rows, filler], axis=0)
    for i, out in ((1, send), (0, keep)):
        at = slice(i * half, (i + 1) * half)
        out[:, :light] = tn(normed[reach : reach + rows, at], grad_queries[...]).astype(BF16)
        out[:, light : 3 * light] = tn(normed[:, at], grad_pairs[...]).astype(BF16)
        out[:, 3 * light :] = columns[:, at].T.astype(BF16)


def halo_body(from_prev, from_next, grad_mine, to_own, out):
    reach = RADIUS
    rows = grad_mine.shape[0]
    order = to_own[...]
    out[...] = grad_mine[...]
    out[:reach] = out[:reach] + nn(from_prev[...], order)
    out[rows - reach :] = out[rows - reach :] + nn(from_next[...], order)


def finish_body(keyed_grads, key_select, grads, grad_middle, raw, vectors, to_own, out):
    reach = RADIUS
    rows, width = grads.shape
    order = to_own[...]
    keyed = keyed_grads[...]
    if keyed.shape[0] < key_select.shape[0]:
        rest = key_select.shape[0] - keyed.shape[0]
        tail = [keyed[i * rest : (i + 1) * rest, width:] for i in range(keyed.shape[0] // rest)]
        keyed = jnp.concatenate([keyed[:, :width], jnp.concatenate(tail, axis=1)], axis=0)
    keyed = nn(keyed.astype(BF16), order).astype(BF16)
    total = grads[...] + tn(key_select[...], keyed)
    unit, scale = unit_rms(raw[reach : reach + rows].astype(F32))
    total = grad_middle[...] + norm_back(total, vectors[0:1], unit, scale)
    out[...] = reorder_back(total, order)


def heavy_forward_wide(query_doc, key_doc, select, normed, vectors, to_own, s0, s1, keyed_raw):
    heavy = HH * HDH
    q_at, kv_at = slice(0, heavy), slice(heavy, 3 * heavy)
    unit, unused = unit_rms(nn(keyed_raw, to_own))
    keyed = (unit * vectors[0:1]).astype(BF16)
    pairs = into(keyed, s0[:, kv_at], s1[:, kv_at]).astype(BF16)
    routed = nn(select, normed[RADIUS : normed.shape[0] - RADIUS]).astype(BF16)
    queries = into(routed, s0[:, q_at], s1[:, q_at]).astype(BF16)

    def heads(array):
        return array.reshape(-1, HH, HDH)

    scores = jnp.einsum(
        "qhd,khd->hqk", heads(queries), heads(pairs[:, :heavy]), preferred_element_type=F32
    ) / math.sqrt(HDH)
    probs = soft(jnp.where((query_doc == key_doc)[None], scores, NEG))
    mixed = jnp.einsum(
        "hqk,khd->qhd", probs.astype(BF16), heads(pairs[:, heavy:]), preferred_element_type=F32
    )
    return keyed, pairs, routed, queries, mixed.reshape(-1, heavy).astype(BF16), probs


def heavy_backward_wide(
    grad_middle, query_select, routed, keyed, pairs, queries, light_mixed, heavy_mixed, heavy_branch, probs,
    vectors, to_own, o0, o1, s0, s1
):
    heavy = HH * HDH
    scale = 1.0 / math.sqrt(HDH)
    half = s0.shape[0]
    q_at, kv_at = slice(0, heavy), slice(heavy, 3 * heavy)
    score = sigmoid(jnp.sum(routed.astype(F32) * vectors[1:2], -1, keepdims=True))
    grad_rows = take_rows(query_select, grad_middle)
    grad_branch = (score * grad_rows).astype(BF16)
    logit = jnp.sum(grad_rows * heavy_branch, -1, keepdims=True) * score * (1.0 - score)
    at = slice(0, heavy)
    grad_mixed = into(grad_branch, o0[:, at], o1[:, at]).astype(BF16)

    def heads(array):
        return array.reshape(-1, HH, HDH)

    def mix(pattern, left, right):
        return jnp.einsum(pattern, left, right, preferred_element_type=F32)

    grad_probs = mix("qhd,khd->hqk", heads(grad_mixed), heads(pairs[:, heavy:]))
    delta = jnp.sum(probs * grad_probs, -1, keepdims=True)
    grad_scores = (probs * (grad_probs - delta)).astype(BF16)
    grad_queries = mix("hqk,khd->qhd", grad_scores, heads(pairs[:, :heavy])) * scale
    grad_queries = grad_queries.reshape(-1, heavy).astype(BF16)
    grad_keys = mix("hqk,qhd->khd", grad_scores, heads(queries)) * scale
    grad_values = mix("hqk,qhd->khd", probs.astype(BF16), heads(grad_mixed))
    grad_pairs = jnp.concatenate(
        [grad_keys.reshape(-1, heavy).astype(BF16), grad_values.reshape(-1, heavy).astype(BF16)], axis=1
    )
    grad_routed = onto(grad_queries, s0[:, q_at], s1[:, q_at]) + logit * vectors[1:2]
    grads = onto(grad_pairs, s0[:, kv_at], s1[:, kv_at])
    vector_grads = jnp.concatenate(
        [
            jnp.sum(grads * keyed.astype(F32), 0, keepdims=True) / vectors[0:1],
            jnp.sum(routed.astype(F32) * logit, 0, keepdims=True),
            jnp.zeros((6, grads.shape[1]), F32),
        ],
        axis=0,
    )
    moved = nt(grads.astype(BF16), to_own).astype(BF16)
    low = grad_middle.astype(BF16)
    sides = []
    for at in (slice(0, half), slice(half, None)):
        columns = (
            tn(grad_branch[:, at], heavy_mixed),
            tn(low[:, at], light_mixed),
            tn(routed[:, at], grad_queries),
            tn(keyed[:, at], grad_pairs),
        )
        sides.append(jnp.concatenate(columns, axis=1).astype(BF16))
    return sides[0], sides[1], grad_routed, vector_grads, moved


def per_device(
    tokens,
    query_small,
    key_small,
    value_small,
    out_small,
    query_large,
    key_large,
    value_large,
    out_large,
    attend_gain,
    attend_router,
    gate_small,
    up_small,
    down_small,
    gate_large,
    up_large,
    down_large,
    feed_gain,
    feed_router,
    lengths,
    query_route,
    key_route,
    feed_route,
    cotangent,
):
    net = Net()
    rows, width = tokens.shape
    blocks = net.count
    part = width // blocks
    half = width // 2
    first = net.device * rows
    light = HL * HDL
    heavy = HH * HDH
    narrow = down_small.shape[0]
    wide = down_large.shape[0]
    slots = query_route.shape[1]
    members = 2 * net.depth
    share = wide // members
    pooled = members * slots
    keys = blocks * slots
    rest = slots - part
    packed = part % 8 == 0 and rest > 0 and rest % 8 == 0 and part % rest == 0 and keys <= 2048

    step = [(i, i + 1) for i in range(blocks - 1)]
    back = [(i + 1, i) for i in range(blocks - 1)]
    vector_pack = jnp.stack([attend_gain, attend_router, feed_gain, feed_router], axis=1)
    vector_pack = jnp.pad(vector_pack, ((0, 0), (0, 124)))
    first_pack = (query_small, key_small, value_small, vector_pack, out_large.T, out_small.T)
    moves, at = [], 0
    for i, piece in enumerate(first_pack):
        moves.append((i, (0, part), (0, piece.shape[1]), 0, at))
        at += piece.shape[1]
    (first_set,) = rearrange("pack_first", first_pack, [((part, at), moves)], room=56 << 20)
    first_parts = net.from_z(first_set)
    cut = 3 * light + vector_pack.shape[1]
    column = jnp.arange(width, dtype=jnp.int32)
    own_order = net.target(column // part) * part + column % part
    bits = column % half // (part * net.depth)
    bits = jnp.where(net.core == 1, bits, reverse_bits(bits, net.levels))
    member = (net.core ^ (column // half)) * net.depth + (net.z ^ (column // part % net.depth))
    slice_order = ((net.pair ^ bits) * members + member) * part + column % part
    orders = jnp.stack([own_order, slice_order])
    place = jnp.stack([first, lengths[0], lengths[1], jnp.int32(rows * blocks), net.device, net.core, net.z])
    square = ((width, width), BF16)
    chosen = ((slots, rows), BF16)

    if packed:
        tall = blocks * part
        spot = jnp.arange(keys, dtype=jnp.int32)
        spot_block = jnp.where(spot < tall, spot // part, (spot - tall) // rest)
        spot_slot = jnp.where(spot < tall, spot % part, part + (spot - tall) % rest)
        second_set, third_set, slices_keep, slices_send, key_docs = run(
            pack_body,
            "pack",
            [
                ((part, 4 * width + width * rest // part), BF16),
                ((part, 3 * narrow), BF16),
                ((net.depth * part, 3 * share), BF16),
                ((net.depth * part, 3 * share), BF16),
                ((1, keys), jnp.int32),
            ],
            (
                place, jnp.stack([net.target(spot_block), spot_slot]), tokens, key_route,
                query_large, key_large, value_large,
                gate_small, up_small, down_small.T, gate_large, up_large, down_large.T,
            ),
            smem=1,
            room=56 << 20,
        )
    else:
        second_set = jnp.concatenate([query_large, key_large, value_large], axis=1)
        third_set = jnp.concatenate([gate_small, up_small, down_small.T], axis=1)
        stacked = jnp.stack([gate_large, up_large, down_large.T], axis=0)
        stacked = stacked.reshape(3, part, members, share).transpose(2, 1, 0, 3)
        stacked = jnp.take(stacked.reshape(members, part, 3 * share), net.members(), axis=0)
        slices_keep, slices_send = stacked.reshape(2, net.depth * part, 3 * share)
    order = Order()
    top_bit = net.levels - 1

    def take_z(pieces):
        return order.note(stack_rows([order.hold(pieces[0])] + pieces[1:]))

    def take(whole, moved):
        return order.note(stack_rows([whole, order.hold(moved)]))

    def first_moved(whole):
        return net.by_bit(whole, 0)

    def rest_moved(whole, moved):
        for j in range(1, net.levels):
            whole = take(whole, moved)
            moved = net.by_bit(whole, j)
        return whole, moved

    order.note(second_set)
    first_set = take_z(first_parts)
    first_moving = first_moved(first_set)
    second_parts = net.from_z(after(second_set, first_set))
    slices_got = net.by_core(slices_send)
    to_own, to_slice = run(orders_body, "orders", [square, square], (order.hold(orders),))
    order.note(to_own)
    third_parts = pair_up(third_set, order.hold(slices_keep), slices_got, part)
    order.note(third_parts[0])
    first_set, first_moving = rest_moved(first_set, first_moving)
    second_set = take_z(second_parts)
    third_parts = net.exchange_z([after(p, second_set) for p in third_parts])
    cot, query_select, key_select, feed_select, query_docs = run(
        select_body,
        "select",
        [((rows, width), BF16), chosen, chosen, chosen, ((slots, 1), jnp.int32)],
        (place, to_own, query_route, key_route, feed_route, order.hold(cotangent)),
        smem=1,
    )
    order.note(cot)
    a0 = take(first_set, first_moving)
    a1 = net.by_core(a0)
    f0, f1 = (Columns(a, 0, cut) for a in (a0, a1))
    o0, o1 = (Columns(a, cut, a0.shape[1]) for a in (a0, a1))
    second_moving = first_moved(after(second_set, a0))
    second_set, second_moving = rest_moved(second_set, second_moving)
    third_set = order.note(stack_both([order.hold(third_parts[0])] + third_parts[1:], "weave"))
    third_moving = first_moved(third_set)
    near_tokens = after(tokens, third_set)
    above = lax.ppermute(near_tokens[rows - RADIUS :], AXES, step)
    below = lax.ppermute(near_tokens[:RADIUS], AXES, back)
    s0 = take(second_set, second_moving)
    s1 = net.by_core(s0)
    for j in range(1, net.levels):
        third_set = order.note(stack_both([third_set, order.hold(third_moving)]))
        third_moving = net.by_bit(third_set, j)
    (raw,) = run(
        prepare_body,
        "prepare",
        [((rows + 2 * RADIUS, width), BF16)],
        (order.hold(to_own), above, tokens, below),
    )
    order.note(raw)

    normed_ext, query_rows, pair_rows, vectors = run(
        light_rows_body,
        "light_rows",
        [
            ((rows + 2 * RADIUS, width), BF16),
            ((rows, light), BF16),
            ((rows + 2 * RADIUS, 2 * light), BF16),
            ((8, width), F32),
        ],
        (order.hold(raw), f0, f1),
    )
    order.note(query_rows)
    light_mixed, light_sums = run(
        light_forward_body,
        "light_forward",
        [((rows, light), BF16), ((rows, 128), F32)],
        (place, order.hold(query_rows), pair_rows),
        smem=1,
    )
    order.note(light_mixed)
    if packed:
        (keyed,) = run(
            functools.partial(heavy_rows_body, slots),
            "heavy_rows",
            [((keys, width), BF16)],
            (order.hold(vectors), to_own, s0, s1),
            scratch=[pltpu.VMEM((keys, width), BF16)],
        )
        order.note(keyed)
        heavy_pairs, routed, routed_query = run(
            heavy_pairs_body,
            "heavy_pairs",
            [((keys, 2 * heavy), BF16), ((slots, width), BF16), ((slots, heavy), BF16)],
            (order.hold(query_select), normed_ext, keyed, s0, s1),
        )
        order.note(routed_query)
        heavy_mixed, heavy_sums = run(
            heavy_forward_body,
            "heavy_forward",
            [((slots, heavy), BF16), ((2 * slots, 128), F32)],
            (query_docs, key_docs, order.hold(routed_query), heavy_pairs),
        )
    else:
        relative = net.target(jnp.arange(blocks, dtype=jnp.int32))
        near_routes = jnp.take(key_route, relative, axis=0)
        key_docs = document_of(relative[:, None] * rows + near_routes, lengths)
        key_docs = jnp.where(near_routes < rows, key_docs, -1).reshape(1, -1)
        keyed_raw = net.gather(nn(key_select, tokens).astype(BF16))
        keyed, heavy_pairs, routed, routed_query, heavy_mixed, heavy_sums = heavy_forward_wide(
            query_docs, key_docs, query_select, normed_ext, vectors, to_own,
            s0, s1, jnp.concatenate(keyed_raw, axis=0),
        )
    order.note(heavy_mixed)

    middle, normed_two, heavy_branch, feed_rows, feed_grads, sent = run(
        join_body,
        "join",
        [
            ((rows, width), F32),
            ((rows, width), BF16),
            ((slots, width), F32),
            ((slots, width), BF16),
            ((slots, width), F32),
            ((slots, 2 * width), BF16),
        ],
        (
            raw, light_mixed, order.hold(heavy_mixed), routed, query_select, feed_select, vectors, cot, to_own, o0, o1,
        ),
    )
    order.note(sent)

    got_parts = net.from_z(sent)
    got0 = take_z(got_parts)
    got1 = net.by_core(got0)
    t0, expert = part_both([third_set, order.hold(third_moving)], "part_both")
    order.note(t0)
    t1 = net.by_core(t0)
    keep, send, expert_keep, expert_send = run(
        expert_body,
        "expert",
        [
            ((pooled // 2, 2 * width), BF16),
            ((pooled // 2, 2 * width), BF16),
            ((half // 2, 6 * share), BF16),
            ((half // 2, 6 * share), BF16),
        ],
        (order.hold(got0), got1, to_slice, expert),
        scratch=[
            pltpu.VMEM((pooled, width), BF16),
            pltpu.VMEM((pooled, width), BF16),
            pltpu.VMEM((pooled, 2 * share), F32),
            pltpu.VMEM((pooled, share), F32),
            pltpu.VMEM((pooled, share), BF16),
            pltpu.VMEM((pooled, 2 * share), BF16),
        ],
    )
    order.note(send)
    moving = net.by_core(send)
    expert_moving = net.by_bit(expert_send, top_bit)
    feed_light, grad_normed, hidden, hidden_grads = run(
        feed_body,
        "feed",
        [
            ((rows, width), F32),
            ((rows, width), F32),
            ((rows, narrow), BF16),
            ((rows, 2 * narrow), BF16),
        ],
        (order.hold(normed_two), cot, t0, t1),
        scratch=[pltpu.VMEM((rows, 2 * narrow), F32), pltpu.VMEM((rows, narrow), F32)],
    )
    order.note(hidden)
    def give(keep, moved, pieces):
        out = fold(keep, order.hold(moved), pieces)
        order.note(out[0])
        return out

    def descend(keep, moved):
        for j in reversed(range(net.levels - 1)):
            keep, send = give(keep, moved, 2)
            moved = net.by_bit(send, j)
        return keep, moved

    summed = net.exchange_z(give(keep, moving, net.depth))
    third_keep, third_send = run(
        feed_weight_body,
        "feed_weight",
        [((half, 3 * narrow), BF16), ((half, 3 * narrow), BF16)],
        (order.hold(normed_two), cot, hidden, hidden_grads),
    )
    order.note(third_send)
    third_moving = net.by_core(third_send)

    third_keep, third_send = give(third_keep, third_moving, 2)
    third_moving = net.by_bit(third_send, top_bit)

    result, grad_middle, feed_vectors = run(
        turn_body,
        "turn",
        [((rows, width), BF16), ((rows, width), F32), ((8, width), F32)],
        (
            order.hold(summed[0]), *summed[1:], middle, feed_light, grad_normed, feed_rows, feed_grads, feed_select,
            vectors, cot, to_own,
        ),
    )
    order.note(grad_middle)
    if packed:
        grad_branch, grad_queries, grad_heavy_pairs, logits = run(
            heavy_scores_body,
            "heavy_scores",
            [
                ((slots, width), BF16),
                ((slots, heavy), BF16),
                ((keys, 2 * heavy), BF16),
                ((slots, 128), F32),
            ],
            (
                query_docs, key_docs, order.hold(grad_middle), query_select, routed, heavy_pairs, routed_query,
                heavy_branch, heavy_sums, vectors, o0, o1,
            ),
        )
        order.note(grad_branch)
    expert_keep, expert_moving = descend(expert_keep, expert_moving)
    if packed:
        second_keep, second_send, heavy_vectors = run(
            heavy_weights_body,
            "heavy_weights",
            [
                ((half, 5 * width + light + width * rest // part), BF16),
                ((half, 5 * width + light + width * rest // part), BF16),
                ((8, width), F32),
            ],
            (
                grad_middle, routed, keyed, light_mixed, heavy_mixed, order.hold(grad_branch), grad_queries,
                grad_heavy_pairs, logits, vectors, to_own, s0, s1,
            ),
            scratch=[pltpu.VMEM((keys, width), BF16)],
        )
    else:
        second_keep, second_send, grad_routed, heavy_vectors, keyed_grads = heavy_backward_wide(
            grad_middle, query_select, routed, keyed, heavy_pairs, routed_query, light_mixed, heavy_mixed,
            heavy_branch, heavy_sums, vectors, to_own, o0.array[:, cut:], o1.array[:, cut:], s0, s1,
        )
    order.note(second_send)
    second_moving = net.by_core(second_send)
    third_keep, third_moving = descend(third_keep, third_moving)
    expert_parts = net.exchange_z(give(expert_keep, expert_moving, net.depth))
    if packed:
        (grad_routed,) = run(
            routed_body,
            "routed",
            [((slots, width), F32)],
            (order.hold(grad_queries), logits, vectors, s0, s1),
        )
        order.note(grad_routed)
    second_keep, second_send = give(second_keep, second_moving, 2)
    second_moving = net.by_bit(second_send, top_bit)
    grad_queries, grad_pairs = run(
        light_scores_body,
        "light_scores",
        [((rows, light), BF16), ((rows + 2 * RADIUS, 2 * light), BF16)],
        (place, order.hold(grad_middle), query_rows, pair_rows, light_sums, o0, o1),
        smem=1,
        scratch=[pltpu.VMEM((rows + 2 * RADIUS, 2 * light), F32)],
    )
    order.note(grad_queries)
    third_parts = net.exchange_z(give(third_keep, third_moving, net.depth))
    first_keep, first_send, outer, grad_mine = run(
        light_weights_body,
        "light_weights",
        [
            ((half, 3 * light + 128), BF16),
            ((half, 3 * light + 128), BF16),
            ((2 * RADIUS, width), BF16),
            ((rows, width), F32),
        ],
        (
            raw, normed_ext, order.hold(grad_queries), grad_pairs, grad_routed, query_select, feed_vectors, heavy_vectors,
            to_own, f0, f1,
        ),
    )
    order.note(first_send)
    first_moving = net.by_core(first_send)
    from_next = lax.ppermute(outer[:RADIUS], AXES, back)
    from_prev = lax.ppermute(outer[RADIUS:], AXES, step)

    expert_keep, expert_send = take_apart([order.hold(expert_parts[0])] + expert_parts[1:], part)
    order.note(expert_send)
    expert_got = net.by_core(expert_send)
    third_grad = settle([order.hold(third_parts[0])] + third_parts[1:], [narrow] * 3, "settle_third")
    order.note(third_grad[0])
    second_keep, second_moving = descend(second_keep, second_moving)
    first_keep, first_send = give(first_keep, first_moving, 2)
    first_moving = net.by_bit(first_send, top_bit)
    (grad_near,) = run(
        halo_body, "halo", [((rows, width), F32)], (from_prev, from_next, order.hold(grad_mine), to_own)
    )
    order.note(grad_near)
    if packed:
        gate_grad, up_grad, down_grad = run(
            unpack_body,
            "unpack",
            [((part, wide), F32)] * 3,
            (place, order.hold(expert_keep), expert_got),
            smem=1,
        )
    else:
        expert_grad = jnp.concatenate([order.hold(expert_keep), expert_got], axis=0)
        expert_grad = jnp.take(expert_grad.reshape(members, part, 3 * share), net.members(), axis=0)
        expert_grad = expert_grad.reshape(members, part, 3, share).transpose(2, 1, 0, 3)
        gate_grad, up_grad, down_grad = expert_grad.reshape(3, part, wide).astype(F32)
    order.note(gate_grad)
    second_parts = net.exchange_z(give(second_keep, second_moving, net.depth))
    first_keep, first_moving = descend(first_keep, first_moving)
    first_parts = net.exchange_z(give(first_keep, first_moving, net.depth))
    widths = [width, light, heavy, heavy, heavy]
    if packed:
        widths.append(width + width * rest // part)
    second_grad = settle([order.hold(second_parts[0])] + second_parts[1:], widths, "settle_second")
    order.note(second_grad[0])
    if packed:
        keyed_own = second_grad[5]
    else:
        cut = keys // 2
        keyed_own = settle(net.reduce(keyed_grads[:cut], keyed_grads[cut:]), [width], "settle_keyed")[0]
    (tokens_grad,) = run(
        finish_body,
        "finish",
        [((rows, width), F32)],
        (order.hold(keyed_own), key_select, grad_near, grad_middle, raw, vectors, to_own),
    )
    order.note(tokens_grad)
    first_grad = settle(
        [order.hold(first_parts[0])] + first_parts[1:], [light, light, light, 128], "settle_first"
    )
    vector_out = first_grad[3][:, :4].T
    return (
        result,
        tokens_grad,
        first_grad[0],
        first_grad[1],
        first_grad[2],
        second_grad[1].T,
        second_grad[2],
        second_grad[3],
        second_grad[4],
        second_grad[0].T,
        vector_out[0],
        vector_out[1],
        third_grad[0],
        third_grad[1],
        third_grad[2].T,
        gate_grad,
        up_grad,
        down_grad.T,
        vector_out[2],
        vector_out[3],
    )


def solution(mesh):
    by_rows = P(AXES, None)
    by_columns = P(None, AXES)
    vector = P(AXES)
    return jax.shard_map(
        per_device,
        mesh=mesh,
        in_specs=(
            by_rows,
            by_rows,
            by_rows,
            by_rows,
            by_columns,
            by_rows,
            by_rows,
            by_rows,
            by_columns,
            vector,
            vector,
            by_rows,
            by_rows,
            by_columns,
            by_rows,
            by_rows,
            by_columns,
            vector,
            vector,
            P(),
            P(),
            P(),
            by_rows,
            by_rows,
        ),
        out_specs=(
            by_rows,
            by_rows,
            by_rows,
            by_rows,
            by_rows,
            by_columns,
            by_rows,
            by_rows,
            by_rows,
            by_columns,
            vector,
            vector,
            by_rows,
            by_rows,
            by_columns,
            by_rows,
            by_rows,
            by_columns,
            vector,
            vector,
        ),
        check_vma=False,
    )
```

```python
import functools
import math

import jax
import jax.numpy as jnp
from jax import lax
from jax.experimental import pallas as pl
from jax.experimental.pallas import tpu as pltpu
from jax.sharding import PartitionSpec as P

HL = 8
HDL = 64
HH = 12
HDH = 64
RADIUS = 128

NEG = -1e30
EPS = 1e-06
HIGH = lax.Precision.HIGHEST
AXES = ("seq", "fsdp")
F32 = jnp.float32
BF16 = jnp.bfloat16
ROOM = 12 << 20
LENGTHS = {
    "select": 60,
    "weave": 20,
    "light_forward": 60,
    "heavy_pairs": 60,
    "expert": 60,
    "feed": 60,
    "feed_weight": 20,
    "turn": 5.6,
    "routed": 60,
    "settle_third": 12,
}


def declared(name):
    flops = int(LENGTHS.get(name, 0.05) * 1e9)
    return pl.CostEstimate(flops=flops, bytes_accessed=10**10, transcendentals=0)


class Columns:
    def __init__(self, array, start, stop):
        self.array, self.start, self.stop = array, start, stop


def dot(left, right, dims):
    return lax.dot_general(left, right, (dims, ((), ())), preferred_element_type=F32)


def nn(left, right):
    return dot(left, right, ((1,), (0,)))


def nt(left, right):
    return dot(left, right, ((1,), (1,)))


def tn(left, right):
    return dot(left, right, ((0,), (0,)))


def reverse_bits(value, count):
    out = value * 0
    for j in range(count):
        out = out | (((value >> j) & 1) << (count - 1 - j))
    return out


class Net:
    def __init__(self):
        self.seq = lax.axis_size("seq")
        self.depth = lax.axis_size("fsdp")
        self.levels = (self.seq // 2).bit_length() - 1
        self.count = self.seq * self.depth
        s = lax.axis_index("seq")
        self.core, self.pair = s & 1, s >> 1
        self.z = lax.axis_index("fsdp")
        self.device = s * self.depth + self.z

    def pairs(self, move):
        out = []
        for s in range(self.seq):
            for z in range(self.depth):
                pair, core, to_z = move(s >> 1, s & 1, z)
                out.append((s * self.depth + z, (pair * 2 + core) * self.depth + to_z))
        return out

    def by_core(self, array):
        return lax.ppermute(array, AXES, self.pairs(lambda p, c, z: (p, 1 - c, z)))

    def by_bit(self, array, j):
        top = self.levels - 1 - j
        return lax.ppermute(
            array, AXES, self.pairs(lambda p, c, z: (p ^ (1 << (j if c else top)), c, z))
        )

    def by_z(self, array, k):
        return lax.ppermute(array, AXES, self.pairs(lambda p, c, z: (p, c, z ^ k)))

    def target(self, relative):
        zr = relative % self.depth
        bits = (relative // self.depth) % (self.seq // 2)
        core = self.core ^ (relative // (self.count // 2))
        pair = self.pair ^ jnp.where(core == 1, bits, reverse_bits(bits, self.levels))
        return (pair * 2 + core) * self.depth + (self.z ^ zr)

    def from_z(self, shard):
        return [shard] + [self.by_z(shard, k) for k in range(1, self.depth)]

    def exchange_z(self, pieces):
        return [pieces[0]] + [self.by_z(pieces[k], k) for k in range(1, self.depth)]

    def gather(self, shard):
        shard = jnp.concatenate(self.from_z(shard), axis=0)
        for j in range(self.levels):
            shard = jnp.concatenate([shard, self.by_bit(shard, j)], axis=0)
        return shard, self.by_core(shard)

    def reduce(self, keep, send):
        keep, send = fold(keep, self.by_core(send), 2)
        for j in reversed(range(self.levels)):
            pieces = 2 if j else self.depth
            out = fold(keep, self.by_bit(send, j), pieces)
            keep, send = out[0], out[1]
        return self.exchange_z(out)

    def members(self):
        relative = jnp.arange(2 * self.depth, dtype=jnp.int32)
        core = self.core ^ (relative // self.depth)
        return core * self.depth + (self.z ^ (relative % self.depth))


def by_columns(width, step):
    chunk = 256 if width % 256 == 0 else 128
    if width % chunk or width <= 4 * chunk:
        step(slice(0, width))
        return

    def at(i, carry):
        step(pl.ds(pl.multiple_of(i * chunk, chunk), chunk))
        return carry

    lax.fori_loop(0, width // chunk, at, 0)


class Order:
    def __init__(self):
        self.last = ()

    def hold(self, array):
        return after(array, *self.last)

    def note(self, array):
        self.last = (array,)
        return array


def stack_rows(arrays):
    height = sum(a.shape[0] for a in arrays)
    if any(a.shape[0] % 8 for a in arrays):
        return jnp.concatenate(arrays, axis=0)

    def body(*refs):
        def copy(columns):
            at = 0
            for ref in refs[:-1]:
                refs[-1][at : at + ref.shape[0], columns] = ref[:, columns]
                at += ref.shape[0]

        by_columns(arrays[0].shape[1], copy)

    return run(body, "stack", [((height, arrays[0].shape[1]), arrays[0].dtype)], arrays)[0]


def after(array, *earlier):
    return lax.optimization_barrier((array, *earlier))[0]


def unit_rms(values):
    scale = lax.rsqrt(jnp.mean(values * values, -1, keepdims=True) + EPS)
    return values * scale, scale


def norm_back(grad, gain, unit, scale):
    scaled = grad * gain
    return scale * (scaled - unit * jnp.mean(scaled * unit, -1, keepdims=True))


def document_of(places, lengths):
    return (places >= lengths[0]).astype(jnp.int32)


def sigmoid(values):
    return 1.0 / (1.0 + jnp.exp(-values))


def soft(scores):
    top = jnp.max(scores, -1, keepdims=True)
    expo = jnp.exp(scores - top)
    return expo / jnp.sum(expo, -1, keepdims=True)


def two_parts(values):
    high = values.astype(BF16)
    return high, (values - high.astype(F32)).astype(BF16)


def place_rows(select, values):
    high, low = two_parts(values)
    return tn(select, high) + tn(select, low)


def take_rows(select, values):
    high, low = two_parts(values)
    return nn(select, high) + nn(select, low)


def reorder(values, order):
    high, low = two_parts(values)
    return nn(high, order) + nn(low, order)


def reorder_back(values, order):
    high, low = two_parts(values)
    return nt(high, order) + nt(low, order)


def into(values, first, second):
    half = first.shape[0]
    return nn(values[:, :half], first) + nn(values[:, half:], second)


def onto(values, first, second):
    return jnp.concatenate([nt(values, first), nt(values, second)], axis=1)


def lanes(rows, width=128):
    return lax.broadcasted_iota(jnp.int32, (rows, width), 1)


def both_heads(pair):
    first = lanes(pair.shape[0]) < HDL
    zero = jnp.zeros_like(pair)
    return jnp.concatenate([jnp.where(first, pair, zero), jnp.where(first, zero, pair)], axis=0)


def pair_at(p, start=0):
    return pl.ds(pl.multiple_of(start + p * 128, 128), 128)


def column_at(array, index):
    return jnp.sum(jnp.where(lanes(*array.shape) == index, array, 0.0), -1, keepdims=True)


def one_pair(stacked):
    rows = stacked.shape[0] // 2
    return jnp.where(lanes(rows) < HDL, stacked[:rows], stacked[rows:])


def run(body, name, outs, args, smem=0, scratch=(), room=ROOM):
    vmem = pl.BlockSpec(memory_space=pltpu.VMEM)
    held = sum(math.prod(piece.shape) * jnp.dtype(piece.dtype).itemsize for piece in scratch)
    cuts = {i: a for i, a in enumerate(args) if isinstance(a, Columns)}

    def kernel(*refs):
        refs = list(refs)
        for i, cut in cuts.items():
            refs[i] = refs[i].at[:, cut.start : cut.stop]
        body(*refs)

    return pl.pallas_call(
        kernel,
        name=name,
        compiler_params=pltpu.CompilerParams(vmem_limit_bytes=held + room),
        out_shape=[jax.ShapeDtypeStruct(shape, kind) for shape, kind in outs],
        in_specs=[pl.BlockSpec(memory_space=pltpu.SMEM)] * smem + [vmem] * (len(args) - smem),
        out_specs=[vmem] * len(outs),
        scratch_shapes=list(scratch),
        cost_estimate=declared(name),
    )(*[a.array if isinstance(a, Columns) else a for a in args])


def rearrange(name, sources, outs, room=ROOM):
    bounds = [b for unused, moves in outs for m in moves for b in (*m[1], m[3])]
    if any(b % 8 for b in bounds):
        made = []
        for shape, moves in outs:
            out = jnp.zeros(shape, BF16)
            for i, (r0, r1), (c0, c1), row, column in moves:
                out = lax.dynamic_update_slice(out, sources[i][r0:r1, c0:c1], (row, column))
            made.append(out)
        return made

    spans = {(c0, c1, column) for unused, moves in outs for i, rows, (c0, c1), row, column in moves}

    def body(*refs):
        def copy(columns=None):
            for out, (unused, moves) in zip(refs[len(sources) :], outs):
                for i, (r0, r1), (c0, c1), row, column in moves:
                    to = columns or slice(column, column + c1 - c0)
                    out[row : row + r1 - r0, to] = refs[i][r0:r1, columns or slice(c0, c1)]

        if len(spans) == 1 and all(c0 == column for c0, c1, column in spans):
            by_columns(max(c1 for c0, c1, column in spans), copy)
        else:
            copy()

    return run(body, name, [(shape, BF16) for shape, unused in outs], sources, room=room)


def fold(keep, moved, pieces, kind=BF16):
    height, width = keep.shape
    piece = height // pieces
    parts = 2 if piece % 32 == 0 else 1
    step = piece // parts

    def body(*refs):
        def add(columns):
            for k in range(pieces):
                total = refs[k][:, columns].astype(F32) + refs[pieces + k][:, columns].astype(F32)
                refs[2 * pieces + k][:, columns] = total.astype(kind)

        by_columns(width, add)

    def spec(k):
        return pl.BlockSpec((step, width), lambda i, k=k: (k * parts + i, 0))

    if piece % 8:
        total = keep.astype(F32) + moved.astype(F32)
        return [total[k * piece : (k + 1) * piece].astype(kind) for k in range(pieces)]
    return pl.pallas_call(
        body,
        name="fold",
        compiler_params=pltpu.CompilerParams(vmem_limit_bytes=ROOM),
        grid=(parts,),
        out_shape=[jax.ShapeDtypeStruct((piece, width), kind)] * pieces,
        in_specs=[spec(k) for k in range(pieces)] * 2,
        out_specs=[spec(0)] * pieces,
        cost_estimate=declared("fold"),
    )(*([keep] * pieces + [moved] * pieces))


def settle(pieces, widths, name, rows=None):
    rows = rows or pieces[0].shape[0]

    def body(*refs):
        parts, outs = refs[: len(pieces)], refs[len(pieces) :]
        at = 0
        for out, width in zip(outs, widths):
            total = parts[0][:rows, at : at + width].astype(F32)
            for part in parts[1:]:
                total = total + part[:rows, at : at + width].astype(F32)
            out[...] = total
            at += width

    return run(body, name, [((rows, width), F32) for width in widths], pieces)


def hot(column, rows):
    return jnp.where(column == lanes(column.shape[0], rows), 1.0, 0.0).astype(BF16)


def as_column(row):
    count = row.shape[1]
    eye = lax.broadcasted_iota(jnp.int32, (count, count), 0) == lanes(count, count)
    spread = jnp.where(eye, row.astype(F32), 0.0)
    return jnp.sum(spread, -1, keepdims=True).astype(jnp.int32)


def order_matrix(order):
    width = order.shape[1]
    rows = lax.broadcasted_iota(jnp.int32, (width, width), 0)
    return jnp.where(rows == order, 1.0, 0.0).astype(BF16)


def orders_body(orders, to_own, to_slice):
    to_own[...] = order_matrix(orders[0:1])
    to_slice[...] = order_matrix(orders[1:2])


def select_body(
    place, to_own, query_route, key_route, feed_route, cotangent, cot, query_select, key_select, feed_select, query_doc
):
    rows = cotangent.shape[0]
    cot[...] = nn(cotangent[...], to_own[...]).astype(BF16)
    queries = as_column(query_route[pl.ds(place[4], 1)])
    query_select[...] = hot(queries, rows)
    key_select[...] = hot(as_column(key_route[pl.ds(place[4], 1)]), rows)
    feed_select[...] = hot(as_column(feed_route[...]), rows)
    query_doc[...] = jnp.where(place[0] + queries >= place[1], 1, 0)


def pack_body(
    place, key_spots, tokens, key_route, q_l, k_l, v_l,
    gate_s, up_s, down_s, gate_l, up_l, down_l, second, third, expert_keep, expert_send, key_docs
):
    part, width = q_l.shape
    at = 0
    for ref in (q_l, k_l, v_l):
        second[:, at : at + ref.shape[1]] = ref[...]
        at += ref.shape[1]
    keyed = nn(hot(as_column(key_route[pl.ds(place[4], 1)]), tokens.shape[0]), tokens[...])
    second[:, at : at + width] = keyed[:part].astype(BF16)
    rest = keyed[part:]
    chunk = width * rest.shape[0] // part
    pieces = [rest[:, i * chunk : (i + 1) * chunk] for i in range(width // chunk)]
    second[:, at + width :] = jnp.concatenate(pieces, axis=0).astype(BF16)
    narrow = gate_s.shape[1]
    for i, ref in enumerate((gate_s, up_s, down_s)):
        third[:, i * narrow : (i + 1) * narrow] = ref[...]
    share = expert_keep.shape[1] // 3
    depth = expert_keep.shape[0] // part
    for c, expert in enumerate((expert_keep, expert_send)):
        for k in range(depth):
            at = ((place[5] ^ c) * depth + (place[6] ^ k)) * share
            at = pl.ds(pl.multiple_of(at, share), share)
            for i, ref in enumerate((gate_l, up_l, down_l)):
                expert[k * part : (k + 1) * part, i * share : (i + 1) * share] = ref[:, at]
    blocks, slots = key_route.shape
    keys = key_spots.shape[1]
    block = lax.broadcasted_iota(jnp.int32, (blocks, keys), 0) == key_spots[0:1]
    table = key_route[...].astype(F32).T.astype(BF16)
    found = nn(table, jnp.where(block, 1.0, 0.0).astype(BF16))
    slot = lax.broadcasted_iota(jnp.int32, (slots, keys), 0) == key_spots[1:2]
    position = jnp.sum(jnp.where(slot, found, 0.0), 0, keepdims=True).astype(jnp.int32)
    rows = tokens.shape[0]
    document = jnp.where(key_spots[0:1] * rows + position >= place[1], 1, 0)
    key_docs[...] = jnp.where(position < rows, document, -1)


def prepare_body(to_own, above, tokens, below, raw):
    order = to_own[...]
    at = 0
    for ref in (above, tokens, below):
        raw[at : at + ref.shape[0]] = nn(ref[...], order).astype(BF16)
        at += ref.shape[0]


def unpack_body(place, keep, got, gate, up, down):
    part = gate.shape[0]
    depth = keep.shape[0] // part
    share = keep.shape[1] // 3
    for c, source in enumerate((keep, got)):
        for k in range(depth):
            at = ((place[5] ^ c) * depth + (place[6] ^ k)) * share
            at = pl.ds(pl.multiple_of(at, share), share)
            for i, out in enumerate((gate, up, down)):
                piece = source[k * part : (k + 1) * part, i * share : (i + 1) * share]
                out[:, at] = piece.astype(F32)


def pair_up(shard, first, second, part):
    count = first.shape[0] // part
    width = first.shape[1]
    whole, own = (0, part), (0, width)
    outs = []
    for k in range(count):
        at = (k * part, (k + 1) * part)
        moves = [(0, whole, (0, 2 * width), 0, 0), (1, at, own, part, 0), (2, at, own, part, width)]
        outs.append(((2 * part, 2 * width), moves))
    return rearrange("pair_up", (shard, first, second), outs)


def stack_both(pieces, name="stack_both"):
    height = sum(p.shape[0] for p in pieces)
    width = pieces[0].shape[1]
    moves, row = [], 0
    for i, piece in enumerate(pieces):
        n = piece.shape[0] // 2
        moves.append((i, (0, n), (0, width), row, 0))
        moves.append((i, (n, 2 * n), (0, width), height // 2 + row, 0))
        row += n
    return rearrange(name, pieces, [((height, width), moves)])[0]


def part_both(pieces, name):
    height = sum(p.shape[0] for p in pieces) // 2
    width = pieces[0].shape[1]
    first, second, row = [], [], 0
    for i, piece in enumerate(pieces):
        n = piece.shape[0] // 2
        first.append((i, (0, n), (0, width), row, 0))
        second.append((i, (n, 2 * n), (0, width), row, 0))
        row += n
    return rearrange(name, pieces, [((height, width), first), ((height, width), second)])


def take_apart(pieces, part):
    width = pieces[0].shape[1] // 2
    outs = []
    for side in range(2):
        columns = (side * width, (side + 1) * width)
        moves = [(k, (0, part), columns, k * part, 0) for k in range(len(pieces))]
        outs.append(((len(pieces) * part, width), moves))
    return rearrange("take_apart", pieces, outs)


def local_mask(place, tile, reach, stacked, span):
    shape = (stacked, span)
    row = lax.broadcasted_iota(jnp.int32, shape, 0) & (reach - 1)
    query = place[0] + tile * reach + row
    key = place[0] + (tile - 1) * reach + lax.broadcasted_iota(jnp.int32, shape, 1)
    split, live, total = place[1], place[1] + place[2], place[3]
    inside = (key >= 0) & (key < total)
    same = jnp.where(query >= split, 1, 0) == jnp.where(key >= split, 1, 0)
    near = jnp.abs(query - key) <= reach
    both = ((query < live) & (key < live)) | (query == key)
    return near & inside & same & both


def light_rows_body(raw, w0, w1, normed, queries, pairs, vectors):
    light = HL * HDL
    reach = RADIUS
    rows = queries.shape[0]
    columns = [w[:, 3 * light :].astype(F32).T[:8] for w in (w0, w1)]
    vectors[...] = jnp.concatenate(columns, axis=1)
    unit, unused = unit_rms(raw[...].astype(F32))
    normed[...] = (unit * vectors[0:1]).astype(BF16)
    own = normed[reach : reach + rows]
    queries[...] = into(own, w0[:, :light], w1[:, :light]).astype(BF16)
    pairs[...] = into(normed[...], w0[:, light : 3 * light], w1[:, light : 3 * light]).astype(BF16)


def light_forward_body(place, queries, pairs, mixed, sums):
    light = HL * HDL
    reach = RADIUS
    rows = queries.shape[0]
    scale = 1.0 / math.sqrt(HDL)
    lane = lanes(reach)
    for tile in range(rows // reach):
        mine = slice(tile * reach, (tile + 1) * reach)
        seen = slice(tile * reach, (tile + 3) * reach)
        mask = local_mask(place, tile, reach, 2 * reach, 3 * reach)

        def pair(p, logs):
            query = both_heads(queries[mine, pair_at(p)])
            scores = jnp.where(mask, nt(query, pairs[seen, pair_at(p)]) * scale, NEG)
            top = jnp.max(scores, -1, keepdims=True)
            expo = jnp.exp(scores - top)
            total = jnp.sum(expo, -1, keepdims=True)
            probs = (expo * (1.0 / total)).astype(BF16)
            mixed[mine, pair_at(p)] = one_pair(nn(probs, pairs[seen, pair_at(p, light)])).astype(BF16)
            log = top + jnp.log(total)
            logs = jnp.where(lane == 2 * p, log[:reach], logs)
            return jnp.where(lane == 2 * p + 1, log[reach:], logs)

        logs = lax.fori_loop(0, HL // 2, pair, jnp.zeros((reach, 128), F32))
        sums[mine] = logs


def piece_select(block_rows, rest, part, piece):
    shape = (block_rows // part * rest, block_rows)
    k = lax.broadcasted_iota(jnp.int32, shape, 0)
    row = lax.broadcasted_iota(jnp.int32, shape, 1)
    shift = rest.bit_length() - 1
    want = (k >> shift) * part + piece * rest + (k & (rest - 1))
    return jnp.where(row == want, 1.0, 0.0).astype(BF16)


def heavy_rows_body(slots, vectors, to_own, s0, s1, keyed, held):
    width = to_own.shape[0]
    half = s0.shape[0]
    at = 3 * HH * HDH
    part = half // (keyed.shape[0] // slots // 2)
    rest = slots - part
    chunk = width * rest // part
    for i, ref in enumerate((s0, s1)):
        held[i * half : (i + 1) * half] = ref[:, at : at + width]
        low = 2 * half + i * (half // part * rest)
        for piece in range(part // rest):
            picked = nn(piece_select(half, rest, part, piece), ref[:, at + width :])
            held[low : low + half // part * rest, piece * chunk : (piece + 1) * chunk] = picked.astype(BF16)
    step = 256

    def project(t, carry):
        rows = pl.ds(pl.multiple_of(t * step, step), step)
        unit, unused = unit_rms(nn(held[rows], to_own[...]))
        keyed[rows] = (unit * vectors[0:1]).astype(BF16)
        return carry

    lax.fori_loop(0, keyed.shape[0] // step, project, 0)


def heavy_pairs_body(select, normed, keyed, s0, s1, pairs, routed, queries):
    heavy = HH * HDH
    q_at = slice(0, heavy)
    kv_at = slice(heavy, 3 * heavy)
    step = 256

    def project(t, carry):
        rows = pl.ds(pl.multiple_of(t * step, step), step)
        pairs[rows] = into(keyed[rows], s0[:, kv_at], s1[:, kv_at]).astype(BF16)
        return carry

    lax.fori_loop(0, keyed.shape[0] // step, project, 0)
    own = normed[RADIUS : normed.shape[0] - RADIUS]
    routed[...] = nn(select[...], own).astype(BF16)
    queries[...] = into(routed[...], s0[:, q_at], s1[:, q_at]).astype(BF16)


def heavy_forward_body(query_doc, key_doc, queries, pairs, mixed, sums):
    heavy = HH * HDH
    slots = queries.shape[0]
    scale = 1.0 / math.sqrt(HDH)
    mask = jnp.concatenate([query_doc[...], query_doc[...]], axis=0) == key_doc[...]

    def pair(p, logs):
        scores = jnp.where(mask, nt(both_heads(queries[:, pair_at(p)]), pairs[:, pair_at(p)]) * scale, NEG)
        top = jnp.max(scores, -1, keepdims=True)
        expo = jnp.exp(scores - top)
        total = jnp.sum(expo, -1, keepdims=True)
        probs = (expo * (1.0 / total)).astype(BF16)
        mixed[:, pair_at(p)] = one_pair(nn(probs, pairs[:, pair_at(p, heavy)])).astype(BF16)
        return jnp.where(lanes(2 * slots) == p, top + jnp.log(total), logs)

    logs = lax.fori_loop(0, HH // 2, pair, jnp.zeros((2 * slots, 128), F32))
    sums[...] = logs


def join_body(
    raw, light_mixed, heavy_mixed, routed, query_select, feed_select, vectors, cot, to_own, s0, s1,
    middle, normed, heavy_branch, feed_rows, feed_grads, sent
):
    heavy = HH * HDH
    width = raw.shape[1]
    rows = middle.shape[0]
    at = slice(heavy, heavy + HL * HDL)
    light_branch = onto(light_mixed[...], s0[:, at], s1[:, at])
    at = slice(0, heavy)
    heavy_branch[...] = onto(heavy_mixed[...], s0[:, at], s1[:, at])
    score = sigmoid(jnp.sum(routed[...].astype(F32) * vectors[1:2], -1, keepdims=True))
    inputs = raw[RADIUS : RADIUS + rows].astype(F32)
    middle[...] = inputs + light_branch + place_rows(query_select[...], score * heavy_branch[...])
    unit, unused = unit_rms(middle[...])
    normed[...] = (unit * vectors[2:3]).astype(BF16)
    feed_rows[...] = nn(feed_select[...], normed[...]).astype(BF16)
    feed_grads[...] = nn(feed_select[...], cot[...])
    score = sigmoid(jnp.sum(feed_rows[...].astype(F32) * vectors[3:4], -1, keepdims=True))
    sent[:, :width] = nt(feed_rows[...], to_own[...]).astype(BF16)
    sent[:, width:] = nt((score * feed_grads[...]).astype(BF16), to_own[...]).astype(BF16)


def geglu_rows(gate, upper, grad_hidden):
    c0, c1 = 0.7978845608028654, 0.044715
    square = gate * gate
    bent = jnp.tanh(c0 * gate * (1.0 + c1 * square))
    bell = 0.5 * (1.0 + bent)
    gelu = gate * bell
    slope = bell + 0.5 * gate * (1.0 - bent * bent) * (c0 * (1.0 + 3.0 * c1 * square))
    return gelu * upper, grad_hidden * upper * slope, grad_hidden * gelu


def geglu_loop(wide, grad_hidden, hidden, grads):
    count = hidden.shape[1]
    step = 32

    def rows_at(t, carry):
        rows = pl.ds(pl.multiple_of(t * step, step), step)
        out, grad_gate, grad_upper = geglu_rows(
            wide[rows, :count], wide[rows, count:], grad_hidden[rows]
        )
        hidden[rows] = out.astype(BF16)
        grads[rows, :count] = grad_gate.astype(BF16)
        grads[rows, count:] = grad_upper.astype(BF16)
        return carry

    lax.fori_loop(0, hidden.shape[0] // step, rows_at, 0)


def feed_body(normed, cot, t0, t1, feed, grad_normed, hidden, grads, wide, grad_hidden):
    narrow = hidden.shape[1]
    wide[...] = into(normed[...], t0[:, : 2 * narrow], t1[:, : 2 * narrow])
    grad_hidden[...] = into(cot[...], t0[:, 2 * narrow :], t1[:, 2 * narrow :])
    geglu_loop(wide, grad_hidden, hidden, grads)
    feed[...] = onto(hidden[...], t0[:, 2 * narrow :], t1[:, 2 * narrow :])
    grad_normed[...] = onto(grads[...], t0[:, : 2 * narrow], t1[:, : 2 * narrow])


def feed_weight_body(normed, cot, hidden, grads, keep, send):
    narrow = hidden.shape[1]
    half = keep.shape[0]
    for out, at in ((send, slice(half, None)), (keep, slice(0, half))):
        out[:, : 2 * narrow] = tn(normed[:, at], grads[...]).astype(out.dtype)
        out[:, 2 * narrow :] = tn(cot[:, at], hidden[...]).astype(out.dtype)


def expert_body(got0, got1, to_slice, weights, keep, send, grad_keep, grad_send, rows, row_grads, wide, grad_hidden, hidden, grads):
    width = to_slice.shape[0]
    share = hidden.shape[1]
    count = got0.shape[0]
    for i, got in enumerate((got0, got1)):
        at = slice(i * count, (i + 1) * count)
        rows[at] = nn(got[:, :width], to_slice[...]).astype(BF16)
        row_grads[at] = nn(got[:, width:], to_slice[...]).astype(BF16)
    first, second = weights[:, : 2 * share], weights[:, 3 * share : 5 * share]
    first_down, second_down = weights[:, 2 * share : 3 * share], weights[:, 5 * share :]
    wide[...] = into(rows[...], first, second)
    grad_hidden[...] = into(row_grads[...], first_down, second_down)
    geglu_loop(wide, grad_hidden, hidden, grads)
    for out, at in ((send, slice(count, None)), (keep, slice(0, count))):
        feed = onto(hidden[at], first_down, second_down).astype(BF16)
        back = onto(grads[at], first, second).astype(BF16)
        out[:, :width] = nt(feed, to_slice[...]).astype(out.dtype)
        out[:, width:] = nt(back, to_slice[...]).astype(out.dtype)
    half = weights.shape[0]
    low = grad_keep.shape[0]
    for i in range(2):
        at = slice(i * half, (i + 1) * half)
        to = 3 * share * i
        for left, right, columns in (
            (rows, grads, slice(to, to + 2 * share)), (row_grads, hidden, slice(to + 2 * share, to + 3 * share))
        ):
            product = tn(left[:, at], right[...]).astype(BF16)
            grad_keep[:, columns] = product[:low]
            grad_send[:, columns] = product[low:]


def turn_body(*refs):
    pieces = refs[:-12]
    (
        middle, feed, grad_normed, feed_rows, feed_grads, feed_select, vectors, cot, to_own,
        result, grad_middle, vector_grads,
    ) = refs[-12:]
    width = middle.shape[1]
    summed = pieces[0][...].astype(F32)
    for piece in pieces[1:]:
        summed = summed + piece[...].astype(F32)
    feed_heavy = reorder(summed[:, :width], to_own[...])
    grad_rows = reorder(summed[:, width:], to_own[...])
    rows = feed_rows[...].astype(F32)
    score = sigmoid(jnp.sum(rows * vectors[3:4], -1, keepdims=True))
    logit = jnp.sum(feed_grads[...] * feed_heavy, -1, keepdims=True) * score * (1.0 - score)
    grad_rows = grad_rows + logit * vectors[3:4]
    grads = grad_normed[...] + place_rows(feed_select[...], grad_rows)
    unit, scale = unit_rms(middle[...])
    grad_middle[...] = cot[...].astype(F32) + norm_back(grads, vectors[2:3], unit, scale)
    vector_grads[...] = jnp.concatenate(
        [
            jnp.zeros((2, width), F32),
            jnp.sum(grads * unit, 0, keepdims=True),
            jnp.sum(rows * logit, 0, keepdims=True),
            jnp.zeros((4, width), F32),
        ],
        axis=0,
    )
    out = middle[...] + feed[...] + place_rows(feed_select[...], score * feed_heavy)
    result[...] = nt(out.astype(BF16), to_own[...]).astype(BF16)


def heavy_scores_body(
    query_doc, key_doc, grad_middle, query_select, routed, pairs, queries, heavy_branch, sums, vectors, s0, s1,
    grad_branch, grad_queries, grad_pairs, logits, held
):
    heavy = HH * HDH
    score = sigmoid(jnp.sum(routed[...].astype(F32) * vectors[1:2], -1, keepdims=True))
    grad_rows = take_rows(query_select[...], grad_middle[...])
    grad_branch[...] = (score * grad_rows).astype(BF16)
    logit = jnp.sum(grad_rows * heavy_branch[...], -1, keepdims=True) * score * (1.0 - score)
    logits[...] = jnp.broadcast_to(logit, logits.shape)
    at = slice(0, heavy)
    grad_mixed = into(grad_branch[...], s0[:, at], s1[:, at]).astype(BF16)
    scale = 1.0 / math.sqrt(HDH)
    mask = jnp.concatenate([query_doc[...], query_doc[...]], axis=0) == key_doc[...]
    held[...] = grad_mixed
    logs = sums[...]

    def pair(p, carry):
        query = both_heads(queries[:, pair_at(p)])
        grad_out = both_heads(held[:, pair_at(p)])
        key = pairs[:, pair_at(p)]
        scores = jnp.where(mask, nt(query, key) * scale, NEG)
        probs = jnp.exp(scores - column_at(logs, p))
        grad_probs = nt(grad_out, pairs[:, pair_at(p, heavy)])
        delta = jnp.sum(probs * grad_probs, -1, keepdims=True)
        grad_scores = (probs * (grad_probs - delta)).astype(BF16)
        grad_queries[:, pair_at(p)] = one_pair(nn(grad_scores, key) * scale).astype(BF16)
        grad_pairs[:, pair_at(p)] = (tn(grad_scores, query) * scale).astype(BF16)
        grad_pairs[:, pair_at(p, heavy)] = tn(probs.astype(BF16), grad_out).astype(BF16)
        return carry

    lax.fori_loop(0, HH // 2, pair, 0)


def heavy_weights_body(
    grad_middle, routed, keyed, light_mixed, heavy_mixed, grad_branch, grad_queries, grad_pairs, logits, vectors, to_own, s0, s1,
    keep, send, vector_grads, moved
):
    width = grad_middle.shape[1]
    heavy = HH * HDH
    light = HL * HDL
    half = s0.shape[0]
    slots = routed.shape[0]
    q_at = slice(width + light, width + light + heavy)
    kv_at = slice(width + light + heavy, width + light + 3 * heavy)
    logit = logits[:, 0:1]
    step = 256

    def back(t, gain):
        rows = pl.ds(pl.multiple_of(t * step, step), step)
        grads = onto(grad_pairs[rows], s0[:, heavy : 3 * heavy], s1[:, heavy : 3 * heavy])
        moved[rows] = nt(grads.astype(BF16), to_own[...]).astype(BF16)
        return gain + jnp.sum(grads * keyed[rows].astype(F32), 0, keepdims=True)

    gain = lax.fori_loop(0, keyed.shape[0] // step, back, jnp.zeros((1, width), F32))
    vector_grads[...] = jnp.concatenate(
        [
            gain / vectors[0:1],
            jnp.sum(routed[...].astype(F32) * logit, 0, keepdims=True),
            jnp.zeros((6, width), F32),
        ],
        axis=0,
    )
    low = grad_middle[...].astype(BF16)
    part = half // (keyed.shape[0] // slots // 2)
    rest = slots - part
    chunk = width * rest // part
    for i, out in ((1, send), (0, keep)):
        at = slice(i * half, (i + 1) * half)
        out[:, :width] = tn(grad_branch[:, at], heavy_mixed[...]).astype(BF16)
        out[:, width : width + light] = tn(low[:, at], light_mixed[...]).astype(BF16)
        out[:, q_at] = tn(routed[:, at], grad_queries[...]).astype(BF16)
        out[:, kv_at] = tn(keyed[:, at], grad_pairs[...]).astype(BF16)
        to = width + light + 3 * heavy
        out[:, to : to + width] = moved[at]
        at = 2 * half + i * (half // part * rest)
        total = 0.0
        for piece in range(part // rest):
            block = moved[at : at + half // part * rest, piece * chunk : (piece + 1) * chunk]
            total = total + tn(piece_select(half, rest, part, piece), block)
        out[:, to + width :] = total.astype(BF16)


def routed_body(grad_queries, logits, vectors, s0, s1, grad_routed):
    at = slice(0, HH * HDH)
    grad_routed[...] = onto(grad_queries[...], s0[:, at], s1[:, at]) + logits[:, 0:1] * vectors[1:2]


def light_scores_body(place, grad_middle, queries, pairs, sums, s0, s1, grad_queries, grad_pairs, held, grad_out_all):
    light = HL * HDL
    heavy = HH * HDH
    reach = RADIUS
    rows = queries.shape[0]
    at = slice(heavy, heavy + light)
    grad_out_all[...] = into(grad_middle[...].astype(BF16), s0[:, at], s1[:, at]).astype(BF16)
    held[...] = jnp.zeros_like(held)
    scale = 1.0 / math.sqrt(HDL)
    for tile in range(rows // reach):
        mine = slice(tile * reach, (tile + 1) * reach)
        seen = slice(tile * reach, (tile + 3) * reach)
        mask = local_mask(place, tile, reach, 2 * reach, 3 * reach)
        logs = sums[mine]

        def pair(p, carry):
            query = both_heads(queries[mine, pair_at(p)])
            grad_out = both_heads(grad_out_all[mine, pair_at(p)])
            key = pairs[seen, pair_at(p)]
            log = jnp.concatenate([column_at(logs, 2 * p), column_at(logs, 2 * p + 1)], axis=0)
            probs = jnp.exp(jnp.where(mask, nt(query, key) * scale, NEG) - log)
            grad_probs = nt(grad_out, pairs[seen, pair_at(p, light)])
            delta = jnp.sum(probs * grad_probs, -1, keepdims=True)
            grad_scores = (probs * (grad_probs - delta)).astype(BF16)
            grad_queries[mine, pair_at(p)] = one_pair(nn(grad_scores, key) * scale).astype(BF16)
            held[seen, pair_at(p)] = held[seen, pair_at(p)] + tn(grad_scores, query) * scale
            beyond = pair_at(p, light)
            held[seen, beyond] = held[seen, beyond] + tn(probs.astype(BF16), grad_out)
            return carry

        lax.fori_loop(0, HL // 2, pair, 0)
    grad_pairs[...] = held[...].astype(BF16)


def light_weights_body(
    raw, normed, grad_queries, grad_pairs, grad_routed, query_select, feed_vectors, heavy_vectors, to_own, f0, f1,
    keep, send, outer, grad_mine
):
    light = HL * HDL
    reach = RADIUS
    rows = grad_queries.shape[0]
    half = f0.shape[0]
    grads = onto(grad_pairs[...], f0[:, light : 3 * light], f1[:, light : 3 * light])
    for i, at in enumerate((slice(0, reach), slice(reach + rows, None))):
        outer[i * reach : (i + 1) * reach] = nt(grads[at].astype(BF16), to_own[...]).astype(BF16)
    own = onto(grad_queries[...], f0[:, :light], f1[:, :light])
    own = own + grads[reach : reach + rows] + place_rows(query_select[...], grad_routed[...])
    grad_mine[...] = own
    unit, unused = unit_rms(raw[...].astype(F32))
    gain = jnp.sum(own * unit[reach : reach + rows], 0, keepdims=True)
    for at in (slice(0, reach), slice(reach + rows, None)):
        gain = gain + jnp.sum(grads[at] * unit[at], 0, keepdims=True)
    vector_rows = feed_vectors[...] + heavy_vectors[...]
    first = lax.broadcasted_iota(jnp.int32, vector_rows.shape, 0) == 0
    vector_rows = vector_rows + jnp.where(first, gain, 0.0)
    filler = jnp.zeros((120, raw.shape[1]), F32)
    columns = jnp.concatenate([vector_rows, filler], axis=0)
    for i, out in ((1, send), (0, keep)):
        at = slice(i * half, (i + 1) * half)
        out[:, :light] = tn(normed[reach : reach + rows, at], grad_queries[...]).astype(BF16)
        out[:, light : 3 * light] = tn(normed[:, at], grad_pairs[...]).astype(BF16)
        out[:, 3 * light :] = columns[:, at].T.astype(BF16)


def halo_body(from_prev, from_next, grad_mine, to_own, out):
    reach = RADIUS
    rows = grad_mine.shape[0]
    order = to_own[...]
    out[...] = grad_mine[...]
    out[:reach] = out[:reach] + nn(from_prev[...], order)
    out[rows - reach :] = out[rows - reach :] + nn(from_next[...], order)


def finish_body(keyed_grads, key_select, grads, grad_middle, raw, vectors, to_own, out):
    reach = RADIUS
    rows, width = grads.shape
    order = to_own[...]
    keyed = keyed_grads[...]
    if keyed.shape[0] < key_select.shape[0]:
        rest = key_select.shape[0] - keyed.shape[0]
        tail = [keyed[i * rest : (i + 1) * rest, width:] for i in range(keyed.shape[0] // rest)]
        keyed = jnp.concatenate([keyed[:, :width], jnp.concatenate(tail, axis=1)], axis=0)
    keyed = nn(keyed.astype(BF16), order).astype(BF16)
    total = grads[...] + tn(key_select[...], keyed)
    unit, scale = unit_rms(raw[reach : reach + rows].astype(F32))
    total = grad_middle[...] + norm_back(total, vectors[0:1], unit, scale)
    out[...] = reorder_back(total, order)


def heavy_forward_wide(query_doc, key_doc, select, normed, vectors, to_own, s0, s1, keyed_raw):
    heavy = HH * HDH
    q_at, kv_at = slice(0, heavy), slice(heavy, 3 * heavy)
    unit, unused = unit_rms(nn(keyed_raw, to_own))
    keyed = (unit * vectors[0:1]).astype(BF16)
    pairs = into(keyed, s0[:, kv_at], s1[:, kv_at]).astype(BF16)
    routed = nn(select, normed[RADIUS : normed.shape[0] - RADIUS]).astype(BF16)
    queries = into(routed, s0[:, q_at], s1[:, q_at]).astype(BF16)

    def heads(array):
        return array.reshape(-1, HH, HDH)

    scores = jnp.einsum(
        "qhd,khd->hqk", heads(queries), heads(pairs[:, :heavy]), preferred_element_type=F32
    ) / math.sqrt(HDH)
    probs = soft(jnp.where((query_doc == key_doc)[None], scores, NEG))
    mixed = jnp.einsum(
        "hqk,khd->qhd", probs.astype(BF16), heads(pairs[:, heavy:]), preferred_element_type=F32
    )
    return keyed, pairs, routed, queries, mixed.reshape(-1, heavy).astype(BF16), probs


def heavy_backward_wide(
    grad_middle, query_select, routed, keyed, pairs, queries, light_mixed, heavy_mixed, heavy_branch, probs,
    vectors, to_own, o0, o1, s0, s1
):
    heavy = HH * HDH
    scale = 1.0 / math.sqrt(HDH)
    half = s0.shape[0]
    q_at, kv_at = slice(0, heavy), slice(heavy, 3 * heavy)
    score = sigmoid(jnp.sum(routed.astype(F32) * vectors[1:2], -1, keepdims=True))
    grad_rows = take_rows(query_select, grad_middle)
    grad_branch = (score * grad_rows).astype(BF16)
    logit = jnp.sum(grad_rows * heavy_branch, -1, keepdims=True) * score * (1.0 - score)
    at = slice(0, heavy)
    grad_mixed = into(grad_branch, o0[:, at], o1[:, at]).astype(BF16)

    def heads(array):
        return array.reshape(-1, HH, HDH)

    def mix(pattern, left, right):
        return jnp.einsum(pattern, left, right, preferred_element_type=F32)

    grad_probs = mix("qhd,khd->hqk", heads(grad_mixed), heads(pairs[:, heavy:]))
    delta = jnp.sum(probs * grad_probs, -1, keepdims=True)
    grad_scores = (probs * (grad_probs - delta)).astype(BF16)
    grad_queries = mix("hqk,khd->qhd", grad_scores, heads(pairs[:, :heavy])) * scale
    grad_queries = grad_queries.reshape(-1, heavy).astype(BF16)
    grad_keys = mix("hqk,qhd->khd", grad_scores, heads(queries)) * scale
    grad_values = mix("hqk,qhd->khd", probs.astype(BF16), heads(grad_mixed))
    grad_pairs = jnp.concatenate(
        [grad_keys.reshape(-1, heavy).astype(BF16), grad_values.reshape(-1, heavy).astype(BF16)], axis=1
    )
    grad_routed = onto(grad_queries, s0[:, q_at], s1[:, q_at]) + logit * vectors[1:2]
    grads = onto(grad_pairs, s0[:, kv_at], s1[:, kv_at])
    vector_grads = jnp.concatenate(
        [
            jnp.sum(grads * keyed.astype(F32), 0, keepdims=True) / vectors[0:1],
            jnp.sum(routed.astype(F32) * logit, 0, keepdims=True),
            jnp.zeros((6, grads.shape[1]), F32),
        ],
        axis=0,
    )
    moved = nt(grads.astype(BF16), to_own).astype(BF16)
    low = grad_middle.astype(BF16)
    sides = []
    for at in (slice(0, half), slice(half, None)):
        columns = (
            tn(grad_branch[:, at], heavy_mixed),
            tn(low[:, at], light_mixed),
            tn(routed[:, at], grad_queries),
            tn(keyed[:, at], grad_pairs),
        )
        sides.append(jnp.concatenate(columns, axis=1).astype(BF16))
    return sides[0], sides[1], grad_routed, vector_grads, moved


def per_device(
    tokens,
    query_small,
    key_small,
    value_small,
    out_small,
    query_large,
    key_large,
    value_large,
    out_large,
    attend_gain,
    attend_router,
    gate_small,
    up_small,
    down_small,
    gate_large,
    up_large,
    down_large,
    feed_gain,
    feed_router,
    lengths,
    query_route,
    key_route,
    feed_route,
    cotangent,
):
    net = Net()
    rows, width = tokens.shape
    blocks = net.count
    part = width // blocks
    half = width // 2
    first = net.device * rows
    light = HL * HDL
    heavy = HH * HDH
    narrow = down_small.shape[0]
    wide = down_large.shape[0]
    slots = query_route.shape[1]
    members = 2 * net.depth
    share = wide // members
    pooled = members * slots
    keys = blocks * slots
    rest = slots - part
    packed = part % 8 == 0 and rest > 0 and rest % 8 == 0 and part % rest == 0 and keys <= 2048

    step = [(i, i + 1) for i in range(blocks - 1)]
    back = [(i + 1, i) for i in range(blocks - 1)]
    vector_pack = jnp.stack([attend_gain, attend_router, feed_gain, feed_router], axis=1)
    vector_pack = jnp.pad(vector_pack, ((0, 0), (0, 124)))
    first_pack = (query_small, key_small, value_small, vector_pack, out_large.T, out_small.T)
    moves, at = [], 0
    for i, piece in enumerate(first_pack):
        moves.append((i, (0, part), (0, piece.shape[1]), 0, at))
        at += piece.shape[1]
    (first_set,) = rearrange("pack_first", first_pack, [((part, at), moves)], room=56 << 20)
    first_parts = net.from_z(first_set)
    cut = 3 * light + vector_pack.shape[1]
    column = jnp.arange(width, dtype=jnp.int32)
    own_order = net.target(column // part) * part + column % part
    bits = column % half // (part * net.depth)
    bits = jnp.where(net.core == 1, bits, reverse_bits(bits, net.levels))
    member = (net.core ^ (column // half)) * net.depth + (net.z ^ (column // part % net.depth))
    slice_order = ((net.pair ^ bits) * members + member) * part + column % part
    orders = jnp.stack([own_order, slice_order])
    place = jnp.stack([first, lengths[0], lengths[1], jnp.int32(rows * blocks), net.device, net.core, net.z])
    square = ((width, width), BF16)
    chosen = ((slots, rows), BF16)

    if packed:
        tall = blocks * part
        spot = jnp.arange(keys, dtype=jnp.int32)
        spot_block = jnp.where(spot < tall, spot // part, (spot - tall) // rest)
        spot_slot = jnp.where(spot < tall, spot % part, part + (spot - tall) % rest)
        second_set, third_set, slices_keep, slices_send, key_docs = run(
            pack_body,
            "pack",
            [
                ((part, 4 * width + width * rest // part), BF16),
                ((part, 3 * narrow), BF16),
                ((net.depth * part, 3 * share), BF16),
                ((net.depth * part, 3 * share), BF16),
                ((1, keys), jnp.int32),
            ],
            (
                place, jnp.stack([net.target(spot_block), spot_slot]), tokens, key_route,
                query_large, key_large, value_large,
                gate_small, up_small, down_small.T, gate_large, up_large, down_large.T,
            ),
            smem=1,
            room=56 << 20,
        )
    else:
        second_set = jnp.concatenate([query_large, key_large, value_large], axis=1)
        third_set = jnp.concatenate([gate_small, up_small, down_small.T], axis=1)
        stacked = jnp.stack([gate_large, up_large, down_large.T], axis=0)
        stacked = stacked.reshape(3, part, members, share).transpose(2, 1, 0, 3)
        stacked = jnp.take(stacked.reshape(members, part, 3 * share), net.members(), axis=0)
        slices_keep, slices_send = stacked.reshape(2, net.depth * part, 3 * share)
    order = Order()
    top_bit = net.levels - 1

    def take_z(pieces):
        return order.note(stack_rows([order.hold(pieces[0])] + pieces[1:]))

    def take(whole, moved):
        return order.note(stack_rows([whole, order.hold(moved)]))

    def first_moved(whole):
        return net.by_bit(whole, 0)

    def rest_moved(whole, moved):
        for j in range(1, net.levels):
            whole = take(whole, moved)
            moved = net.by_bit(whole, j)
        return whole, moved

    order.note(second_set)
    first_set = take_z(first_parts)
    first_moving = first_moved(first_set)
    second_parts = net.from_z(after(second_set, first_set))
    slices_got = net.by_core(slices_send)
    to_own, to_slice = run(orders_body, "orders", [square, square], (order.hold(orders),))
    order.note(to_own)
    third_parts = pair_up(third_set, order.hold(slices_keep), slices_got, part)
    order.note(third_parts[0])
    first_set, first_moving = rest_moved(first_set, first_moving)
    second_set = take_z(second_parts)
    third_parts = net.exchange_z([after(p, second_set) for p in third_parts])
    cot, query_select, key_select, feed_select, query_docs = run(
        select_body,
        "select",
        [((rows, width), BF16), chosen, chosen, chosen, ((slots, 1), jnp.int32)],
        (place, to_own, query_route, key_route, feed_route, order.hold(cotangent)),
        smem=1,
    )
    order.note(cot)
    a0 = take(first_set, first_moving)
    a1 = net.by_core(a0)
    f0, f1 = (Columns(a, 0, cut) for a in (a0, a1))
    o0, o1 = (Columns(a, cut, a0.shape[1]) for a in (a0, a1))
    second_moving = first_moved(after(second_set, a0))
    second_set, second_moving = rest_moved(second_set, second_moving)
    third_set = order.note(stack_both([order.hold(third_parts[0])] + third_parts[1:], "weave"))
    third_moving = first_moved(third_set)
    near_tokens = after(tokens, third_set)
    above = lax.ppermute(near_tokens[rows - RADIUS :], AXES, step)
    below = lax.ppermute(near_tokens[:RADIUS], AXES, back)
    s0 = take(second_set, second_moving)
    s1 = net.by_core(s0)
    for j in range(1, net.levels):
        third_set = order.note(stack_both([third_set, order.hold(third_moving)]))
        third_moving = net.by_bit(third_set, j)
    (raw,) = run(
        prepare_body,
        "prepare",
        [((rows + 2 * RADIUS, width), BF16)],
        (order.hold(to_own), above, tokens, below),
    )
    order.note(raw)

    normed_ext, query_rows, pair_rows, vectors = run(
        light_rows_body,
        "light_rows",
        [
            ((rows + 2 * RADIUS, width), BF16),
            ((rows, light), BF16),
            ((rows + 2 * RADIUS, 2 * light), BF16),
            ((8, width), F32),
        ],
        (order.hold(raw), f0, f1),
    )
    order.note(query_rows)
    light_mixed, light_sums = run(
        light_forward_body,
        "light_forward",
        [((rows, light), BF16), ((rows, 128), F32)],
        (place, order.hold(query_rows), pair_rows),
        smem=1,
    )
    order.note(light_mixed)
    if packed:
        (keyed,) = run(
            functools.partial(heavy_rows_body, slots),
            "heavy_rows",
            [((keys, width), BF16)],
            (order.hold(vectors), to_own, s0, s1),
            scratch=[pltpu.VMEM((keys, width), BF16)],
        )
        order.note(keyed)
        heavy_pairs, routed, routed_query = run(
            heavy_pairs_body,
            "heavy_pairs",
            [((keys, 2 * heavy), BF16), ((slots, width), BF16), ((slots, heavy), BF16)],
            (order.hold(query_select), normed_ext, keyed, s0, s1),
        )
        order.note(routed_query)
        heavy_mixed, heavy_sums = run(
            heavy_forward_body,
            "heavy_forward",
            [((slots, heavy), BF16), ((2 * slots, 128), F32)],
            (query_docs, key_docs, order.hold(routed_query), heavy_pairs),
        )
    else:
        relative = net.target(jnp.arange(blocks, dtype=jnp.int32))
        near_routes = jnp.take(key_route, relative, axis=0)
        key_docs = document_of(relative[:, None] * rows + near_routes, lengths)
        key_docs = jnp.where(near_routes < rows, key_docs, -1).reshape(1, -1)
        keyed_raw = net.gather(nn(key_select, tokens).astype(BF16))
        keyed, heavy_pairs, routed, routed_query, heavy_mixed, heavy_sums = heavy_forward_wide(
            query_docs, key_docs, query_select, normed_ext, vectors, to_own,
            s0, s1, jnp.concatenate(keyed_raw, axis=0),
        )
    order.note(heavy_mixed)

    middle, normed_two, heavy_branch, feed_rows, feed_grads, sent = run(
        join_body,
        "join",
        [
            ((rows, width), F32),
            ((rows, width), BF16),
            ((slots, width), F32),
            ((slots, width), BF16),
            ((slots, width), F32),
            ((slots, 2 * width), BF16),
        ],
        (
            raw, light_mixed, order.hold(heavy_mixed), routed, query_select, feed_select, vectors, cot, to_own, o0, o1,
        ),
    )
    order.note(sent)

    got_parts = net.from_z(sent)
    got0 = take_z(got_parts)
    got1 = net.by_core(got0)
    t0, expert = part_both([third_set, order.hold(third_moving)], "part_both")
    order.note(t0)
    t1 = net.by_core(t0)
    keep, send, expert_keep, expert_send = run(
        expert_body,
        "expert",
        [
            ((pooled // 2, 2 * width), BF16),
            ((pooled // 2, 2 * width), BF16),
            ((half // 2, 6 * share), BF16),
            ((half // 2, 6 * share), BF16),
        ],
        (order.hold(got0), got1, to_slice, expert),
        scratch=[
            pltpu.VMEM((pooled, width), BF16),
            pltpu.VMEM((pooled, width), BF16),
            pltpu.VMEM((pooled, 2 * share), F32),
            pltpu.VMEM((pooled, share), F32),
            pltpu.VMEM((pooled, share), BF16),
            pltpu.VMEM((pooled, 2 * share), BF16),
        ],
    )
    order.note(send)
    moving = net.by_core(send)
    expert_moving = net.by_bit(expert_send, top_bit)
    feed_light, grad_normed, hidden, hidden_grads = run(
        feed_body,
        "feed",
        [
            ((rows, width), F32),
            ((rows, width), F32),
            ((rows, narrow), BF16),
            ((rows, 2 * narrow), BF16),
        ],
        (order.hold(normed_two), cot, t0, t1),
        scratch=[pltpu.VMEM((rows, 2 * narrow), F32), pltpu.VMEM((rows, narrow), F32)],
    )
    order.note(hidden)
    def give(keep, moved, pieces):
        out = fold(keep, order.hold(moved), pieces)
        order.note(out[0])
        return out

    def descend(keep, moved):
        for j in reversed(range(net.levels - 1)):
            keep, send = give(keep, moved, 2)
            moved = net.by_bit(send, j)
        return keep, moved

    summed = net.exchange_z(give(keep, moving, net.depth))
    third_keep, third_send = run(
        feed_weight_body,
        "feed_weight",
        [((half, 3 * narrow), BF16), ((half, 3 * narrow), BF16)],
        (order.hold(normed_two), cot, hidden, hidden_grads),
    )
    order.note(third_send)
    third_moving = net.by_core(third_send)

    third_keep, third_send = give(third_keep, third_moving, 2)
    third_moving = net.by_bit(third_send, top_bit)

    result, grad_middle, feed_vectors = run(
        turn_body,
        "turn",
        [((rows, width), BF16), ((rows, width), F32), ((8, width), F32)],
        (
            order.hold(summed[0]), *summed[1:], middle, feed_light, grad_normed, feed_rows, feed_grads, feed_select,
            vectors, cot, to_own,
        ),
    )
    order.note(grad_middle)
    if packed:
        grad_branch, grad_queries, grad_heavy_pairs, logits = run(
            heavy_scores_body,
            "heavy_scores",
            [
                ((slots, width), BF16),
                ((slots, heavy), BF16),
                ((keys, 2 * heavy), BF16),
                ((slots, 128), F32),
            ],
            (
                query_docs, key_docs, order.hold(grad_middle), query_select, routed, heavy_pairs, routed_query,
                heavy_branch, heavy_sums, vectors, o0, o1,
            ),
            scratch=[pltpu.VMEM((slots, heavy), BF16)],
        )
        order.note(grad_branch)
    expert_keep, expert_moving = descend(expert_keep, expert_moving)
    if packed:
        second_keep, second_send, heavy_vectors = run(
            heavy_weights_body,
            "heavy_weights",
            [
                ((half, 5 * width + light + width * rest // part), BF16),
                ((half, 5 * width + light + width * rest // part), BF16),
                ((8, width), F32),
            ],
            (
                grad_middle, routed, keyed, light_mixed, heavy_mixed, order.hold(grad_branch), grad_queries,
                grad_heavy_pairs, logits, vectors, to_own, s0, s1,
            ),
            scratch=[pltpu.VMEM((keys, width), BF16)],
        )
    else:
        second_keep, second_send, grad_routed, heavy_vectors, keyed_grads = heavy_backward_wide(
            grad_middle, query_select, routed, keyed, heavy_pairs, routed_query, light_mixed, heavy_mixed,
            heavy_branch, heavy_sums, vectors, to_own, o0.array[:, cut:], o1.array[:, cut:], s0, s1,
        )
    order.note(second_send)
    second_moving = net.by_core(second_send)
    third_keep, third_moving = descend(third_keep, third_moving)
    expert_parts = net.exchange_z(give(expert_keep, expert_moving, net.depth))
    if packed:
        (grad_routed,) = run(
            routed_body,
            "routed",
            [((slots, width), F32)],
            (order.hold(grad_queries), logits, vectors, s0, s1),
        )
        order.note(grad_routed)
    second_keep, second_send = give(second_keep, second_moving, 2)
    second_moving = net.by_bit(second_send, top_bit)
    grad_queries, grad_pairs = run(
        light_scores_body,
        "light_scores",
        [((rows, light), BF16), ((rows + 2 * RADIUS, 2 * light), BF16)],
        (place, order.hold(grad_middle), query_rows, pair_rows, light_sums, o0, o1),
        smem=1,
        scratch=[pltpu.VMEM((rows + 2 * RADIUS, 2 * light), F32), pltpu.VMEM((rows, light), BF16)],
    )
    order.note(grad_queries)
    third_parts = net.exchange_z(give(third_keep, third_moving, net.depth))
    first_keep, first_send, outer, grad_mine = run(
        light_weights_body,
        "light_weights",
        [
            ((half, 3 * light + 128), BF16),
            ((half, 3 * light + 128), BF16),
            ((2 * RADIUS, width), BF16),
            ((rows, width), F32),
        ],
        (
            raw, normed_ext, order.hold(grad_queries), grad_pairs, grad_routed, query_select, feed_vectors, heavy_vectors,
            to_own, f0, f1,
        ),
    )
    order.note(first_send)
    first_moving = net.by_core(first_send)
    from_next = lax.ppermute(outer[:RADIUS], AXES, back)
    from_prev = lax.ppermute(outer[RADIUS:], AXES, step)

    expert_keep, expert_send = take_apart([order.hold(expert_parts[0])] + expert_parts[1:], part)
    order.note(expert_send)
    expert_got = net.by_core(expert_send)
    third_grad = settle([order.hold(third_parts[0])] + third_parts[1:], [narrow] * 3, "settle_third")
    order.note(third_grad[0])
    second_keep, second_moving = descend(second_keep, second_moving)
    first_keep, first_send = give(first_keep, first_moving, 2)
    first_moving = net.by_bit(first_send, top_bit)
    (grad_near,) = run(
        halo_body, "halo", [((rows, width), F32)], (from_prev, from_next, order.hold(grad_mine), to_own)
    )
    order.note(grad_near)
    if packed:
        gate_grad, up_grad, down_grad = run(
            unpack_body,
            "unpack",
            [((part, wide), F32)] * 3,
            (place, order.hold(expert_keep), expert_got),
            smem=1,
        )
    else:
        expert_grad = jnp.concatenate([order.hold(expert_keep), expert_got], axis=0)
        expert_grad = jnp.take(expert_grad.reshape(members, part, 3 * share), net.members(), axis=0)
        expert_grad = expert_grad.reshape(members, part, 3, share).transpose(2, 1, 0, 3)
        gate_grad, up_grad, down_grad = expert_grad.reshape(3, part, wide).astype(F32)
    order.note(gate_grad)
    second_parts = net.exchange_z(give(second_keep, second_moving, net.depth))
    first_keep, first_moving = descend(first_keep, first_moving)
    first_parts = net.exchange_z(give(first_keep, first_moving, net.depth))
    widths = [width, light, heavy, heavy, heavy]
    if packed:
        widths.append(width + width * rest // part)
    second_grad = settle([order.hold(second_parts[0])] + second_parts[1:], widths, "settle_second")
    order.note(second_grad[0])
    if packed:
        keyed_own = second_grad[5]
    else:
        cut = keys // 2
        keyed_own = settle(net.reduce(keyed_grads[:cut], keyed_grads[cut:]), [width], "settle_keyed")[0]
    (tokens_grad,) = run(
        finish_body,
        "finish",
        [((rows, width), F32)],
        (order.hold(keyed_own), key_select, grad_near, grad_middle, raw, vectors, to_own),
    )
    order.note(tokens_grad)
    first_grad = settle(
        [order.hold(first_parts[0])] + first_parts[1:], [light, light, light, 128], "settle_first"
    )
    vector_out = first_grad[3][:, :4].T
    return (
        result,
        tokens_grad,
        first_grad[0],
        first_grad[1],
        first_grad[2],
        second_grad[1].T,
        second_grad[2],
        second_grad[3],
        second_grad[4],
        second_grad[0].T,
        vector_out[0],
        vector_out[1],
        third_grad[0],
        third_grad[1],
        third_grad[2].T,
        gate_grad,
        up_grad,
        down_grad.T,
        vector_out[2],
        vector_out[3],
    )


def solution(mesh):
    by_rows = P(AXES, None)
    by_columns = P(None, AXES)
    vector = P(AXES)
    return jax.shard_map(
        per_device,
        mesh=mesh,
        in_specs=(
            by_rows,
            by_rows,
            by_rows,
            by_rows,
            by_columns,
            by_rows,
            by_rows,
            by_rows,
            by_columns,
            vector,
            vector,
            by_rows,
            by_rows,
            by_columns,
            by_rows,
            by_rows,
            by_columns,
            vector,
            vector,
            P(),
            P(),
            P(),
            by_rows,
            by_rows,
        ),
        out_specs=(
            by_rows,
            by_rows,
            by_rows,
            by_rows,
            by_rows,
            by_columns,
            by_rows,
            by_rows,
            by_rows,
            by_columns,
            vector,
            vector,
            by_rows,
            by_rows,
            by_columns,
            by_rows,
            by_rows,
            by_columns,
            vector,
            vector,
        ),
        check_vma=False,
    )
```

```python
import functools
import math

import jax
import jax.numpy as jnp
from jax import lax
from jax.experimental import pallas as pl
from jax.experimental.pallas import tpu as pltpu
from jax.sharding import PartitionSpec as P

HL = 8
HDL = 64
HH = 12
HDH = 64
RADIUS = 128

NEG = -1e30
EPS = 1e-06
HIGH = lax.Precision.HIGHEST
AXES = ("seq", "fsdp")
F32 = jnp.float32
BF16 = jnp.bfloat16
ROOM = 12 << 20
LENGTHS = {
    "select": 60,
    "weave": 20,
    "light_forward": 60,
    "heavy_pairs": 60,
    "expert": 60,
    "feed": 60,
    "feed_weight": 20,
    "turn": 5.6,
    "routed": 60,
    "settle_third": 12,
}


def declared(name):
    flops = int(LENGTHS.get(name, 0.05) * 1e9)
    return pl.CostEstimate(flops=flops, bytes_accessed=10**10, transcendentals=0)


class Columns:
    def __init__(self, array, start, stop):
        self.array, self.start, self.stop = array, start, stop


def dot(left, right, dims):
    return lax.dot_general(left, right, (dims, ((), ())), preferred_element_type=F32)


def nn(left, right):
    return dot(left, right, ((1,), (0,)))


def nt(left, right):
    return dot(left, right, ((1,), (1,)))


def tn(left, right):
    return dot(left, right, ((0,), (0,)))


def reverse_bits(value, count):
    out = value * 0
    for j in range(count):
        out = out | (((value >> j) & 1) << (count - 1 - j))
    return out


class Net:
    def __init__(self):
        self.seq = lax.axis_size("seq")
        self.depth = lax.axis_size("fsdp")
        self.levels = (self.seq // 2).bit_length() - 1
        self.count = self.seq * self.depth
        s = lax.axis_index("seq")
        self.core, self.pair = s & 1, s >> 1
        self.z = lax.axis_index("fsdp")
        self.device = s * self.depth + self.z

    def pairs(self, move):
        out = []
        for s in range(self.seq):
            for z in range(self.depth):
                pair, core, to_z = move(s >> 1, s & 1, z)
                out.append((s * self.depth + z, (pair * 2 + core) * self.depth + to_z))
        return out

    def by_core(self, array):
        return lax.ppermute(array, AXES, self.pairs(lambda p, c, z: (p, 1 - c, z)))

    def by_bit(self, array, j):
        top = self.levels - 1 - j
        return lax.ppermute(
            array, AXES, self.pairs(lambda p, c, z: (p ^ (1 << (j if c else top)), c, z))
        )

    def by_z(self, array, k):
        return lax.ppermute(array, AXES, self.pairs(lambda p, c, z: (p, c, z ^ k)))

    def target(self, relative):
        zr = relative % self.depth
        bits = (relative // self.depth) % (self.seq // 2)
        core = self.core ^ (relative // (self.count // 2))
        pair = self.pair ^ jnp.where(core == 1, bits, reverse_bits(bits, self.levels))
        return (pair * 2 + core) * self.depth + (self.z ^ zr)

    def from_z(self, shard):
        return [shard] + [self.by_z(shard, k) for k in range(1, self.depth)]

    def exchange_z(self, pieces):
        return [pieces[0]] + [self.by_z(pieces[k], k) for k in range(1, self.depth)]

    def gather(self, shard):
        shard = jnp.concatenate(self.from_z(shard), axis=0)
        for j in range(self.levels):
            shard = jnp.concatenate([shard, self.by_bit(shard, j)], axis=0)
        return shard, self.by_core(shard)

    def reduce(self, keep, send):
        keep, send = fold(keep, self.by_core(send), 2)
        for j in reversed(range(self.levels)):
            pieces = 2 if j else self.depth
            out = fold(keep, self.by_bit(send, j), pieces)
            keep, send = out[0], out[1]
        return self.exchange_z(out)

    def members(self):
        relative = jnp.arange(2 * self.depth, dtype=jnp.int32)
        core = self.core ^ (relative // self.depth)
        return core * self.depth + (self.z ^ (relative % self.depth))


def by_columns(width, step):
    chunk = next(c for c in (512, 256, 128, width) if width % c == 0)
    if width % chunk or width <= 4 * chunk:
        step(slice(0, width))
        return

    def at(i, carry):
        step(pl.ds(pl.multiple_of(i * chunk, chunk), chunk))
        return carry

    lax.fori_loop(0, width // chunk, at, 0)


class Order:
    def __init__(self):
        self.last = ()

    def hold(self, array):
        return after(array, *self.last)

    def note(self, array):
        self.last = (array,)
        return array


def stack_rows(arrays):
    height = sum(a.shape[0] for a in arrays)
    if any(a.shape[0] % 8 for a in arrays):
        return jnp.concatenate(arrays, axis=0)

    def body(*refs):
        def copy(columns):
            at = 0
            for ref in refs[:-1]:
                refs[-1][at : at + ref.shape[0], columns] = ref[:, columns]
                at += ref.shape[0]

        by_columns(arrays[0].shape[1], copy)

    return run(body, "stack", [((height, arrays[0].shape[1]), arrays[0].dtype)], arrays)[0]


def after(array, *earlier):
    return lax.optimization_barrier((array, *earlier))[0]


def unit_rms(values):
    scale = lax.rsqrt(jnp.mean(values * values, -1, keepdims=True) + EPS)
    return values * scale, scale


def norm_back(grad, gain, unit, scale):
    scaled = grad * gain
    return scale * (scaled - unit * jnp.mean(scaled * unit, -1, keepdims=True))


def document_of(places, lengths):
    return (places >= lengths[0]).astype(jnp.int32)


def sigmoid(values):
    return 1.0 / (1.0 + jnp.exp(-values))


def soft(scores):
    top = jnp.max(scores, -1, keepdims=True)
    expo = jnp.exp(scores - top)
    return expo / jnp.sum(expo, -1, keepdims=True)


def two_parts(values):
    high = values.astype(BF16)
    return high, (values - high.astype(F32)).astype(BF16)


def place_rows(select, values):
    high, low = two_parts(values)
    return tn(select, high) + tn(select, low)


def take_rows(select, values):
    high, low = two_parts(values)
    return nn(select, high) + nn(select, low)


def reorder(values, order):
    high, low = two_parts(values)
    return nn(high, order) + nn(low, order)


def reorder_back(values, order):
    high, low = two_parts(values)
    return nt(high, order) + nt(low, order)


def into(values, first, second):
    half = first.shape[0]
    return nn(values[:, :half], first) + nn(values[:, half:], second)


def onto(values, first, second):
    return jnp.concatenate([nt(values, first), nt(values, second)], axis=1)


def lanes(rows, width=128):
    return lax.broadcasted_iota(jnp.int32, (rows, width), 1)


def both_heads(pair):
    first = lanes(pair.shape[0]) < HDL
    zero = jnp.zeros_like(pair)
    return jnp.concatenate([jnp.where(first, pair, zero), jnp.where(first, zero, pair)], axis=0)


def pair_at(p, start=0):
    return pl.ds(pl.multiple_of(start + p * 128, 128), 128)


def column_at(array, index):
    return jnp.sum(jnp.where(lanes(*array.shape) == index, array, 0.0), -1, keepdims=True)


def one_pair(stacked):
    rows = stacked.shape[0] // 2
    return jnp.where(lanes(rows) < HDL, stacked[:rows], stacked[rows:])


def run(body, name, outs, args, smem=0, scratch=(), room=ROOM):
    vmem = pl.BlockSpec(memory_space=pltpu.VMEM)
    held = sum(math.prod(piece.shape) * jnp.dtype(piece.dtype).itemsize for piece in scratch)
    cuts = {i: a for i, a in enumerate(args) if isinstance(a, Columns)}

    def kernel(*refs):
        refs = list(refs)
        for i, cut in cuts.items():
            refs[i] = refs[i].at[:, cut.start : cut.stop]
        body(*refs)

    return pl.pallas_call(
        kernel,
        name=name,
        compiler_params=pltpu.CompilerParams(vmem_limit_bytes=held + room),
        out_shape=[jax.ShapeDtypeStruct(shape, kind) for shape, kind in outs],
        in_specs=[pl.BlockSpec(memory_space=pltpu.SMEM)] * smem + [vmem] * (len(args) - smem),
        out_specs=[vmem] * len(outs),
        scratch_shapes=list(scratch),
        cost_estimate=declared(name),
    )(*[a.array if isinstance(a, Columns) else a for a in args])


def rearrange(name, sources, outs, room=ROOM):
    bounds = [b for unused, moves in outs for m in moves for b in (*m[1], m[3])]
    if any(b % 8 for b in bounds):
        made = []
        for shape, moves in outs:
            out = jnp.zeros(shape, BF16)
            for i, (r0, r1), (c0, c1), row, column in moves:
                out = lax.dynamic_update_slice(out, sources[i][r0:r1, c0:c1], (row, column))
            made.append(out)
        return made

    spans = {(c0, c1, column) for unused, moves in outs for i, rows, (c0, c1), row, column in moves}

    def body(*refs):
        def copy(columns=None):
            for out, (unused, moves) in zip(refs[len(sources) :], outs):
                for i, (r0, r1), (c0, c1), row, column in moves:
                    to = columns or slice(column, column + c1 - c0)
                    out[row : row + r1 - r0, to] = refs[i][r0:r1, columns or slice(c0, c1)]

        if len(spans) == 1 and all(c0 == column for c0, c1, column in spans):
            by_columns(max(c1 for c0, c1, column in spans), copy)
        else:
            copy()

    return run(body, name, [(shape, BF16) for shape, unused in outs], sources, room=room)


def fold(keep, moved, pieces, kind=BF16):
    height, width = keep.shape
    piece = height // pieces
    parts = 2 if piece % 32 == 0 else 1
    step = piece // parts

    def body(*refs):
        def add(columns):
            for k in range(pieces):
                total = refs[k][:, columns].astype(F32) + refs[pieces + k][:, columns].astype(F32)
                refs[2 * pieces + k][:, columns] = total.astype(kind)

        by_columns(width, add)

    def spec(k):
        return pl.BlockSpec((step, width), lambda i, k=k: (k * parts + i, 0))

    if piece % 8:
        total = keep.astype(F32) + moved.astype(F32)
        return [total[k * piece : (k + 1) * piece].astype(kind) for k in range(pieces)]
    return pl.pallas_call(
        body,
        name="fold",
        compiler_params=pltpu.CompilerParams(vmem_limit_bytes=ROOM),
        grid=(parts,),
        out_shape=[jax.ShapeDtypeStruct((piece, width), kind)] * pieces,
        in_specs=[spec(k) for k in range(pieces)] * 2,
        out_specs=[spec(0)] * pieces,
        cost_estimate=declared("fold"),
    )(*([keep] * pieces + [moved] * pieces))


def settle(pieces, widths, name, rows=None):
    rows = rows or pieces[0].shape[0]

    def body(*refs):
        parts, outs = refs[: len(pieces)], refs[len(pieces) :]
        at = 0
        for out, width in zip(outs, widths):
            total = parts[0][:rows, at : at + width].astype(F32)
            for part in parts[1:]:
                total = total + part[:rows, at : at + width].astype(F32)
            out[...] = total
            at += width

    return run(body, name, [((rows, width), F32) for width in widths], pieces)


def hot(column, rows):
    return jnp.where(column == lanes(column.shape[0], rows), 1.0, 0.0).astype(BF16)


def as_column(row):
    count = row.shape[1]
    eye = lax.broadcasted_iota(jnp.int32, (count, count), 0) == lanes(count, count)
    spread = jnp.where(eye, row.astype(F32), 0.0)
    return jnp.sum(spread, -1, keepdims=True).astype(jnp.int32)


def order_matrix(order):
    width = order.shape[1]
    rows = lax.broadcasted_iota(jnp.int32, (width, width), 0)
    return jnp.where(rows == order, 1.0, 0.0).astype(BF16)


def orders_body(orders, to_own, to_slice):
    to_own[...] = order_matrix(orders[0:1])
    to_slice[...] = order_matrix(orders[1:2])


def select_body(
    place, to_own, query_route, key_route, feed_route, cotangent, cot, query_select, key_select, feed_select, query_doc
):
    rows = cotangent.shape[0]
    cot[...] = nn(cotangent[...], to_own[...]).astype(BF16)
    queries = as_column(query_route[pl.ds(place[4], 1)])
    query_select[...] = hot(queries, rows)
    key_select[...] = hot(as_column(key_route[pl.ds(place[4], 1)]), rows)
    feed_select[...] = hot(as_column(feed_route[...]), rows)
    query_doc[...] = jnp.where(place[0] + queries >= place[1], 1, 0)


def pack_body(
    place, key_spots, tokens, key_route, q_l, k_l, v_l,
    gate_s, up_s, down_s, gate_l, up_l, down_l, second, third, expert_keep, expert_send, key_docs
):
    part, width = q_l.shape
    at = 0
    for ref in (q_l, k_l, v_l):
        second[:, at : at + ref.shape[1]] = ref[...]
        at += ref.shape[1]
    keyed = nn(hot(as_column(key_route[pl.ds(place[4], 1)]), tokens.shape[0]), tokens[...])
    second[:, at : at + width] = keyed[:part].astype(BF16)
    rest = keyed[part:]
    chunk = width * rest.shape[0] // part
    pieces = [rest[:, i * chunk : (i + 1) * chunk] for i in range(width // chunk)]
    second[:, at + width :] = jnp.concatenate(pieces, axis=0).astype(BF16)
    narrow = gate_s.shape[1]
    for i, ref in enumerate((gate_s, up_s, down_s)):
        third[:, i * narrow : (i + 1) * narrow] = ref[...]
    share = expert_keep.shape[1] // 3
    depth = expert_keep.shape[0] // part
    for c, expert in enumerate((expert_keep, expert_send)):
        for k in range(depth):
            at = ((place[5] ^ c) * depth + (place[6] ^ k)) * share
            at = pl.ds(pl.multiple_of(at, share), share)
            for i, ref in enumerate((gate_l, up_l, down_l)):
                expert[k * part : (k + 1) * part, i * share : (i + 1) * share] = ref[:, at]
    blocks, slots = key_route.shape
    keys = key_spots.shape[1]
    block = lax.broadcasted_iota(jnp.int32, (blocks, keys), 0) == key_spots[0:1]
    table = key_route[...].astype(F32).T.astype(BF16)
    found = nn(table, jnp.where(block, 1.0, 0.0).astype(BF16))
    slot = lax.broadcasted_iota(jnp.int32, (slots, keys), 0) == key_spots[1:2]
    position = jnp.sum(jnp.where(slot, found, 0.0), 0, keepdims=True).astype(jnp.int32)
    rows = tokens.shape[0]
    document = jnp.where(key_spots[0:1] * rows + position >= place[1], 1, 0)
    key_docs[...] = jnp.where(position < rows, document, -1)


def prepare_body(to_own, above, tokens, below, raw):
    order = to_own[...]
    at = 0
    for ref in (above, tokens, below):
        raw[at : at + ref.shape[0]] = nn(ref[...], order).astype(BF16)
        at += ref.shape[0]


def unpack_body(place, keep, got, gate, up, down):
    part = gate.shape[0]
    depth = keep.shape[0] // part
    share = keep.shape[1] // 3
    for c, source in enumerate((keep, got)):
        for k in range(depth):
            at = ((place[5] ^ c) * depth + (place[6] ^ k)) * share
            at = pl.ds(pl.multiple_of(at, share), share)
            for i, out in enumerate((gate, up, down)):
                piece = source[k * part : (k + 1) * part, i * share : (i + 1) * share]
                out[:, at] = piece.astype(F32)


def pair_up(shard, first, second, part):
    count = first.shape[0] // part
    width = first.shape[1]
    whole, own = (0, part), (0, width)
    outs = []
    for k in range(count):
        at = (k * part, (k + 1) * part)
        moves = [(0, whole, (0, 2 * width), 0, 0), (1, at, own, part, 0), (2, at, own, part, width)]
        outs.append(((2 * part, 2 * width), moves))
    return rearrange("pair_up", (shard, first, second), outs)


def stack_both(pieces, name="stack_both"):
    height = sum(p.shape[0] for p in pieces)
    width = pieces[0].shape[1]
    moves, row = [], 0
    for i, piece in enumerate(pieces):
        n = piece.shape[0] // 2
        moves.append((i, (0, n), (0, width), row, 0))
        moves.append((i, (n, 2 * n), (0, width), height // 2 + row, 0))
        row += n
    return rearrange(name, pieces, [((height, width), moves)])[0]


def part_both(pieces, name):
    height = sum(p.shape[0] for p in pieces) // 2
    width = pieces[0].shape[1]
    first, second, row = [], [], 0
    for i, piece in enumerate(pieces):
        n = piece.shape[0] // 2
        first.append((i, (0, n), (0, width), row, 0))
        second.append((i, (n, 2 * n), (0, width), row, 0))
        row += n
    return rearrange(name, pieces, [((height, width), first), ((height, width), second)])


def take_apart(pieces, part):
    width = pieces[0].shape[1] // 2
    outs = []
    for side in range(2):
        columns = (side * width, (side + 1) * width)
        moves = [(k, (0, part), columns, k * part, 0) for k in range(len(pieces))]
        outs.append(((len(pieces) * part, width), moves))
    return rearrange("take_apart", pieces, outs)


def local_mask(place, tile, reach, stacked, span):
    shape = (stacked, span)
    row = lax.broadcasted_iota(jnp.int32, shape, 0) & (reach - 1)
    query = place[0] + tile * reach + row
    key = place[0] + (tile - 1) * reach + lax.broadcasted_iota(jnp.int32, shape, 1)
    split, live, total = place[1], place[1] + place[2], place[3]
    inside = (key >= 0) & (key < total)
    same = jnp.where(query >= split, 1, 0) == jnp.where(key >= split, 1, 0)
    near = jnp.abs(query - key) <= reach
    both = ((query < live) & (key < live)) | (query == key)
    return near & inside & same & both


def light_rows_body(raw, w0, w1, normed, queries, pairs, vectors):
    light = HL * HDL
    reach = RADIUS
    rows = queries.shape[0]
    columns = [w[:, 3 * light :].astype(F32).T[:8] for w in (w0, w1)]
    vectors[...] = jnp.concatenate(columns, axis=1)
    unit, unused = unit_rms(raw[...].astype(F32))
    normed[...] = (unit * vectors[0:1]).astype(BF16)
    own = normed[reach : reach + rows]
    queries[...] = into(own, w0[:, :light], w1[:, :light]).astype(BF16)
    pairs[...] = into(normed[...], w0[:, light : 3 * light], w1[:, light : 3 * light]).astype(BF16)


def light_forward_body(place, queries, pairs, mixed, sums):
    light = HL * HDL
    reach = RADIUS
    rows = queries.shape[0]
    scale = 1.0 / math.sqrt(HDL)
    lane = lanes(reach)
    for tile in range(rows // reach):
        mine = slice(tile * reach, (tile + 1) * reach)
        seen = slice(tile * reach, (tile + 3) * reach)
        mask = local_mask(place, tile, reach, 2 * reach, 3 * reach)

        def pair(p, logs):
            query = both_heads(queries[mine, pair_at(p)])
            scores = jnp.where(mask, nt(query, pairs[seen, pair_at(p)]) * scale, NEG)
            top = jnp.max(scores, -1, keepdims=True)
            expo = jnp.exp(scores - top)
            total = jnp.sum(expo, -1, keepdims=True)
            probs = (expo * (1.0 / total)).astype(BF16)
            mixed[mine, pair_at(p)] = one_pair(nn(probs, pairs[seen, pair_at(p, light)])).astype(BF16)
            log = top + jnp.log(total)
            logs = jnp.where(lane == 2 * p, log[:reach], logs)
            return jnp.where(lane == 2 * p + 1, log[reach:], logs)

        logs = lax.fori_loop(0, HL // 2, pair, jnp.zeros((reach, 128), F32))
        sums[mine] = logs


def piece_select(block_rows, rest, part, piece):
    shape = (block_rows // part * rest, block_rows)
    k = lax.broadcasted_iota(jnp.int32, shape, 0)
    row = lax.broadcasted_iota(jnp.int32, shape, 1)
    shift = rest.bit_length() - 1
    want = (k >> shift) * part + piece * rest + (k & (rest - 1))
    return jnp.where(row == want, 1.0, 0.0).astype(BF16)


def heavy_rows_body(slots, vectors, to_own, s0, s1, keyed, held):
    width = to_own.shape[0]
    half = s0.shape[0]
    at = 3 * HH * HDH
    part = half // (keyed.shape[0] // slots // 2)
    rest = slots - part
    chunk = width * rest // part
    for i, ref in enumerate((s0, s1)):
        held[i * half : (i + 1) * half] = ref[:, at : at + width]
        low = 2 * half + i * (half // part * rest)
        for piece in range(part // rest):
            picked = nn(piece_select(half, rest, part, piece), ref[:, at + width :])
            held[low : low + half // part * rest, piece * chunk : (piece + 1) * chunk] = picked.astype(BF16)
    step = 256

    def project(t, carry):
        rows = pl.ds(pl.multiple_of(t * step, step), step)
        unit, unused = unit_rms(nn(held[rows], to_own[...]))
        keyed[rows] = (unit * vectors[0:1]).astype(BF16)
        return carry

    lax.fori_loop(0, keyed.shape[0] // step, project, 0)


def heavy_pairs_body(select, normed, keyed, s0, s1, pairs, routed, queries):
    heavy = HH * HDH
    q_at = slice(0, heavy)
    kv_at = slice(heavy, 3 * heavy)
    step = 256

    def project(t, carry):
        rows = pl.ds(pl.multiple_of(t * step, step), step)
        pairs[rows] = into(keyed[rows], s0[:, kv_at], s1[:, kv_at]).astype(BF16)
        return carry

    lax.fori_loop(0, keyed.shape[0] // step, project, 0)
    own = normed[RADIUS : normed.shape[0] - RADIUS]
    routed[...] = nn(select[...], own).astype(BF16)
    queries[...] = into(routed[...], s0[:, q_at], s1[:, q_at]).astype(BF16)


def heavy_forward_body(query_doc, key_doc, queries, pairs, mixed, sums):
    heavy = HH * HDH
    slots = queries.shape[0]
    scale = 1.0 / math.sqrt(HDH)
    mask = jnp.concatenate([query_doc[...], query_doc[...]], axis=0) == key_doc[...]

    def pair(p, logs):
        scores = jnp.where(mask, nt(both_heads(queries[:, pair_at(p)]), pairs[:, pair_at(p)]) * scale, NEG)
        top = jnp.max(scores, -1, keepdims=True)
        expo = jnp.exp(scores - top)
        total = jnp.sum(expo, -1, keepdims=True)
        probs = (expo * (1.0 / total)).astype(BF16)
        mixed[:, pair_at(p)] = one_pair(nn(probs, pairs[:, pair_at(p, heavy)])).astype(BF16)
        return jnp.where(lanes(2 * slots) == p, top + jnp.log(total), logs)

    logs = lax.fori_loop(0, HH // 2, pair, jnp.zeros((2 * slots, 128), F32))
    sums[...] = logs


def join_body(
    raw, light_mixed, heavy_mixed, routed, query_select, feed_select, vectors, cot, to_own, s0, s1,
    middle, normed, heavy_branch, feed_rows, feed_grads, sent
):
    heavy = HH * HDH
    width = raw.shape[1]
    rows = middle.shape[0]
    at = slice(heavy, heavy + HL * HDL)
    light_branch = onto(light_mixed[...], s0[:, at], s1[:, at])
    at = slice(0, heavy)
    heavy_branch[...] = onto(heavy_mixed[...], s0[:, at], s1[:, at])
    score = sigmoid(jnp.sum(routed[...].astype(F32) * vectors[1:2], -1, keepdims=True))
    inputs = raw[RADIUS : RADIUS + rows].astype(F32)
    middle[...] = inputs + light_branch + place_rows(query_select[...], score * heavy_branch[...])
    unit, unused = unit_rms(middle[...])
    normed[...] = (unit * vectors[2:3]).astype(BF16)
    feed_rows[...] = nn(feed_select[...], normed[...]).astype(BF16)
    feed_grads[...] = nn(feed_select[...], cot[...])
    score = sigmoid(jnp.sum(feed_rows[...].astype(F32) * vectors[3:4], -1, keepdims=True))
    sent[:, :width] = nt(feed_rows[...], to_own[...]).astype(BF16)
    sent[:, width:] = nt((score * feed_grads[...]).astype(BF16), to_own[...]).astype(BF16)


def geglu_rows(gate, upper, grad_hidden):
    c0, c1 = 0.7978845608028654, 0.044715
    square = gate * gate
    bent = jnp.tanh(c0 * gate * (1.0 + c1 * square))
    bell = 0.5 * (1.0 + bent)
    gelu = gate * bell
    slope = bell + 0.5 * gate * (1.0 - bent * bent) * (c0 * (1.0 + 3.0 * c1 * square))
    return gelu * upper, grad_hidden * upper * slope, grad_hidden * gelu


def geglu_loop(wide, grad_hidden, hidden, grads):
    count = hidden.shape[1]
    step = 32

    def rows_at(t, carry):
        rows = pl.ds(pl.multiple_of(t * step, step), step)
        out, grad_gate, grad_upper = geglu_rows(
            wide[rows, :count], wide[rows, count:], grad_hidden[rows]
        )
        hidden[rows] = out.astype(BF16)
        grads[rows, :count] = grad_gate.astype(BF16)
        grads[rows, count:] = grad_upper.astype(BF16)
        return carry

    lax.fori_loop(0, hidden.shape[0] // step, rows_at, 0)


def feed_body(normed, cot, t0, t1, feed, grad_normed, hidden, grads, wide, grad_hidden):
    narrow = hidden.shape[1]
    wide[...] = into(normed[...], t0[:, : 2 * narrow], t1[:, : 2 * narrow])
    grad_hidden[...] = into(cot[...], t0[:, 2 * narrow :], t1[:, 2 * narrow :])
    geglu_loop(wide, grad_hidden, hidden, grads)
    feed[...] = onto(hidden[...], t0[:, 2 * narrow :], t1[:, 2 * narrow :])
    grad_normed[...] = onto(grads[...], t0[:, : 2 * narrow], t1[:, : 2 * narrow])


def feed_weight_body(normed, cot, hidden, grads, keep, send):
    narrow = hidden.shape[1]
    half = keep.shape[0]
    for out, at in ((send, slice(half, None)), (keep, slice(0, half))):
        out[:, : 2 * narrow] = tn(normed[:, at], grads[...]).astype(out.dtype)
        out[:, 2 * narrow :] = tn(cot[:, at], hidden[...]).astype(out.dtype)


def expert_body(got0, got1, to_slice, weights, keep, send, grad_keep, grad_send, rows, row_grads, wide, grad_hidden, hidden, grads):
    width = to_slice.shape[0]
    share = hidden.shape[1]
    count = got0.shape[0]
    for i, got in enumerate((got0, got1)):
        at = slice(i * count, (i + 1) * count)
        rows[at] = nn(got[:, :width], to_slice[...]).astype(BF16)
        row_grads[at] = nn(got[:, width:], to_slice[...]).astype(BF16)
    first, second = weights[:, : 2 * share], weights[:, 3 * share : 5 * share]
    first_down, second_down = weights[:, 2 * share : 3 * share], weights[:, 5 * share :]
    wide[...] = into(rows[...], first, second)
    grad_hidden[...] = into(row_grads[...], first_down, second_down)
    geglu_loop(wide, grad_hidden, hidden, grads)
    for out, at in ((send, slice(count, None)), (keep, slice(0, count))):
        feed = onto(hidden[at], first_down, second_down).astype(BF16)
        back = onto(grads[at], first, second).astype(BF16)
        out[:, :width] = nt(feed, to_slice[...]).astype(out.dtype)
        out[:, width:] = nt(back, to_slice[...]).astype(out.dtype)
    half = weights.shape[0]
    low = grad_keep.shape[0]
    for i in range(2):
        at = slice(i * half, (i + 1) * half)
        to = 3 * share * i
        for left, right, columns in (
            (rows, grads, slice(to, to + 2 * share)), (row_grads, hidden, slice(to + 2 * share, to + 3 * share))
        ):
            product = tn(left[:, at], right[...]).astype(BF16)
            grad_keep[:, columns] = product[:low]
            grad_send[:, columns] = product[low:]


def turn_body(*refs):
    pieces = refs[:-12]
    (
        middle, feed, grad_normed, feed_rows, feed_grads, feed_select, vectors, cot, to_own,
        result, grad_middle, vector_grads,
    ) = refs[-12:]
    width = middle.shape[1]
    summed = pieces[0][...].astype(F32)
    for piece in pieces[1:]:
        summed = summed + piece[...].astype(F32)
    feed_heavy = reorder(summed[:, :width], to_own[...])
    grad_rows = reorder(summed[:, width:], to_own[...])
    rows = feed_rows[...].astype(F32)
    score = sigmoid(jnp.sum(rows * vectors[3:4], -1, keepdims=True))
    logit = jnp.sum(feed_grads[...] * feed_heavy, -1, keepdims=True) * score * (1.0 - score)
    grad_rows = grad_rows + logit * vectors[3:4]
    grads = grad_normed[...] + place_rows(feed_select[...], grad_rows)
    unit, scale = unit_rms(middle[...])
    grad_middle[...] = cot[...].astype(F32) + norm_back(grads, vectors[2:3], unit, scale)
    vector_grads[...] = jnp.concatenate(
        [
            jnp.zeros((2, width), F32),
            jnp.sum(grads * unit, 0, keepdims=True),
            jnp.sum(rows * logit, 0, keepdims=True),
            jnp.zeros((4, width), F32),
        ],
        axis=0,
    )
    out = middle[...] + feed[...] + place_rows(feed_select[...], score * feed_heavy)
    result[...] = nt(out.astype(BF16), to_own[...]).astype(BF16)


def heavy_scores_body(
    query_doc, key_doc, grad_middle, query_select, routed, pairs, queries, heavy_branch, sums, vectors, s0, s1,
    grad_branch, grad_queries, grad_pairs, logits, held
):
    heavy = HH * HDH
    score = sigmoid(jnp.sum(routed[...].astype(F32) * vectors[1:2], -1, keepdims=True))
    grad_rows = take_rows(query_select[...], grad_middle[...])
    grad_branch[...] = (score * grad_rows).astype(BF16)
    logit = jnp.sum(grad_rows * heavy_branch[...], -1, keepdims=True) * score * (1.0 - score)
    logits[...] = jnp.broadcast_to(logit, logits.shape)
    at = slice(0, heavy)
    grad_mixed = into(grad_branch[...], s0[:, at], s1[:, at]).astype(BF16)
    scale = 1.0 / math.sqrt(HDH)
    mask = jnp.concatenate([query_doc[...], query_doc[...]], axis=0) == key_doc[...]
    held[...] = grad_mixed
    logs = sums[...]

    def pair(p, carry):
        query = both_heads(queries[:, pair_at(p)])
        grad_out = both_heads(held[:, pair_at(p)])
        key = pairs[:, pair_at(p)]
        scores = jnp.where(mask, nt(query, key) * scale, NEG)
        probs = jnp.exp(scores - column_at(logs, p))
        grad_probs = nt(grad_out, pairs[:, pair_at(p, heavy)])
        delta = jnp.sum(probs * grad_probs, -1, keepdims=True)
        grad_scores = (probs * (grad_probs - delta)).astype(BF16)
        grad_queries[:, pair_at(p)] = one_pair(nn(grad_scores, key) * scale).astype(BF16)
        grad_pairs[:, pair_at(p)] = (tn(grad_scores, query) * scale).astype(BF16)
        grad_pairs[:, pair_at(p, heavy)] = tn(probs.astype(BF16), grad_out).astype(BF16)
        return carry

    lax.fori_loop(0, HH // 2, pair, 0)


def heavy_weights_body(
    grad_middle, routed, keyed, light_mixed, heavy_mixed, grad_branch, grad_queries, grad_pairs, logits, vectors, to_own, s0, s1,
    keep, send, vector_grads, moved
):
    width = grad_middle.shape[1]
    heavy = HH * HDH
    light = HL * HDL
    half = s0.shape[0]
    slots = routed.shape[0]
    q_at = slice(width + light, width + light + heavy)
    kv_at = slice(width + light + heavy, width + light + 3 * heavy)
    logit = logits[:, 0:1]
    step = 256

    def back(t, gain):
        rows = pl.ds(pl.multiple_of(t * step, step), step)
        grads = onto(grad_pairs[rows], s0[:, heavy : 3 * heavy], s1[:, heavy : 3 * heavy])
        moved[rows] = nt(grads.astype(BF16), to_own[...]).astype(BF16)
        return gain + jnp.sum(grads * keyed[rows].astype(F32), 0, keepdims=True)

    gain = lax.fori_loop(0, keyed.shape[0] // step, back, jnp.zeros((1, width), F32))
    vector_grads[...] = jnp.concatenate(
        [
            gain / vectors[0:1],
            jnp.sum(routed[...].astype(F32) * logit, 0, keepdims=True),
            jnp.zeros((6, width), F32),
        ],
        axis=0,
    )
    low = grad_middle[...].astype(BF16)
    part = half // (keyed.shape[0] // slots // 2)
    rest = slots - part
    chunk = width * rest // part
    for i, out in ((1, send), (0, keep)):
        at = slice(i * half, (i + 1) * half)
        out[:, :width] = tn(grad_branch[:, at], heavy_mixed[...]).astype(BF16)
        out[:, width : width + light] = tn(low[:, at], light_mixed[...]).astype(BF16)
        out[:, q_at] = tn(routed[:, at], grad_queries[...]).astype(BF16)
        out[:, kv_at] = tn(keyed[:, at], grad_pairs[...]).astype(BF16)
        to = width + light + 3 * heavy
        out[:, to : to + width] = moved[at]
        at = 2 * half + i * (half // part * rest)
        total = 0.0
        for piece in range(part // rest):
            block = moved[at : at + half // part * rest, piece * chunk : (piece + 1) * chunk]
            total = total + tn(piece_select(half, rest, part, piece), block)
        out[:, to + width :] = total.astype(BF16)


def routed_body(grad_queries, logits, vectors, s0, s1, grad_routed):
    at = slice(0, HH * HDH)
    grad_routed[...] = onto(grad_queries[...], s0[:, at], s1[:, at]) + logits[:, 0:1] * vectors[1:2]


def light_scores_body(place, grad_middle, queries, pairs, sums, s0, s1, grad_queries, grad_pairs, held, grad_out_all):
    light = HL * HDL
    heavy = HH * HDH
    reach = RADIUS
    rows = queries.shape[0]
    at = slice(heavy, heavy + light)
    grad_out_all[...] = into(grad_middle[...].astype(BF16), s0[:, at], s1[:, at]).astype(BF16)
    held[...] = jnp.zeros_like(held)
    scale = 1.0 / math.sqrt(HDL)
    for tile in range(rows // reach):
        mine = slice(tile * reach, (tile + 1) * reach)
        seen = slice(tile * reach, (tile + 3) * reach)
        mask = local_mask(place, tile, reach, 2 * reach, 3 * reach)
        logs = sums[mine]

        def pair(p, carry):
            query = both_heads(queries[mine, pair_at(p)])
            grad_out = both_heads(grad_out_all[mine, pair_at(p)])
            key = pairs[seen, pair_at(p)]
            log = jnp.concatenate([column_at(logs, 2 * p), column_at(logs, 2 * p + 1)], axis=0)
            probs = jnp.exp(jnp.where(mask, nt(query, key) * scale, NEG) - log)
            grad_probs = nt(grad_out, pairs[seen, pair_at(p, light)])
            delta = jnp.sum(probs * grad_probs, -1, keepdims=True)
            grad_scores = (probs * (grad_probs - delta)).astype(BF16)
            grad_queries[mine, pair_at(p)] = one_pair(nn(grad_scores, key) * scale).astype(BF16)
            held[seen, pair_at(p)] = held[seen, pair_at(p)] + tn(grad_scores, query) * scale
            beyond = pair_at(p, light)
            held[seen, beyond] = held[seen, beyond] + tn(probs.astype(BF16), grad_out)
            return carry

        lax.fori_loop(0, HL // 2, pair, 0)
    grad_pairs[...] = held[...].astype(BF16)


def light_weights_body(
    raw, normed, grad_queries, grad_pairs, grad_routed, query_select, feed_vectors, heavy_vectors, to_own, f0, f1,
    keep, send, outer, grad_mine
):
    light = HL * HDL
    reach = RADIUS
    rows = grad_queries.shape[0]
    half = f0.shape[0]
    grads = onto(grad_pairs[...], f0[:, light : 3 * light], f1[:, light : 3 * light])
    for i, at in enumerate((slice(0, reach), slice(reach + rows, None))):
        outer[i * reach : (i + 1) * reach] = nt(grads[at].astype(BF16), to_own[...]).astype(BF16)
    own = onto(grad_queries[...], f0[:, :light], f1[:, :light])
    own = own + grads[reach : reach + rows] + place_rows(query_select[...], grad_routed[...])
    grad_mine[...] = own
    unit, unused = unit_rms(raw[...].astype(F32))
    gain = jnp.sum(own * unit[reach : reach + rows], 0, keepdims=True)
    for at in (slice(0, reach), slice(reach + rows, None)):
        gain = gain + jnp.sum(grads[at] * unit[at], 0, keepdims=True)
    vector_rows = feed_vectors[...] + heavy_vectors[...]
    first = lax.broadcasted_iota(jnp.int32, vector_rows.shape, 0) == 0
    vector_rows = vector_rows + jnp.where(first, gain, 0.0)
    filler = jnp.zeros((120, raw.shape[1]), F32)
    columns = jnp.concatenate([vector_rows, filler], axis=0)
    for i, out in ((1, send), (0, keep)):
        at = slice(i * half, (i + 1) * half)
        out[:, :light] = tn(normed[reach : reach + rows, at], grad_queries[...]).astype(BF16)
        out[:, light : 3 * light] = tn(normed[:, at], grad_pairs[...]).astype(BF16)
        out[:, 3 * light :] = columns[:, at].T.astype(BF16)


def halo_body(from_prev, from_next, grad_mine, to_own, out):
    reach = RADIUS
    rows = grad_mine.shape[0]
    order = to_own[...]
    out[...] = grad_mine[...]
    out[:reach] = out[:reach] + nn(from_prev[...], order)
    out[rows - reach :] = out[rows - reach :] + nn(from_next[...], order)


def finish_body(keyed_grads, key_select, grads, grad_middle, raw, vectors, to_own, out):
    reach = RADIUS
    rows, width = grads.shape
    order = to_own[...]
    keyed = keyed_grads[...]
    if keyed.shape[0] < key_select.shape[0]:
        rest = key_select.shape[0] - keyed.shape[0]
        tail = [keyed[i * rest : (i + 1) * rest, width:] for i in range(keyed.shape[0] // rest)]
        keyed = jnp.concatenate([keyed[:, :width], jnp.concatenate(tail, axis=1)], axis=0)
    keyed = nn(keyed.astype(BF16), order).astype(BF16)
    total = grads[...] + tn(key_select[...], keyed)
    unit, scale = unit_rms(raw[reach : reach + rows].astype(F32))
    total = grad_middle[...] + norm_back(total, vectors[0:1], unit, scale)
    out[...] = reorder_back(total, order)


def heavy_forward_wide(query_doc, key_doc, select, normed, vectors, to_own, s0, s1, keyed_raw):
    heavy = HH * HDH
    q_at, kv_at = slice(0, heavy), slice(heavy, 3 * heavy)
    unit, unused = unit_rms(nn(keyed_raw, to_own))
    keyed = (unit * vectors[0:1]).astype(BF16)
    pairs = into(keyed, s0[:, kv_at], s1[:, kv_at]).astype(BF16)
    routed = nn(select, normed[RADIUS : normed.shape[0] - RADIUS]).astype(BF16)
    queries = into(routed, s0[:, q_at], s1[:, q_at]).astype(BF16)

    def heads(array):
        return array.reshape(-1, HH, HDH)

    scores = jnp.einsum(
        "qhd,khd->hqk", heads(queries), heads(pairs[:, :heavy]), preferred_element_type=F32
    ) / math.sqrt(HDH)
    probs = soft(jnp.where((query_doc == key_doc)[None], scores, NEG))
    mixed = jnp.einsum(
        "hqk,khd->qhd", probs.astype(BF16), heads(pairs[:, heavy:]), preferred_element_type=F32
    )
    return keyed, pairs, routed, queries, mixed.reshape(-1, heavy).astype(BF16), probs


def heavy_backward_wide(
    grad_middle, query_select, routed, keyed, pairs, queries, light_mixed, heavy_mixed, heavy_branch, probs,
    vectors, to_own, o0, o1, s0, s1
):
    heavy = HH * HDH
    scale = 1.0 / math.sqrt(HDH)
    half = s0.shape[0]
    q_at, kv_at = slice(0, heavy), slice(heavy, 3 * heavy)
    score = sigmoid(jnp.sum(routed.astype(F32) * vectors[1:2], -1, keepdims=True))
    grad_rows = take_rows(query_select, grad_middle)
    grad_branch = (score * grad_rows).astype(BF16)
    logit = jnp.sum(grad_rows * heavy_branch, -1, keepdims=True) * score * (1.0 - score)
    at = slice(0, heavy)
    grad_mixed = into(grad_branch, o0[:, at], o1[:, at]).astype(BF16)

    def heads(array):
        return array.reshape(-1, HH, HDH)

    def mix(pattern, left, right):
        return jnp.einsum(pattern, left, right, preferred_element_type=F32)

    grad_probs = mix("qhd,khd->hqk", heads(grad_mixed), heads(pairs[:, heavy:]))
    delta = jnp.sum(probs * grad_probs, -1, keepdims=True)
    grad_scores = (probs * (grad_probs - delta)).astype(BF16)
    grad_queries = mix("hqk,khd->qhd", grad_scores, heads(pairs[:, :heavy])) * scale
    grad_queries = grad_queries.reshape(-1, heavy).astype(BF16)
    grad_keys = mix("hqk,qhd->khd", grad_scores, heads(queries)) * scale
    grad_values = mix("hqk,qhd->khd", probs.astype(BF16), heads(grad_mixed))
    grad_pairs = jnp.concatenate(
        [grad_keys.reshape(-1, heavy).astype(BF16), grad_values.reshape(-1, heavy).astype(BF16)], axis=1
    )
    grad_routed = onto(grad_queries, s0[:, q_at], s1[:, q_at]) + logit * vectors[1:2]
    grads = onto(grad_pairs, s0[:, kv_at], s1[:, kv_at])
    vector_grads = jnp.concatenate(
        [
            jnp.sum(grads * keyed.astype(F32), 0, keepdims=True) / vectors[0:1],
            jnp.sum(routed.astype(F32) * logit, 0, keepdims=True),
            jnp.zeros((6, grads.shape[1]), F32),
        ],
        axis=0,
    )
    moved = nt(grads.astype(BF16), to_own).astype(BF16)
    low = grad_middle.astype(BF16)
    sides = []
    for at in (slice(0, half), slice(half, None)):
        columns = (
            tn(grad_branch[:, at], heavy_mixed),
            tn(low[:, at], light_mixed),
            tn(routed[:, at], grad_queries),
            tn(keyed[:, at], grad_pairs),
        )
        sides.append(jnp.concatenate(columns, axis=1).astype(BF16))
    return sides[0], sides[1], grad_routed, vector_grads, moved


def per_device(
    tokens,
    query_small,
    key_small,
    value_small,
    out_small,
    query_large,
    key_large,
    value_large,
    out_large,
    attend_gain,
    attend_router,
    gate_small,
    up_small,
    down_small,
    gate_large,
    up_large,
    down_large,
    feed_gain,
    feed_router,
    lengths,
    query_route,
    key_route,
    feed_route,
    cotangent,
):
    net = Net()
    rows, width = tokens.shape
    blocks = net.count
    part = width // blocks
    half = width // 2
    first = net.device * rows
    light = HL * HDL
    heavy = HH * HDH
    narrow = down_small.shape[0]
    wide = down_large.shape[0]
    slots = query_route.shape[1]
    members = 2 * net.depth
    share = wide // members
    pooled = members * slots
    keys = blocks * slots
    rest = slots - part
    packed = part % 8 == 0 and rest > 0 and rest % 8 == 0 and part % rest == 0 and keys <= 2048

    step = [(i, i + 1) for i in range(blocks - 1)]
    back = [(i + 1, i) for i in range(blocks - 1)]
    vector_pack = jnp.stack([attend_gain, attend_router, feed_gain, feed_router], axis=1)
    vector_pack = jnp.pad(vector_pack, ((0, 0), (0, 124)))
    first_pack = (query_small, key_small, value_small, vector_pack, out_large.T, out_small.T)
    moves, at = [], 0
    for i, piece in enumerate(first_pack):
        moves.append((i, (0, part), (0, piece.shape[1]), 0, at))
        at += piece.shape[1]
    (first_set,) = rearrange("pack_first", first_pack, [((part, at), moves)], room=56 << 20)
    first_parts = net.from_z(first_set)
    cut = 3 * light + vector_pack.shape[1]
    column = jnp.arange(width, dtype=jnp.int32)
    own_order = net.target(column // part) * part + column % part
    bits = column % half // (part * net.depth)
    bits = jnp.where(net.core == 1, bits, reverse_bits(bits, net.levels))
    member = (net.core ^ (column // half)) * net.depth + (net.z ^ (column // part % net.depth))
    slice_order = ((net.pair ^ bits) * members + member) * part + column % part
    orders = jnp.stack([own_order, slice_order])
    place = jnp.stack([first, lengths[0], lengths[1], jnp.int32(rows * blocks), net.device, net.core, net.z])
    square = ((width, width), BF16)
    chosen = ((slots, rows), BF16)

    if packed:
        tall = blocks * part
        spot = jnp.arange(keys, dtype=jnp.int32)
        spot_block = jnp.where(spot < tall, spot // part, (spot - tall) // rest)
        spot_slot = jnp.where(spot < tall, spot % part, part + (spot - tall) % rest)
        second_set, third_set, slices_keep, slices_send, key_docs = run(
            pack_body,
            "pack",
            [
                ((part, 4 * width + width * rest // part), BF16),
                ((part, 3 * narrow), BF16),
                ((net.depth * part, 3 * share), BF16),
                ((net.depth * part, 3 * share), BF16),
                ((1, keys), jnp.int32),
            ],
            (
                place, jnp.stack([net.target(spot_block), spot_slot]), tokens, key_route,
                query_large, key_large, value_large,
                gate_small, up_small, down_small.T, gate_large, up_large, down_large.T,
            ),
            smem=1,
            room=56 << 20,
        )
    else:
        second_set = jnp.concatenate([query_large, key_large, value_large], axis=1)
        third_set = jnp.concatenate([gate_small, up_small, down_small.T], axis=1)
        stacked = jnp.stack([gate_large, up_large, down_large.T], axis=0)
        stacked = stacked.reshape(3, part, members, share).transpose(2, 1, 0, 3)
        stacked = jnp.take(stacked.reshape(members, part, 3 * share), net.members(), axis=0)
        slices_keep, slices_send = stacked.reshape(2, net.depth * part, 3 * share)
    order = Order()
    top_bit = net.levels - 1

    def take_z(pieces):
        return order.note(stack_rows([order.hold(pieces[0])] + pieces[1:]))

    def take(whole, moved):
        return order.note(stack_rows([whole, order.hold(moved)]))

    def first_moved(whole):
        return net.by_bit(whole, 0)

    def rest_moved(whole, moved):
        for j in range(1, net.levels):
            whole = take(whole, moved)
            moved = net.by_bit(whole, j)
        return whole, moved

    order.note(second_set)
    first_set = take_z(first_parts)
    first_moving = first_moved(first_set)
    second_parts = net.from_z(after(second_set, first_set))
    slices_got = net.by_core(slices_send)
    to_own, to_slice = run(orders_body, "orders", [square, square], (order.hold(orders),))
    order.note(to_own)
    third_parts = pair_up(third_set, order.hold(slices_keep), slices_got, part)
    order.note(third_parts[0])
    first_set, first_moving = rest_moved(first_set, first_moving)
    second_set = take_z(second_parts)
    third_parts = net.exchange_z([after(p, second_set) for p in third_parts])
    cot, query_select, key_select, feed_select, query_docs = run(
        select_body,
        "select",
        [((rows, width), BF16), chosen, chosen, chosen, ((slots, 1), jnp.int32)],
        (place, to_own, query_route, key_route, feed_route, order.hold(cotangent)),
        smem=1,
    )
    order.note(cot)
    a0 = take(first_set, first_moving)
    a1 = net.by_core(a0)
    f0, f1 = (Columns(a, 0, cut) for a in (a0, a1))
    o0, o1 = (Columns(a, cut, a0.shape[1]) for a in (a0, a1))
    second_moving = first_moved(after(second_set, a0))
    second_set, second_moving = rest_moved(second_set, second_moving)
    third_set = order.note(stack_both([order.hold(third_parts[0])] + third_parts[1:], "weave"))
    third_moving = first_moved(third_set)
    near_tokens = after(tokens, third_set)
    above = lax.ppermute(near_tokens[rows - RADIUS :], AXES, step)
    below = lax.ppermute(near_tokens[:RADIUS], AXES, back)
    s0 = take(second_set, second_moving)
    s1 = net.by_core(s0)
    (raw,) = run(
        prepare_body,
        "prepare",
        [((rows + 2 * RADIUS, width), BF16)],
        (order.hold(to_own), above, tokens, below),
    )
    order.note(raw)

    normed_ext, query_rows, pair_rows, vectors = run(
        light_rows_body,
        "light_rows",
        [
            ((rows + 2 * RADIUS, width), BF16),
            ((rows, light), BF16),
            ((rows + 2 * RADIUS, 2 * light), BF16),
            ((8, width), F32),
        ],
        (order.hold(raw), f0, f1),
    )
    order.note(query_rows)
    for j in range(1, net.levels):
        third_set = order.note(stack_both([third_set, order.hold(third_moving)]))
        third_moving = net.by_bit(third_set, j)
    light_mixed, light_sums = run(
        light_forward_body,
        "light_forward",
        [((rows, light), BF16), ((rows, 128), F32)],
        (place, order.hold(query_rows), pair_rows),
        smem=1,
    )
    order.note(light_mixed)
    if packed:
        (keyed,) = run(
            functools.partial(heavy_rows_body, slots),
            "heavy_rows",
            [((keys, width), BF16)],
            (order.hold(vectors), to_own, s0, s1),
            scratch=[pltpu.VMEM((keys, width), BF16)],
        )
        order.note(keyed)
        heavy_pairs, routed, routed_query = run(
            heavy_pairs_body,
            "heavy_pairs",
            [((keys, 2 * heavy), BF16), ((slots, width), BF16), ((slots, heavy), BF16)],
            (order.hold(query_select), normed_ext, keyed, s0, s1),
        )
        order.note(routed_query)
        heavy_mixed, heavy_sums = run(
            heavy_forward_body,
            "heavy_forward",
            [((slots, heavy), BF16), ((2 * slots, 128), F32)],
            (query_docs, key_docs, order.hold(routed_query), heavy_pairs),
        )
    else:
        relative = net.target(jnp.arange(blocks, dtype=jnp.int32))
        near_routes = jnp.take(key_route, relative, axis=0)
        key_docs = document_of(relative[:, None] * rows + near_routes, lengths)
        key_docs = jnp.where(near_routes < rows, key_docs, -1).reshape(1, -1)
        keyed_raw = net.gather(nn(key_select, tokens).astype(BF16))
        keyed, heavy_pairs, routed, routed_query, heavy_mixed, heavy_sums = heavy_forward_wide(
            query_docs, key_docs, query_select, normed_ext, vectors, to_own,
            s0, s1, jnp.concatenate(keyed_raw, axis=0),
        )
    order.note(heavy_mixed)

    middle, normed_two, heavy_branch, feed_rows, feed_grads, sent = run(
        join_body,
        "join",
        [
            ((rows, width), F32),
            ((rows, width), BF16),
            ((slots, width), F32),
            ((slots, width), BF16),
            ((slots, width), F32),
            ((slots, 2 * width), BF16),
        ],
        (
            raw, light_mixed, order.hold(heavy_mixed), routed, query_select, feed_select, vectors, cot, to_own, o0, o1,
        ),
    )
    order.note(sent)

    got_parts = net.from_z(sent)
    got0 = take_z(got_parts)
    got1 = net.by_core(got0)
    t0, expert = part_both([third_set, order.hold(third_moving)], "part_both")
    order.note(t0)
    t1 = net.by_core(t0)
    keep, send, expert_keep, expert_send = run(
        expert_body,
        "expert",
        [
            ((pooled // 2, 2 * width), BF16),
            ((pooled // 2, 2 * width), BF16),
            ((half // 2, 6 * share), BF16),
            ((half // 2, 6 * share), BF16),
        ],
        (order.hold(got0), got1, to_slice, expert),
        scratch=[
            pltpu.VMEM((pooled, width), BF16),
            pltpu.VMEM((pooled, width), BF16),
            pltpu.VMEM((pooled, 2 * share), F32),
            pltpu.VMEM((pooled, share), F32),
            pltpu.VMEM((pooled, share), BF16),
            pltpu.VMEM((pooled, 2 * share), BF16),
        ],
    )
    order.note(send)
    moving = net.by_core(send)
    expert_moving = net.by_bit(expert_send, top_bit)
    feed_light, grad_normed, hidden, hidden_grads = run(
        feed_body,
        "feed",
        [
            ((rows, width), F32),
            ((rows, width), F32),
            ((rows, narrow), BF16),
            ((rows, 2 * narrow), BF16),
        ],
        (order.hold(normed_two), cot, t0, t1),
        scratch=[pltpu.VMEM((rows, 2 * narrow), F32), pltpu.VMEM((rows, narrow), F32)],
    )
    order.note(hidden)
    def give(keep, moved, pieces):
        out = fold(keep, order.hold(moved), pieces)
        order.note(out[0])
        return out

    def descend(keep, moved):
        for j in reversed(range(net.levels - 1)):
            keep, send = give(keep, moved, 2)
            moved = net.by_bit(send, j)
        return keep, moved

    summed = net.exchange_z(give(keep, moving, net.depth))
    third_keep, third_send = run(
        feed_weight_body,
        "feed_weight",
        [((half, 3 * narrow), BF16), ((half, 3 * narrow), BF16)],
        (order.hold(normed_two), cot, hidden, hidden_grads),
    )
    order.note(third_send)
    third_moving = net.by_core(third_send)

    third_keep, third_send = give(third_keep, third_moving, 2)
    third_moving = net.by_bit(third_send, top_bit)

    result, grad_middle, feed_vectors = run(
        turn_body,
        "turn",
        [((rows, width), BF16), ((rows, width), F32), ((8, width), F32)],
        (
            order.hold(summed[0]), *summed[1:], middle, feed_light, grad_normed, feed_rows, feed_grads, feed_select,
            vectors, cot, to_own,
        ),
    )
    order.note(grad_middle)
    if packed:
        grad_branch, grad_queries, grad_heavy_pairs, logits = run(
            heavy_scores_body,
            "heavy_scores",
            [
                ((slots, width), BF16),
                ((slots, heavy), BF16),
                ((keys, 2 * heavy), BF16),
                ((slots, 128), F32),
            ],
            (
                query_docs, key_docs, order.hold(grad_middle), query_select, routed, heavy_pairs, routed_query,
                heavy_branch, heavy_sums, vectors, o0, o1,
            ),
            scratch=[pltpu.VMEM((slots, heavy), BF16)],
        )
        order.note(grad_branch)
    expert_keep, expert_moving = descend(expert_keep, expert_moving)
    if packed:
        second_keep, second_send, heavy_vectors = run(
            heavy_weights_body,
            "heavy_weights",
            [
                ((half, 5 * width + light + width * rest // part), BF16),
                ((half, 5 * width + light + width * rest // part), BF16),
                ((8, width), F32),
            ],
            (
                grad_middle, routed, keyed, light_mixed, heavy_mixed, order.hold(grad_branch), grad_queries,
                grad_heavy_pairs, logits, vectors, to_own, s0, s1,
            ),
            scratch=[pltpu.VMEM((keys, width), BF16)],
        )
    else:
        second_keep, second_send, grad_routed, heavy_vectors, keyed_grads = heavy_backward_wide(
            grad_middle, query_select, routed, keyed, heavy_pairs, routed_query, light_mixed, heavy_mixed,
            heavy_branch, heavy_sums, vectors, to_own, o0.array[:, cut:], o1.array[:, cut:], s0, s1,
        )
    order.note(second_send)
    second_moving = net.by_core(second_send)
    third_keep, third_moving = descend(third_keep, third_moving)
    expert_parts = net.exchange_z(give(expert_keep, expert_moving, net.depth))
    if packed:
        (grad_routed,) = run(
            routed_body,
            "routed",
            [((slots, width), F32)],
            (order.hold(grad_queries), logits, vectors, s0, s1),
        )
        order.note(grad_routed)
    second_keep, second_send = give(second_keep, second_moving, 2)
    second_moving = net.by_bit(second_send, top_bit)
    grad_queries, grad_pairs = run(
        light_scores_body,
        "light_scores",
        [((rows, light), BF16), ((rows + 2 * RADIUS, 2 * light), BF16)],
        (place, order.hold(grad_middle), query_rows, pair_rows, light_sums, o0, o1),
        smem=1,
        scratch=[pltpu.VMEM((rows + 2 * RADIUS, 2 * light), F32), pltpu.VMEM((rows, light), BF16)],
    )
    order.note(grad_queries)
    third_parts = net.exchange_z(give(third_keep, third_moving, net.depth))
    first_keep, first_send, outer, grad_mine = run(
        light_weights_body,
        "light_weights",
        [
            ((half, 3 * light + 128), BF16),
            ((half, 3 * light + 128), BF16),
            ((2 * RADIUS, width), BF16),
            ((rows, width), F32),
        ],
        (
            raw, normed_ext, order.hold(grad_queries), grad_pairs, grad_routed, query_select, feed_vectors, heavy_vectors,
            to_own, f0, f1,
        ),
    )
    order.note(first_send)
    first_moving = net.by_core(first_send)
    from_next = lax.ppermute(outer[:RADIUS], AXES, back)
    from_prev = lax.ppermute(outer[RADIUS:], AXES, step)

    expert_keep, expert_send = take_apart([order.hold(expert_parts[0])] + expert_parts[1:], part)
    order.note(expert_send)
    expert_got = net.by_core(expert_send)
    third_grad = settle([order.hold(third_parts[0])] + third_parts[1:], [narrow] * 3, "settle_third")
    order.note(third_grad[0])
    second_keep, second_moving = descend(second_keep, second_moving)
    first_keep, first_send = give(first_keep, first_moving, 2)
    first_moving = net.by_bit(first_send, top_bit)
    (grad_near,) = run(
        halo_body, "halo", [((rows, width), F32)], (from_prev, from_next, order.hold(grad_mine), to_own)
    )
    order.note(grad_near)
    if packed:
        gate_grad, up_grad, down_grad = run(
            unpack_body,
            "unpack",
            [((part, wide), F32)] * 3,
            (place, order.hold(expert_keep), expert_got),
            smem=1,
        )
    else:
        expert_grad = jnp.concatenate([order.hold(expert_keep), expert_got], axis=0)
        expert_grad = jnp.take(expert_grad.reshape(members, part, 3 * share), net.members(), axis=0)
        expert_grad = expert_grad.reshape(members, part, 3, share).transpose(2, 1, 0, 3)
        gate_grad, up_grad, down_grad = expert_grad.reshape(3, part, wide).astype(F32)
    order.note(gate_grad)
    second_parts = net.exchange_z(give(second_keep, second_moving, net.depth))
    first_keep, first_moving = descend(first_keep, first_moving)
    first_parts = net.exchange_z(give(first_keep, first_moving, net.depth))
    widths = [width, light, heavy, heavy, heavy]
    if packed:
        widths.append(width + width * rest // part)
    second_grad = settle([order.hold(second_parts[0])] + second_parts[1:], widths, "settle_second")
    order.note(second_grad[0])
    if packed:
        keyed_own = second_grad[5]
    else:
        cut = keys // 2
        keyed_own = settle(net.reduce(keyed_grads[:cut], keyed_grads[cut:]), [width], "settle_keyed")[0]
    (tokens_grad,) = run(
        finish_body,
        "finish",
        [((rows, width), F32)],
        (order.hold(keyed_own), key_select, grad_near, grad_middle, raw, vectors, to_own),
    )
    order.note(tokens_grad)
    first_grad = settle(
        [order.hold(first_parts[0])] + first_parts[1:], [light, light, light, 128], "settle_first"
    )
    vector_out = first_grad[3][:, :4].T
    return (
        result,
        tokens_grad,
        first_grad[0],
        first_grad[1],
        first_grad[2],
        second_grad[1].T,
        second_grad[2],
        second_grad[3],
        second_grad[4],
        second_grad[0].T,
        vector_out[0],
        vector_out[1],
        third_grad[0],
        third_grad[1],
        third_grad[2].T,
        gate_grad,
        up_grad,
        down_grad.T,
        vector_out[2],
        vector_out[3],
    )


def solution(mesh):
    by_rows = P(AXES, None)
    by_columns = P(None, AXES)
    vector = P(AXES)
    return jax.shard_map(
        per_device,
        mesh=mesh,
        in_specs=(
            by_rows,
            by_rows,
            by_rows,
            by_rows,
            by_columns,
            by_rows,
            by_rows,
            by_rows,
            by_columns,
            vector,
            vector,
            by_rows,
            by_rows,
            by_columns,
            by_rows,
            by_rows,
            by_columns,
            vector,
            vector,
            P(),
            P(),
            P(),
            by_rows,
            by_rows,
        ),
        out_specs=(
            by_rows,
            by_rows,
            by_rows,
            by_rows,
            by_rows,
            by_columns,
            by_rows,
            by_rows,
            by_rows,
            by_columns,
            vector,
            vector,
            by_rows,
            by_rows,
            by_columns,
            by_rows,
            by_rows,
            by_columns,
            vector,
            vector,
        ),
        check_vma=False,
    )
```

```python
import functools
import math

import jax
import jax.numpy as jnp
from jax import lax
from jax.experimental import pallas as pl
from jax.experimental.pallas import tpu as pltpu
from jax.sharding import PartitionSpec as P

HL = 8
HDL = 64
HH = 12
HDH = 64
RADIUS = 128

NEG = -1e30
EPS = 1e-06
HIGH = lax.Precision.HIGHEST
AXES = ("seq", "fsdp")
F32 = jnp.float32
BF16 = jnp.bfloat16
ROOM = 12 << 20
LENGTHS = {
    "select": 60,
    "weave": 20,
    "light_forward": 60,
    "heavy_pairs": 60,
    "expert": 60,
    "feed": 60,
    "feed_weight": 20,
    "turn": 5.6,
    "routed": 60,
    "settle_third": 14,
}


def declared(name):
    flops = int(LENGTHS.get(name, 0.05) * 1e9)
    return pl.CostEstimate(flops=flops, bytes_accessed=10**10, transcendentals=0)


class Columns:
    def __init__(self, array, start, stop):
        self.array, self.start, self.stop = array, start, stop


def dot(left, right, dims):
    return lax.dot_general(left, right, (dims, ((), ())), preferred_element_type=F32)


def nn(left, right):
    return dot(left, right, ((1,), (0,)))


def nt(left, right):
    return dot(left, right, ((1,), (1,)))


def tn(left, right):
    return dot(left, right, ((0,), (0,)))


def reverse_bits(value, count):
    out = value * 0
    for j in range(count):
        out = out | (((value >> j) & 1) << (count - 1 - j))
    return out


class Net:
    def __init__(self):
        self.seq = lax.axis_size("seq")
        self.depth = lax.axis_size("fsdp")
        self.levels = (self.seq // 2).bit_length() - 1
        self.count = self.seq * self.depth
        s = lax.axis_index("seq")
        self.core, self.pair = s & 1, s >> 1
        self.z = lax.axis_index("fsdp")
        self.device = s * self.depth + self.z

    def pairs(self, move):
        out = []
        for s in range(self.seq):
            for z in range(self.depth):
                pair, core, to_z = move(s >> 1, s & 1, z)
                out.append((s * self.depth + z, (pair * 2 + core) * self.depth + to_z))
        return out

    def by_core(self, array):
        return lax.ppermute(array, AXES, self.pairs(lambda p, c, z: (p, 1 - c, z)))

    def by_bit(self, array, j):
        top = self.levels - 1 - j
        return lax.ppermute(
            array, AXES, self.pairs(lambda p, c, z: (p ^ (1 << (j if c else top)), c, z))
        )

    def by_z(self, array, k):
        return lax.ppermute(array, AXES, self.pairs(lambda p, c, z: (p, c, z ^ k)))

    def target(self, relative):
        zr = relative % self.depth
        bits = (relative // self.depth) % (self.seq // 2)
        core = self.core ^ (relative // (self.count // 2))
        pair = self.pair ^ jnp.where(core == 1, bits, reverse_bits(bits, self.levels))
        return (pair * 2 + core) * self.depth + (self.z ^ zr)

    def from_z(self, shard):
        return [shard] + [self.by_z(shard, k) for k in range(1, self.depth)]

    def exchange_z(self, pieces):
        return [pieces[0]] + [self.by_z(pieces[k], k) for k in range(1, self.depth)]

    def gather(self, shard):
        shard = jnp.concatenate(self.from_z(shard), axis=0)
        for j in range(self.levels):
            shard = jnp.concatenate([shard, self.by_bit(shard, j)], axis=0)
        return shard, self.by_core(shard)

    def reduce(self, keep, send):
        keep, send = fold(keep, self.by_core(send), 2)
        for j in reversed(range(self.levels)):
            pieces = 2 if j else self.depth
            out = fold(keep, self.by_bit(send, j), pieces)
            keep, send = out[0], out[1]
        return self.exchange_z(out)

    def members(self):
        relative = jnp.arange(2 * self.depth, dtype=jnp.int32)
        core = self.core ^ (relative // self.depth)
        return core * self.depth + (self.z ^ (relative % self.depth))


def by_columns(width, step):
    chunk = next(c for c in (512, 256, 128, width) if width % c == 0)
    if width % chunk or width <= 4 * chunk:
        step(slice(0, width))
        return

    def at(i, carry):
        step(pl.ds(pl.multiple_of(i * chunk, chunk), chunk))
        return carry

    lax.fori_loop(0, width // chunk, at, 0)


class Order:
    def __init__(self):
        self.last = ()

    def hold(self, array):
        return after(array, *self.last)

    def note(self, array):
        self.last = (array,)
        return array


def stack_rows(arrays):
    height = sum(a.shape[0] for a in arrays)
    if any(a.shape[0] % 8 for a in arrays):
        return jnp.concatenate(arrays, axis=0)

    def body(*refs):
        def copy(columns):
            at = 0
            for ref in refs[:-1]:
                refs[-1][at : at + ref.shape[0], columns] = ref[:, columns]
                at += ref.shape[0]

        by_columns(arrays[0].shape[1], copy)

    return run(body, "stack", [((height, arrays[0].shape[1]), arrays[0].dtype)], arrays)[0]


def after(array, *earlier):
    return lax.optimization_barrier((array, *earlier))[0]


def unit_rms(values):
    scale = lax.rsqrt(jnp.mean(values * values, -1, keepdims=True) + EPS)
    return values * scale, scale


def norm_back(grad, gain, unit, scale):
    scaled = grad * gain
    return scale * (scaled - unit * jnp.mean(scaled * unit, -1, keepdims=True))


def document_of(places, lengths):
    return (places >= lengths[0]).astype(jnp.int32)


def sigmoid(values):
    return 1.0 / (1.0 + jnp.exp(-values))


def soft(scores):
    top = jnp.max(scores, -1, keepdims=True)
    expo = jnp.exp(scores - top)
    return expo / jnp.sum(expo, -1, keepdims=True)


def two_parts(values):
    high = values.astype(BF16)
    return high, (values - high.astype(F32)).astype(BF16)


def place_rows(select, values):
    high, low = two_parts(values)
    return tn(select, high) + tn(select, low)


def take_rows(select, values):
    high, low = two_parts(values)
    return nn(select, high) + nn(select, low)


def reorder(values, order):
    high, low = two_parts(values)
    return nn(high, order) + nn(low, order)


def reorder_back(values, order):
    high, low = two_parts(values)
    return nt(high, order) + nt(low, order)


def into(values, first, second):
    half = first.shape[0]
    return nn(values[:, :half], first) + nn(values[:, half:], second)


def onto(values, first, second):
    return jnp.concatenate([nt(values, first), nt(values, second)], axis=1)


def lanes(rows, width=128):
    return lax.broadcasted_iota(jnp.int32, (rows, width), 1)


def both_heads(pair):
    first = lanes(pair.shape[0]) < HDL
    zero = jnp.zeros_like(pair)
    return jnp.concatenate([jnp.where(first, pair, zero), jnp.where(first, zero, pair)], axis=0)


def pair_at(p, start=0):
    return pl.ds(pl.multiple_of(start + p * 128, 128), 128)


def column_at(array, index):
    return jnp.sum(jnp.where(lanes(*array.shape) == index, array, 0.0), -1, keepdims=True)


def one_pair(stacked):
    rows = stacked.shape[0] // 2
    return jnp.where(lanes(rows) < HDL, stacked[:rows], stacked[rows:])


def run(body, name, outs, args, smem=0, scratch=(), room=ROOM):
    vmem = pl.BlockSpec(memory_space=pltpu.VMEM)
    held = sum(math.prod(piece.shape) * jnp.dtype(piece.dtype).itemsize for piece in scratch)
    cuts = {i: a for i, a in enumerate(args) if isinstance(a, Columns)}

    def kernel(*refs):
        refs = list(refs)
        for i, cut in cuts.items():
            refs[i] = refs[i].at[:, cut.start : cut.stop]
        body(*refs)

    return pl.pallas_call(
        kernel,
        name=name,
        compiler_params=pltpu.CompilerParams(vmem_limit_bytes=held + room),
        out_shape=[jax.ShapeDtypeStruct(shape, kind) for shape, kind in outs],
        in_specs=[pl.BlockSpec(memory_space=pltpu.SMEM)] * smem + [vmem] * (len(args) - smem),
        out_specs=[vmem] * len(outs),
        scratch_shapes=list(scratch),
        cost_estimate=declared(name),
    )(*[a.array if isinstance(a, Columns) else a for a in args])


def rearrange(name, sources, outs, room=ROOM):
    bounds = [b for unused, moves in outs for m in moves for b in (*m[1], m[3])]
    if any(b % 8 for b in bounds):
        made = []
        for shape, moves in outs:
            out = jnp.zeros(shape, BF16)
            for i, (r0, r1), (c0, c1), row, column in moves:
                out = lax.dynamic_update_slice(out, sources[i][r0:r1, c0:c1], (row, column))
            made.append(out)
        return made

    spans = {(c0, c1, column) for unused, moves in outs for i, rows, (c0, c1), row, column in moves}

    def body(*refs):
        def copy(columns=None):
            for out, (unused, moves) in zip(refs[len(sources) :], outs):
                for i, (r0, r1), (c0, c1), row, column in moves:
                    to = columns or slice(column, column + c1 - c0)
                    out[row : row + r1 - r0, to] = refs[i][r0:r1, columns or slice(c0, c1)]

        if len(spans) == 1 and all(c0 == column for c0, c1, column in spans):
            by_columns(max(c1 for c0, c1, column in spans), copy)
        else:
            copy()

    return run(body, name, [(shape, BF16) for shape, unused in outs], sources, room=room)


def fold(keep, moved, pieces, kind=BF16):
    height, width = keep.shape
    piece = height // pieces
    parts = 2 if piece % 32 == 0 else 1
    step = piece // parts

    def body(*refs):
        def add(columns):
            for k in range(pieces):
                total = refs[k][:, columns].astype(F32) + refs[pieces + k][:, columns].astype(F32)
                refs[2 * pieces + k][:, columns] = total.astype(kind)

        by_columns(width, add)

    def spec(k):
        return pl.BlockSpec((step, width), lambda i, k=k: (k * parts + i, 0))

    if piece % 8:
        total = keep.astype(F32) + moved.astype(F32)
        return [total[k * piece : (k + 1) * piece].astype(kind) for k in range(pieces)]
    return pl.pallas_call(
        body,
        name="fold",
        compiler_params=pltpu.CompilerParams(vmem_limit_bytes=ROOM),
        grid=(parts,),
        out_shape=[jax.ShapeDtypeStruct((piece, width), kind)] * pieces,
        in_specs=[spec(k) for k in range(pieces)] * 2,
        out_specs=[spec(0)] * pieces,
        cost_estimate=declared("fold"),
    )(*([keep] * pieces + [moved] * pieces))


def settle(pieces, widths, name, rows=None):
    rows = rows or pieces[0].shape[0]

    def body(*refs):
        parts, outs = refs[: len(pieces)], refs[len(pieces) :]
        at = 0
        for out, width in zip(outs, widths):
            total = parts[0][:rows, at : at + width].astype(F32)
            for part in parts[1:]:
                total = total + part[:rows, at : at + width].astype(F32)
            out[...] = total
            at += width

    return run(body, name, [((rows, width), F32) for width in widths], pieces)


def hot(column, rows):
    return jnp.where(column == lanes(column.shape[0], rows), 1.0, 0.0).astype(BF16)


def as_column(row):
    count = row.shape[1]
    eye = lax.broadcasted_iota(jnp.int32, (count, count), 0) == lanes(count, count)
    spread = jnp.where(eye, row.astype(F32), 0.0)
    return jnp.sum(spread, -1, keepdims=True).astype(jnp.int32)


def order_matrix(order):
    width = order.shape[1]
    rows = lax.broadcasted_iota(jnp.int32, (width, width), 0)
    return jnp.where(rows == order, 1.0, 0.0).astype(BF16)


def orders_body(orders, to_own, to_slice):
    to_own[...] = order_matrix(orders[0:1])
    to_slice[...] = order_matrix(orders[1:2])


def select_body(
    place, to_own, query_route, key_route, feed_route, cotangent, cot, query_select, key_select, feed_select, query_doc
):
    rows = cotangent.shape[0]
    cot[...] = nn(cotangent[...], to_own[...]).astype(BF16)
    queries = as_column(query_route[pl.ds(place[4], 1)])
    query_select[...] = hot(queries, rows)
    key_select[...] = hot(as_column(key_route[pl.ds(place[4], 1)]), rows)
    feed_select[...] = hot(as_column(feed_route[...]), rows)
    query_doc[...] = jnp.where(place[0] + queries >= place[1], 1, 0)


def pack_body(
    place, key_spots, tokens, key_route, q_l, k_l, v_l,
    gate_s, up_s, down_s, gate_l, up_l, down_l, second, third, expert_keep, expert_send, key_docs
):
    part, width = q_l.shape
    at = 0
    for ref in (q_l, k_l, v_l):
        second[:, at : at + ref.shape[1]] = ref[...]
        at += ref.shape[1]
    keyed = nn(hot(as_column(key_route[pl.ds(place[4], 1)]), tokens.shape[0]), tokens[...])
    second[:, at : at + width] = keyed[:part].astype(BF16)
    rest = keyed[part:]
    chunk = width * rest.shape[0] // part
    pieces = [rest[:, i * chunk : (i + 1) * chunk] for i in range(width // chunk)]
    second[:, at + width :] = jnp.concatenate(pieces, axis=0).astype(BF16)
    narrow = gate_s.shape[1]
    for i, ref in enumerate((gate_s, up_s, down_s)):
        third[:, i * narrow : (i + 1) * narrow] = ref[...]
    share = expert_keep.shape[1] // 3
    depth = expert_keep.shape[0] // part
    for c, expert in enumerate((expert_keep, expert_send)):
        for k in range(depth):
            at = ((place[5] ^ c) * depth + (place[6] ^ k)) * share
            at = pl.ds(pl.multiple_of(at, share), share)
            for i, ref in enumerate((gate_l, up_l, down_l)):
                expert[k * part : (k + 1) * part, i * share : (i + 1) * share] = ref[:, at]
    blocks, slots = key_route.shape
    keys = key_spots.shape[1]
    block = lax.broadcasted_iota(jnp.int32, (blocks, keys), 0) == key_spots[0:1]
    table = key_route[...].astype(F32).T.astype(BF16)
    found = nn(table, jnp.where(block, 1.0, 0.0).astype(BF16))
    slot = lax.broadcasted_iota(jnp.int32, (slots, keys), 0) == key_spots[1:2]
    position = jnp.sum(jnp.where(slot, found, 0.0), 0, keepdims=True).astype(jnp.int32)
    rows = tokens.shape[0]
    document = jnp.where(key_spots[0:1] * rows + position >= place[1], 1, 0)
    key_docs[...] = jnp.where(position < rows, document, -1)


def prepare_body(to_own, above, tokens, below, raw):
    order = to_own[...]
    at = 0
    for ref in (above, tokens, below):
        raw[at : at + ref.shape[0]] = nn(ref[...], order).astype(BF16)
        at += ref.shape[0]


def unpack_body(place, keep, got, gate, up, down):
    part = gate.shape[0]
    depth = keep.shape[0] // part
    share = keep.shape[1] // 3
    for c, source in enumerate((keep, got)):
        for k in range(depth):
            at = ((place[5] ^ c) * depth + (place[6] ^ k)) * share
            at = pl.ds(pl.multiple_of(at, share), share)
            for i, out in enumerate((gate, up, down)):
                piece = source[k * part : (k + 1) * part, i * share : (i + 1) * share]
                out[:, at] = piece.astype(F32)


def pair_up(shard, first, second, part):
    count = first.shape[0] // part
    width = first.shape[1]
    whole, own = (0, part), (0, width)
    outs = []
    for k in range(count):
        at = (k * part, (k + 1) * part)
        moves = [(0, whole, (0, 2 * width), 0, 0), (1, at, own, part, 0), (2, at, own, part, width)]
        outs.append(((2 * part, 2 * width), moves))
    return rearrange("pair_up", (shard, first, second), outs)


def stack_both(pieces, name="stack_both"):
    height = sum(p.shape[0] for p in pieces)
    width = pieces[0].shape[1]
    moves, row = [], 0
    for i, piece in enumerate(pieces):
        n = piece.shape[0] // 2
        moves.append((i, (0, n), (0, width), row, 0))
        moves.append((i, (n, 2 * n), (0, width), height // 2 + row, 0))
        row += n
    return rearrange(name, pieces, [((height, width), moves)])[0]


def part_both(pieces, name):
    height = sum(p.shape[0] for p in pieces) // 2
    width = pieces[0].shape[1]
    first, second, row = [], [], 0
    for i, piece in enumerate(pieces):
        n = piece.shape[0] // 2
        first.append((i, (0, n), (0, width), row, 0))
        second.append((i, (n, 2 * n), (0, width), row, 0))
        row += n
    return rearrange(name, pieces, [((height, width), first), ((height, width), second)])


def take_apart(pieces, part):
    width = pieces[0].shape[1] // 2
    outs = []
    for side in range(2):
        columns = (side * width, (side + 1) * width)
        moves = [(k, (0, part), columns, k * part, 0) for k in range(len(pieces))]
        outs.append(((len(pieces) * part, width), moves))
    return rearrange("take_apart", pieces, outs)


def local_mask(place, tile, reach, stacked, span):
    shape = (stacked, span)
    row = lax.broadcasted_iota(jnp.int32, shape, 0) & (reach - 1)
    query = place[0] + tile * reach + row
    key = place[0] + (tile - 1) * reach + lax.broadcasted_iota(jnp.int32, shape, 1)
    split, live, total = place[1], place[1] + place[2], place[3]
    inside = (key >= 0) & (key < total)
    same = jnp.where(query >= split, 1, 0) == jnp.where(key >= split, 1, 0)
    near = jnp.abs(query - key) <= reach
    both = ((query < live) & (key < live)) | (query == key)
    return near & inside & same & both


def light_rows_body(raw, w0, w1, normed, queries, pairs, vectors):
    light = HL * HDL
    reach = RADIUS
    rows = queries.shape[0]
    columns = [w[:, 3 * light :].astype(F32).T[:8] for w in (w0, w1)]
    vectors[...] = jnp.concatenate(columns, axis=1)
    unit, unused = unit_rms(raw[...].astype(F32))
    normed[...] = (unit * vectors[0:1]).astype(BF16)
    own = normed[reach : reach + rows]
    queries[...] = into(own, w0[:, :light], w1[:, :light]).astype(BF16)
    pairs[...] = into(normed[...], w0[:, light : 3 * light], w1[:, light : 3 * light]).astype(BF16)


def light_forward_body(place, queries, pairs, mixed, sums):
    light = HL * HDL
    reach = RADIUS
    rows = queries.shape[0]
    scale = 1.0 / math.sqrt(HDL)
    lane = lanes(reach)
    for tile in range(rows // reach):
        mine = slice(tile * reach, (tile + 1) * reach)
        seen = slice(tile * reach, (tile + 3) * reach)
        mask = local_mask(place, tile, reach, 2 * reach, 3 * reach)

        def pair(p, logs):
            query = both_heads(queries[mine, pair_at(p)])
            scores = jnp.where(mask, nt(query, pairs[seen, pair_at(p)]) * scale, NEG)
            top = jnp.max(scores, -1, keepdims=True)
            expo = jnp.exp(scores - top)
            total = jnp.sum(expo, -1, keepdims=True)
            probs = (expo * (1.0 / total)).astype(BF16)
            mixed[mine, pair_at(p)] = one_pair(nn(probs, pairs[seen, pair_at(p, light)])).astype(BF16)
            log = top + jnp.log(total)
            logs = jnp.where(lane == 2 * p, log[:reach], logs)
            return jnp.where(lane == 2 * p + 1, log[reach:], logs)

        logs = lax.fori_loop(0, HL // 2, pair, jnp.zeros((reach, 128), F32))
        sums[mine] = logs


def piece_select(block_rows, rest, part, piece):
    shape = (block_rows // part * rest, block_rows)
    k = lax.broadcasted_iota(jnp.int32, shape, 0)
    row = lax.broadcasted_iota(jnp.int32, shape, 1)
    shift = rest.bit_length() - 1
    want = (k >> shift) * part + piece * rest + (k & (rest - 1))
    return jnp.where(row == want, 1.0, 0.0).astype(BF16)


def heavy_rows_body(slots, vectors, to_own, s0, s1, keyed, held):
    width = to_own.shape[0]
    half = s0.shape[0]
    at = 3 * HH * HDH
    part = half // (keyed.shape[0] // slots // 2)
    rest = slots - part
    chunk = width * rest // part
    for i, ref in enumerate((s0, s1)):
        held[i * half : (i + 1) * half] = ref[:, at : at + width]
        low = 2 * half + i * (half // part * rest)
        for piece in range(part // rest):
            picked = nn(piece_select(half, rest, part, piece), ref[:, at + width :])
            held[low : low + half // part * rest, piece * chunk : (piece + 1) * chunk] = picked.astype(BF16)
    step = 256

    def project(t, carry):
        rows = pl.ds(pl.multiple_of(t * step, step), step)
        unit, unused = unit_rms(nn(held[rows], to_own[...]))
        keyed[rows] = (unit * vectors[0:1]).astype(BF16)
        return carry

    lax.fori_loop(0, keyed.shape[0] // step, project, 0)


def heavy_pairs_body(select, normed, keyed, s0, s1, pairs, routed, queries):
    heavy = HH * HDH
    q_at = slice(0, heavy)
    kv_at = slice(heavy, 3 * heavy)
    step = 256

    def project(t, carry):
        rows = pl.ds(pl.multiple_of(t * step, step), step)
        pairs[rows] = into(keyed[rows], s0[:, kv_at], s1[:, kv_at]).astype(BF16)
        return carry

    lax.fori_loop(0, keyed.shape[0] // step, project, 0)
    own = normed[RADIUS : normed.shape[0] - RADIUS]
    routed[...] = nn(select[...], own).astype(BF16)
    queries[...] = into(routed[...], s0[:, q_at], s1[:, q_at]).astype(BF16)


def heavy_forward_body(query_doc, key_doc, queries, pairs, mixed, sums):
    heavy = HH * HDH
    slots = queries.shape[0]
    scale = 1.0 / math.sqrt(HDH)
    mask = jnp.concatenate([query_doc[...], query_doc[...]], axis=0) == key_doc[...]

    def pair(p, logs):
        scores = jnp.where(mask, nt(both_heads(queries[:, pair_at(p)]), pairs[:, pair_at(p)]) * scale, NEG)
        top = jnp.max(scores, -1, keepdims=True)
        expo = jnp.exp(scores - top)
        total = jnp.sum(expo, -1, keepdims=True)
        probs = (expo * (1.0 / total)).astype(BF16)
        mixed[:, pair_at(p)] = one_pair(nn(probs, pairs[:, pair_at(p, heavy)])).astype(BF16)
        return jnp.where(lanes(2 * slots) == p, top + jnp.log(total), logs)

    logs = lax.fori_loop(0, HH // 2, pair, jnp.zeros((2 * slots, 128), F32))
    sums[...] = logs


def join_body(
    raw, light_mixed, heavy_mixed, routed, query_select, feed_select, vectors, cot, to_own, s0, s1,
    middle, normed, heavy_branch, feed_rows, feed_grads, sent
):
    heavy = HH * HDH
    width = raw.shape[1]
    rows = middle.shape[0]
    at = slice(heavy, heavy + HL * HDL)
    light_branch = onto(light_mixed[...], s0[:, at], s1[:, at])
    at = slice(0, heavy)
    heavy_branch[...] = onto(heavy_mixed[...], s0[:, at], s1[:, at])
    score = sigmoid(jnp.sum(routed[...].astype(F32) * vectors[1:2], -1, keepdims=True))
    inputs = raw[RADIUS : RADIUS + rows].astype(F32)
    middle[...] = inputs + light_branch + place_rows(query_select[...], score * heavy_branch[...])
    unit, unused = unit_rms(middle[...])
    normed[...] = (unit * vectors[2:3]).astype(BF16)
    feed_rows[...] = nn(feed_select[...], normed[...]).astype(BF16)
    feed_grads[...] = nn(feed_select[...], cot[...])
    score = sigmoid(jnp.sum(feed_rows[...].astype(F32) * vectors[3:4], -1, keepdims=True))
    sent[:, :width] = nt(feed_rows[...], to_own[...]).astype(BF16)
    sent[:, width:] = nt((score * feed_grads[...]).astype(BF16), to_own[...]).astype(BF16)


def geglu_rows(gate, upper, grad_hidden):
    c0, c1 = 0.7978845608028654, 0.044715
    square = gate * gate
    bent = jnp.tanh(c0 * gate * (1.0 + c1 * square))
    bell = 0.5 * (1.0 + bent)
    gelu = gate * bell
    slope = bell + 0.5 * gate * (1.0 - bent * bent) * (c0 * (1.0 + 3.0 * c1 * square))
    return gelu * upper, grad_hidden * upper * slope, grad_hidden * gelu


def geglu_loop(wide, grad_hidden, hidden, grads):
    count = hidden.shape[1]
    step = 32

    def rows_at(t, carry):
        rows = pl.ds(pl.multiple_of(t * step, step), step)
        out, grad_gate, grad_upper = geglu_rows(
            wide[rows, :count], wide[rows, count:], grad_hidden[rows]
        )
        hidden[rows] = out.astype(BF16)
        grads[rows, :count] = grad_gate.astype(BF16)
        grads[rows, count:] = grad_upper.astype(BF16)
        return carry

    lax.fori_loop(0, hidden.shape[0] // step, rows_at, 0)


def feed_body(normed, cot, t0, t1, feed, grad_normed, hidden, grads, wide, grad_hidden):
    narrow = hidden.shape[1]
    wide[...] = into(normed[...], t0[:, : 2 * narrow], t1[:, : 2 * narrow])
    grad_hidden[...] = into(cot[...], t0[:, 2 * narrow :], t1[:, 2 * narrow :])
    geglu_loop(wide, grad_hidden, hidden, grads)
    feed[...] = onto(hidden[...], t0[:, 2 * narrow :], t1[:, 2 * narrow :])
    grad_normed[...] = onto(grads[...], t0[:, : 2 * narrow], t1[:, : 2 * narrow])


def feed_weight_body(normed, cot, hidden, grads, keep, send):
    narrow = hidden.shape[1]
    half = keep.shape[0]
    for out, at in ((send, slice(half, None)), (keep, slice(0, half))):
        out[:, : 2 * narrow] = tn(normed[:, at], grads[...]).astype(out.dtype)
        out[:, 2 * narrow :] = tn(cot[:, at], hidden[...]).astype(out.dtype)


def expert_body(got0, got1, to_slice, weights, keep, send, grad_keep, grad_send, rows, row_grads, wide, grad_hidden, hidden, grads):
    width = to_slice.shape[0]
    share = hidden.shape[1]
    count = got0.shape[0]
    for i, got in enumerate((got0, got1)):
        at = slice(i * count, (i + 1) * count)
        rows[at] = nn(got[:, :width], to_slice[...]).astype(BF16)
        row_grads[at] = nn(got[:, width:], to_slice[...]).astype(BF16)
    first, second = weights[:, : 2 * share], weights[:, 3 * share : 5 * share]
    first_down, second_down = weights[:, 2 * share : 3 * share], weights[:, 5 * share :]
    wide[...] = into(rows[...], first, second)
    grad_hidden[...] = into(row_grads[...], first_down, second_down)
    geglu_loop(wide, grad_hidden, hidden, grads)
    for out, at in ((send, slice(count, None)), (keep, slice(0, count))):
        feed = onto(hidden[at], first_down, second_down).astype(BF16)
        back = onto(grads[at], first, second).astype(BF16)
        out[:, :width] = nt(feed, to_slice[...]).astype(out.dtype)
        out[:, width:] = nt(back, to_slice[...]).astype(out.dtype)
    half = weights.shape[0]
    low = grad_keep.shape[0]
    for i in range(2):
        at = slice(i * half, (i + 1) * half)
        to = 3 * share * i
        for left, right, columns in (
            (rows, grads, slice(to, to + 2 * share)), (row_grads, hidden, slice(to + 2 * share, to + 3 * share))
        ):
            product = tn(left[:, at], right[...]).astype(BF16)
            grad_keep[:, columns] = product[:low]
            grad_send[:, columns] = product[low:]


def turn_body(*refs):
    pieces = refs[:-12]
    (
        middle, feed, grad_normed, feed_rows, feed_grads, feed_select, vectors, cot, to_own,
        result, grad_middle, vector_grads,
    ) = refs[-12:]
    width = middle.shape[1]
    summed = pieces[0][...].astype(F32)
    for piece in pieces[1:]:
        summed = summed + piece[...].astype(F32)
    feed_heavy = reorder(summed[:, :width], to_own[...])
    grad_rows = reorder(summed[:, width:], to_own[...])
    rows = feed_rows[...].astype(F32)
    score = sigmoid(jnp.sum(rows * vectors[3:4], -1, keepdims=True))
    logit = jnp.sum(feed_grads[...] * feed_heavy, -1, keepdims=True) * score * (1.0 - score)
    grad_rows = grad_rows + logit * vectors[3:4]
    grads = grad_normed[...] + place_rows(feed_select[...], grad_rows)
    unit, scale = unit_rms(middle[...])
    grad_middle[...] = cot[...].astype(F32) + norm_back(grads, vectors[2:3], unit, scale)
    vector_grads[...] = jnp.concatenate(
        [
            jnp.zeros((2, width), F32),
            jnp.sum(grads * unit, 0, keepdims=True),
            jnp.sum(rows * logit, 0, keepdims=True),
            jnp.zeros((4, width), F32),
        ],
        axis=0,
    )
    out = middle[...] + feed[...] + place_rows(feed_select[...], score * feed_heavy)
    result[...] = nt(out.astype(BF16), to_own[...]).astype(BF16)


def heavy_scores_body(
    query_doc, key_doc, grad_middle, query_select, routed, pairs, queries, heavy_branch, sums, vectors, s0, s1,
    grad_branch, grad_queries, grad_pairs, logits, held
):
    heavy = HH * HDH
    score = sigmoid(jnp.sum(routed[...].astype(F32) * vectors[1:2], -1, keepdims=True))
    grad_rows = take_rows(query_select[...], grad_middle[...])
    grad_branch[...] = (score * grad_rows).astype(BF16)
    logit = jnp.sum(grad_rows * heavy_branch[...], -1, keepdims=True) * score * (1.0 - score)
    logits[...] = jnp.broadcast_to(logit, logits.shape)
    at = slice(0, heavy)
    grad_mixed = into(grad_branch[...], s0[:, at], s1[:, at]).astype(BF16)
    scale = 1.0 / math.sqrt(HDH)
    mask = jnp.concatenate([query_doc[...], query_doc[...]], axis=0) == key_doc[...]
    held[...] = grad_mixed
    logs = sums[...]

    def pair(p, carry):
        query = both_heads(queries[:, pair_at(p)])
        grad_out = both_heads(held[:, pair_at(p)])
        key = pairs[:, pair_at(p)]
        scores = jnp.where(mask, nt(query, key) * scale, NEG)
        probs = jnp.exp(scores - column_at(logs, p))
        grad_probs = nt(grad_out, pairs[:, pair_at(p, heavy)])
        delta = jnp.sum(probs * grad_probs, -1, keepdims=True)
        grad_scores = (probs * (grad_probs - delta)).astype(BF16)
        grad_queries[:, pair_at(p)] = one_pair(nn(grad_scores, key) * scale).astype(BF16)
        grad_pairs[:, pair_at(p)] = (tn(grad_scores, query) * scale).astype(BF16)
        grad_pairs[:, pair_at(p, heavy)] = tn(probs.astype(BF16), grad_out).astype(BF16)
        return carry

    lax.fori_loop(0, HH // 2, pair, 0)


def heavy_weights_body(
    grad_middle, routed, keyed, light_mixed, heavy_mixed, grad_branch, grad_queries, grad_pairs, logits, vectors, to_own, s0, s1,
    keep, send, vector_grads, moved
):
    width = grad_middle.shape[1]
    heavy = HH * HDH
    light = HL * HDL
    half = s0.shape[0]
    slots = routed.shape[0]
    q_at = slice(width + light, width + light + heavy)
    kv_at = slice(width + light + heavy, width + light + 3 * heavy)
    logit = logits[:, 0:1]
    step = 256

    def back(t, gain):
        rows = pl.ds(pl.multiple_of(t * step, step), step)
        grads = onto(grad_pairs[rows], s0[:, heavy : 3 * heavy], s1[:, heavy : 3 * heavy])
        moved[rows] = nt(grads.astype(BF16), to_own[...]).astype(BF16)
        return gain + jnp.sum(grads * keyed[rows].astype(F32), 0, keepdims=True)

    gain = lax.fori_loop(0, keyed.shape[0] // step, back, jnp.zeros((1, width), F32))
    vector_grads[...] = jnp.concatenate(
        [
            gain / vectors[0:1],
            jnp.sum(routed[...].astype(F32) * logit, 0, keepdims=True),
            jnp.zeros((6, width), F32),
        ],
        axis=0,
    )
    low = grad_middle[...].astype(BF16)
    part = half // (keyed.shape[0] // slots // 2)
    rest = slots - part
    chunk = width * rest // part
    for i, out in ((1, send), (0, keep)):
        at = slice(i * half, (i + 1) * half)
        out[:, :width] = tn(grad_branch[:, at], heavy_mixed[...]).astype(BF16)
        out[:, width : width + light] = tn(low[:, at], light_mixed[...]).astype(BF16)
        out[:, q_at] = tn(routed[:, at], grad_queries[...]).astype(BF16)
        out[:, kv_at] = tn(keyed[:, at], grad_pairs[...]).astype(BF16)
        to = width + light + 3 * heavy
        out[:, to : to + width] = moved[at]
        at = 2 * half + i * (half // part * rest)
        total = 0.0
        for piece in range(part // rest):
            block = moved[at : at + half // part * rest, piece * chunk : (piece + 1) * chunk]
            total = total + tn(piece_select(half, rest, part, piece), block)
        out[:, to + width :] = total.astype(BF16)


def routed_body(grad_queries, logits, vectors, s0, s1, grad_routed):
    at = slice(0, HH * HDH)
    grad_routed[...] = onto(grad_queries[...], s0[:, at], s1[:, at]) + logits[:, 0:1] * vectors[1:2]


def light_scores_body(place, grad_middle, queries, pairs, sums, s0, s1, grad_queries, grad_pairs, held, grad_out_all):
    light = HL * HDL
    heavy = HH * HDH
    reach = RADIUS
    rows = queries.shape[0]
    at = slice(heavy, heavy + light)
    grad_out_all[...] = into(grad_middle[...].astype(BF16), s0[:, at], s1[:, at]).astype(BF16)
    held[...] = jnp.zeros_like(held)
    scale = 1.0 / math.sqrt(HDL)
    for tile in range(rows // reach):
        mine = slice(tile * reach, (tile + 1) * reach)
        seen = slice(tile * reach, (tile + 3) * reach)
        mask = local_mask(place, tile, reach, 2 * reach, 3 * reach)
        logs = sums[mine]

        def pair(p, carry):
            query = both_heads(queries[mine, pair_at(p)])
            grad_out = both_heads(grad_out_all[mine, pair_at(p)])
            key = pairs[seen, pair_at(p)]
            log = jnp.concatenate([column_at(logs, 2 * p), column_at(logs, 2 * p + 1)], axis=0)
            probs = jnp.exp(jnp.where(mask, nt(query, key) * scale, NEG) - log)
            grad_probs = nt(grad_out, pairs[seen, pair_at(p, light)])
            delta = jnp.sum(probs * grad_probs, -1, keepdims=True)
            grad_scores = (probs * (grad_probs - delta)).astype(BF16)
            grad_queries[mine, pair_at(p)] = one_pair(nn(grad_scores, key) * scale).astype(BF16)
            held[seen, pair_at(p)] = held[seen, pair_at(p)] + tn(grad_scores, query) * scale
            beyond = pair_at(p, light)
            held[seen, beyond] = held[seen, beyond] + tn(probs.astype(BF16), grad_out)
            return carry

        lax.fori_loop(0, HL // 2, pair, 0, unroll=2)
    grad_pairs[...] = held[...].astype(BF16)


def light_weights_body(
    raw, normed, grad_queries, grad_pairs, grad_routed, query_select, feed_vectors, heavy_vectors, to_own, f0, f1,
    keep, send, outer, grad_mine
):
    light = HL * HDL
    reach = RADIUS
    rows = grad_queries.shape[0]
    half = f0.shape[0]
    grads = onto(grad_pairs[...], f0[:, light : 3 * light], f1[:, light : 3 * light])
    for i, at in enumerate((slice(0, reach), slice(reach + rows, None))):
        outer[i * reach : (i + 1) * reach] = nt(grads[at].astype(BF16), to_own[...]).astype(BF16)
    own = onto(grad_queries[...], f0[:, :light], f1[:, :light])
    own = own + grads[reach : reach + rows] + place_rows(query_select[...], grad_routed[...])
    grad_mine[...] = own
    unit, unused = unit_rms(raw[...].astype(F32))
    gain = jnp.sum(own * unit[reach : reach + rows], 0, keepdims=True)
    for at in (slice(0, reach), slice(reach + rows, None)):
        gain = gain + jnp.sum(grads[at] * unit[at], 0, keepdims=True)
    vector_rows = feed_vectors[...] + heavy_vectors[...]
    first = lax.broadcasted_iota(jnp.int32, vector_rows.shape, 0) == 0
    vector_rows = vector_rows + jnp.where(first, gain, 0.0)
    filler = jnp.zeros((120, raw.shape[1]), F32)
    columns = jnp.concatenate([vector_rows, filler], axis=0)
    for i, out in ((1, send), (0, keep)):
        at = slice(i * half, (i + 1) * half)
        out[:, :light] = tn(normed[reach : reach + rows, at], grad_queries[...]).astype(BF16)
        out[:, light : 3 * light] = tn(normed[:, at], grad_pairs[...]).astype(BF16)
        out[:, 3 * light :] = columns[:, at].T.astype(BF16)


def halo_body(from_prev, from_next, grad_mine, to_own, out):
    reach = RADIUS
    rows = grad_mine.shape[0]
    order = to_own[...]
    out[...] = grad_mine[...]
    out[:reach] = out[:reach] + nn(from_prev[...], order)
    out[rows - reach :] = out[rows - reach :] + nn(from_next[...], order)


def finish_body(keyed_grads, key_select, grads, grad_middle, raw, vectors, to_own, out):
    reach = RADIUS
    rows, width = grads.shape
    order = to_own[...]
    keyed = keyed_grads[...]
    if keyed.shape[0] < key_select.shape[0]:
        rest = key_select.shape[0] - keyed.shape[0]
        tail = [keyed[i * rest : (i + 1) * rest, width:] for i in range(keyed.shape[0] // rest)]
        keyed = jnp.concatenate([keyed[:, :width], jnp.concatenate(tail, axis=1)], axis=0)
    keyed = nn(keyed.astype(BF16), order).astype(BF16)
    total = grads[...] + tn(key_select[...], keyed)
    unit, scale = unit_rms(raw[reach : reach + rows].astype(F32))
    total = grad_middle[...] + norm_back(total, vectors[0:1], unit, scale)
    out[...] = reorder_back(total, order)


def heavy_forward_wide(query_doc, key_doc, select, normed, vectors, to_own, s0, s1, keyed_raw):
    heavy = HH * HDH
    q_at, kv_at = slice(0, heavy), slice(heavy, 3 * heavy)
    unit, unused = unit_rms(nn(keyed_raw, to_own))
    keyed = (unit * vectors[0:1]).astype(BF16)
    pairs = into(keyed, s0[:, kv_at], s1[:, kv_at]).astype(BF16)
    routed = nn(select, normed[RADIUS : normed.shape[0] - RADIUS]).astype(BF16)
    queries = into(routed, s0[:, q_at], s1[:, q_at]).astype(BF16)

    def heads(array):
        return array.reshape(-1, HH, HDH)

    scores = jnp.einsum(
        "qhd,khd->hqk", heads(queries), heads(pairs[:, :heavy]), preferred_element_type=F32
    ) / math.sqrt(HDH)
    probs = soft(jnp.where((query_doc == key_doc)[None], scores, NEG))
    mixed = jnp.einsum(
        "hqk,khd->qhd", probs.astype(BF16), heads(pairs[:, heavy:]), preferred_element_type=F32
    )
    return keyed, pairs, routed, queries, mixed.reshape(-1, heavy).astype(BF16), probs


def heavy_backward_wide(
    grad_middle, query_select, routed, keyed, pairs, queries, light_mixed, heavy_mixed, heavy_branch, probs,
    vectors, to_own, o0, o1, s0, s1
):
    heavy = HH * HDH
    scale = 1.0 / math.sqrt(HDH)
    half = s0.shape[0]
    q_at, kv_at = slice(0, heavy), slice(heavy, 3 * heavy)
    score = sigmoid(jnp.sum(routed.astype(F32) * vectors[1:2], -1, keepdims=True))
    grad_rows = take_rows(query_select, grad_middle)
    grad_branch = (score * grad_rows).astype(BF16)
    logit = jnp.sum(grad_rows * heavy_branch, -1, keepdims=True) * score * (1.0 - score)
    at = slice(0, heavy)
    grad_mixed = into(grad_branch, o0[:, at], o1[:, at]).astype(BF16)

    def heads(array):
        return array.reshape(-1, HH, HDH)

    def mix(pattern, left, right):
        return jnp.einsum(pattern, left, right, preferred_element_type=F32)

    grad_probs = mix("qhd,khd->hqk", heads(grad_mixed), heads(pairs[:, heavy:]))
    delta = jnp.sum(probs * grad_probs, -1, keepdims=True)
    grad_scores = (probs * (grad_probs - delta)).astype(BF16)
    grad_queries = mix("hqk,khd->qhd", grad_scores, heads(pairs[:, :heavy])) * scale
    grad_queries = grad_queries.reshape(-1, heavy).astype(BF16)
    grad_keys = mix("hqk,qhd->khd", grad_scores, heads(queries)) * scale
    grad_values = mix("hqk,qhd->khd", probs.astype(BF16), heads(grad_mixed))
    grad_pairs = jnp.concatenate(
        [grad_keys.reshape(-1, heavy).astype(BF16), grad_values.reshape(-1, heavy).astype(BF16)], axis=1
    )
    grad_routed = onto(grad_queries, s0[:, q_at], s1[:, q_at]) + logit * vectors[1:2]
    grads = onto(grad_pairs, s0[:, kv_at], s1[:, kv_at])
    vector_grads = jnp.concatenate(
        [
            jnp.sum(grads * keyed.astype(F32), 0, keepdims=True) / vectors[0:1],
            jnp.sum(routed.astype(F32) * logit, 0, keepdims=True),
            jnp.zeros((6, grads.shape[1]), F32),
        ],
        axis=0,
    )
    moved = nt(grads.astype(BF16), to_own).astype(BF16)
    low = grad_middle.astype(BF16)
    sides = []
    for at in (slice(0, half), slice(half, None)):
        columns = (
            tn(grad_branch[:, at], heavy_mixed),
            tn(low[:, at], light_mixed),
            tn(routed[:, at], grad_queries),
            tn(keyed[:, at], grad_pairs),
        )
        sides.append(jnp.concatenate(columns, axis=1).astype(BF16))
    return sides[0], sides[1], grad_routed, vector_grads, moved


def per_device(
    tokens,
    query_small,
    key_small,
    value_small,
    out_small,
    query_large,
    key_large,
    value_large,
    out_large,
    attend_gain,
    attend_router,
    gate_small,
    up_small,
    down_small,
    gate_large,
    up_large,
    down_large,
    feed_gain,
    feed_router,
    lengths,
    query_route,
    key_route,
    feed_route,
    cotangent,
):
    net = Net()
    rows, width = tokens.shape
    blocks = net.count
    part = width // blocks
    half = width // 2
    first = net.device * rows
    light = HL * HDL
    heavy = HH * HDH
    narrow = down_small.shape[0]
    wide = down_large.shape[0]
    slots = query_route.shape[1]
    members = 2 * net.depth
    share = wide // members
    pooled = members * slots
    keys = blocks * slots
    rest = slots - part
    packed = part % 8 == 0 and rest > 0 and rest % 8 == 0 and part % rest == 0 and keys <= 2048

    step = [(i, i + 1) for i in range(blocks - 1)]
    back = [(i + 1, i) for i in range(blocks - 1)]
    vector_pack = jnp.stack([attend_gain, attend_router, feed_gain, feed_router], axis=1)
    vector_pack = jnp.pad(vector_pack, ((0, 0), (0, 124)))
    first_pack = (query_small, key_small, value_small, vector_pack, out_large.T, out_small.T)
    moves, at = [], 0
    for i, piece in enumerate(first_pack):
        moves.append((i, (0, part), (0, piece.shape[1]), 0, at))
        at += piece.shape[1]
    (first_set,) = rearrange("pack_first", first_pack, [((part, at), moves)], room=56 << 20)
    first_parts = net.from_z(first_set)
    cut = 3 * light + vector_pack.shape[1]
    column = jnp.arange(width, dtype=jnp.int32)
    own_order = net.target(column // part) * part + column % part
    bits = column % half // (part * net.depth)
    bits = jnp.where(net.core == 1, bits, reverse_bits(bits, net.levels))
    member = (net.core ^ (column // half)) * net.depth + (net.z ^ (column // part % net.depth))
    slice_order = ((net.pair ^ bits) * members + member) * part + column % part
    orders = jnp.stack([own_order, slice_order])
    place = jnp.stack([first, lengths[0], lengths[1], jnp.int32(rows * blocks), net.device, net.core, net.z])
    square = ((width, width), BF16)
    chosen = ((slots, rows), BF16)

    if packed:
        tall = blocks * part
        spot = jnp.arange(keys, dtype=jnp.int32)
        spot_block = jnp.where(spot < tall, spot // part, (spot - tall) // rest)
        spot_slot = jnp.where(spot < tall, spot % part, part + (spot - tall) % rest)
        second_set, third_set, slices_keep, slices_send, key_docs = run(
            pack_body,
            "pack",
            [
                ((part, 4 * width + width * rest // part), BF16),
                ((part, 3 * narrow), BF16),
                ((net.depth * part, 3 * share), BF16),
                ((net.depth * part, 3 * share), BF16),
                ((1, keys), jnp.int32),
            ],
            (
                place, jnp.stack([net.target(spot_block), spot_slot]), tokens, key_route,
                query_large, key_large, value_large,
                gate_small, up_small, down_small.T, gate_large, up_large, down_large.T,
            ),
            smem=1,
            room=56 << 20,
        )
    else:
        second_set = jnp.concatenate([query_large, key_large, value_large], axis=1)
        third_set = jnp.concatenate([gate_small, up_small, down_small.T], axis=1)
        stacked = jnp.stack([gate_large, up_large, down_large.T], axis=0)
        stacked = stacked.reshape(3, part, members, share).transpose(2, 1, 0, 3)
        stacked = jnp.take(stacked.reshape(members, part, 3 * share), net.members(), axis=0)
        slices_keep, slices_send = stacked.reshape(2, net.depth * part, 3 * share)
    order = Order()
    top_bit = net.levels - 1

    def take_z(pieces):
        return order.note(stack_rows([order.hold(pieces[0])] + pieces[1:]))

    def take(whole, moved):
        return order.note(stack_rows([whole, order.hold(moved)]))

    def first_moved(whole):
        return net.by_bit(whole, 0)

    def rest_moved(whole, moved):
        for j in range(1, net.levels):
            whole = take(whole, moved)
            moved = net.by_bit(whole, j)
        return whole, moved

    order.note(second_set)
    first_set = take_z(first_parts)
    first_moving = first_moved(first_set)
    second_parts = net.from_z(after(second_set, first_set))
    slices_got = net.by_core(slices_send)
    to_own, to_slice = run(orders_body, "orders", [square, square], (order.hold(orders),))
    order.note(to_own)
    third_parts = pair_up(third_set, order.hold(slices_keep), slices_got, part)
    order.note(third_parts[0])
    first_set, first_moving = rest_moved(first_set, first_moving)
    second_set = take_z(second_parts)
    third_parts = net.exchange_z([after(p, second_set) for p in third_parts])
    cot, query_select, key_select, feed_select, query_docs = run(
        select_body,
        "select",
        [((rows, width), BF16), chosen, chosen, chosen, ((slots, 1), jnp.int32)],
        (place, to_own, query_route, key_route, feed_route, order.hold(cotangent)),
        smem=1,
    )
    order.note(cot)
    a0 = take(first_set, first_moving)
    a1 = net.by_core(a0)
    f0, f1 = (Columns(a, 0, cut) for a in (a0, a1))
    o0, o1 = (Columns(a, cut, a0.shape[1]) for a in (a0, a1))
    second_moving = first_moved(after(second_set, a0))
    second_set, second_moving = rest_moved(second_set, second_moving)
    third_set = order.note(stack_both([order.hold(third_parts[0])] + third_parts[1:], "weave"))
    third_moving = first_moved(third_set)
    near_tokens = after(tokens, third_set)
    above = lax.ppermute(near_tokens[rows - RADIUS :], AXES, step)
    below = lax.ppermute(near_tokens[:RADIUS], AXES, back)
    s0 = take(second_set, second_moving)
    s1 = net.by_core(s0)
    (raw,) = run(
        prepare_body,
        "prepare",
        [((rows + 2 * RADIUS, width), BF16)],
        (order.hold(to_own), above, tokens, below),
    )
    order.note(raw)

    normed_ext, query_rows, pair_rows, vectors = run(
        light_rows_body,
        "light_rows",
        [
            ((rows + 2 * RADIUS, width), BF16),
            ((rows, light), BF16),
            ((rows + 2 * RADIUS, 2 * light), BF16),
            ((8, width), F32),
        ],
        (order.hold(raw), f0, f1),
    )
    order.note(query_rows)
    for j in range(1, net.levels):
        third_set = order.note(stack_both([third_set, order.hold(third_moving)]))
        third_moving = net.by_bit(third_set, j)
    light_mixed, light_sums = run(
        light_forward_body,
        "light_forward",
        [((rows, light), BF16), ((rows, 128), F32)],
        (place, order.hold(query_rows), pair_rows),
        smem=1,
    )
    order.note(light_mixed)
    if packed:
        (keyed,) = run(
            functools.partial(heavy_rows_body, slots),
            "heavy_rows",
            [((keys, width), BF16)],
            (order.hold(vectors), to_own, s0, s1),
            scratch=[pltpu.VMEM((keys, width), BF16)],
        )
        order.note(keyed)
        heavy_pairs, routed, routed_query = run(
            heavy_pairs_body,
            "heavy_pairs",
            [((keys, 2 * heavy), BF16), ((slots, width), BF16), ((slots, heavy), BF16)],
            (order.hold(query_select), normed_ext, keyed, s0, s1),
        )
        order.note(routed_query)
        heavy_mixed, heavy_sums = run(
            heavy_forward_body,
            "heavy_forward",
            [((slots, heavy), BF16), ((2 * slots, 128), F32)],
            (query_docs, key_docs, order.hold(routed_query), heavy_pairs),
        )
    else:
        relative = net.target(jnp.arange(blocks, dtype=jnp.int32))
        near_routes = jnp.take(key_route, relative, axis=0)
        key_docs = document_of(relative[:, None] * rows + near_routes, lengths)
        key_docs = jnp.where(near_routes < rows, key_docs, -1).reshape(1, -1)
        keyed_raw = net.gather(nn(key_select, tokens).astype(BF16))
        keyed, heavy_pairs, routed, routed_query, heavy_mixed, heavy_sums = heavy_forward_wide(
            query_docs, key_docs, query_select, normed_ext, vectors, to_own,
            s0, s1, jnp.concatenate(keyed_raw, axis=0),
        )
    order.note(heavy_mixed)

    middle, normed_two, heavy_branch, feed_rows, feed_grads, sent = run(
        join_body,
        "join",
        [
            ((rows, width), F32),
            ((rows, width), BF16),
            ((slots, width), F32),
            ((slots, width), BF16),
            ((slots, width), F32),
            ((slots, 2 * width), BF16),
        ],
        (
            raw, light_mixed, order.hold(heavy_mixed), routed, query_select, feed_select, vectors, cot, to_own, o0, o1,
        ),
    )
    order.note(sent)

    got_parts = net.from_z(sent)
    got0 = take_z(got_parts)
    got1 = net.by_core(got0)
    t0, expert = part_both([third_set, order.hold(third_moving)], "part_both")
    order.note(t0)
    t1 = net.by_core(t0)
    keep, send, expert_keep, expert_send = run(
        expert_body,
        "expert",
        [
            ((pooled // 2, 2 * width), BF16),
            ((pooled // 2, 2 * width), BF16),
            ((half // 2, 6 * share), BF16),
            ((half // 2, 6 * share), BF16),
        ],
        (order.hold(got0), got1, to_slice, expert),
        scratch=[
            pltpu.VMEM((pooled, width), BF16),
            pltpu.VMEM((pooled, width), BF16),
            pltpu.VMEM((pooled, 2 * share), F32),
            pltpu.VMEM((pooled, share), F32),
            pltpu.VMEM((pooled, share), BF16),
            pltpu.VMEM((pooled, 2 * share), BF16),
        ],
    )
    order.note(send)
    moving = net.by_core(send)
    expert_moving = net.by_bit(expert_send, top_bit)
    feed_light, grad_normed, hidden, hidden_grads = run(
        feed_body,
        "feed",
        [
            ((rows, width), F32),
            ((rows, width), F32),
            ((rows, narrow), BF16),
            ((rows, 2 * narrow), BF16),
        ],
        (order.hold(normed_two), cot, t0, t1),
        scratch=[pltpu.VMEM((rows, 2 * narrow), F32), pltpu.VMEM((rows, narrow), F32)],
    )
    order.note(hidden)
    def give(keep, moved, pieces):
        out = fold(keep, order.hold(moved), pieces)
        order.note(out[0])
        return out

    def descend(keep, moved):
        for j in reversed(range(net.levels - 1)):
            keep, send = give(keep, moved, 2)
            moved = net.by_bit(send, j)
        return keep, moved

    summed = net.exchange_z(give(keep, moving, net.depth))
    third_keep, third_send = run(
        feed_weight_body,
        "feed_weight",
        [((half, 3 * narrow), BF16), ((half, 3 * narrow), BF16)],
        (order.hold(normed_two), cot, hidden, hidden_grads),
    )
    order.note(third_send)
    third_moving = net.by_core(third_send)

    third_keep, third_send = give(third_keep, third_moving, 2)
    third_moving = net.by_bit(third_send, top_bit)

    result, grad_middle, feed_vectors = run(
        turn_body,
        "turn",
        [((rows, width), BF16), ((rows, width), F32), ((8, width), F32)],
        (
            order.hold(summed[0]), *summed[1:], middle, feed_light, grad_normed, feed_rows, feed_grads, feed_select,
            vectors, cot, to_own,
        ),
    )
    order.note(grad_middle)
    if packed:
        grad_branch, grad_queries, grad_heavy_pairs, logits = run(
            heavy_scores_body,
            "heavy_scores",
            [
                ((slots, width), BF16),
                ((slots, heavy), BF16),
                ((keys, 2 * heavy), BF16),
                ((slots, 128), F32),
            ],
            (
                query_docs, key_docs, order.hold(grad_middle), query_select, routed, heavy_pairs, routed_query,
                heavy_branch, heavy_sums, vectors, o0, o1,
            ),
            scratch=[pltpu.VMEM((slots, heavy), BF16)],
        )
        order.note(grad_branch)
    expert_keep, expert_moving = descend(expert_keep, expert_moving)
    if packed:
        second_keep, second_send, heavy_vectors = run(
            heavy_weights_body,
            "heavy_weights",
            [
                ((half, 5 * width + light + width * rest // part), BF16),
                ((half, 5 * width + light + width * rest // part), BF16),
                ((8, width), F32),
            ],
            (
                grad_middle, routed, keyed, light_mixed, heavy_mixed, order.hold(grad_branch), grad_queries,
                grad_heavy_pairs, logits, vectors, to_own, s0, s1,
            ),
            scratch=[pltpu.VMEM((keys, width), BF16)],
        )
    else:
        second_keep, second_send, grad_routed, heavy_vectors, keyed_grads = heavy_backward_wide(
            grad_middle, query_select, routed, keyed, heavy_pairs, routed_query, light_mixed, heavy_mixed,
            heavy_branch, heavy_sums, vectors, to_own, o0.array[:, cut:], o1.array[:, cut:], s0, s1,
        )
    order.note(second_send)
    second_moving = net.by_core(second_send)
    third_keep, third_moving = descend(third_keep, third_moving)
    expert_parts = net.exchange_z(give(expert_keep, expert_moving, net.depth))
    if packed:
        (grad_routed,) = run(
            routed_body,
            "routed",
            [((slots, width), F32)],
            (order.hold(grad_queries), logits, vectors, s0, s1),
        )
        order.note(grad_routed)
    second_keep, second_send = give(second_keep, second_moving, 2)
    second_moving = net.by_bit(second_send, top_bit)
    grad_queries, grad_pairs = run(
        light_scores_body,
        "light_scores",
        [((rows, light), BF16), ((rows + 2 * RADIUS, 2 * light), BF16)],
        (place, order.hold(grad_middle), query_rows, pair_rows, light_sums, o0, o1),
        smem=1,
        scratch=[pltpu.VMEM((rows + 2 * RADIUS, 2 * light), F32), pltpu.VMEM((rows, light), BF16)],
    )
    order.note(grad_queries)
    third_parts = net.exchange_z(give(third_keep, third_moving, net.depth))
    first_keep, first_send, outer, grad_mine = run(
        light_weights_body,
        "light_weights",
        [
            ((half, 3 * light + 128), BF16),
            ((half, 3 * light + 128), BF16),
            ((2 * RADIUS, width), BF16),
            ((rows, width), F32),
        ],
        (
            raw, normed_ext, order.hold(grad_queries), grad_pairs, grad_routed, query_select, feed_vectors, heavy_vectors,
            to_own, f0, f1,
        ),
    )
    order.note(first_send)
    first_moving = net.by_core(first_send)
    from_next = lax.ppermute(outer[:RADIUS], AXES, back)
    from_prev = lax.ppermute(outer[RADIUS:], AXES, step)

    expert_keep, expert_send = take_apart([order.hold(expert_parts[0])] + expert_parts[1:], part)
    order.note(expert_send)
    expert_got = net.by_core(expert_send)
    third_grad = settle([order.hold(third_parts[0])] + third_parts[1:], [narrow] * 3, "settle_third")
    order.note(third_grad[0])
    second_keep, second_moving = descend(second_keep, second_moving)
    first_keep, first_send = give(first_keep, first_moving, 2)
    first_moving = net.by_bit(first_send, top_bit)
    (grad_near,) = run(
        halo_body, "halo", [((rows, width), F32)], (from_prev, from_next, order.hold(grad_mine), to_own)
    )
    order.note(grad_near)
    if packed:
        gate_grad, up_grad, down_grad = run(
            unpack_body,
            "unpack",
            [((part, wide), F32)] * 3,
            (place, order.hold(expert_keep), expert_got),
            smem=1,
        )
    else:
        expert_grad = jnp.concatenate([order.hold(expert_keep), expert_got], axis=0)
        expert_grad = jnp.take(expert_grad.reshape(members, part, 3 * share), net.members(), axis=0)
        expert_grad = expert_grad.reshape(members, part, 3, share).transpose(2, 1, 0, 3)
        gate_grad, up_grad, down_grad = expert_grad.reshape(3, part, wide).astype(F32)
    order.note(gate_grad)
    second_parts = net.exchange_z(give(second_keep, second_moving, net.depth))
    first_keep, first_moving = descend(first_keep, first_moving)
    first_parts = net.exchange_z(give(first_keep, first_moving, net.depth))
    widths = [width, light, heavy, heavy, heavy]
    if packed:
        widths.append(width + width * rest // part)
    second_grad = settle([order.hold(second_parts[0])] + second_parts[1:], widths, "settle_second")
    order.note(second_grad[0])
    if packed:
        keyed_own = second_grad[5]
    else:
        cut = keys // 2
        keyed_own = settle(net.reduce(keyed_grads[:cut], keyed_grads[cut:]), [width], "settle_keyed")[0]
    (tokens_grad,) = run(
        finish_body,
        "finish",
        [((rows, width), F32)],
        (order.hold(keyed_own), key_select, grad_near, grad_middle, raw, vectors, to_own),
    )
    order.note(tokens_grad)
    first_grad = settle(
        [order.hold(first_parts[0])] + first_parts[1:], [light, light, light, 128], "settle_first"
    )
    vector_out = first_grad[3][:, :4].T
    return (
        result,
        tokens_grad,
        first_grad[0],
        first_grad[1],
        first_grad[2],
        second_grad[1].T,
        second_grad[2],
        second_grad[3],
        second_grad[4],
        second_grad[0].T,
        vector_out[0],
        vector_out[1],
        third_grad[0],
        third_grad[1],
        third_grad[2].T,
        gate_grad,
        up_grad,
        down_grad.T,
        vector_out[2],
        vector_out[3],
    )


def solution(mesh):
    by_rows = P(AXES, None)
    by_columns = P(None, AXES)
    vector = P(AXES)
    return jax.shard_map(
        per_device,
        mesh=mesh,
        in_specs=(
            by_rows,
            by_rows,
            by_rows,
            by_rows,
            by_columns,
            by_rows,
            by_rows,
            by_rows,
            by_columns,
            vector,
            vector,
            by_rows,
            by_rows,
            by_columns,
            by_rows,
            by_rows,
            by_columns,
            vector,
            vector,
            P(),
            P(),
            P(),
            by_rows,
            by_rows,
        ),
        out_specs=(
            by_rows,
            by_rows,
            by_rows,
            by_rows,
            by_rows,
            by_columns,
            by_rows,
            by_rows,
            by_rows,
            by_columns,
            vector,
            vector,
            by_rows,
            by_rows,
            by_columns,
            by_rows,
            by_rows,
            by_columns,
            vector,
            vector,
        ),
        check_vma=False,
    )
```
